512 devices in a mesh: dp: 2 (over core), ctx: 64 (over z, y), head: 4 (over x).
Axes of the slice: x: 4, y: 8, z: 8, core: 2. Of those that a mesh axis runs over, the one named last changes fastest.
Arguments:
- queries: bfloat16 [2, 8192, 2560], P('dp', 'ctx', 'head'), may hold values from -25 to 25
- keys: bfloat16 [2, 8192, 2560], P('dp', 'ctx', 'head'), may hold values from -25 to 25
- values: bfloat16 [2, 8192, 2560], P('dp', 'ctx', 'head'), may hold values from -6 to 6
- grad_y: bfloat16 [2, 8192, 2560], P('dp', 'ctx', 'head'), may hold values from -6 to 6
- out_gain: float32 [2560], P('head'), may hold values from 0.1 to 1.9
- offsets: int32 [2, 20], P(None, 'head'), may hold values from 0 to 63, as said below
Outputs:
- attended: bfloat16 [2, 8192, 2560], P('dp', 'ctx', 'head')
- query_grad: bfloat16 [2, 8192, 2560], P('dp', 'ctx', 'head')
- key_grad: bfloat16 [2, 8192, 2560], P('dp', 'ctx', 'head')
- value_grad: bfloat16 [2, 8192, 2560], P('dp', 'ctx', 'head')
- gain_grad: float32 [2560], P('head')
The draws below stay inside these ranges and needn't reach their ends.
Inputs may be any that keep to these rules, and one draw needn't show every extreme that they name: Row 0 holds offsets below 8, row 1 offsets below 64.
All inputs are finite; a program needn't handle non-finite values.
Results may differ from the reference program's by a relative error of at most 0.011.
Values may be sent and summed in bfloat16 or wider, within the bound.
A program may use at most 64 MiB of HBM per device.

```python
import math
import jax
import jax.numpy as jnp
from jax import lax

D = 2560
HEADS = 20
TOK_DEV = 128
SPAN = 4
R1 = 8
SEQS = 2
LEN = 8192
R2 = 64


def paired_rows(base_key):
    shape = (SEQS, LEN, D)
    split_keys = jax.random.split(base_key, 2)
    base_rows = jnp.clip(jax.random.normal(split_keys[0], shape, jnp.float32), -4.5, 4.5)
    other_rows = jnp.clip(jax.random.normal(split_keys[1], shape, jnp.float32), -4.5, 4.5)
    query_rows = base_rows
    key_rows = other_rows
    return (query_rows, key_rows)


def draw_queries(key, part):
    return paired_rows(jax.random.fold_in(key, 11))[0].astype(jnp.bfloat16)


def draw_keys(key, part):
    return paired_rows(jax.random.fold_in(key, 11))[1].astype(jnp.bfloat16)


def draw_offsets(key, part):
    split_keys = jax.random.split(key, 5)
    head_ids = jnp.arange(HEADS, dtype=jnp.int32)
    middle = jax.random.randint(split_keys[0], (HEADS,), 0, R1, dtype=jnp.int32)
    outer = jax.random.randint(split_keys[1], (HEADS,), 0, R2, dtype=jnp.int32)
    low_head = jax.random.randint(split_keys[2], (), 0, HEADS, dtype=jnp.int32)
    step_head = jax.random.randint(split_keys[3], (), 1, HEADS, dtype=jnp.int32)
    high_head = (low_head + step_head) % HEADS
    outer_head = jax.random.randint(split_keys[4], (), 0, HEADS, dtype=jnp.int32)
    middle = jnp.where(head_ids == high_head, R1 - 1, middle)
    middle = jnp.where(head_ids == low_head, 0, middle)
    outer = jnp.where(head_ids == outer_head, R2 - 1, outer)
    return jnp.stack([middle, outer]).astype(jnp.int32)


def levels(stream_key, shape, pieces, smallest, top_value):
    def one(position, blocks):
        heights = jax.random.uniform(jax.random.fold_in(jax.random.fold_in(stream_key, 6), position), (blocks,), jnp.float32, smallest / len(pieces), top_value / len(pieces))
        return jnp.repeat(jnp.exp(heights), shape[position] // blocks).reshape((-1,) + (1,) * (len(shape) - position - 1))

    factor_of = one(*pieces[0])
    for cut in pieces[1:]:
        factor_of = factor_of * one(*cut)
    return factor_of


def noise(rng, dims, scale, most, shards=(), kind=jnp.bfloat16):
    factor_of = levels(rng, dims, shards, -0.22, 0.18) if shards else 1.0
    array = jax.random.normal(rng, dims, jnp.float32) * scale * factor_of
    return jnp.minimum(jnp.maximum(array, -most), most).astype(kind)


def setup_inputs(seed: int = 0) -> dict:
    arg_keys = jax.random.split(jax.random.key(seed), 7)
    queries = draw_queries(jax.random.fold_in(arg_keys[6], 71), 0)
    keys = draw_keys(jax.random.fold_in(arg_keys[6], 71), 0)
    values = noise(arg_keys[2], (SEQS, LEN, D), 1.0, 6.0, ((0, 2), (1, 64), (2, 4)))
    grad_y = noise(arg_keys[3], (SEQS, LEN, D), 1.0, 6.0, ((0, 2), (1, 64), (2, 4)))
    out_gain = jnp.clip(1.0 + 0.18 * jax.random.normal(arg_keys[4], (D,), jnp.float32), 0.1, 1.9)
    offsets = draw_offsets(jax.random.fold_in(arg_keys[6], 71), 0)
    return dict(queries=queries, keys=keys, values=values, grad_y=grad_y, out_gain=out_gain, offsets=offsets)


EPS = 1e-06

def pick_rows(source_rows, dilation, shifts):
    seq_count, row_count, head_count, head_width = source_rows.shape
    grouped = source_rows.reshape(seq_count, row_count // dilation, dilation, head_count, head_width)
    pick_index = jnp.broadcast_to(shifts.astype(jnp.int32).reshape(1, 1, 1, head_count, 1), (seq_count, row_count // dilation, 1, head_count, head_width))
    return jnp.take_along_axis(grouped, pick_index, axis=2)[:, :, 0]

def place_rows(row_values, dilation, shifts):
    seq_count, row_count, head_count, head_width = row_values.shape
    hit_mask = jnp.arange(dilation, dtype=jnp.int32).reshape(1, 1, dilation, 1, 1) == shifts.astype(jnp.int32).reshape(1, 1, 1, head_count, 1)
    spread = jnp.where(hit_mask, row_values[:, :, None], jnp.zeros((), row_values.dtype))
    return spread.reshape(seq_count, row_count * dilation, head_count, head_width)

def to_segments(row_values, per_seg):
    seq_count, row_count, head_count, head_width = row_values.shape
    split_rows = row_values.reshape(seq_count, row_count // per_seg, per_seg, head_count, head_width)
    return jnp.transpose(split_rows, (3, 0, 1, 2, 4)).reshape(head_count, seq_count * (row_count // per_seg), per_seg, head_width)

def from_segments(blocks, seq_count):
    head_count, groups, per_seg, head_width = blocks.shape
    split_rows = blocks.reshape(head_count, seq_count, groups // seq_count, per_seg, head_width)
    return jnp.transpose(split_rows, (1, 2, 3, 0, 4)).reshape(seq_count, groups // seq_count * per_seg, head_count, head_width)

def level_scores(q_rows, k_rows):
    score_scale = 1.0 / math.sqrt(q_rows.shape[-1])
    return jnp.einsum('gqe,gke->gqk', q_rows.astype(jnp.float32), k_rows.astype(jnp.float32)) * score_scale

def forward_block(inputs):
    q_rows, k_rows, v_rows = inputs
    scores = level_scores(q_rows, k_rows)
    row_max = lax.optimization_barrier(jnp.max(scores, axis=-1, keepdims=True))
    log_total = row_max[..., 0] + jnp.log(lax.optimization_barrier(jnp.sum(jnp.exp(scores - row_max), axis=-1)))
    soft_rows = jnp.exp(scores - log_total[..., None]).astype(jnp.bfloat16)
    level_out = jnp.einsum('gqk,gke->gqe', soft_rows.astype(jnp.float32), v_rows.astype(jnp.float32))
    return (level_out, log_total)

def backward_block(inputs):
    q_rows, k_rows, v_rows, log_total, grad_out, row_shift = inputs
    score_scale = 1.0 / math.sqrt(q_rows.shape[-1])
    scores = level_scores(q_rows, k_rows)
    exact_soft = jnp.exp(scores - log_total[..., None])
    grad_low = grad_out.astype(jnp.bfloat16)
    prob_grad = jnp.einsum('gqe,gke->gqk', grad_low.astype(jnp.float32), v_rows.astype(jnp.float32))
    score_grad = (exact_soft * (prob_grad + row_shift[..., None]) * score_scale).astype(jnp.bfloat16)
    soft_low = exact_soft.astype(jnp.bfloat16)
    q_part = jnp.einsum('gqk,gke->gqe', score_grad.astype(jnp.float32), k_rows.astype(jnp.float32))
    k_part = jnp.einsum('gqk,gqe->gke', score_grad.astype(jnp.float32), q_rows.astype(jnp.float32))
    v_part = jnp.einsum('gqk,gqe->gke', soft_low.astype(jnp.float32), grad_low.astype(jnp.float32))
    return (q_part, k_part, v_part)

def reference(queries, keys, values, grad_y, out_gain, offsets):
    seq_count, seq_len, model_width = queries.shape
    head_count = HEADS
    head_width = model_width // head_count
    full_shape = (seq_count, seq_len, head_count, head_width)
    q_all = queries.reshape(full_shape)
    k_all = keys.reshape(full_shape)
    v_all = values.reshape(full_shape)
    plans = ((1, TOK_DEV, jnp.zeros((head_count,), jnp.int32)), (R1, SPAN * TOK_DEV, offsets[0]), (R2, seq_len, offsets[1]))
    positions = jnp.arange(seq_len, dtype=jnp.int32)
    level_out = []
    level_total = []
    level_hit = []
    level_parts = []
    level_blocks = []
    for dilation, segment, shifts in plans:
        per_seg = segment // dilation
        parts = tuple((to_segments(pick_rows(source_rows, dilation, shifts), per_seg) for source_rows in (q_all, k_all, v_all)))
        out_blocks, total_blocks = lax.map(forward_block, parts)
        compact_out = from_segments(out_blocks, seq_count)
        compact_total = from_segments(total_blocks[..., None], seq_count)
        level_out.append(place_rows(compact_out, dilation, shifts))
        level_total.append(place_rows(compact_total, dilation, shifts)[..., 0])
        level_hit.append((positions % dilation)[None, :, None] == shifts.astype(jnp.int32)[None, None, :])
        level_parts.append(parts)
        level_blocks.append(total_blocks)
    row_max = level_total[0]
    for level in (1, 2):
        row_max = jnp.maximum(row_max, jnp.where(level_hit[level], level_total[level], level_total[0]))
    expos = [jnp.where(level_hit[level], jnp.exp(level_total[level] - row_max), 0.0) for level in range(3)]
    denom = expos[0] + expos[1] + expos[2]
    shares = [expo / denom for expo in expos]
    attn = shares[0][..., None] * level_out[0] + shares[1][..., None] * level_out[1] + shares[2][..., None] * level_out[2]
    inv_rms = lax.rsqrt(lax.optimization_barrier(jnp.mean(attn * attn, axis=-1, keepdims=True)) + EPS)
    normed = attn * inv_rms
    gain_rows = out_gain.reshape(head_count, head_width)
    attended = (normed * gain_rows).astype(jnp.bfloat16).reshape(seq_count, seq_len, model_width)
    grad_full = grad_y.astype(jnp.float32).reshape(full_shape)
    gain_grad = lax.optimization_barrier(jnp.sum(grad_full * normed, axis=(0, 1))).reshape(model_width)
    grad_norm = grad_full * gain_rows
    grad_attn = inv_rms * (grad_norm - normed * lax.optimization_barrier(jnp.mean(grad_norm * normed, axis=-1, keepdims=True)))
    inner = lax.optimization_barrier(jnp.sum(grad_attn * attn, axis=-1))
    sums = []
    for level, (dilation, segment, shifts) in enumerate(plans):
        per_seg = segment // dilation
        share_sel = pick_rows(shares[level][..., None], dilation, shifts)[..., 0]
        grad_out = share_sel[..., None] * pick_rows(grad_attn, dilation, shifts)
        row_shift = -(share_sel * pick_rows(inner[..., None], dilation, shifts)[..., 0])
        q_seg, k_seg, v_seg = level_parts[level]
        shift_seg = to_segments(row_shift[..., None], per_seg)[..., 0]
        grads = lax.map(backward_block, (q_seg, k_seg, v_seg, level_blocks[level], to_segments(grad_out, per_seg), shift_seg))
        sums.append(tuple((place_rows(from_segments(part, seq_count), dilation, shifts) for part in grads)))
    outputs = []
    for which in range(3):
        total = sums[0][which] + sums[1][which] + sums[2][which]
        outputs.append(total.astype(jnp.bfloat16).reshape(seq_count, seq_len, model_width))
    return (attended, outputs[0], outputs[1], outputs[2], gain_grad)
```

```python
import math

import jax
import jax.numpy as jnp
from jax import lax
from jax.sharding import PartitionSpec as P

HEAD_DIM = 128
SPAN = 4
R1 = 8


EPS = 1e-06


def group_gather(block, axis, group):
    count = lax.axis_size(axis)
    pieces = [block]
    for shift in range(1, group):
        route = []
        for src in range(count):
            base = src - src % group
            route.append((src, base + (src % group + shift) % group))
        pieces.append(lax.ppermute(block, axis, route))
    return jnp.concatenate(pieces, 0)


def pick_rows(source_rows, dilation, shifts):
    row_count, head_count, head_width = source_rows.shape
    grouped = source_rows.reshape(row_count // dilation, dilation, head_count, head_width)
    hit_mask = jnp.arange(dilation, dtype=jnp.int32).reshape(1, dilation, 1, 1) == shifts.reshape(
        1, 1, head_count, 1
    )
    chosen = jnp.where(hit_mask, grouped, jnp.zeros((), source_rows.dtype))
    return jnp.sum(chosen, axis=1, dtype=source_rows.dtype)


def place_rows(row_values, dilation, shifts):
    row_count, head_count, head_width = row_values.shape
    hit_mask = jnp.arange(dilation, dtype=jnp.int32).reshape(1, dilation, 1, 1) == shifts.reshape(
        1, 1, head_count, 1
    )
    spread = jnp.where(hit_mask, row_values[:, None], jnp.zeros((), row_values.dtype))
    return spread.reshape(row_count * dilation, head_count, head_width)


def level_scores(q_rows, k_rows):
    score_scale = 1.0 / math.sqrt(q_rows.shape[-1])
    return (
        jnp.einsum("qhe,khe->hqk", q_rows, k_rows, preferred_element_type=jnp.float32) * score_scale
    )


def attend(q_rows, k_rows, v_rows):
    scores = level_scores(q_rows, k_rows)
    row_max = jnp.max(scores, axis=-1, keepdims=True)
    log_total = row_max[..., 0] + jnp.log(jnp.sum(jnp.exp(scores - row_max), axis=-1))
    soft_rows = jnp.exp(scores - log_total[..., None]).astype(jnp.bfloat16)
    level_out = jnp.einsum("hqk,khe->qhe", soft_rows, v_rows, preferred_element_type=jnp.float32)
    return (level_out, log_total.T)


def score_grads(q_rows, k_rows, v_rows, log_total, grad_low, row_shift):
    score_scale = 1.0 / math.sqrt(q_rows.shape[-1])
    scores = level_scores(q_rows, k_rows)
    exact_soft = jnp.exp(scores - log_total.T[..., None])
    prob_grad = jnp.einsum("qhe,khe->hqk", grad_low, v_rows, preferred_element_type=jnp.float32)
    score_grad = (exact_soft * (prob_grad + row_shift.T[..., None]) * score_scale).astype(
        jnp.bfloat16
    )
    return (score_grad, exact_soft.astype(jnp.bfloat16))


def key_parts(score_grad, soft_low, q_rows, grad_low):
    k_part = jnp.einsum("hqk,qhe->khe", score_grad, q_rows, preferred_element_type=jnp.float32)
    v_part = jnp.einsum("hqk,qhe->khe", soft_low, grad_low, preferred_element_type=jnp.float32)
    return (k_part, v_part)


def query_part(score_grad, k_rows):
    return jnp.einsum("hqk,khe->qhe", score_grad, k_rows, preferred_element_type=jnp.float32)


def split_qkv(packed, head_count):
    width = head_count * HEAD_DIM
    shape = (packed.shape[0], head_count, HEAD_DIM)
    return tuple(packed[:, i * width : (i + 1) * width].reshape(shape) for i in range(3))


def pack_grads(grad_low, row_shift):
    rows = grad_low.shape[0]
    return jnp.concatenate(
        [grad_low.astype(jnp.float32).reshape(rows, -1), row_shift.astype(jnp.float32)], 1
    )


def unpack_grads(packed, head_count):
    width = head_count * HEAD_DIM
    grad_low = packed[:, :width].astype(jnp.bfloat16).reshape(-1, head_count, HEAD_DIM)
    return grad_low, packed[:, width:]


def shards(queries, keys, values, grad_y, out_gain, offsets):
    tokens = queries.shape[1]
    flat_width = queries.shape[2]
    head_count = flat_width // HEAD_DIM
    row_shape = (tokens, head_count, HEAD_DIM)
    q_own = queries[0].reshape(row_shape)
    k_own = keys[0].reshape(row_shape)
    v_own = values[0].reshape(row_shape)
    ctx_size = lax.axis_size("ctx")
    my_place = lax.axis_index("ctx")
    mid_shift = offsets[0]
    top_shift = offsets[1]
    positions = jnp.arange(tokens, dtype=jnp.int32)
    mid_hit = (positions % R1)[:, None] == mid_shift[None, :]
    top_hit = (positions % ctx_size)[:, None] == top_shift[None, :]
    mid_pack = jnp.concatenate(
        [pick_rows(x, R1, mid_shift).reshape(-1, flat_width) for x in (q_own, k_own, v_own)], 1
    )
    top_pack = jnp.concatenate(
        [pick_rows(x, ctx_size, top_shift).reshape(-1, flat_width) for x in (q_own, k_own, v_own)],
        1,
    )
    mid_rows = mid_pack.shape[0]
    top_rows = top_pack.shape[0]
    mid_all = group_gather(mid_pack, "ctx", SPAN)
    top_all = lax.all_gather(top_pack, "ctx", axis=0, tiled=True)
    mid_q, mid_k, mid_v = split_qkv(mid_all, head_count)
    top_q, top_k, top_v = split_qkv(top_all, head_count)
    top_start = my_place * top_rows
    base_out, base_total = attend(q_own, k_own, v_own)
    mid_out_all, mid_total_all = attend(mid_q, mid_k, mid_v)
    top_out_all, top_total_all = attend(top_q, top_k, top_v)
    mid_out = mid_out_all[:mid_rows]
    mid_total = mid_total_all[:mid_rows]
    top_out = lax.dynamic_slice_in_dim(top_out_all, top_start, top_rows, 0)
    top_total = lax.dynamic_slice_in_dim(top_total_all, top_start, top_rows, 0)
    mid_full = place_rows(mid_total[..., None], R1, mid_shift)[..., 0]
    top_full = place_rows(top_total[..., None], ctx_size, top_shift)[..., 0]
    row_max = jnp.maximum(base_total, jnp.where(mid_hit, mid_full, base_total))
    row_max = jnp.maximum(row_max, jnp.where(top_hit, top_full, base_total))
    base_expo = jnp.exp(base_total - row_max)
    mid_expo = jnp.where(mid_hit, jnp.exp(mid_full - row_max), 0.0)
    top_expo = jnp.where(top_hit, jnp.exp(top_full - row_max), 0.0)
    denom = base_expo + mid_expo + top_expo
    base_share = base_expo / denom
    mid_share = mid_expo / denom
    top_share = top_expo / denom
    attn = (
        base_share[..., None] * base_out
        + mid_share[..., None] * place_rows(mid_out, R1, mid_shift)
        + top_share[..., None] * place_rows(top_out, ctx_size, top_shift)
    )
    inv_rms = lax.rsqrt(jnp.mean(attn * attn, axis=-1, keepdims=True) + EPS)
    normed = attn * inv_rms
    gain_rows = out_gain.reshape(head_count, HEAD_DIM)
    attended = (normed * gain_rows).astype(jnp.bfloat16).reshape(1, tokens, flat_width)
    grad_full = grad_y[0].reshape(row_shape).astype(jnp.float32)
    gain_part = jnp.sum(grad_full * normed, axis=0).reshape(flat_width)
    gain_grad = lax.psum(gain_part, ("dp", "ctx"))
    grad_norm = grad_full * gain_rows
    grad_attn = inv_rms * (
        grad_norm - normed * jnp.mean(grad_norm * normed, axis=-1, keepdims=True)
    )
    inner = jnp.sum(grad_attn * attn, axis=-1)
    base_low = (base_share[..., None] * grad_attn).astype(jnp.bfloat16)
    base_shift = -(base_share * inner)
    base_grad, base_soft = score_grads(q_own, k_own, v_own, base_total, base_low, base_shift)
    base_dq = query_part(base_grad, k_own)
    base_dk, base_dv = key_parts(base_grad, base_soft, q_own, base_low)

    mid_sel = pick_rows(mid_share[..., None], R1, mid_shift)[..., 0]
    mid_low = (mid_sel[..., None] * pick_rows(grad_attn, R1, mid_shift)).astype(jnp.bfloat16)
    mid_row_shift = -(mid_sel * pick_rows(inner[..., None], R1, mid_shift)[..., 0])
    top_sel = pick_rows(top_share[..., None], ctx_size, top_shift)[..., 0]
    top_low = (top_sel[..., None] * pick_rows(grad_attn, ctx_size, top_shift)).astype(jnp.bfloat16)
    top_row_shift = -(top_sel * pick_rows(inner[..., None], ctx_size, top_shift)[..., 0])

    mid_low_all, mid_shift_all = unpack_grads(
        group_gather(pack_grads(mid_low, mid_row_shift), "ctx", SPAN), head_count
    )
    top_low_all, top_shift_all = unpack_grads(
        lax.all_gather(pack_grads(top_low, top_row_shift), "ctx", axis=0, tiled=True), head_count
    )

    mid_grad, mid_soft = score_grads(
        mid_q, mid_k, mid_v, mid_total_all, mid_low_all, mid_shift_all
    )
    mid_dq = query_part(mid_grad[:, :mid_rows], mid_k)
    mid_dk, mid_dv = key_parts(
        mid_grad[:, :, :mid_rows], mid_soft[:, :, :mid_rows], mid_q, mid_low_all
    )
    top_grad, top_soft = score_grads(
        top_q, top_k, top_v, top_total_all, top_low_all, top_shift_all
    )
    own_grad = lax.dynamic_slice_in_dim(top_grad, top_start, top_rows, 1)
    top_dq = query_part(own_grad, top_k)
    key_grad_cols = lax.dynamic_slice_in_dim(top_grad, top_start, top_rows, 2)
    key_soft_cols = lax.dynamic_slice_in_dim(top_soft, top_start, top_rows, 2)
    top_dk, top_dv = key_parts(key_grad_cols, key_soft_cols, top_q, top_low_all)
    query_grad = (
        base_dq + place_rows(mid_dq, R1, mid_shift) + place_rows(top_dq, ctx_size, top_shift)
    )
    key_grad = base_dk + place_rows(mid_dk, R1, mid_shift) + place_rows(top_dk, ctx_size, top_shift)
    value_grad = (
        base_dv + place_rows(mid_dv, R1, mid_shift) + place_rows(top_dv, ctx_size, top_shift)
    )
    out_shape = (1, tokens, flat_width)
    return (
        attended,
        query_grad.astype(jnp.bfloat16).reshape(out_shape),
        key_grad.astype(jnp.bfloat16).reshape(out_shape),
        value_grad.astype(jnp.bfloat16).reshape(out_shape),
        gain_grad,
    )


def solution(mesh):
    in_specs = (
        P("dp", "ctx", "head"),
        P("dp", "ctx", "head"),
        P("dp", "ctx", "head"),
        P("dp", "ctx", "head"),
        P("head"),
        P(None, "head"),
    )
    out_specs = (
        P("dp", "ctx", "head"),
        P("dp", "ctx", "head"),
        P("dp", "ctx", "head"),
        P("dp", "ctx", "head"),
        P("head"),
    )
    return jax.shard_map(shards, mesh=mesh, in_specs=in_specs, out_specs=out_specs, check_vma=False)
```

```python
import math

import jax
import jax.numpy as jnp
from jax import lax
from jax.sharding import PartitionSpec as P

HEAD_DIM = 128
SPAN = 4
R1 = 8


EPS = 1e-06


def group_gather(block, axis, group):
    count = lax.axis_size(axis)
    pieces = [block]
    for shift in range(1, group):
        route = []
        for src in range(count):
            base = src - src % group
            route.append((src, base + (src % group + shift) % group))
        pieces.append(lax.ppermute(block, axis, route))
    return jnp.concatenate(pieces, 0)


def pick_rows(source_rows, dilation, shifts):
    row_count, head_count, head_width = source_rows.shape
    grouped = source_rows.reshape(row_count // dilation, dilation, head_count, head_width)
    hit_mask = jnp.arange(dilation, dtype=jnp.int32).reshape(1, dilation, 1, 1) == shifts.reshape(
        1, 1, head_count, 1
    )
    chosen = jnp.where(hit_mask, grouped, jnp.zeros((), source_rows.dtype))
    return jnp.sum(chosen, axis=1, dtype=source_rows.dtype)


def place_rows(row_values, dilation, shifts):
    row_count, head_count, head_width = row_values.shape
    hit_mask = jnp.arange(dilation, dtype=jnp.int32).reshape(1, dilation, 1, 1) == shifts.reshape(
        1, 1, head_count, 1
    )
    spread = jnp.where(hit_mask, row_values[:, None], jnp.zeros((), row_values.dtype))
    return spread.reshape(row_count * dilation, head_count, head_width)


def level_scores(q_rows, k_rows):
    score_scale = 1.0 / math.sqrt(q_rows.shape[-1])
    return (
        jnp.einsum("qhe,khe->hqk", q_rows, k_rows, preferred_element_type=jnp.float32) * score_scale
    )


def attend(q_rows, k_rows, v_rows):
    scores = level_scores(q_rows, k_rows)
    row_max = jnp.max(scores, axis=-1, keepdims=True)
    log_total = row_max[..., 0] + jnp.log(jnp.sum(jnp.exp(scores - row_max), axis=-1))
    soft_rows = jnp.exp(scores - log_total[..., None]).astype(jnp.bfloat16)
    level_out = jnp.einsum("hqk,khe->qhe", soft_rows, v_rows, preferred_element_type=jnp.float32)
    return (level_out, log_total.T)


def score_grads(q_rows, k_rows, v_rows, log_total, grad_low, row_shift):
    score_scale = 1.0 / math.sqrt(q_rows.shape[-1])
    scores = level_scores(q_rows, k_rows)
    exact_soft = jnp.exp(scores - log_total.T[..., None])
    prob_grad = jnp.einsum("qhe,khe->hqk", grad_low, v_rows, preferred_element_type=jnp.float32)
    score_grad = (exact_soft * (prob_grad + row_shift.T[..., None]) * score_scale).astype(
        jnp.bfloat16
    )
    return (score_grad, exact_soft.astype(jnp.bfloat16))


def key_parts(score_grad, soft_low, q_rows, grad_low):
    k_part = jnp.einsum("hqk,qhe->khe", score_grad, q_rows, preferred_element_type=jnp.float32)
    v_part = jnp.einsum("hqk,qhe->khe", soft_low, grad_low, preferred_element_type=jnp.float32)
    return (k_part, v_part)


def query_part(score_grad, k_rows):
    return jnp.einsum("hqk,khe->qhe", score_grad, k_rows, preferred_element_type=jnp.float32)


def split_qkv(packed, head_count):
    width = head_count * HEAD_DIM
    shape = (packed.shape[0], head_count, HEAD_DIM)
    return tuple(packed[:, i * width : (i + 1) * width].reshape(shape) for i in range(3))


def pack_grads(grad_low, row_shift):
    rows = grad_low.shape[0]
    return jnp.concatenate(
        [grad_low.astype(jnp.float32).reshape(rows, -1), row_shift.astype(jnp.float32)], 1
    )


def unpack_grads(packed, head_count):
    width = head_count * HEAD_DIM
    grad_low = packed[:, :width].astype(jnp.bfloat16).reshape(-1, head_count, HEAD_DIM)
    return grad_low, packed[:, width:]


def shards(queries, keys, values, grad_y, out_gain, offsets):
    tokens = queries.shape[1]
    flat_width = queries.shape[2]
    head_count = flat_width // HEAD_DIM
    row_shape = (tokens, head_count, HEAD_DIM)
    q_own = queries[0].reshape(row_shape)
    k_own = keys[0].reshape(row_shape)
    v_own = values[0].reshape(row_shape)
    ctx_size = lax.axis_size("ctx")
    my_place = lax.axis_index("ctx")
    mid_shift = offsets[0]
    top_shift = offsets[1]
    positions = jnp.arange(tokens, dtype=jnp.int32)
    mid_hit = (positions % R1)[:, None] == mid_shift[None, :]
    top_hit = (positions % ctx_size)[:, None] == top_shift[None, :]
    mid_pack = jnp.concatenate(
        [pick_rows(x, R1, mid_shift).reshape(-1, flat_width) for x in (q_own, k_own, v_own)], 1
    )
    top_pack = jnp.concatenate(
        [pick_rows(x, ctx_size, top_shift).reshape(-1, flat_width) for x in (q_own, k_own, v_own)],
        1,
    )
    mid_rows = mid_pack.shape[0]
    top_rows = top_pack.shape[0]
    mid_all = group_gather(mid_pack, "ctx", SPAN)
    top_all = lax.all_gather(top_pack, "ctx", axis=0, tiled=True)
    mid_q, mid_k, mid_v = split_qkv(mid_all, head_count)
    top_q, top_k, top_v = split_qkv(top_all, head_count)
    top_start = my_place * top_rows
    base_out, base_total = attend(q_own, k_own, v_own)
    mid_out_all, mid_total_all = attend(mid_q, mid_k, mid_v)
    top_out_all, top_total_all = attend(top_q, top_k, top_v)
    mid_out = mid_out_all[:mid_rows]
    mid_total = mid_total_all[:mid_rows]
    top_out = lax.dynamic_slice_in_dim(top_out_all, top_start, top_rows, 0)
    top_total = lax.dynamic_slice_in_dim(top_total_all, top_start, top_rows, 0)
    mid_full = place_rows(mid_total[..., None], R1, mid_shift)[..., 0]
    top_full = place_rows(top_total[..., None], ctx_size, top_shift)[..., 0]
    row_max = jnp.maximum(base_total, jnp.where(mid_hit, mid_full, base_total))
    row_max = jnp.maximum(row_max, jnp.where(top_hit, top_full, base_total))
    base_expo = jnp.exp(base_total - row_max)
    mid_expo = jnp.where(mid_hit, jnp.exp(mid_full - row_max), 0.0)
    top_expo = jnp.where(top_hit, jnp.exp(top_full - row_max), 0.0)
    denom = base_expo + mid_expo + top_expo
    base_share = base_expo / denom
    mid_share = mid_expo / denom
    top_share = top_expo / denom
    attn = (
        base_share[..., None] * base_out
        + mid_share[..., None] * place_rows(mid_out, R1, mid_shift)
        + top_share[..., None] * place_rows(top_out, ctx_size, top_shift)
    )
    inv_rms = lax.rsqrt(jnp.mean(attn * attn, axis=-1, keepdims=True) + EPS)
    normed = attn * inv_rms
    gain_rows = out_gain.reshape(head_count, HEAD_DIM)
    attended = (normed * gain_rows).astype(jnp.bfloat16).reshape(1, tokens, flat_width)
    grad_full = grad_y[0].reshape(row_shape).astype(jnp.float32)
    gain_part = jnp.sum(grad_full * normed, axis=0).reshape(flat_width)
    grad_norm = grad_full * gain_rows
    grad_attn = inv_rms * (
        grad_norm - normed * jnp.mean(grad_norm * normed, axis=-1, keepdims=True)
    )
    inner = jnp.sum(grad_attn * attn, axis=-1)
    base_low = (base_share[..., None] * grad_attn).astype(jnp.bfloat16)
    base_shift = -(base_share * inner)
    base_grad, base_soft = score_grads(q_own, k_own, v_own, base_total, base_low, base_shift)
    base_dq = query_part(base_grad, k_own)
    base_dk, base_dv = key_parts(base_grad, base_soft, q_own, base_low)

    mid_sel = pick_rows(mid_share[..., None], R1, mid_shift)[..., 0]
    mid_low = (mid_sel[..., None] * pick_rows(grad_attn, R1, mid_shift)).astype(jnp.bfloat16)
    mid_row_shift = -(mid_sel * pick_rows(inner[..., None], R1, mid_shift)[..., 0])
    top_sel = pick_rows(top_share[..., None], ctx_size, top_shift)[..., 0]
    top_low = (top_sel[..., None] * pick_rows(grad_attn, ctx_size, top_shift)).astype(jnp.bfloat16)
    top_row_shift = -(top_sel * pick_rows(inner[..., None], ctx_size, top_shift)[..., 0])

    mid_low_all, mid_shift_all = unpack_grads(
        group_gather(pack_grads(mid_low, mid_row_shift), "ctx", SPAN), head_count
    )
    top_grads = pack_grads(top_low, top_row_shift)
    gain_row = jnp.pad(gain_part, (0, top_grads.shape[1] - flat_width))[None]
    gathered = lax.all_gather(jnp.concatenate([top_grads, gain_row], 0), "ctx", axis=0)
    top_low_all, top_shift_all = unpack_grads(
        gathered[:, :top_rows].reshape(-1, top_grads.shape[1]), head_count
    )
    gain_grad = lax.psum(jnp.sum(gathered[:, top_rows, :flat_width], axis=0), "dp")

    mid_grad, mid_soft = score_grads(
        mid_q, mid_k, mid_v, mid_total_all, mid_low_all, mid_shift_all
    )
    mid_dq = query_part(mid_grad[:, :mid_rows], mid_k)
    mid_dk, mid_dv = key_parts(
        mid_grad[:, :, :mid_rows], mid_soft[:, :, :mid_rows], mid_q, mid_low_all
    )
    top_grad, top_soft = score_grads(
        top_q, top_k, top_v, top_total_all, top_low_all, top_shift_all
    )
    own_grad = lax.dynamic_slice_in_dim(top_grad, top_start, top_rows, 1)
    top_dq = query_part(own_grad, top_k)
    key_grad_cols = lax.dynamic_slice_in_dim(top_grad, top_start, top_rows, 2)
    key_soft_cols = lax.dynamic_slice_in_dim(top_soft, top_start, top_rows, 2)
    top_dk, top_dv = key_parts(key_grad_cols, key_soft_cols, top_q, top_low_all)
    query_grad = (
        base_dq + place_rows(mid_dq, R1, mid_shift) + place_rows(top_dq, ctx_size, top_shift)
    )
    key_grad = base_dk + place_rows(mid_dk, R1, mid_shift) + place_rows(top_dk, ctx_size, top_shift)
    value_grad = (
        base_dv + place_rows(mid_dv, R1, mid_shift) + place_rows(top_dv, ctx_size, top_shift)
    )
    out_shape = (1, tokens, flat_width)
    return (
        attended,
        query_grad.astype(jnp.bfloat16).reshape(out_shape),
        key_grad.astype(jnp.bfloat16).reshape(out_shape),
        value_grad.astype(jnp.bfloat16).reshape(out_shape),
        gain_grad,
    )


def solution(mesh):
    in_specs = (
        P("dp", "ctx", "head"),
        P("dp", "ctx", "head"),
        P("dp", "ctx", "head"),
        P("dp", "ctx", "head"),
        P("head"),
        P(None, "head"),
    )
    out_specs = (
        P("dp", "ctx", "head"),
        P("dp", "ctx", "head"),
        P("dp", "ctx", "head"),
        P("dp", "ctx", "head"),
        P("head"),
    )
    return jax.shard_map(shards, mesh=mesh, in_specs=in_specs, out_specs=out_specs, check_vma=False)
```

```python
import functools
import math

import jax
import jax.numpy as jnp
from jax import lax
from jax.experimental import pallas as pl
from jax.experimental.pallas import tpu as pltpu
from jax.sharding import PartitionSpec as P

HEAD_DIM = 128
SPAN = 4
R1 = 8


EPS = 1e-06


def gather_kernel(group, mid_x, top_x, mid_out, top_out, send_mid, recv_mid, send_top, recv_top):
    count = lax.axis_size("ctx")
    me = lax.axis_index("ctx")
    row = lax.axis_index("dp")
    col = lax.axis_index("head")
    base = me - me % group
    barrier = pltpu.get_barrier_semaphore()

    def greet(j, carry):
        peer = lax.rem(me + j, count)
        pl.semaphore_signal(
            barrier, 1, device_id=(row, peer, col), device_id_type=pl.DeviceIdType.MESH
        )
        return carry

    lax.fori_loop(1, count, greet, 0)
    pl.semaphore_wait(barrier, count - 1)

    def mid_copy(j):
        peer = base + lax.rem(me % group + j, group)
        return pltpu.make_async_remote_copy(
            mid_x, mid_out.at[j], send_mid.at[j], recv_mid.at[j],
            device_id=(row, peer, col), device_id_type=pl.DeviceIdType.MESH,
        )

    def top_copy(j):
        peer = lax.rem(me + j, count)
        return pltpu.make_async_remote_copy(
            top_x, top_out.at[j], send_top.at[j], recv_top.at[j],
            device_id=(row, peer, col), device_id_type=pl.DeviceIdType.MESH,
        )

    for j in range(1, group):
        mid_copy(j).start()

    def start_top(j, carry):
        top_copy(j).start()
        return carry

    lax.fori_loop(1, count, start_top, 0)
    mid_out[0] = mid_x[...]
    top_out[0] = top_x[...]
    for j in range(1, group):
        mid_copy(j).wait()

    def wait_top(j, carry):
        top_copy(j).wait()
        return carry

    lax.fori_loop(1, count, wait_top, 0)


def ctx_gather(mid_x, top_x, group, tag):
    count = lax.axis_size("ctx")
    return pl.pallas_call(
        functools.partial(gather_kernel, group),
        out_shape=(
            jax.ShapeDtypeStruct((group,) + mid_x.shape, mid_x.dtype),
            jax.ShapeDtypeStruct((count,) + top_x.shape, top_x.dtype),
        ),
        in_specs=[pl.BlockSpec(memory_space=pltpu.VMEM)] * 2,
        out_specs=(pl.BlockSpec(memory_space=pltpu.VMEM),) * 2,
        scratch_shapes=[
            pltpu.SemaphoreType.DMA((group,)),
            pltpu.SemaphoreType.DMA((group,)),
            pltpu.SemaphoreType.DMA((count,)),
            pltpu.SemaphoreType.DMA((count,)),
        ],
        compiler_params=pltpu.CompilerParams(collective_id=tag, has_side_effects=True),
    )(mid_x, top_x)


def pick_rows(source_rows, dilation, shifts):
    row_count, head_count, head_width = source_rows.shape
    grouped = source_rows.reshape(row_count // dilation, dilation, head_count, head_width)
    hit_mask = jnp.arange(dilation, dtype=jnp.int32).reshape(1, dilation, 1, 1) == shifts.reshape(
        1, 1, head_count, 1
    )
    chosen = jnp.where(hit_mask, grouped, jnp.zeros((), source_rows.dtype))
    return jnp.sum(chosen, axis=1, dtype=source_rows.dtype)


def place_rows(row_values, dilation, shifts):
    row_count, head_count, head_width = row_values.shape
    hit_mask = jnp.arange(dilation, dtype=jnp.int32).reshape(1, dilation, 1, 1) == shifts.reshape(
        1, 1, head_count, 1
    )
    spread = jnp.where(hit_mask, row_values[:, None], jnp.zeros((), row_values.dtype))
    return spread.reshape(row_count * dilation, head_count, head_width)


def level_scores(q_rows, k_rows):
    score_scale = 1.0 / math.sqrt(q_rows.shape[-1])
    return (
        jnp.einsum("qhe,khe->hqk", q_rows, k_rows, preferred_element_type=jnp.float32) * score_scale
    )


def attend(q_rows, k_rows, v_rows):
    scores = level_scores(q_rows, k_rows)
    row_max = jnp.max(scores, axis=-1, keepdims=True)
    log_total = row_max[..., 0] + jnp.log(jnp.sum(jnp.exp(scores - row_max), axis=-1))
    soft_rows = jnp.exp(scores - log_total[..., None]).astype(jnp.bfloat16)
    level_out = jnp.einsum("hqk,khe->qhe", soft_rows, v_rows, preferred_element_type=jnp.float32)
    return (level_out, log_total.T)


def score_grads(q_rows, k_rows, v_rows, log_total, grad_low, row_shift):
    score_scale = 1.0 / math.sqrt(q_rows.shape[-1])
    scores = level_scores(q_rows, k_rows)
    exact_soft = jnp.exp(scores - log_total.T[..., None])
    prob_grad = jnp.einsum("qhe,khe->hqk", grad_low, v_rows, preferred_element_type=jnp.float32)
    score_grad = (exact_soft * (prob_grad + row_shift.T[..., None]) * score_scale).astype(
        jnp.bfloat16
    )
    return (score_grad, exact_soft.astype(jnp.bfloat16))


def key_parts(score_grad, soft_low, q_rows, grad_low):
    k_part = jnp.einsum("hqk,qhe->khe", score_grad, q_rows, preferred_element_type=jnp.float32)
    v_part = jnp.einsum("hqk,qhe->khe", soft_low, grad_low, preferred_element_type=jnp.float32)
    return (k_part, v_part)


def query_part(score_grad, k_rows):
    return jnp.einsum("hqk,khe->qhe", score_grad, k_rows, preferred_element_type=jnp.float32)


def split_qkv(packed, head_count):
    width = head_count * HEAD_DIM
    shape = (packed.shape[0], head_count, HEAD_DIM)
    return tuple(packed[:, i * width : (i + 1) * width].reshape(shape) for i in range(3))


def pack_grads(grad_low, row_shift):
    rows = grad_low.shape[0]
    pad = jnp.zeros((rows, HEAD_DIM - row_shift.shape[1]), jnp.float32)
    return jnp.concatenate(
        [grad_low.astype(jnp.float32).reshape(rows, -1), row_shift.astype(jnp.float32), pad], 1
    )


def unpack_grads(packed, head_count):
    width = head_count * HEAD_DIM
    grad_low = packed[:, :width].astype(jnp.bfloat16).reshape(-1, head_count, HEAD_DIM)
    return grad_low, packed[:, width : width + head_count]


def shards(queries, keys, values, grad_y, out_gain, offsets):
    tokens = queries.shape[1]
    flat_width = queries.shape[2]
    head_count = flat_width // HEAD_DIM
    row_shape = (tokens, head_count, HEAD_DIM)
    q_own = queries[0].reshape(row_shape)
    k_own = keys[0].reshape(row_shape)
    v_own = values[0].reshape(row_shape)
    ctx_size = lax.axis_size("ctx")
    mid_shift = offsets[0]
    top_shift = offsets[1]
    positions = jnp.arange(tokens, dtype=jnp.int32)
    mid_hit = (positions % R1)[:, None] == mid_shift[None, :]
    top_hit = (positions % ctx_size)[:, None] == top_shift[None, :]
    mid_pack = jnp.concatenate(
        [pick_rows(x, R1, mid_shift).reshape(-1, flat_width) for x in (q_own, k_own, v_own)], 1
    )
    top_pack = jnp.concatenate(
        [pick_rows(x, ctx_size, top_shift).reshape(-1, flat_width) for x in (q_own, k_own, v_own)],
        1,
    )
    mid_rows = mid_pack.shape[0]
    top_rows = top_pack.shape[0]
    mid_all, top_all = ctx_gather(mid_pack, top_pack, SPAN, 0)
    mid_all = mid_all.reshape(-1, mid_pack.shape[1])
    top_all = top_all.reshape(-1, top_pack.shape[1])
    mid_q, mid_k, mid_v = split_qkv(mid_all, head_count)
    top_q, top_k, top_v = split_qkv(top_all, head_count)
    base_out, base_total = attend(q_own, k_own, v_own)
    mid_out_all, mid_total_all = attend(mid_q, mid_k, mid_v)
    top_out_all, top_total_all = attend(top_q, top_k, top_v)
    mid_out = mid_out_all[:mid_rows]
    mid_total = mid_total_all[:mid_rows]
    top_out = top_out_all[:top_rows]
    top_total = top_total_all[:top_rows]
    mid_full = place_rows(mid_total[..., None], R1, mid_shift)[..., 0]
    top_full = place_rows(top_total[..., None], ctx_size, top_shift)[..., 0]
    row_max = jnp.maximum(base_total, jnp.where(mid_hit, mid_full, base_total))
    row_max = jnp.maximum(row_max, jnp.where(top_hit, top_full, base_total))
    base_expo = jnp.exp(base_total - row_max)
    mid_expo = jnp.where(mid_hit, jnp.exp(mid_full - row_max), 0.0)
    top_expo = jnp.where(top_hit, jnp.exp(top_full - row_max), 0.0)
    denom = base_expo + mid_expo + top_expo
    base_share = base_expo / denom
    mid_share = mid_expo / denom
    top_share = top_expo / denom
    attn = (
        base_share[..., None] * base_out
        + mid_share[..., None] * place_rows(mid_out, R1, mid_shift)
        + top_share[..., None] * place_rows(top_out, ctx_size, top_shift)
    )
    inv_rms = lax.rsqrt(jnp.mean(attn * attn, axis=-1, keepdims=True) + EPS)
    normed = attn * inv_rms
    gain_rows = out_gain.reshape(head_count, HEAD_DIM)
    attended = (normed * gain_rows).astype(jnp.bfloat16).reshape(1, tokens, flat_width)
    grad_full = grad_y[0].reshape(row_shape).astype(jnp.float32)
    gain_part = jnp.sum(grad_full * normed, axis=0).reshape(flat_width)
    grad_norm = grad_full * gain_rows
    grad_attn = inv_rms * (
        grad_norm - normed * jnp.mean(grad_norm * normed, axis=-1, keepdims=True)
    )
    inner = jnp.sum(grad_attn * attn, axis=-1)
    base_low = (base_share[..., None] * grad_attn).astype(jnp.bfloat16)
    base_shift = -(base_share * inner)
    base_grad, base_soft = score_grads(q_own, k_own, v_own, base_total, base_low, base_shift)
    base_dq = query_part(base_grad, k_own)
    base_dk, base_dv = key_parts(base_grad, base_soft, q_own, base_low)

    mid_sel = pick_rows(mid_share[..., None], R1, mid_shift)[..., 0]
    mid_low = (mid_sel[..., None] * pick_rows(grad_attn, R1, mid_shift)).astype(jnp.bfloat16)
    mid_row_shift = -(mid_sel * pick_rows(inner[..., None], R1, mid_shift)[..., 0])
    top_sel = pick_rows(top_share[..., None], ctx_size, top_shift)[..., 0]
    top_low = (top_sel[..., None] * pick_rows(grad_attn, ctx_size, top_shift)).astype(jnp.bfloat16)
    top_row_shift = -(top_sel * pick_rows(inner[..., None], ctx_size, top_shift)[..., 0])

    top_grads = pack_grads(top_low, top_row_shift)
    gain_row = jnp.pad(gain_part, (0, top_grads.shape[1] - flat_width))[None]
    mid_gathered, gathered = ctx_gather(
        pack_grads(mid_low, mid_row_shift), jnp.concatenate([top_grads, gain_row], 0), SPAN, 1
    )
    mid_low_all, mid_shift_all = unpack_grads(
        mid_gathered.reshape(-1, mid_gathered.shape[-1]), head_count
    )
    top_low_all, top_shift_all = unpack_grads(
        gathered[:, :top_rows].reshape(-1, top_grads.shape[1]), head_count
    )
    gain_grad = lax.psum(jnp.sum(gathered[:, top_rows, :flat_width], axis=0), "dp")

    mid_grad, mid_soft = score_grads(
        mid_q, mid_k, mid_v, mid_total_all, mid_low_all, mid_shift_all
    )
    mid_dq = query_part(mid_grad[:, :mid_rows], mid_k)
    mid_dk, mid_dv = key_parts(
        mid_grad[:, :, :mid_rows], mid_soft[:, :, :mid_rows], mid_q, mid_low_all
    )
    top_grad, top_soft = score_grads(
        top_q, top_k, top_v, top_total_all, top_low_all, top_shift_all
    )
    top_dq = query_part(top_grad[:, :top_rows], top_k)
    top_dk, top_dv = key_parts(
        top_grad[:, :, :top_rows], top_soft[:, :, :top_rows], top_q, top_low_all
    )
    query_grad = (
        base_dq + place_rows(mid_dq, R1, mid_shift) + place_rows(top_dq, ctx_size, top_shift)
    )
    key_grad = base_dk + place_rows(mid_dk, R1, mid_shift) + place_rows(top_dk, ctx_size, top_shift)
    value_grad = (
        base_dv + place_rows(mid_dv, R1, mid_shift) + place_rows(top_dv, ctx_size, top_shift)
    )
    out_shape = (1, tokens, flat_width)
    return (
        attended,
        query_grad.astype(jnp.bfloat16).reshape(out_shape),
        key_grad.astype(jnp.bfloat16).reshape(out_shape),
        value_grad.astype(jnp.bfloat16).reshape(out_shape),
        gain_grad,
    )


def solution(mesh):
    in_specs = (
        P("dp", "ctx", "head"),
        P("dp", "ctx", "head"),
        P("dp", "ctx", "head"),
        P("dp", "ctx", "head"),
        P("head"),
        P(None, "head"),
    )
    out_specs = (
        P("dp", "ctx", "head"),
        P("dp", "ctx", "head"),
        P("dp", "ctx", "head"),
        P("dp", "ctx", "head"),
        P("head"),
    )
    return jax.shard_map(shards, mesh=mesh, in_specs=in_specs, out_specs=out_specs, check_vma=False)
```

```python
import functools
import math

import jax
import jax.numpy as jnp
from jax import lax
from jax.experimental import pallas as pl
from jax.experimental.pallas import tpu as pltpu
from jax.sharding import PartitionSpec as P

HEAD_DIM = 128
SPAN = 4
R1 = 8


EPS = 1e-06


def gather_kernel(group, mid_x, top_x, mid_out, top_out, send_mid, recv_mid, send_top, recv_top):
    count = lax.axis_size("ctx")
    me = lax.axis_index("ctx")
    row = lax.axis_index("dp")
    col = lax.axis_index("head")
    base = me - me % group
    barrier = pltpu.get_barrier_semaphore()

    def greet(j, carry):
        peer = lax.rem(me + j, count)
        pl.semaphore_signal(
            barrier, 1, device_id=(row, peer, col), device_id_type=pl.DeviceIdType.MESH
        )
        return carry

    lax.fori_loop(1, count, greet, 0)
    pl.semaphore_wait(barrier, count - 1)

    def mid_copy(j):
        peer = base + lax.rem(me % group + j, group)
        return pltpu.make_async_remote_copy(
            mid_x, mid_out.at[j], send_mid.at[j], recv_mid.at[j],
            device_id=(row, peer, col), device_id_type=pl.DeviceIdType.MESH,
        )

    def top_copy(j):
        peer = lax.rem(me + j, count)
        return pltpu.make_async_remote_copy(
            top_x, top_out.at[j], send_top.at[j], recv_top.at[j],
            device_id=(row, peer, col), device_id_type=pl.DeviceIdType.MESH,
        )

    for j in range(1, group):
        mid_copy(j).start()

    def start_top(j, carry):
        top_copy(j).start()
        return carry

    lax.fori_loop(1, count, start_top, 0)
    mid_out[0] = mid_x[...]
    top_out[0] = top_x[...]
    for j in range(1, group):
        mid_copy(j).wait()

    def wait_top(j, carry):
        top_copy(j).wait()
        return carry

    lax.fori_loop(1, count, wait_top, 0)


def ctx_gather(mid_x, top_x, group, tag):
    count = lax.axis_size("ctx")
    return pl.pallas_call(
        functools.partial(gather_kernel, group),
        out_shape=(
            jax.ShapeDtypeStruct((group,) + mid_x.shape, mid_x.dtype),
            jax.ShapeDtypeStruct((count,) + top_x.shape, top_x.dtype),
        ),
        in_specs=[pl.BlockSpec(memory_space=pltpu.VMEM)] * 2,
        out_specs=(pl.BlockSpec(memory_space=pltpu.VMEM),) * 2,
        scratch_shapes=[
            pltpu.SemaphoreType.DMA((group,)),
            pltpu.SemaphoreType.DMA((group,)),
            pltpu.SemaphoreType.DMA((count,)),
            pltpu.SemaphoreType.DMA((count,)),
        ],
        compiler_params=pltpu.CompilerParams(collective_id=tag, has_side_effects=True),
    )(mid_x, top_x)


def lane_dense(block):
    return block.reshape(-1, HEAD_DIM)


def pick_rows(source_rows, dilation, shifts):
    row_count, head_count, head_width = source_rows.shape
    grouped = source_rows.reshape(row_count // dilation, dilation, head_count, head_width)
    hit_mask = jnp.arange(dilation, dtype=jnp.int32).reshape(1, dilation, 1, 1) == shifts.reshape(
        1, 1, head_count, 1
    )
    chosen = jnp.where(hit_mask, grouped, jnp.zeros((), source_rows.dtype))
    return jnp.sum(chosen, axis=1, dtype=source_rows.dtype)


def place_rows(row_values, dilation, shifts):
    row_count, head_count, head_width = row_values.shape
    hit_mask = jnp.arange(dilation, dtype=jnp.int32).reshape(1, dilation, 1, 1) == shifts.reshape(
        1, 1, head_count, 1
    )
    spread = jnp.where(hit_mask, row_values[:, None], jnp.zeros((), row_values.dtype))
    return spread.reshape(row_count * dilation, head_count, head_width)


def level_scores(q_rows, k_rows):
    score_scale = 1.0 / math.sqrt(q_rows.shape[-1])
    return (
        jnp.einsum("qhe,khe->hqk", q_rows, k_rows, preferred_element_type=jnp.float32) * score_scale
    )


def attend(q_rows, k_rows, v_rows):
    scores = level_scores(q_rows, k_rows)
    row_max = jnp.max(scores, axis=-1, keepdims=True)
    log_total = row_max[..., 0] + jnp.log(jnp.sum(jnp.exp(scores - row_max), axis=-1))
    soft_rows = jnp.exp(scores - log_total[..., None]).astype(jnp.bfloat16)
    level_out = jnp.einsum("hqk,khe->qhe", soft_rows, v_rows, preferred_element_type=jnp.float32)
    return (level_out, log_total.T)


def score_grads(q_rows, k_rows, v_rows, log_total, grad_low, row_shift):
    score_scale = 1.0 / math.sqrt(q_rows.shape[-1])
    scores = level_scores(q_rows, k_rows)
    exact_soft = jnp.exp(scores - log_total.T[..., None])
    prob_grad = jnp.einsum("qhe,khe->hqk", grad_low, v_rows, preferred_element_type=jnp.float32)
    score_grad = (exact_soft * (prob_grad + row_shift.T[..., None]) * score_scale).astype(
        jnp.bfloat16
    )
    return (score_grad, exact_soft.astype(jnp.bfloat16))


def key_parts(score_grad, soft_low, q_rows, grad_low):
    k_part = jnp.einsum("hqk,qhe->khe", score_grad, q_rows, preferred_element_type=jnp.float32)
    v_part = jnp.einsum("hqk,qhe->khe", soft_low, grad_low, preferred_element_type=jnp.float32)
    return (k_part, v_part)


def query_part(score_grad, k_rows):
    return jnp.einsum("hqk,khe->qhe", score_grad, k_rows, preferred_element_type=jnp.float32)


def split_qkv(packed, head_count):
    width = head_count * HEAD_DIM
    shape = (packed.shape[0], head_count, HEAD_DIM)
    return tuple(packed[:, i * width : (i + 1) * width].reshape(shape) for i in range(3))


def pack_grads(grad_low, row_shift):
    rows = grad_low.shape[0]
    pad = jnp.zeros((rows, HEAD_DIM - row_shift.shape[1]), jnp.float32)
    return jnp.concatenate(
        [grad_low.astype(jnp.float32).reshape(rows, -1), row_shift.astype(jnp.float32), pad], 1
    )


def unpack_grads(packed, head_count):
    width = head_count * HEAD_DIM
    grad_low = packed[:, :width].astype(jnp.bfloat16).reshape(-1, head_count, HEAD_DIM)
    return grad_low, packed[:, width : width + head_count]


def shards(queries, keys, values, grad_y, out_gain, offsets):
    tokens = queries.shape[1]
    flat_width = queries.shape[2]
    head_count = flat_width // HEAD_DIM
    row_shape = (tokens, head_count, HEAD_DIM)
    q_own = queries[0].reshape(row_shape)
    k_own = keys[0].reshape(row_shape)
    v_own = values[0].reshape(row_shape)
    ctx_size = lax.axis_size("ctx")
    mid_shift = offsets[0]
    top_shift = offsets[1]
    positions = jnp.arange(tokens, dtype=jnp.int32)
    mid_hit = (positions % R1)[:, None] == mid_shift[None, :]
    top_hit = (positions % ctx_size)[:, None] == top_shift[None, :]
    mid_pack = jnp.concatenate(
        [pick_rows(x, R1, mid_shift).reshape(-1, flat_width) for x in (q_own, k_own, v_own)], 1
    )
    top_pack = jnp.concatenate(
        [pick_rows(x, ctx_size, top_shift).reshape(-1, flat_width) for x in (q_own, k_own, v_own)],
        1,
    )
    mid_rows = mid_pack.shape[0]
    top_rows = top_pack.shape[0]
    mid_all, top_all = ctx_gather(mid_pack, lane_dense(top_pack), SPAN, 0)
    mid_all = mid_all.reshape(-1, mid_pack.shape[1])
    top_all = top_all.reshape(-1, top_pack.shape[1])
    mid_q, mid_k, mid_v = split_qkv(mid_all, head_count)
    top_q, top_k, top_v = split_qkv(top_all, head_count)
    base_out, base_total = attend(q_own, k_own, v_own)
    mid_out_all, mid_total_all = attend(mid_q, mid_k, mid_v)
    top_out_all, top_total_all = attend(top_q, top_k, top_v)
    mid_out = mid_out_all[:mid_rows]
    mid_total = mid_total_all[:mid_rows]
    top_out = top_out_all[:top_rows]
    top_total = top_total_all[:top_rows]
    mid_full = place_rows(mid_total[..., None], R1, mid_shift)[..., 0]
    top_full = place_rows(top_total[..., None], ctx_size, top_shift)[..., 0]
    row_max = jnp.maximum(base_total, jnp.where(mid_hit, mid_full, base_total))
    row_max = jnp.maximum(row_max, jnp.where(top_hit, top_full, base_total))
    base_expo = jnp.exp(base_total - row_max)
    mid_expo = jnp.where(mid_hit, jnp.exp(mid_full - row_max), 0.0)
    top_expo = jnp.where(top_hit, jnp.exp(top_full - row_max), 0.0)
    denom = base_expo + mid_expo + top_expo
    base_share = base_expo / denom
    mid_share = mid_expo / denom
    top_share = top_expo / denom
    attn = (
        base_share[..., None] * base_out
        + mid_share[..., None] * place_rows(mid_out, R1, mid_shift)
        + top_share[..., None] * place_rows(top_out, ctx_size, top_shift)
    )
    inv_rms = lax.rsqrt(jnp.mean(attn * attn, axis=-1, keepdims=True) + EPS)
    normed = attn * inv_rms
    gain_rows = out_gain.reshape(head_count, HEAD_DIM)
    attended = (normed * gain_rows).astype(jnp.bfloat16).reshape(1, tokens, flat_width)
    grad_full = grad_y[0].reshape(row_shape).astype(jnp.float32)
    gain_part = jnp.sum(grad_full * normed, axis=0).reshape(flat_width)
    grad_norm = grad_full * gain_rows
    grad_attn = inv_rms * (
        grad_norm - normed * jnp.mean(grad_norm * normed, axis=-1, keepdims=True)
    )
    inner = jnp.sum(grad_attn * attn, axis=-1)
    base_low = (base_share[..., None] * grad_attn).astype(jnp.bfloat16)
    base_shift = -(base_share * inner)
    base_grad, base_soft = score_grads(q_own, k_own, v_own, base_total, base_low, base_shift)
    base_dq = query_part(base_grad, k_own)
    base_dk, base_dv = key_parts(base_grad, base_soft, q_own, base_low)

    mid_sel = pick_rows(mid_share[..., None], R1, mid_shift)[..., 0]
    mid_low = (mid_sel[..., None] * pick_rows(grad_attn, R1, mid_shift)).astype(jnp.bfloat16)
    mid_row_shift = -(mid_sel * pick_rows(inner[..., None], R1, mid_shift)[..., 0])
    top_sel = pick_rows(top_share[..., None], ctx_size, top_shift)[..., 0]
    top_low = (top_sel[..., None] * pick_rows(grad_attn, ctx_size, top_shift)).astype(jnp.bfloat16)
    top_row_shift = -(top_sel * pick_rows(inner[..., None], ctx_size, top_shift)[..., 0])

    top_grads = pack_grads(top_low, top_row_shift)
    gain_row = jnp.pad(gain_part, (0, top_grads.shape[1] - flat_width))[None]
    top_block = jnp.concatenate([top_grads, gain_row], 0)
    mid_gathered, gathered = ctx_gather(
        pack_grads(mid_low, mid_row_shift), lane_dense(top_block), SPAN, 1
    )
    gathered = gathered.reshape((-1,) + top_block.shape)
    mid_low_all, mid_shift_all = unpack_grads(
        mid_gathered.reshape(-1, mid_gathered.shape[-1]), head_count
    )
    top_low_all, top_shift_all = unpack_grads(
        gathered[:, :top_rows].reshape(-1, top_grads.shape[1]), head_count
    )
    gain_grad = lax.psum(jnp.sum(gathered[:, top_rows, :flat_width], axis=0), "dp")

    mid_grad, mid_soft = score_grads(
        mid_q, mid_k, mid_v, mid_total_all, mid_low_all, mid_shift_all
    )
    mid_dq = query_part(mid_grad[:, :mid_rows], mid_k)
    mid_dk, mid_dv = key_parts(
        mid_grad[:, :, :mid_rows], mid_soft[:, :, :mid_rows], mid_q, mid_low_all
    )
    top_grad, top_soft = score_grads(
        top_q, top_k, top_v, top_total_all, top_low_all, top_shift_all
    )
    top_dq = query_part(top_grad[:, :top_rows], top_k)
    top_dk, top_dv = key_parts(
        top_grad[:, :, :top_rows], top_soft[:, :, :top_rows], top_q, top_low_all
    )
    query_grad = (
        base_dq + place_rows(mid_dq, R1, mid_shift) + place_rows(top_dq, ctx_size, top_shift)
    )
    key_grad = base_dk + place_rows(mid_dk, R1, mid_shift) + place_rows(top_dk, ctx_size, top_shift)
    value_grad = (
        base_dv + place_rows(mid_dv, R1, mid_shift) + place_rows(top_dv, ctx_size, top_shift)
    )
    out_shape = (1, tokens, flat_width)
    return (
        attended,
        query_grad.astype(jnp.bfloat16).reshape(out_shape),
        key_grad.astype(jnp.bfloat16).reshape(out_shape),
        value_grad.astype(jnp.bfloat16).reshape(out_shape),
        gain_grad,
    )


def solution(mesh):
    in_specs = (
        P("dp", "ctx", "head"),
        P("dp", "ctx", "head"),
        P("dp", "ctx", "head"),
        P("dp", "ctx", "head"),
        P("head"),
        P(None, "head"),
    )
    out_specs = (
        P("dp", "ctx", "head"),
        P("dp", "ctx", "head"),
        P("dp", "ctx", "head"),
        P("dp", "ctx", "head"),
        P("head"),
    )
    return jax.shard_map(shards, mesh=mesh, in_specs=in_specs, out_specs=out_specs, check_vma=False)
```

```python
import functools
import math

import jax
import jax.numpy as jnp
from jax import lax
from jax.experimental import pallas as pl
from jax.experimental.pallas import tpu as pltpu
from jax.sharding import PartitionSpec as P

HEAD_DIM = 128
SPAN = 4
R1 = 8
RING = 8


EPS = 1e-06


def gather_kernel(
    group, inner, mid_x, top_x, mid_out, top_out, stage,
    send_mid, recv_mid, send_a, recv_a, send_b, recv_b, local_sem,
):
    count = lax.axis_size("ctx")
    outer = count // inner
    me = lax.axis_index("ctx")
    row = lax.axis_index("dp")
    col = lax.axis_index("head")
    lo = me % inner
    hi = me // inner
    base = me - me % group
    mesh_ids = pl.DeviceIdType.MESH

    def inner_peer(j):
        return hi * inner + lax.rem(lo + j, inner)

    def outer_peer(j):
        return lax.rem(hi + j, outer) * inner + lo

    barrier = pltpu.get_barrier_semaphore()
    for j in range(1, inner):
        pl.semaphore_signal(barrier, 1, device_id=(row, inner_peer(j), col), device_id_type=mesh_ids)
    for j in range(1, outer):
        pl.semaphore_signal(barrier, 1, device_id=(row, outer_peer(j), col), device_id_type=mesh_ids)
    pl.semaphore_wait(barrier, inner + outer - 2)

    def mid_copy(j):
        peer = base + lax.rem(me % group + j, group)
        return pltpu.make_async_remote_copy(
            mid_x, mid_out.at[j], send_mid.at[j], recv_mid.at[j],
            device_id=(row, peer, col), device_id_type=mesh_ids,
        )

    def copy_a(j):
        return pltpu.make_async_remote_copy(
            top_x, stage.at[j], send_a.at[j], recv_a.at[j],
            device_id=(row, inner_peer(j), col), device_id_type=mesh_ids,
        )

    def copy_b(j):
        return pltpu.make_async_remote_copy(
            stage, top_out.at[j], send_b.at[j], recv_b.at[j],
            device_id=(row, outer_peer(j), col), device_id_type=mesh_ids,
        )

    for j in range(1, inner):
        copy_a(j).start()
    for j in range(1, group):
        mid_copy(j).start()
    own = pltpu.make_async_copy(top_x, stage.at[0], local_sem)
    own.start()
    mid_out[0] = mid_x[...]
    own.wait()
    for j in range(1, inner):
        copy_a(j).wait()
    for j in range(1, outer):
        copy_b(j).start()
    top_out[0] = stage[...]
    for j in range(1, group):
        mid_copy(j).wait()
    for j in range(1, outer):
        copy_b(j).wait()


def ctx_gather(mid_x, top_x, group, tag):
    count = lax.axis_size("ctx")
    inner = RING
    return pl.pallas_call(
        functools.partial(gather_kernel, group, inner),
        out_shape=(
            jax.ShapeDtypeStruct((group,) + mid_x.shape, mid_x.dtype),
            jax.ShapeDtypeStruct((count // inner, inner) + top_x.shape, top_x.dtype),
        ),
        in_specs=[pl.BlockSpec(memory_space=pltpu.VMEM)] * 2,
        out_specs=(pl.BlockSpec(memory_space=pltpu.VMEM),) * 2,
        scratch_shapes=[
            pltpu.VMEM((inner,) + top_x.shape, top_x.dtype),
            pltpu.SemaphoreType.DMA((group,)),
            pltpu.SemaphoreType.DMA((group,)),
            pltpu.SemaphoreType.DMA((inner,)),
            pltpu.SemaphoreType.DMA((inner,)),
            pltpu.SemaphoreType.DMA((count // inner,)),
            pltpu.SemaphoreType.DMA((count // inner,)),
            pltpu.SemaphoreType.DMA,
        ],
        compiler_params=pltpu.CompilerParams(collective_id=tag, has_side_effects=True),
    )(mid_x, top_x)


def lane_dense(block):
    return block.reshape(-1, HEAD_DIM)


def pick_rows(source_rows, dilation, shifts):
    row_count, head_count, head_width = source_rows.shape
    grouped = source_rows.reshape(row_count // dilation, dilation, head_count, head_width)
    hit_mask = jnp.arange(dilation, dtype=jnp.int32).reshape(1, dilation, 1, 1) == shifts.reshape(
        1, 1, head_count, 1
    )
    chosen = jnp.where(hit_mask, grouped, jnp.zeros((), source_rows.dtype))
    return jnp.sum(chosen, axis=1, dtype=source_rows.dtype)


def place_rows(row_values, dilation, shifts):
    row_count, head_count, head_width = row_values.shape
    hit_mask = jnp.arange(dilation, dtype=jnp.int32).reshape(1, dilation, 1, 1) == shifts.reshape(
        1, 1, head_count, 1
    )
    spread = jnp.where(hit_mask, row_values[:, None], jnp.zeros((), row_values.dtype))
    return spread.reshape(row_count * dilation, head_count, head_width)


def level_scores(q_rows, k_rows):
    score_scale = 1.0 / math.sqrt(q_rows.shape[-1])
    return (
        jnp.einsum("qhe,khe->hqk", q_rows, k_rows, preferred_element_type=jnp.float32) * score_scale
    )


def attend(q_rows, k_rows, v_rows):
    scores = level_scores(q_rows, k_rows)
    row_max = jnp.max(scores, axis=-1, keepdims=True)
    log_total = row_max[..., 0] + jnp.log(jnp.sum(jnp.exp(scores - row_max), axis=-1))
    soft_rows = jnp.exp(scores - log_total[..., None]).astype(jnp.bfloat16)
    level_out = jnp.einsum("hqk,khe->qhe", soft_rows, v_rows, preferred_element_type=jnp.float32)
    return (level_out, log_total.T)


def score_grads(q_rows, k_rows, v_rows, log_total, grad_low, row_shift):
    score_scale = 1.0 / math.sqrt(q_rows.shape[-1])
    scores = level_scores(q_rows, k_rows)
    exact_soft = jnp.exp(scores - log_total.T[..., None])
    prob_grad = jnp.einsum("qhe,khe->hqk", grad_low, v_rows, preferred_element_type=jnp.float32)
    score_grad = (exact_soft * (prob_grad + row_shift.T[..., None]) * score_scale).astype(
        jnp.bfloat16
    )
    return (score_grad, exact_soft.astype(jnp.bfloat16))


def key_parts(score_grad, soft_low, q_rows, grad_low):
    k_part = jnp.einsum("hqk,qhe->khe", score_grad, q_rows, preferred_element_type=jnp.float32)
    v_part = jnp.einsum("hqk,qhe->khe", soft_low, grad_low, preferred_element_type=jnp.float32)
    return (k_part, v_part)


def query_part(score_grad, k_rows):
    return jnp.einsum("hqk,khe->qhe", score_grad, k_rows, preferred_element_type=jnp.float32)


def split_qkv(packed, head_count):
    width = head_count * HEAD_DIM
    shape = (packed.shape[0], head_count, HEAD_DIM)
    return tuple(packed[:, i * width : (i + 1) * width].reshape(shape) for i in range(3))


def pack_grads(grad_low, row_shift):
    rows = grad_low.shape[0]
    pad = jnp.zeros((rows, HEAD_DIM - row_shift.shape[1]), jnp.float32)
    return jnp.concatenate(
        [grad_low.astype(jnp.float32).reshape(rows, -1), row_shift.astype(jnp.float32), pad], 1
    )


def unpack_grads(packed, head_count):
    width = head_count * HEAD_DIM
    grad_low = packed[:, :width].astype(jnp.bfloat16).reshape(-1, head_count, HEAD_DIM)
    return grad_low, packed[:, width : width + head_count]


def shards(queries, keys, values, grad_y, out_gain, offsets):
    tokens = queries.shape[1]
    flat_width = queries.shape[2]
    head_count = flat_width // HEAD_DIM
    row_shape = (tokens, head_count, HEAD_DIM)
    q_own = queries[0].reshape(row_shape)
    k_own = keys[0].reshape(row_shape)
    v_own = values[0].reshape(row_shape)
    ctx_size = lax.axis_size("ctx")
    mid_shift = offsets[0]
    top_shift = offsets[1]
    positions = jnp.arange(tokens, dtype=jnp.int32)
    mid_hit = (positions % R1)[:, None] == mid_shift[None, :]
    top_hit = (positions % ctx_size)[:, None] == top_shift[None, :]
    mid_pack = jnp.concatenate(
        [pick_rows(x, R1, mid_shift).reshape(-1, flat_width) for x in (q_own, k_own, v_own)], 1
    )
    top_pack = jnp.concatenate(
        [pick_rows(x, ctx_size, top_shift).reshape(-1, flat_width) for x in (q_own, k_own, v_own)],
        1,
    )
    mid_rows = mid_pack.shape[0]
    top_rows = top_pack.shape[0]
    mid_all, top_all = ctx_gather(mid_pack, lane_dense(top_pack), SPAN, 0)
    mid_all = mid_all.reshape(-1, mid_pack.shape[1])
    top_all = top_all.reshape(-1, top_pack.shape[1])
    mid_q, mid_k, mid_v = split_qkv(mid_all, head_count)
    top_q, top_k, top_v = split_qkv(top_all, head_count)
    base_out, base_total = attend(q_own, k_own, v_own)
    mid_out_all, mid_total_all = attend(mid_q, mid_k, mid_v)
    top_out_all, top_total_all = attend(top_q, top_k, top_v)
    mid_out = mid_out_all[:mid_rows]
    mid_total = mid_total_all[:mid_rows]
    top_out = top_out_all[:top_rows]
    top_total = top_total_all[:top_rows]
    mid_full = place_rows(mid_total[..., None], R1, mid_shift)[..., 0]
    top_full = place_rows(top_total[..., None], ctx_size, top_shift)[..., 0]
    row_max = jnp.maximum(base_total, jnp.where(mid_hit, mid_full, base_total))
    row_max = jnp.maximum(row_max, jnp.where(top_hit, top_full, base_total))
    base_expo = jnp.exp(base_total - row_max)
    mid_expo = jnp.where(mid_hit, jnp.exp(mid_full - row_max), 0.0)
    top_expo = jnp.where(top_hit, jnp.exp(top_full - row_max), 0.0)
    denom = base_expo + mid_expo + top_expo
    base_share = base_expo / denom
    mid_share = mid_expo / denom
    top_share = top_expo / denom
    attn = (
        base_share[..., None] * base_out
        + mid_share[..., None] * place_rows(mid_out, R1, mid_shift)
        + top_share[..., None] * place_rows(top_out, ctx_size, top_shift)
    )
    inv_rms = lax.rsqrt(jnp.mean(attn * attn, axis=-1, keepdims=True) + EPS)
    normed = attn * inv_rms
    gain_rows = out_gain.reshape(head_count, HEAD_DIM)
    attended = (normed * gain_rows).astype(jnp.bfloat16).reshape(1, tokens, flat_width)
    grad_full = grad_y[0].reshape(row_shape).astype(jnp.float32)
    gain_part = jnp.sum(grad_full * normed, axis=0).reshape(flat_width)
    grad_norm = grad_full * gain_rows
    grad_attn = inv_rms * (
        grad_norm - normed * jnp.mean(grad_norm * normed, axis=-1, keepdims=True)
    )
    inner = jnp.sum(grad_attn * attn, axis=-1)
    base_low = (base_share[..., None] * grad_attn).astype(jnp.bfloat16)
    base_shift = -(base_share * inner)
    base_grad, base_soft = score_grads(q_own, k_own, v_own, base_total, base_low, base_shift)
    base_dq = query_part(base_grad, k_own)
    base_dk, base_dv = key_parts(base_grad, base_soft, q_own, base_low)

    mid_sel = pick_rows(mid_share[..., None], R1, mid_shift)[..., 0]
    mid_low = (mid_sel[..., None] * pick_rows(grad_attn, R1, mid_shift)).astype(jnp.bfloat16)
    mid_row_shift = -(mid_sel * pick_rows(inner[..., None], R1, mid_shift)[..., 0])
    top_sel = pick_rows(top_share[..., None], ctx_size, top_shift)[..., 0]
    top_low = (top_sel[..., None] * pick_rows(grad_attn, ctx_size, top_shift)).astype(jnp.bfloat16)
    top_row_shift = -(top_sel * pick_rows(inner[..., None], ctx_size, top_shift)[..., 0])

    top_grads = pack_grads(top_low, top_row_shift)
    gain_row = jnp.pad(gain_part, (0, top_grads.shape[1] - flat_width))[None]
    top_block = jnp.concatenate([top_grads, gain_row], 0)
    mid_gathered, gathered = ctx_gather(
        pack_grads(mid_low, mid_row_shift), lane_dense(top_block), SPAN, 1
    )
    gathered = gathered.reshape((-1,) + top_block.shape)
    mid_low_all, mid_shift_all = unpack_grads(
        mid_gathered.reshape(-1, mid_gathered.shape[-1]), head_count
    )
    top_low_all, top_shift_all = unpack_grads(
        gathered[:, :top_rows].reshape(-1, top_grads.shape[1]), head_count
    )
    gain_grad = lax.psum(jnp.sum(gathered[:, top_rows, :flat_width], axis=0), "dp")

    mid_grad, mid_soft = score_grads(
        mid_q, mid_k, mid_v, mid_total_all, mid_low_all, mid_shift_all
    )
    mid_dq = query_part(mid_grad[:, :mid_rows], mid_k)
    mid_dk, mid_dv = key_parts(
        mid_grad[:, :, :mid_rows], mid_soft[:, :, :mid_rows], mid_q, mid_low_all
    )
    top_grad, top_soft = score_grads(
        top_q, top_k, top_v, top_total_all, top_low_all, top_shift_all
    )
    top_dq = query_part(top_grad[:, :top_rows], top_k)
    top_dk, top_dv = key_parts(
        top_grad[:, :, :top_rows], top_soft[:, :, :top_rows], top_q, top_low_all
    )
    query_grad = (
        base_dq + place_rows(mid_dq, R1, mid_shift) + place_rows(top_dq, ctx_size, top_shift)
    )
    key_grad = base_dk + place_rows(mid_dk, R1, mid_shift) + place_rows(top_dk, ctx_size, top_shift)
    value_grad = (
        base_dv + place_rows(mid_dv, R1, mid_shift) + place_rows(top_dv, ctx_size, top_shift)
    )
    out_shape = (1, tokens, flat_width)
    return (
        attended,
        query_grad.astype(jnp.bfloat16).reshape(out_shape),
        key_grad.astype(jnp.bfloat16).reshape(out_shape),
        value_grad.astype(jnp.bfloat16).reshape(out_shape),
        gain_grad,
    )


def solution(mesh):
    in_specs = (
        P("dp", "ctx", "head"),
        P("dp", "ctx", "head"),
        P("dp", "ctx", "head"),
        P("dp", "ctx", "head"),
        P("head"),
        P(None, "head"),
    )
    out_specs = (
        P("dp", "ctx", "head"),
        P("dp", "ctx", "head"),
        P("dp", "ctx", "head"),
        P("dp", "ctx", "head"),
        P("head"),
    )
    return jax.shard_map(shards, mesh=mesh, in_specs=in_specs, out_specs=out_specs, check_vma=False)
```

```python
import functools
import math

import jax
import jax.numpy as jnp
from jax import lax
from jax.experimental import pallas as pl
from jax.experimental.pallas import tpu as pltpu
from jax.sharding import PartitionSpec as P

HEAD_DIM = 128
SPAN = 4
R1 = 8
RING = 8


EPS = 1e-06


def gather_kernel(
    group, inner, mid_x, top_x, mid_out, top_out, stage,
    send_mid, recv_mid, send_a, recv_a, send_b, recv_b, local_sem,
):
    count = lax.axis_size("ctx")
    outer = count // inner
    me = lax.axis_index("ctx")
    row = lax.axis_index("dp")
    col = lax.axis_index("head")
    lo = me % inner
    hi = me // inner
    base = me - me % group
    mesh_ids = pl.DeviceIdType.MESH

    def inner_peer(j):
        return hi * inner + lax.rem(lo + j, inner)

    def outer_peer(j):
        return lax.rem(hi + j, outer) * inner + lo

    barrier = pltpu.get_barrier_semaphore()
    for j in range(1, inner):
        pl.semaphore_signal(barrier, 1, device_id=(row, inner_peer(j), col), device_id_type=mesh_ids)
    for j in range(1, outer):
        pl.semaphore_signal(barrier, 1, device_id=(row, outer_peer(j), col), device_id_type=mesh_ids)
    pl.semaphore_wait(barrier, inner + outer - 2)

    def mid_copy(j):
        peer = base + lax.rem(me % group + j, group)
        return pltpu.make_async_remote_copy(
            mid_x, mid_out.at[j], send_mid.at[j], recv_mid.at[j],
            device_id=(row, peer, col), device_id_type=mesh_ids,
        )

    def copy_a(j):
        return pltpu.make_async_remote_copy(
            top_x, stage.at[j], send_a.at[j], recv_a.at[j],
            device_id=(row, inner_peer(j), col), device_id_type=mesh_ids,
        )

    def copy_b(j):
        return pltpu.make_async_remote_copy(
            stage, top_out.at[j], send_b.at[j], recv_b.at[j],
            device_id=(row, outer_peer(j), col), device_id_type=mesh_ids,
        )

    for j in range(1, inner):
        copy_a(j).start()
    for j in range(1, group):
        mid_copy(j).start()
    own = pltpu.make_async_copy(top_x, stage.at[0], local_sem)
    own.start()
    mid_out[0] = mid_x[...]
    own.wait()
    for j in range(1, inner):
        copy_a(j).wait()
    for j in range(1, outer):
        copy_b(j).start()
    top_out[0] = stage[...]
    for j in range(1, group):
        mid_copy(j).wait()
    for j in range(1, outer):
        copy_b(j).wait()


def ctx_gather(mid_x, top_x, group, tag):
    count = lax.axis_size("ctx")
    inner = RING
    return pl.pallas_call(
        functools.partial(gather_kernel, group, inner),
        out_shape=(
            jax.ShapeDtypeStruct((group,) + mid_x.shape, mid_x.dtype),
            jax.ShapeDtypeStruct((count // inner, inner) + top_x.shape, top_x.dtype),
        ),
        in_specs=[pl.BlockSpec(memory_space=pltpu.VMEM)] * 2,
        out_specs=(pl.BlockSpec(memory_space=pltpu.VMEM),) * 2,
        scratch_shapes=[
            pltpu.VMEM((inner,) + top_x.shape, top_x.dtype),
            pltpu.SemaphoreType.DMA((group,)),
            pltpu.SemaphoreType.DMA((group,)),
            pltpu.SemaphoreType.DMA((inner,)),
            pltpu.SemaphoreType.DMA((inner,)),
            pltpu.SemaphoreType.DMA((count // inner,)),
            pltpu.SemaphoreType.DMA((count // inner,)),
            pltpu.SemaphoreType.DMA,
        ],
        compiler_params=pltpu.CompilerParams(collective_id=tag, has_side_effects=True),
    )(mid_x, top_x)


def lane_dense(block):
    return block.reshape(-1, HEAD_DIM)


def pick_rows(source_rows, dilation, shifts):
    row_count, head_count, head_width = source_rows.shape
    grouped = source_rows.reshape(row_count // dilation, dilation, head_count, head_width)
    hit_mask = jnp.arange(dilation, dtype=jnp.int32).reshape(1, dilation, 1, 1) == shifts.reshape(
        1, 1, head_count, 1
    )
    chosen = jnp.where(hit_mask, grouped, jnp.zeros((), source_rows.dtype))
    return jnp.sum(chosen, axis=1, dtype=source_rows.dtype)


def place_rows(row_values, dilation, shifts):
    row_count, head_count, head_width = row_values.shape
    hit_mask = jnp.arange(dilation, dtype=jnp.int32).reshape(1, dilation, 1, 1) == shifts.reshape(
        1, 1, head_count, 1
    )
    spread = jnp.where(hit_mask, row_values[:, None], jnp.zeros((), row_values.dtype))
    return spread.reshape(row_count * dilation, head_count, head_width)


def level_scores(q_rows, k_rows):
    score_scale = 1.0 / math.sqrt(q_rows.shape[-1])
    return (
        jnp.einsum("qhe,khe->hqk", q_rows, k_rows, preferred_element_type=jnp.float32) * score_scale
    )


def attend(q_rows, k_rows, v_rows):
    scores = level_scores(q_rows, k_rows)
    row_max = jnp.max(scores, axis=-1, keepdims=True)
    log_total = row_max[..., 0] + jnp.log(jnp.sum(jnp.exp(scores - row_max), axis=-1))
    soft_rows = jnp.exp(scores - log_total[..., None]).astype(jnp.bfloat16)
    level_out = jnp.einsum("hqk,khe->qhe", soft_rows, v_rows, preferred_element_type=jnp.float32)
    return (level_out, log_total.T)


def score_grads(q_rows, k_rows, v_rows, log_total, grad_low, row_shift):
    score_scale = 1.0 / math.sqrt(q_rows.shape[-1])
    scores = level_scores(q_rows, k_rows)
    exact_soft = jnp.exp(scores - log_total.T[..., None])
    prob_grad = jnp.einsum("qhe,khe->hqk", grad_low, v_rows, preferred_element_type=jnp.float32)
    score_grad = (exact_soft * (prob_grad + row_shift.T[..., None]) * score_scale).astype(
        jnp.bfloat16
    )
    return (score_grad, exact_soft.astype(jnp.bfloat16))


def key_parts(score_grad, soft_low, q_rows, grad_low):
    k_part = jnp.einsum("hqk,qhe->khe", score_grad, q_rows, preferred_element_type=jnp.float32)
    v_part = jnp.einsum("hqk,qhe->khe", soft_low, grad_low, preferred_element_type=jnp.float32)
    return (k_part, v_part)


def query_part(score_grad, k_rows):
    return jnp.einsum("hqk,khe->qhe", score_grad, k_rows, preferred_element_type=jnp.float32)


def split_qkv(packed, head_count):
    width = head_count * HEAD_DIM
    shape = (packed.shape[0], head_count, HEAD_DIM)
    return tuple(packed[:, i * width : (i + 1) * width].reshape(shape) for i in range(3))


def split_wide(values):
    high = values.astype(jnp.bfloat16)
    low = (values - high.astype(jnp.float32)).astype(jnp.bfloat16)
    return high, low


def join_wide(high, low):
    return high.astype(jnp.float32) + low.astype(jnp.float32)


def pack_grads(grad_low, row_shift, width):
    rows = grad_low.shape[0]
    high, low = split_wide(row_shift)
    used = grad_low.shape[1] * grad_low.shape[2] + 2 * row_shift.shape[1]
    return jnp.concatenate(
        [grad_low.reshape(rows, -1), high, low, jnp.zeros((rows, width - used), jnp.bfloat16)], 1
    )


def unpack_grads(packed, head_count):
    width = head_count * HEAD_DIM
    grad_low = packed[:, :width].reshape(-1, head_count, HEAD_DIM)
    return grad_low, join_wide(
        packed[:, width : width + head_count], packed[:, width + head_count : width + 2 * head_count]
    )


def shards(queries, keys, values, grad_y, out_gain, offsets):
    tokens = queries.shape[1]
    flat_width = queries.shape[2]
    head_count = flat_width // HEAD_DIM
    row_shape = (tokens, head_count, HEAD_DIM)
    q_own = queries[0].reshape(row_shape)
    k_own = keys[0].reshape(row_shape)
    v_own = values[0].reshape(row_shape)
    ctx_size = lax.axis_size("ctx")
    mid_shift = offsets[0]
    top_shift = offsets[1]
    positions = jnp.arange(tokens, dtype=jnp.int32)
    mid_hit = (positions % R1)[:, None] == mid_shift[None, :]
    top_hit = (positions % ctx_size)[:, None] == top_shift[None, :]
    mid_pack = jnp.concatenate(
        [pick_rows(x, R1, mid_shift).reshape(-1, flat_width) for x in (q_own, k_own, v_own)], 1
    )
    top_pack = jnp.concatenate(
        [pick_rows(x, ctx_size, top_shift).reshape(-1, flat_width) for x in (q_own, k_own, v_own)],
        1,
    )
    mid_rows = mid_pack.shape[0]
    top_rows = top_pack.shape[0]
    mid_all, top_all = ctx_gather(mid_pack, lane_dense(top_pack), SPAN, 0)
    mid_all = mid_all.reshape(-1, mid_pack.shape[1])
    top_all = top_all.reshape(-1, top_pack.shape[1])
    mid_q, mid_k, mid_v = split_qkv(mid_all, head_count)
    top_q, top_k, top_v = split_qkv(top_all, head_count)
    base_out, base_total = attend(q_own, k_own, v_own)
    mid_out_all, mid_total_all = attend(mid_q, mid_k, mid_v)
    top_out_all, top_total_all = attend(top_q, top_k, top_v)
    mid_out = mid_out_all[:mid_rows]
    mid_total = mid_total_all[:mid_rows]
    top_out = top_out_all[:top_rows]
    top_total = top_total_all[:top_rows]
    mid_full = place_rows(mid_total[..., None], R1, mid_shift)[..., 0]
    top_full = place_rows(top_total[..., None], ctx_size, top_shift)[..., 0]
    row_max = jnp.maximum(base_total, jnp.where(mid_hit, mid_full, base_total))
    row_max = jnp.maximum(row_max, jnp.where(top_hit, top_full, base_total))
    base_expo = jnp.exp(base_total - row_max)
    mid_expo = jnp.where(mid_hit, jnp.exp(mid_full - row_max), 0.0)
    top_expo = jnp.where(top_hit, jnp.exp(top_full - row_max), 0.0)
    denom = base_expo + mid_expo + top_expo
    base_share = base_expo / denom
    mid_share = mid_expo / denom
    top_share = top_expo / denom
    attn = (
        base_share[..., None] * base_out
        + mid_share[..., None] * place_rows(mid_out, R1, mid_shift)
        + top_share[..., None] * place_rows(top_out, ctx_size, top_shift)
    )
    inv_rms = lax.rsqrt(jnp.mean(attn * attn, axis=-1, keepdims=True) + EPS)
    normed = attn * inv_rms
    gain_rows = out_gain.reshape(head_count, HEAD_DIM)
    attended = (normed * gain_rows).astype(jnp.bfloat16).reshape(1, tokens, flat_width)
    grad_full = grad_y[0].reshape(row_shape).astype(jnp.float32)
    gain_part = jnp.sum(grad_full * normed, axis=0).reshape(flat_width)
    grad_norm = grad_full * gain_rows
    grad_attn = inv_rms * (
        grad_norm - normed * jnp.mean(grad_norm * normed, axis=-1, keepdims=True)
    )
    inner = jnp.sum(grad_attn * attn, axis=-1)
    base_low = (base_share[..., None] * grad_attn).astype(jnp.bfloat16)
    base_shift = -(base_share * inner)
    base_grad, base_soft = score_grads(q_own, k_own, v_own, base_total, base_low, base_shift)
    base_dq = query_part(base_grad, k_own)
    base_dk, base_dv = key_parts(base_grad, base_soft, q_own, base_low)

    mid_sel = pick_rows(mid_share[..., None], R1, mid_shift)[..., 0]
    mid_low = (mid_sel[..., None] * pick_rows(grad_attn, R1, mid_shift)).astype(jnp.bfloat16)
    mid_row_shift = -(mid_sel * pick_rows(inner[..., None], R1, mid_shift)[..., 0])
    top_sel = pick_rows(top_share[..., None], ctx_size, top_shift)[..., 0]
    top_low = (top_sel[..., None] * pick_rows(grad_attn, ctx_size, top_shift)).astype(jnp.bfloat16)
    top_row_shift = -(top_sel * pick_rows(inner[..., None], ctx_size, top_shift)[..., 0])

    gain_high, gain_low = split_wide(gain_part)
    shift_high, shift_low = split_wide(top_row_shift.reshape(-1))
    top_flat = jnp.concatenate(
        [top_low.reshape(-1), gain_high, gain_low, shift_high, shift_low]
    )
    tile = 16 * HEAD_DIM
    top_flat = jnp.pad(top_flat, (0, -top_flat.shape[0] % tile))
    mid_gathered, gathered = ctx_gather(
        pack_grads(mid_low, mid_row_shift, flat_width + HEAD_DIM),
        lane_dense(top_flat),
        SPAN,
        1,
    )
    mid_low_all, mid_shift_all = unpack_grads(
        mid_gathered.reshape(-1, mid_gathered.shape[-1]), head_count
    )
    gathered = gathered.reshape(ctx_size, -1)
    grad_width = top_rows * flat_width
    top_low_all = gathered[:, :grad_width].reshape(-1, head_count, HEAD_DIM)
    gain_cols = gathered[:, grad_width : grad_width + 2 * flat_width]
    gain_grad = lax.psum(
        jnp.sum(join_wide(gain_cols[:, :flat_width], gain_cols[:, flat_width:]), axis=0), "dp"
    )
    shift_start = grad_width + 2 * flat_width
    shift_count = top_rows * head_count
    top_shift_all = join_wide(
        gathered[:, shift_start : shift_start + shift_count],
        gathered[:, shift_start + shift_count : shift_start + 2 * shift_count],
    ).reshape(-1, head_count)

    mid_grad, mid_soft = score_grads(
        mid_q, mid_k, mid_v, mid_total_all, mid_low_all, mid_shift_all
    )
    mid_dq = query_part(mid_grad[:, :mid_rows], mid_k)
    mid_dk, mid_dv = key_parts(
        mid_grad[:, :, :mid_rows], mid_soft[:, :, :mid_rows], mid_q, mid_low_all
    )
    top_grad, top_soft = score_grads(
        top_q, top_k, top_v, top_total_all, top_low_all, top_shift_all
    )
    top_dq = query_part(top_grad[:, :top_rows], top_k)
    top_dk, top_dv = key_parts(
        top_grad[:, :, :top_rows], top_soft[:, :, :top_rows], top_q, top_low_all
    )
    query_grad = (
        base_dq + place_rows(mid_dq, R1, mid_shift) + place_rows(top_dq, ctx_size, top_shift)
    )
    key_grad = base_dk + place_rows(mid_dk, R1, mid_shift) + place_rows(top_dk, ctx_size, top_shift)
    value_grad = (
        base_dv + place_rows(mid_dv, R1, mid_shift) + place_rows(top_dv, ctx_size, top_shift)
    )
    out_shape = (1, tokens, flat_width)
    return (
        attended,
        query_grad.astype(jnp.bfloat16).reshape(out_shape),
        key_grad.astype(jnp.bfloat16).reshape(out_shape),
        value_grad.astype(jnp.bfloat16).reshape(out_shape),
        gain_grad,
    )


def solution(mesh):
    in_specs = (
        P("dp", "ctx", "head"),
        P("dp", "ctx", "head"),
        P("dp", "ctx", "head"),
        P("dp", "ctx", "head"),
        P("head"),
        P(None, "head"),
    )
    out_specs = (
        P("dp", "ctx", "head"),
        P("dp", "ctx", "head"),
        P("dp", "ctx", "head"),
        P("dp", "ctx", "head"),
        P("head"),
    )
    return jax.shard_map(shards, mesh=mesh, in_specs=in_specs, out_specs=out_specs, check_vma=False)
```

```python
import functools
import math

import jax
import jax.numpy as jnp
from jax import lax
from jax.experimental import pallas as pl
from jax.experimental.pallas import tpu as pltpu
from jax.sharding import PartitionSpec as P

HEAD_DIM = 128
SPAN = 4
R1 = 8
RING = 8


EPS = 1e-06


def gather_kernel(
    group, inner, mid_x, top_x, mid_out, top_out, stage,
    send_mid, recv_mid, send_a, recv_a, send_b, recv_b, local_sem,
):
    count = lax.axis_size("ctx")
    outer = count // inner
    me = lax.axis_index("ctx")
    row = lax.axis_index("dp")
    col = lax.axis_index("head")
    lo = me % inner
    hi = me // inner
    base = me - me % group
    mesh_ids = pl.DeviceIdType.MESH

    def inner_peer(j):
        return hi * inner + lax.rem(lo + j, inner)

    def outer_peer(j):
        return lax.rem(hi + j, outer) * inner + lo

    right = outer_peer(1)
    left = outer_peer(outer - 1)
    barrier = pltpu.get_barrier_semaphore()
    for j in range(1, inner):
        pl.semaphore_signal(barrier, 1, device_id=(row, inner_peer(j), col), device_id_type=mesh_ids)
    for peer in (right, left):
        pl.semaphore_signal(barrier, 1, device_id=(row, peer, col), device_id_type=mesh_ids)
    pl.semaphore_wait(barrier, inner + 1)

    def mid_copy(j):
        peer = base + lax.rem(me % group + j, group)
        return pltpu.make_async_remote_copy(
            mid_x, mid_out.at[j], send_mid.at[j], recv_mid.at[j],
            device_id=(row, peer, col), device_id_type=mesh_ids,
        )

    def copy_a(j):
        return pltpu.make_async_remote_copy(
            top_x, stage.at[j], send_a.at[j], recv_a.at[j],
            device_id=(row, inner_peer(j), col), device_id_type=mesh_ids,
        )

    def ring_copy(slot, source, peer):
        return pltpu.make_async_remote_copy(
            source, top_out.at[slot], send_b.at[slot], recv_b.at[slot],
            device_id=(row, peer, col), device_id_type=mesh_ids,
        )

    right_steps = outer // 2
    left_steps = outer - 1 - right_steps

    def right_copy(step):
        source = stage if step == 1 else top_out.at[step - 1]
        return ring_copy(step, source, right)

    def left_copy(step):
        source = stage if step == 1 else top_out.at[outer - step + 1]
        return ring_copy(outer - step, source, left)

    for j in range(1, inner):
        copy_a(j).start()
    for j in range(1, group):
        mid_copy(j).start()
    own = pltpu.make_async_copy(top_x, stage.at[0], local_sem)
    own.start()
    mid_out[0] = mid_x[...]
    own.wait()
    for j in range(1, inner):
        copy_a(j).wait()
    right_copy(1).start()
    if left_steps >= 1:
        left_copy(1).start()
    top_out[0] = stage[...]
    for step in range(2, right_steps + 1):
        right_copy(step - 1).wait_recv()
        right_copy(step).start()
        if step <= left_steps:
            left_copy(step - 1).wait_recv()
            left_copy(step).start()
    right_copy(right_steps).wait_recv()
    if left_steps >= 1:
        left_copy(left_steps).wait_recv()
    for step in range(1, right_steps + 1):
        right_copy(step).wait_send()
    for step in range(1, left_steps + 1):
        left_copy(step).wait_send()
    for j in range(1, group):
        mid_copy(j).wait()


def ctx_gather(mid_x, top_x, group, tag):
    count = lax.axis_size("ctx")
    inner = RING
    return pl.pallas_call(
        functools.partial(gather_kernel, group, inner),
        out_shape=(
            jax.ShapeDtypeStruct((group,) + mid_x.shape, mid_x.dtype),
            jax.ShapeDtypeStruct((count // inner, inner) + top_x.shape, top_x.dtype),
        ),
        in_specs=[pl.BlockSpec(memory_space=pltpu.VMEM)] * 2,
        out_specs=(pl.BlockSpec(memory_space=pltpu.VMEM),) * 2,
        scratch_shapes=[
            pltpu.VMEM((inner,) + top_x.shape, top_x.dtype),
            pltpu.SemaphoreType.DMA((group,)),
            pltpu.SemaphoreType.DMA((group,)),
            pltpu.SemaphoreType.DMA((inner,)),
            pltpu.SemaphoreType.DMA((inner,)),
            pltpu.SemaphoreType.DMA((count // inner,)),
            pltpu.SemaphoreType.DMA((count // inner,)),
            pltpu.SemaphoreType.DMA,
        ],
        compiler_params=pltpu.CompilerParams(collective_id=tag, has_side_effects=True),
    )(mid_x, top_x)


def lane_dense(block):
    return block.reshape(-1, HEAD_DIM)


def pick_rows(source_rows, dilation, shifts):
    row_count, head_count, head_width = source_rows.shape
    grouped = source_rows.reshape(row_count // dilation, dilation, head_count, head_width)
    hit_mask = jnp.arange(dilation, dtype=jnp.int32).reshape(1, dilation, 1, 1) == shifts.reshape(
        1, 1, head_count, 1
    )
    chosen = jnp.where(hit_mask, grouped, jnp.zeros((), source_rows.dtype))
    return jnp.sum(chosen, axis=1, dtype=source_rows.dtype)


def place_rows(row_values, dilation, shifts):
    row_count, head_count, head_width = row_values.shape
    hit_mask = jnp.arange(dilation, dtype=jnp.int32).reshape(1, dilation, 1, 1) == shifts.reshape(
        1, 1, head_count, 1
    )
    spread = jnp.where(hit_mask, row_values[:, None], jnp.zeros((), row_values.dtype))
    return spread.reshape(row_count * dilation, head_count, head_width)


def level_scores(q_rows, k_rows):
    score_scale = 1.0 / math.sqrt(q_rows.shape[-1])
    return (
        jnp.einsum("qhe,khe->hqk", q_rows, k_rows, preferred_element_type=jnp.float32) * score_scale
    )


def attend(q_rows, k_rows, v_rows):
    scores = level_scores(q_rows, k_rows)
    row_max = jnp.max(scores, axis=-1, keepdims=True)
    log_total = row_max[..., 0] + jnp.log(jnp.sum(jnp.exp(scores - row_max), axis=-1))
    soft_rows = jnp.exp(scores - log_total[..., None]).astype(jnp.bfloat16)
    level_out = jnp.einsum("hqk,khe->qhe", soft_rows, v_rows, preferred_element_type=jnp.float32)
    return (level_out, log_total.T)


def score_grads(q_rows, k_rows, v_rows, log_total, grad_low, row_shift):
    score_scale = 1.0 / math.sqrt(q_rows.shape[-1])
    scores = level_scores(q_rows, k_rows)
    exact_soft = jnp.exp(scores - log_total.T[..., None])
    prob_grad = jnp.einsum("qhe,khe->hqk", grad_low, v_rows, preferred_element_type=jnp.float32)
    score_grad = (exact_soft * (prob_grad + row_shift.T[..., None]) * score_scale).astype(
        jnp.bfloat16
    )
    return (score_grad, exact_soft.astype(jnp.bfloat16))


def key_parts(score_grad, soft_low, q_rows, grad_low):
    k_part = jnp.einsum("hqk,qhe->khe", score_grad, q_rows, preferred_element_type=jnp.float32)
    v_part = jnp.einsum("hqk,qhe->khe", soft_low, grad_low, preferred_element_type=jnp.float32)
    return (k_part, v_part)


def query_part(score_grad, k_rows):
    return jnp.einsum("hqk,khe->qhe", score_grad, k_rows, preferred_element_type=jnp.float32)


def split_qkv(packed, head_count):
    width = head_count * HEAD_DIM
    shape = (packed.shape[0], head_count, HEAD_DIM)
    return tuple(packed[:, i * width : (i + 1) * width].reshape(shape) for i in range(3))


def pack_grads(grad_low, row_shift):
    rows = grad_low.shape[0]
    pad = jnp.zeros((rows, HEAD_DIM - row_shift.shape[1]), jnp.float32)
    return jnp.concatenate(
        [grad_low.astype(jnp.float32).reshape(rows, -1), row_shift.astype(jnp.float32), pad], 1
    )


def unpack_grads(packed, head_count):
    width = head_count * HEAD_DIM
    grad_low = packed[:, :width].astype(jnp.bfloat16).reshape(-1, head_count, HEAD_DIM)
    return grad_low, packed[:, width : width + head_count]


def shards(queries, keys, values, grad_y, out_gain, offsets):
    tokens = queries.shape[1]
    flat_width = queries.shape[2]
    head_count = flat_width // HEAD_DIM
    row_shape = (tokens, head_count, HEAD_DIM)
    q_own = queries[0].reshape(row_shape)
    k_own = keys[0].reshape(row_shape)
    v_own = values[0].reshape(row_shape)
    ctx_size = lax.axis_size("ctx")
    mid_shift = offsets[0]
    top_shift = offsets[1]
    positions = jnp.arange(tokens, dtype=jnp.int32)
    mid_hit = (positions % R1)[:, None] == mid_shift[None, :]
    top_hit = (positions % ctx_size)[:, None] == top_shift[None, :]
    mid_pack = jnp.concatenate(
        [pick_rows(x, R1, mid_shift).reshape(-1, flat_width) for x in (q_own, k_own, v_own)], 1
    )
    top_pack = jnp.concatenate(
        [pick_rows(x, ctx_size, top_shift).reshape(-1, flat_width) for x in (q_own, k_own, v_own)],
        1,
    )
    mid_rows = mid_pack.shape[0]
    top_rows = top_pack.shape[0]
    mid_all, top_all = ctx_gather(mid_pack, lane_dense(top_pack), SPAN, 0)
    mid_all = mid_all.reshape(-1, mid_pack.shape[1])
    top_all = top_all.reshape(-1, top_pack.shape[1])
    mid_q, mid_k, mid_v = split_qkv(mid_all, head_count)
    top_q, top_k, top_v = split_qkv(top_all, head_count)
    base_out, base_total = attend(q_own, k_own, v_own)
    mid_out_all, mid_total_all = attend(mid_q, mid_k, mid_v)
    top_out_all, top_total_all = attend(top_q, top_k, top_v)
    mid_out = mid_out_all[:mid_rows]
    mid_total = mid_total_all[:mid_rows]
    top_out = top_out_all[:top_rows]
    top_total = top_total_all[:top_rows]
    mid_full = place_rows(mid_total[..., None], R1, mid_shift)[..., 0]
    top_full = place_rows(top_total[..., None], ctx_size, top_shift)[..., 0]
    row_max = jnp.maximum(base_total, jnp.where(mid_hit, mid_full, base_total))
    row_max = jnp.maximum(row_max, jnp.where(top_hit, top_full, base_total))
    base_expo = jnp.exp(base_total - row_max)
    mid_expo = jnp.where(mid_hit, jnp.exp(mid_full - row_max), 0.0)
    top_expo = jnp.where(top_hit, jnp.exp(top_full - row_max), 0.0)
    denom = base_expo + mid_expo + top_expo
    base_share = base_expo / denom
    mid_share = mid_expo / denom
    top_share = top_expo / denom
    attn = (
        base_share[..., None] * base_out
        + mid_share[..., None] * place_rows(mid_out, R1, mid_shift)
        + top_share[..., None] * place_rows(top_out, ctx_size, top_shift)
    )
    inv_rms = lax.rsqrt(jnp.mean(attn * attn, axis=-1, keepdims=True) + EPS)
    normed = attn * inv_rms
    gain_rows = out_gain.reshape(head_count, HEAD_DIM)
    attended = (normed * gain_rows).astype(jnp.bfloat16).reshape(1, tokens, flat_width)
    grad_full = grad_y[0].reshape(row_shape).astype(jnp.float32)
    gain_part = jnp.sum(grad_full * normed, axis=0).reshape(flat_width)
    grad_norm = grad_full * gain_rows
    grad_attn = inv_rms * (
        grad_norm - normed * jnp.mean(grad_norm * normed, axis=-1, keepdims=True)
    )
    inner = jnp.sum(grad_attn * attn, axis=-1)
    base_low = (base_share[..., None] * grad_attn).astype(jnp.bfloat16)
    base_shift = -(base_share * inner)
    base_grad, base_soft = score_grads(q_own, k_own, v_own, base_total, base_low, base_shift)
    base_dq = query_part(base_grad, k_own)
    base_dk, base_dv = key_parts(base_grad, base_soft, q_own, base_low)

    mid_sel = pick_rows(mid_share[..., None], R1, mid_shift)[..., 0]
    mid_low = (mid_sel[..., None] * pick_rows(grad_attn, R1, mid_shift)).astype(jnp.bfloat16)
    mid_row_shift = -(mid_sel * pick_rows(inner[..., None], R1, mid_shift)[..., 0])
    top_sel = pick_rows(top_share[..., None], ctx_size, top_shift)[..., 0]
    top_low = (top_sel[..., None] * pick_rows(grad_attn, ctx_size, top_shift)).astype(jnp.bfloat16)
    top_row_shift = -(top_sel * pick_rows(inner[..., None], ctx_size, top_shift)[..., 0])

    top_grads = pack_grads(top_low, top_row_shift)
    gain_row = jnp.pad(gain_part, (0, top_grads.shape[1] - flat_width))[None]
    top_block = jnp.concatenate([top_grads, gain_row], 0)
    mid_gathered, gathered = ctx_gather(
        pack_grads(mid_low, mid_row_shift), lane_dense(top_block), SPAN, 1
    )
    gathered = gathered.reshape((-1,) + top_block.shape)
    mid_low_all, mid_shift_all = unpack_grads(
        mid_gathered.reshape(-1, mid_gathered.shape[-1]), head_count
    )
    top_low_all, top_shift_all = unpack_grads(
        gathered[:, :top_rows].reshape(-1, top_grads.shape[1]), head_count
    )
    gain_grad = lax.psum(jnp.sum(gathered[:, top_rows, :flat_width], axis=0), "dp")

    mid_grad, mid_soft = score_grads(
        mid_q, mid_k, mid_v, mid_total_all, mid_low_all, mid_shift_all
    )
    mid_dq = query_part(mid_grad[:, :mid_rows], mid_k)
    mid_dk, mid_dv = key_parts(
        mid_grad[:, :, :mid_rows], mid_soft[:, :, :mid_rows], mid_q, mid_low_all
    )
    top_grad, top_soft = score_grads(
        top_q, top_k, top_v, top_total_all, top_low_all, top_shift_all
    )
    top_dq = query_part(top_grad[:, :top_rows], top_k)
    top_dk, top_dv = key_parts(
        top_grad[:, :, :top_rows], top_soft[:, :, :top_rows], top_q, top_low_all
    )
    query_grad = (
        base_dq + place_rows(mid_dq, R1, mid_shift) + place_rows(top_dq, ctx_size, top_shift)
    )
    key_grad = base_dk + place_rows(mid_dk, R1, mid_shift) + place_rows(top_dk, ctx_size, top_shift)
    value_grad = (
        base_dv + place_rows(mid_dv, R1, mid_shift) + place_rows(top_dv, ctx_size, top_shift)
    )
    out_shape = (1, tokens, flat_width)
    return (
        attended,
        query_grad.astype(jnp.bfloat16).reshape(out_shape),
        key_grad.astype(jnp.bfloat16).reshape(out_shape),
        value_grad.astype(jnp.bfloat16).reshape(out_shape),
        gain_grad,
    )


def solution(mesh):
    in_specs = (
        P("dp", "ctx", "head"),
        P("dp", "ctx", "head"),
        P("dp", "ctx", "head"),
        P("dp", "ctx", "head"),
        P("head"),
        P(None, "head"),
    )
    out_specs = (
        P("dp", "ctx", "head"),
        P("dp", "ctx", "head"),
        P("dp", "ctx", "head"),
        P("dp", "ctx", "head"),
        P("head"),
    )
    return jax.shard_map(shards, mesh=mesh, in_specs=in_specs, out_specs=out_specs, check_vma=False)
```

```python
import functools
import math

import jax
import jax.numpy as jnp
from jax import lax
from jax.experimental import pallas as pl
from jax.experimental.pallas import tpu as pltpu
from jax.sharding import PartitionSpec as P

HEAD_DIM = 128
SPAN = 4
R1 = 8
RING = 8


EPS = 1e-06


def gather_kernel(
    group, inner, mid_x, top_x, mid_out, top_out, stage,
    send_mid, recv_mid, send_a, recv_a, send_b, recv_b, local_sem,
):
    count = lax.axis_size("ctx")
    outer = count // inner
    me = lax.axis_index("ctx")
    row = lax.axis_index("dp")
    col = lax.axis_index("head")
    lo = me % inner
    hi = me // inner
    base = me - me % group
    mesh_ids = pl.DeviceIdType.MESH

    def inner_peer(j):
        return hi * inner + lax.rem(lo + j, inner)

    def outer_peer(j):
        return lax.rem(hi + j, outer) * inner + lo

    barrier = pltpu.get_barrier_semaphore()
    for j in range(1, inner):
        pl.semaphore_signal(barrier, 1, device_id=(row, inner_peer(j), col), device_id_type=mesh_ids)
    for j in range(1, outer):
        pl.semaphore_signal(barrier, 1, device_id=(row, outer_peer(j), col), device_id_type=mesh_ids)
    pl.semaphore_wait(barrier, inner + outer - 2)

    def mid_copy(j):
        peer = base + lax.rem(me % group + j, group)
        return pltpu.make_async_remote_copy(
            mid_x, mid_out.at[j], send_mid.at[j], recv_mid.at[j],
            device_id=(row, peer, col), device_id_type=mesh_ids,
        )

    def copy_a(j):
        return pltpu.make_async_remote_copy(
            top_x, stage.at[j], send_a.at[j], recv_a.at[j],
            device_id=(row, inner_peer(j), col), device_id_type=mesh_ids,
        )

    def copy_b(j):
        return pltpu.make_async_remote_copy(
            stage, top_out.at[j], send_b.at[j], recv_b.at[j],
            device_id=(row, outer_peer(j), col), device_id_type=mesh_ids,
        )

    for j in range(1, inner):
        copy_a(j).start()
    own = pltpu.make_async_copy(top_x, stage.at[0], local_sem)
    own.start()
    mid_out[0] = mid_x[...]
    own.wait()
    for j in range(1, inner):
        copy_a(j).wait()
    for j in range(1, outer):
        copy_b(j).start()
    for j in range(1, group):
        mid_copy(j).start()
    top_out[0] = stage[...]
    for j in range(1, group):
        mid_copy(j).wait()
    for j in range(1, outer):
        copy_b(j).wait()


def ctx_gather(mid_x, top_x, group, tag):
    count = lax.axis_size("ctx")
    inner = RING
    return pl.pallas_call(
        functools.partial(gather_kernel, group, inner),
        out_shape=(
            jax.ShapeDtypeStruct((group,) + mid_x.shape, mid_x.dtype),
            jax.ShapeDtypeStruct((count // inner, inner) + top_x.shape, top_x.dtype),
        ),
        in_specs=[pl.BlockSpec(memory_space=pltpu.VMEM)] * 2,
        out_specs=(pl.BlockSpec(memory_space=pltpu.VMEM),) * 2,
        scratch_shapes=[
            pltpu.VMEM((inner,) + top_x.shape, top_x.dtype),
            pltpu.SemaphoreType.DMA((group,)),
            pltpu.SemaphoreType.DMA((group,)),
            pltpu.SemaphoreType.DMA((inner,)),
            pltpu.SemaphoreType.DMA((inner,)),
            pltpu.SemaphoreType.DMA((count // inner,)),
            pltpu.SemaphoreType.DMA((count // inner,)),
            pltpu.SemaphoreType.DMA,
        ],
        compiler_params=pltpu.CompilerParams(collective_id=tag, has_side_effects=True),
    )(mid_x, top_x)


def lane_dense(block):
    return block.reshape(-1, HEAD_DIM)


def pick_rows(source_rows, dilation, shifts):
    row_count, head_count, head_width = source_rows.shape
    grouped = source_rows.reshape(row_count // dilation, dilation, head_count, head_width)
    hit_mask = jnp.arange(dilation, dtype=jnp.int32).reshape(1, dilation, 1, 1) == shifts.reshape(
        1, 1, head_count, 1
    )
    chosen = jnp.where(hit_mask, grouped, jnp.zeros((), source_rows.dtype))
    return jnp.sum(chosen, axis=1, dtype=source_rows.dtype)


def place_rows(row_values, dilation, shifts):
    row_count, head_count, head_width = row_values.shape
    hit_mask = jnp.arange(dilation, dtype=jnp.int32).reshape(1, dilation, 1, 1) == shifts.reshape(
        1, 1, head_count, 1
    )
    spread = jnp.where(hit_mask, row_values[:, None], jnp.zeros((), row_values.dtype))
    return spread.reshape(row_count * dilation, head_count, head_width)


def level_scores(q_rows, k_rows):
    score_scale = 1.0 / math.sqrt(q_rows.shape[-1])
    return (
        jnp.einsum("qhe,khe->hqk", q_rows, k_rows, preferred_element_type=jnp.float32) * score_scale
    )


def attend(q_rows, k_rows, v_rows):
    scores = level_scores(q_rows, k_rows)
    row_max = jnp.max(scores, axis=-1, keepdims=True)
    log_total = row_max[..., 0] + jnp.log(jnp.sum(jnp.exp(scores - row_max), axis=-1))
    soft_rows = jnp.exp(scores - log_total[..., None]).astype(jnp.bfloat16)
    level_out = jnp.einsum("hqk,khe->qhe", soft_rows, v_rows, preferred_element_type=jnp.float32)
    return (level_out, log_total.T)


def score_grads(q_rows, k_rows, v_rows, log_total, grad_low, row_shift):
    score_scale = 1.0 / math.sqrt(q_rows.shape[-1])
    scores = level_scores(q_rows, k_rows)
    exact_soft = jnp.exp(scores - log_total.T[..., None])
    prob_grad = jnp.einsum("qhe,khe->hqk", grad_low, v_rows, preferred_element_type=jnp.float32)
    score_grad = (exact_soft * (prob_grad + row_shift.T[..., None]) * score_scale).astype(
        jnp.bfloat16
    )
    return (score_grad, exact_soft.astype(jnp.bfloat16))


def key_parts(score_grad, soft_low, q_rows, grad_low):
    k_part = jnp.einsum("hqk,qhe->khe", score_grad, q_rows, preferred_element_type=jnp.float32)
    v_part = jnp.einsum("hqk,qhe->khe", soft_low, grad_low, preferred_element_type=jnp.float32)
    return (k_part, v_part)


def query_part(score_grad, k_rows):
    return jnp.einsum("hqk,khe->qhe", score_grad, k_rows, preferred_element_type=jnp.float32)


def split_qkv(packed, head_count):
    width = head_count * HEAD_DIM
    shape = (packed.shape[0], head_count, HEAD_DIM)
    return tuple(packed[:, i * width : (i + 1) * width].reshape(shape) for i in range(3))


def pack_grads(grad_low, row_shift):
    rows = grad_low.shape[0]
    pad = jnp.zeros((rows, HEAD_DIM - row_shift.shape[1]), jnp.float32)
    return jnp.concatenate(
        [grad_low.astype(jnp.float32).reshape(rows, -1), row_shift.astype(jnp.float32), pad], 1
    )


def unpack_grads(packed, head_count):
    width = head_count * HEAD_DIM
    grad_low = packed[:, :width].astype(jnp.bfloat16).reshape(-1, head_count, HEAD_DIM)
    return grad_low, packed[:, width : width + head_count]


def shards(queries, keys, values, grad_y, out_gain, offsets):
    tokens = queries.shape[1]
    flat_width = queries.shape[2]
    head_count = flat_width // HEAD_DIM
    row_shape = (tokens, head_count, HEAD_DIM)
    q_own = queries[0].reshape(row_shape)
    k_own = keys[0].reshape(row_shape)
    v_own = values[0].reshape(row_shape)
    ctx_size = lax.axis_size("ctx")
    mid_shift = offsets[0]
    top_shift = offsets[1]
    positions = jnp.arange(tokens, dtype=jnp.int32)
    mid_hit = (positions % R1)[:, None] == mid_shift[None, :]
    top_hit = (positions % ctx_size)[:, None] == top_shift[None, :]
    mid_pack = jnp.concatenate(
        [pick_rows(x, R1, mid_shift).reshape(-1, flat_width) for x in (q_own, k_own, v_own)], 1
    )
    top_pack = jnp.concatenate(
        [pick_rows(x, ctx_size, top_shift).reshape(-1, flat_width) for x in (q_own, k_own, v_own)],
        1,
    )
    mid_rows = mid_pack.shape[0]
    top_rows = top_pack.shape[0]
    mid_all, top_all = ctx_gather(mid_pack, lane_dense(top_pack), SPAN, 0)
    mid_all = mid_all.reshape(-1, mid_pack.shape[1])
    top_all = top_all.reshape(-1, top_pack.shape[1])
    mid_q, mid_k, mid_v = split_qkv(mid_all, head_count)
    top_q, top_k, top_v = split_qkv(top_all, head_count)
    base_out, base_total = attend(q_own, k_own, v_own)
    mid_out_all, mid_total_all = attend(mid_q, mid_k, mid_v)
    top_out_all, top_total_all = attend(top_q, top_k, top_v)
    mid_out = mid_out_all[:mid_rows]
    mid_total = mid_total_all[:mid_rows]
    top_out = top_out_all[:top_rows]
    top_total = top_total_all[:top_rows]
    mid_full = place_rows(mid_total[..., None], R1, mid_shift)[..., 0]
    top_full = place_rows(top_total[..., None], ctx_size, top_shift)[..., 0]
    row_max = jnp.maximum(base_total, jnp.where(mid_hit, mid_full, base_total))
    row_max = jnp.maximum(row_max, jnp.where(top_hit, top_full, base_total))
    base_expo = jnp.exp(base_total - row_max)
    mid_expo = jnp.where(mid_hit, jnp.exp(mid_full - row_max), 0.0)
    top_expo = jnp.where(top_hit, jnp.exp(top_full - row_max), 0.0)
    denom = base_expo + mid_expo + top_expo
    base_share = base_expo / denom
    mid_share = mid_expo / denom
    top_share = top_expo / denom
    attn = (
        base_share[..., None] * base_out
        + mid_share[..., None] * place_rows(mid_out, R1, mid_shift)
        + top_share[..., None] * place_rows(top_out, ctx_size, top_shift)
    )
    inv_rms = lax.rsqrt(jnp.mean(attn * attn, axis=-1, keepdims=True) + EPS)
    normed = attn * inv_rms
    gain_rows = out_gain.reshape(head_count, HEAD_DIM)
    attended = (normed * gain_rows).astype(jnp.bfloat16).reshape(1, tokens, flat_width)
    grad_full = grad_y[0].reshape(row_shape).astype(jnp.float32)
    gain_part = jnp.sum(grad_full * normed, axis=0).reshape(flat_width)
    grad_norm = grad_full * gain_rows
    grad_attn = inv_rms * (
        grad_norm - normed * jnp.mean(grad_norm * normed, axis=-1, keepdims=True)
    )
    inner = jnp.sum(grad_attn * attn, axis=-1)
    base_low = (base_share[..., None] * grad_attn).astype(jnp.bfloat16)
    base_shift = -(base_share * inner)
    base_grad, base_soft = score_grads(q_own, k_own, v_own, base_total, base_low, base_shift)
    base_dq = query_part(base_grad, k_own)
    base_dk, base_dv = key_parts(base_grad, base_soft, q_own, base_low)

    mid_sel = pick_rows(mid_share[..., None], R1, mid_shift)[..., 0]
    mid_low = (mid_sel[..., None] * pick_rows(grad_attn, R1, mid_shift)).astype(jnp.bfloat16)
    mid_row_shift = -(mid_sel * pick_rows(inner[..., None], R1, mid_shift)[..., 0])
    top_sel = pick_rows(top_share[..., None], ctx_size, top_shift)[..., 0]
    top_low = (top_sel[..., None] * pick_rows(grad_attn, ctx_size, top_shift)).astype(jnp.bfloat16)
    top_row_shift = -(top_sel * pick_rows(inner[..., None], ctx_size, top_shift)[..., 0])

    top_grads = pack_grads(top_low, top_row_shift)
    gain_row = jnp.pad(gain_part, (0, top_grads.shape[1] - flat_width))[None]
    top_block = jnp.concatenate([top_grads, gain_row], 0)
    mid_gathered, gathered = ctx_gather(
        pack_grads(mid_low, mid_row_shift), lane_dense(top_block), SPAN, 1
    )
    gathered = gathered.reshape((-1,) + top_block.shape)
    mid_low_all, mid_shift_all = unpack_grads(
        mid_gathered.reshape(-1, mid_gathered.shape[-1]), head_count
    )
    top_low_all, top_shift_all = unpack_grads(
        gathered[:, :top_rows].reshape(-1, top_grads.shape[1]), head_count
    )
    gain_grad = lax.psum(jnp.sum(gathered[:, top_rows, :flat_width], axis=0), "dp")

    mid_grad, mid_soft = score_grads(
        mid_q, mid_k, mid_v, mid_total_all, mid_low_all, mid_shift_all
    )
    mid_dq = query_part(mid_grad[:, :mid_rows], mid_k)
    mid_dk, mid_dv = key_parts(
        mid_grad[:, :, :mid_rows], mid_soft[:, :, :mid_rows], mid_q, mid_low_all
    )
    top_grad, top_soft = score_grads(
        top_q, top_k, top_v, top_total_all, top_low_all, top_shift_all
    )
    top_dq = query_part(top_grad[:, :top_rows], top_k)
    top_dk, top_dv = key_parts(
        top_grad[:, :, :top_rows], top_soft[:, :, :top_rows], top_q, top_low_all
    )
    query_grad = (
        base_dq + place_rows(mid_dq, R1, mid_shift) + place_rows(top_dq, ctx_size, top_shift)
    )
    key_grad = base_dk + place_rows(mid_dk, R1, mid_shift) + place_rows(top_dk, ctx_size, top_shift)
    value_grad = (
        base_dv + place_rows(mid_dv, R1, mid_shift) + place_rows(top_dv, ctx_size, top_shift)
    )
    out_shape = (1, tokens, flat_width)
    return (
        attended,
        query_grad.astype(jnp.bfloat16).reshape(out_shape),
        key_grad.astype(jnp.bfloat16).reshape(out_shape),
        value_grad.astype(jnp.bfloat16).reshape(out_shape),
        gain_grad,
    )


def solution(mesh):
    in_specs = (
        P("dp", "ctx", "head"),
        P("dp", "ctx", "head"),
        P("dp", "ctx", "head"),
        P("dp", "ctx", "head"),
        P("head"),
        P(None, "head"),
    )
    out_specs = (
        P("dp", "ctx", "head"),
        P("dp", "ctx", "head"),
        P("dp", "ctx", "head"),
        P("dp", "ctx", "head"),
        P("head"),
    )
    return jax.shard_map(shards, mesh=mesh, in_specs=in_specs, out_specs=out_specs, check_vma=False)
```

```python
import functools
import math

import jax
import jax.numpy as jnp
from jax import lax
from jax.experimental import pallas as pl
from jax.experimental.pallas import tpu as pltpu
from jax.sharding import PartitionSpec as P

HEAD_DIM = 128
SPAN = 4
R1 = 8
RING = 8


EPS = 1e-06


def gather_kernel(
    group, inner, cores, mid_x, top_x, mid_out, top_out, stage,
    send_mid, recv_mid, send_a, recv_a, send_b, recv_b, local_sem,
):
    count = lax.axis_size("ctx")
    outer = count // inner
    me = lax.axis_index("ctx")
    row = lax.axis_index("dp")
    col = lax.axis_index("head")
    other = 1 - row
    lo = me % inner
    hi = me // inner
    base = me - me % group
    mesh_ids = pl.DeviceIdType.MESH

    def inner_peer(j):
        return hi * inner + lax.rem(lo + j, inner)

    def outer_peer(j):
        return lax.rem(hi + j, outer) * inner + lo

    barrier = pltpu.get_barrier_semaphore()
    for j in range(1, inner):
        pl.semaphore_signal(barrier, 1, device_id=(row, inner_peer(j), col), device_id_type=mesh_ids)
    if cores == 2:
        for j in range(inner):
            pl.semaphore_signal(
                barrier, 1, device_id=(other, inner_peer(j), col), device_id_type=mesh_ids
            )
    for j in range(1, outer):
        pl.semaphore_signal(barrier, 1, device_id=(row, outer_peer(j), col), device_id_type=mesh_ids)
    pl.semaphore_wait(barrier, inner + outer - 2 + (inner if cores == 2 else 0))

    def mid_copy(j):
        peer = base + lax.rem(me % group + j, group)
        return pltpu.make_async_remote_copy(
            mid_x, mid_out.at[j], send_mid.at[j], recv_mid.at[j],
            device_id=(row, peer, col), device_id_type=mesh_ids,
        )

    def copy_a(c, j):
        return pltpu.make_async_remote_copy(
            top_x, stage.at[c, j], send_a.at[c * inner + j], recv_a.at[c * inner + j],
            device_id=(other if c else row, inner_peer(j), col), device_id_type=mesh_ids,
        )

    def copy_b(j):
        return pltpu.make_async_remote_copy(
            stage, top_out.at[j], send_b.at[j], recv_b.at[j],
            device_id=(row, outer_peer(j), col), device_id_type=mesh_ids,
        )

    peers_a = [(0, j) for j in range(1, inner)] + [(1, j) for j in range(inner) if cores == 2]
    for c, j in peers_a:
        copy_a(c, j).start()
    for j in range(1, group):
        mid_copy(j).start()
    own = pltpu.make_async_copy(top_x, stage.at[0, 0], local_sem)
    own.start()
    mid_out[0] = mid_x[...]
    own.wait()
    for c, j in peers_a:
        copy_a(c, j).wait()
    for j in range(1, outer):
        copy_b(j).start()
    top_out[0] = stage[...]
    for j in range(1, group):
        mid_copy(j).wait()
    for j in range(1, outer):
        copy_b(j).wait()


def ctx_gather(mid_x, top_x, group, tag, cores=1):
    count = lax.axis_size("ctx")
    inner = RING
    return pl.pallas_call(
        functools.partial(gather_kernel, group, inner, cores),
        out_shape=(
            jax.ShapeDtypeStruct((group,) + mid_x.shape, mid_x.dtype),
            jax.ShapeDtypeStruct((count // inner, cores, inner) + top_x.shape, top_x.dtype),
        ),
        in_specs=[pl.BlockSpec(memory_space=pltpu.VMEM)] * 2,
        out_specs=(pl.BlockSpec(memory_space=pltpu.VMEM),) * 2,
        scratch_shapes=[
            pltpu.VMEM((cores, inner) + top_x.shape, top_x.dtype),
            pltpu.SemaphoreType.DMA((group,)),
            pltpu.SemaphoreType.DMA((group,)),
            pltpu.SemaphoreType.DMA((cores * inner,)),
            pltpu.SemaphoreType.DMA((cores * inner,)),
            pltpu.SemaphoreType.DMA((count // inner,)),
            pltpu.SemaphoreType.DMA((count // inner,)),
            pltpu.SemaphoreType.DMA,
        ],
        compiler_params=pltpu.CompilerParams(collective_id=tag, has_side_effects=True),
    )(mid_x, top_x)


def lane_dense(block):
    return block.reshape(-1, HEAD_DIM)


def pick_rows(source_rows, dilation, shifts):
    row_count, head_count, head_width = source_rows.shape
    grouped = source_rows.reshape(row_count // dilation, dilation, head_count, head_width)
    hit_mask = jnp.arange(dilation, dtype=jnp.int32).reshape(1, dilation, 1, 1) == shifts.reshape(
        1, 1, head_count, 1
    )
    chosen = jnp.where(hit_mask, grouped, jnp.zeros((), source_rows.dtype))
    return jnp.sum(chosen, axis=1, dtype=source_rows.dtype)


def place_rows(row_values, dilation, shifts):
    row_count, head_count, head_width = row_values.shape
    hit_mask = jnp.arange(dilation, dtype=jnp.int32).reshape(1, dilation, 1, 1) == shifts.reshape(
        1, 1, head_count, 1
    )
    spread = jnp.where(hit_mask, row_values[:, None], jnp.zeros((), row_values.dtype))
    return spread.reshape(row_count * dilation, head_count, head_width)


def level_scores(q_rows, k_rows):
    score_scale = 1.0 / math.sqrt(q_rows.shape[-1])
    return (
        jnp.einsum("qhe,khe->hqk", q_rows, k_rows, preferred_element_type=jnp.float32) * score_scale
    )


def attend(q_rows, k_rows, v_rows):
    scores = level_scores(q_rows, k_rows)
    row_max = jnp.max(scores, axis=-1, keepdims=True)
    log_total = row_max[..., 0] + jnp.log(jnp.sum(jnp.exp(scores - row_max), axis=-1))
    soft_rows = jnp.exp(scores - log_total[..., None]).astype(jnp.bfloat16)
    level_out = jnp.einsum("hqk,khe->qhe", soft_rows, v_rows, preferred_element_type=jnp.float32)
    return (level_out, log_total.T)


def score_grads(q_rows, k_rows, v_rows, log_total, grad_low, row_shift):
    score_scale = 1.0 / math.sqrt(q_rows.shape[-1])
    scores = level_scores(q_rows, k_rows)
    exact_soft = jnp.exp(scores - log_total.T[..., None])
    prob_grad = jnp.einsum("qhe,khe->hqk", grad_low, v_rows, preferred_element_type=jnp.float32)
    score_grad = (exact_soft * (prob_grad + row_shift.T[..., None]) * score_scale).astype(
        jnp.bfloat16
    )
    return (score_grad, exact_soft.astype(jnp.bfloat16))


def key_parts(score_grad, soft_low, q_rows, grad_low):
    k_part = jnp.einsum("hqk,qhe->khe", score_grad, q_rows, preferred_element_type=jnp.float32)
    v_part = jnp.einsum("hqk,qhe->khe", soft_low, grad_low, preferred_element_type=jnp.float32)
    return (k_part, v_part)


def query_part(score_grad, k_rows):
    return jnp.einsum("hqk,khe->qhe", score_grad, k_rows, preferred_element_type=jnp.float32)


def split_qkv(packed, head_count):
    width = head_count * HEAD_DIM
    shape = (packed.shape[0], head_count, HEAD_DIM)
    return tuple(packed[:, i * width : (i + 1) * width].reshape(shape) for i in range(3))


def pack_grads(grad_low, row_shift):
    rows = grad_low.shape[0]
    pad = jnp.zeros((rows, HEAD_DIM - row_shift.shape[1]), jnp.float32)
    return jnp.concatenate(
        [grad_low.astype(jnp.float32).reshape(rows, -1), row_shift.astype(jnp.float32), pad], 1
    )


def unpack_grads(packed, head_count):
    width = head_count * HEAD_DIM
    grad_low = packed[:, :width].astype(jnp.bfloat16).reshape(-1, head_count, HEAD_DIM)
    return grad_low, packed[:, width : width + head_count]


def shards(queries, keys, values, grad_y, out_gain, offsets):
    tokens = queries.shape[1]
    flat_width = queries.shape[2]
    head_count = flat_width // HEAD_DIM
    row_shape = (tokens, head_count, HEAD_DIM)
    q_own = queries[0].reshape(row_shape)
    k_own = keys[0].reshape(row_shape)
    v_own = values[0].reshape(row_shape)
    ctx_size = lax.axis_size("ctx")
    mid_shift = offsets[0]
    top_shift = offsets[1]
    positions = jnp.arange(tokens, dtype=jnp.int32)
    mid_hit = (positions % R1)[:, None] == mid_shift[None, :]
    top_hit = (positions % ctx_size)[:, None] == top_shift[None, :]
    mid_pack = jnp.concatenate(
        [pick_rows(x, R1, mid_shift).reshape(-1, flat_width) for x in (q_own, k_own, v_own)], 1
    )
    top_pack = jnp.concatenate(
        [pick_rows(x, ctx_size, top_shift).reshape(-1, flat_width) for x in (q_own, k_own, v_own)],
        1,
    )
    mid_rows = mid_pack.shape[0]
    top_rows = top_pack.shape[0]
    mid_all, top_all = ctx_gather(mid_pack, lane_dense(top_pack), SPAN, 0)
    mid_all = mid_all.reshape(-1, mid_pack.shape[1])
    top_all = top_all.reshape(-1, top_pack.shape[1])
    mid_q, mid_k, mid_v = split_qkv(mid_all, head_count)
    top_q, top_k, top_v = split_qkv(top_all, head_count)
    base_out, base_total = attend(q_own, k_own, v_own)
    mid_out_all, mid_total_all = attend(mid_q, mid_k, mid_v)
    top_out_all, top_total_all = attend(top_q, top_k, top_v)
    mid_out = mid_out_all[:mid_rows]
    mid_total = mid_total_all[:mid_rows]
    top_out = top_out_all[:top_rows]
    top_total = top_total_all[:top_rows]
    mid_full = place_rows(mid_total[..., None], R1, mid_shift)[..., 0]
    top_full = place_rows(top_total[..., None], ctx_size, top_shift)[..., 0]
    row_max = jnp.maximum(base_total, jnp.where(mid_hit, mid_full, base_total))
    row_max = jnp.maximum(row_max, jnp.where(top_hit, top_full, base_total))
    base_expo = jnp.exp(base_total - row_max)
    mid_expo = jnp.where(mid_hit, jnp.exp(mid_full - row_max), 0.0)
    top_expo = jnp.where(top_hit, jnp.exp(top_full - row_max), 0.0)
    denom = base_expo + mid_expo + top_expo
    base_share = base_expo / denom
    mid_share = mid_expo / denom
    top_share = top_expo / denom
    attn = (
        base_share[..., None] * base_out
        + mid_share[..., None] * place_rows(mid_out, R1, mid_shift)
        + top_share[..., None] * place_rows(top_out, ctx_size, top_shift)
    )
    inv_rms = lax.rsqrt(jnp.mean(attn * attn, axis=-1, keepdims=True) + EPS)
    normed = attn * inv_rms
    gain_rows = out_gain.reshape(head_count, HEAD_DIM)
    attended = (normed * gain_rows).astype(jnp.bfloat16).reshape(1, tokens, flat_width)
    grad_full = grad_y[0].reshape(row_shape).astype(jnp.float32)
    gain_part = jnp.sum(grad_full * normed, axis=0).reshape(flat_width)
    grad_norm = grad_full * gain_rows
    grad_attn = inv_rms * (
        grad_norm - normed * jnp.mean(grad_norm * normed, axis=-1, keepdims=True)
    )
    inner = jnp.sum(grad_attn * attn, axis=-1)
    base_low = (base_share[..., None] * grad_attn).astype(jnp.bfloat16)
    base_shift = -(base_share * inner)
    base_grad, base_soft = score_grads(q_own, k_own, v_own, base_total, base_low, base_shift)
    base_dq = query_part(base_grad, k_own)
    base_dk, base_dv = key_parts(base_grad, base_soft, q_own, base_low)

    mid_sel = pick_rows(mid_share[..., None], R1, mid_shift)[..., 0]
    mid_low = (mid_sel[..., None] * pick_rows(grad_attn, R1, mid_shift)).astype(jnp.bfloat16)
    mid_row_shift = -(mid_sel * pick_rows(inner[..., None], R1, mid_shift)[..., 0])
    top_sel = pick_rows(top_share[..., None], ctx_size, top_shift)[..., 0]
    top_low = (top_sel[..., None] * pick_rows(grad_attn, ctx_size, top_shift)).astype(jnp.bfloat16)
    top_row_shift = -(top_sel * pick_rows(inner[..., None], ctx_size, top_shift)[..., 0])

    top_grads = pack_grads(top_low, top_row_shift)
    gain_row = jnp.pad(gain_part, (0, top_grads.shape[1] - flat_width))[None]
    top_block = jnp.concatenate([top_grads, gain_row], 0)
    mid_gathered, both = ctx_gather(
        pack_grads(mid_low, mid_row_shift), lane_dense(top_block), SPAN, 1, cores=2
    )
    both = both.reshape(both.shape[:3] + top_block.shape)
    gathered = both[:, 0].reshape((-1,) + top_block.shape)
    mid_low_all, mid_shift_all = unpack_grads(
        mid_gathered.reshape(-1, mid_gathered.shape[-1]), head_count
    )
    top_low_all, top_shift_all = unpack_grads(
        gathered[:, :top_rows].reshape(-1, top_grads.shape[1]), head_count
    )
    gain_grad = jnp.sum(both[:, :, :, top_rows, :flat_width], axis=(0, 1, 2))

    mid_grad, mid_soft = score_grads(
        mid_q, mid_k, mid_v, mid_total_all, mid_low_all, mid_shift_all
    )
    mid_dq = query_part(mid_grad[:, :mid_rows], mid_k)
    mid_dk, mid_dv = key_parts(
        mid_grad[:, :, :mid_rows], mid_soft[:, :, :mid_rows], mid_q, mid_low_all
    )
    top_grad, top_soft = score_grads(
        top_q, top_k, top_v, top_total_all, top_low_all, top_shift_all
    )
    top_dq = query_part(top_grad[:, :top_rows], top_k)
    top_dk, top_dv = key_parts(
        top_grad[:, :, :top_rows], top_soft[:, :, :top_rows], top_q, top_low_all
    )
    query_grad = (
        base_dq + place_rows(mid_dq, R1, mid_shift) + place_rows(top_dq, ctx_size, top_shift)
    )
    key_grad = base_dk + place_rows(mid_dk, R1, mid_shift) + place_rows(top_dk, ctx_size, top_shift)
    value_grad = (
        base_dv + place_rows(mid_dv, R1, mid_shift) + place_rows(top_dv, ctx_size, top_shift)
    )
    out_shape = (1, tokens, flat_width)
    return (
        attended,
        query_grad.astype(jnp.bfloat16).reshape(out_shape),
        key_grad.astype(jnp.bfloat16).reshape(out_shape),
        value_grad.astype(jnp.bfloat16).reshape(out_shape),
        gain_grad,
    )


def solution(mesh):
    in_specs = (
        P("dp", "ctx", "head"),
        P("dp", "ctx", "head"),
        P("dp", "ctx", "head"),
        P("dp", "ctx", "head"),
        P("head"),
        P(None, "head"),
    )
    out_specs = (
        P("dp", "ctx", "head"),
        P("dp", "ctx", "head"),
        P("dp", "ctx", "head"),
        P("dp", "ctx", "head"),
        P("head"),
    )
    return jax.shard_map(shards, mesh=mesh, in_specs=in_specs, out_specs=out_specs, check_vma=False)
```

```python
import functools
import math

import jax
import jax.numpy as jnp
from jax import lax
from jax.experimental import pallas as pl
from jax.experimental.pallas import tpu as pltpu
from jax.sharding import PartitionSpec as P

HEAD_DIM = 128
SPAN = 4
R1 = 8
RING = 8


EPS = 1e-06


def gather_kernel(
    group, inner, mid_x, top_x, mid_out, top_out, stage,
    send_mid, recv_mid, send_a, recv_a, send_b, recv_b, local_sem,
):
    count = lax.axis_size("ctx")
    outer = count // inner
    me = lax.axis_index("ctx")
    row = lax.axis_index("dp")
    col = lax.axis_index("head")
    lo = me % inner
    hi = me // inner
    base = me - me % group
    mesh_ids = pl.DeviceIdType.MESH

    def inner_peer(j):
        return hi * inner + lax.rem(lo + j, inner)

    def outer_peer(j):
        return lax.rem(hi + j, outer) * inner + lo

    barrier = pltpu.get_barrier_semaphore()
    for j in range(1, inner):
        pl.semaphore_signal(barrier, 1, device_id=(row, inner_peer(j), col), device_id_type=mesh_ids)
    for j in range(1, outer):
        pl.semaphore_signal(barrier, 1, device_id=(row, outer_peer(j), col), device_id_type=mesh_ids)
    pl.semaphore_wait(barrier, inner + outer - 2)

    def mid_copy(j):
        peer = base + lax.rem(me % group + j, group)
        return pltpu.make_async_remote_copy(
            mid_x, mid_out.at[j], send_mid.at[j], recv_mid.at[j],
            device_id=(row, peer, col), device_id_type=mesh_ids,
        )

    def copy_a(j):
        return pltpu.make_async_remote_copy(
            top_x, stage.at[j], send_a.at[j], recv_a.at[j],
            device_id=(row, inner_peer(j), col), device_id_type=mesh_ids,
        )

    def copy_b(j):
        return pltpu.make_async_remote_copy(
            stage, top_out.at[j], send_b.at[j], recv_b.at[j],
            device_id=(row, outer_peer(j), col), device_id_type=mesh_ids,
        )

    for j in range(1, inner):
        copy_a(j).start()
    for j in range(1, group):
        mid_copy(j).start()
    own = pltpu.make_async_copy(top_x, stage.at[0], local_sem)
    own.start()
    mid_out[0] = mid_x[...]
    own.wait()
    for j in range(1, inner):
        copy_a(j).wait()
    for j in range(1, outer):
        copy_b(j).start()
    top_out[0] = stage[...]
    for j in range(1, group):
        mid_copy(j).wait()
    for j in range(1, outer):
        copy_b(j).wait()


def ctx_gather(mid_x, top_x, group, tag):
    count = lax.axis_size("ctx")
    inner = RING
    return pl.pallas_call(
        functools.partial(gather_kernel, group, inner),
        out_shape=(
            jax.ShapeDtypeStruct((group,) + mid_x.shape, mid_x.dtype),
            jax.ShapeDtypeStruct((count // inner, inner) + top_x.shape, top_x.dtype),
        ),
        in_specs=[pl.BlockSpec(memory_space=pltpu.VMEM)] * 2,
        out_specs=(pl.BlockSpec(memory_space=pltpu.VMEM),) * 2,
        scratch_shapes=[
            pltpu.VMEM((inner,) + top_x.shape, top_x.dtype),
            pltpu.SemaphoreType.DMA((group,)),
            pltpu.SemaphoreType.DMA((group,)),
            pltpu.SemaphoreType.DMA((inner,)),
            pltpu.SemaphoreType.DMA((inner,)),
            pltpu.SemaphoreType.DMA((count // inner,)),
            pltpu.SemaphoreType.DMA((count // inner,)),
            pltpu.SemaphoreType.DMA,
        ],
        compiler_params=pltpu.CompilerParams(collective_id=tag, has_side_effects=True),
    )(mid_x, top_x)


def lane_dense(block):
    return block.reshape(-1, HEAD_DIM)


def pick_rows(source_rows, dilation, shifts):
    row_count, head_count, head_width = source_rows.shape
    grouped = source_rows.reshape(row_count // dilation, dilation, head_count, head_width)
    hit_mask = jnp.arange(dilation, dtype=jnp.int32).reshape(1, dilation, 1, 1) == shifts.reshape(
        1, 1, head_count, 1
    )
    chosen = jnp.where(hit_mask, grouped, jnp.zeros((), source_rows.dtype))
    return jnp.sum(chosen, axis=1, dtype=source_rows.dtype)


def place_rows(row_values, dilation, shifts):
    row_count, head_count, head_width = row_values.shape
    hit_mask = jnp.arange(dilation, dtype=jnp.int32).reshape(1, dilation, 1, 1) == shifts.reshape(
        1, 1, head_count, 1
    )
    spread = jnp.where(hit_mask, row_values[:, None], jnp.zeros((), row_values.dtype))
    return spread.reshape(row_count * dilation, head_count, head_width)


def level_scores(q_rows, k_rows):
    score_scale = 1.0 / math.sqrt(q_rows.shape[-1])
    return (
        jnp.einsum("qhe,khe->hqk", q_rows, k_rows, preferred_element_type=jnp.float32) * score_scale
    )


def attend(q_rows, k_rows, v_rows):
    scores = level_scores(q_rows, k_rows)
    row_max = jnp.max(scores, axis=-1, keepdims=True)
    log_total = row_max[..., 0] + jnp.log(jnp.sum(jnp.exp(scores - row_max), axis=-1))
    soft_rows = jnp.exp(scores - log_total[..., None]).astype(jnp.bfloat16)
    level_out = jnp.einsum("hqk,khe->qhe", soft_rows, v_rows, preferred_element_type=jnp.float32)
    return (level_out, log_total.T)


def score_grads(q_rows, k_rows, v_rows, log_total, grad_low, row_shift):
    score_scale = 1.0 / math.sqrt(q_rows.shape[-1])
    scores = level_scores(q_rows, k_rows)
    exact_soft = jnp.exp(scores - log_total.T[..., None])
    prob_grad = jnp.einsum("qhe,khe->hqk", grad_low, v_rows, preferred_element_type=jnp.float32)
    score_grad = (exact_soft * (prob_grad + row_shift.T[..., None]) * score_scale).astype(
        jnp.bfloat16
    )
    return (score_grad, exact_soft.astype(jnp.bfloat16))


def key_parts(score_grad, soft_low, q_rows, grad_low):
    k_part = jnp.einsum("hqk,qhe->khe", score_grad, q_rows, preferred_element_type=jnp.float32)
    v_part = jnp.einsum("hqk,qhe->khe", soft_low, grad_low, preferred_element_type=jnp.float32)
    return (k_part, v_part)


def query_part(score_grad, k_rows):
    return jnp.einsum("hqk,khe->qhe", score_grad, k_rows, preferred_element_type=jnp.float32)


def split_qkv(packed, head_count):
    width = head_count * HEAD_DIM
    shape = (packed.shape[0], head_count, HEAD_DIM)
    return tuple(packed[:, i * width : (i + 1) * width].reshape(shape) for i in range(3))


def split_wide(values):
    high = values.astype(jnp.bfloat16)
    low = (values - high.astype(jnp.float32)).astype(jnp.bfloat16)
    return high, low


def join_wide(high, low):
    return high.astype(jnp.float32) + low.astype(jnp.float32)


def pack_grads(grad_low, row_shift, width):
    rows = grad_low.shape[0]
    high, low = split_wide(row_shift)
    used = grad_low.shape[1] * grad_low.shape[2] + 2 * row_shift.shape[1]
    return jnp.concatenate(
        [grad_low.reshape(rows, -1), high, low, jnp.zeros((rows, width - used), jnp.bfloat16)], 1
    )


def unpack_grads(packed, head_count):
    width = head_count * HEAD_DIM
    grad_low = packed[:, :width].reshape(-1, head_count, HEAD_DIM)
    return grad_low, join_wide(
        packed[:, width : width + head_count], packed[:, width + head_count : width + 2 * head_count]
    )


def shards(queries, keys, values, grad_y, out_gain, offsets):
    tokens = queries.shape[1]
    flat_width = queries.shape[2]
    head_count = flat_width // HEAD_DIM
    row_shape = (tokens, head_count, HEAD_DIM)
    q_own = queries[0].reshape(row_shape)
    k_own = keys[0].reshape(row_shape)
    v_own = values[0].reshape(row_shape)
    ctx_size = lax.axis_size("ctx")
    mid_shift = offsets[0]
    top_shift = offsets[1]
    positions = jnp.arange(tokens, dtype=jnp.int32)
    mid_hit = (positions % R1)[:, None] == mid_shift[None, :]
    top_hit = (positions % ctx_size)[:, None] == top_shift[None, :]
    mid_pack = jnp.concatenate(
        [pick_rows(x, R1, mid_shift).reshape(-1, flat_width) for x in (q_own, k_own, v_own)], 1
    )
    top_pack = jnp.concatenate(
        [pick_rows(x, ctx_size, top_shift).reshape(-1, flat_width) for x in (q_own, k_own, v_own)],
        1,
    )
    mid_rows = mid_pack.shape[0]
    top_rows = top_pack.shape[0]
    mid_all, top_all = ctx_gather(mid_pack, lane_dense(top_pack), SPAN, 0)
    mid_all = mid_all.reshape(-1, mid_pack.shape[1])
    top_all = top_all.reshape(-1, top_pack.shape[1])
    mid_q, mid_k, mid_v = split_qkv(mid_all, head_count)
    top_q, top_k, top_v = split_qkv(top_all, head_count)
    base_out, base_total = attend(q_own, k_own, v_own)
    mid_out_all, mid_total_all = attend(mid_q, mid_k, mid_v)
    top_out_all, top_total_all = attend(top_q, top_k, top_v)
    mid_out = mid_out_all[:mid_rows]
    mid_total = mid_total_all[:mid_rows]
    top_out = top_out_all[:top_rows]
    top_total = top_total_all[:top_rows]
    mid_full = place_rows(mid_total[..., None], R1, mid_shift)[..., 0]
    top_full = place_rows(top_total[..., None], ctx_size, top_shift)[..., 0]
    row_max = jnp.maximum(base_total, jnp.where(mid_hit, mid_full, base_total))
    row_max = jnp.maximum(row_max, jnp.where(top_hit, top_full, base_total))
    base_expo = jnp.exp(base_total - row_max)
    mid_expo = jnp.where(mid_hit, jnp.exp(mid_full - row_max), 0.0)
    top_expo = jnp.where(top_hit, jnp.exp(top_full - row_max), 0.0)
    denom = base_expo + mid_expo + top_expo
    base_share = base_expo / denom
    mid_share = mid_expo / denom
    top_share = top_expo / denom
    attn = (
        base_share[..., None] * base_out
        + mid_share[..., None] * place_rows(mid_out, R1, mid_shift)
        + top_share[..., None] * place_rows(top_out, ctx_size, top_shift)
    )
    inv_rms = lax.rsqrt(jnp.mean(attn * attn, axis=-1, keepdims=True) + EPS)
    normed = attn * inv_rms
    gain_rows = out_gain.reshape(head_count, HEAD_DIM)
    attended = (normed * gain_rows).astype(jnp.bfloat16).reshape(1, tokens, flat_width)
    grad_full = grad_y[0].reshape(row_shape).astype(jnp.float32)
    gain_part = jnp.sum(grad_full * normed, axis=0).reshape(flat_width)
    grad_norm = grad_full * gain_rows
    grad_attn = inv_rms * (
        grad_norm - normed * jnp.mean(grad_norm * normed, axis=-1, keepdims=True)
    )
    inner = jnp.sum(grad_attn * attn, axis=-1)
    base_low = (base_share[..., None] * grad_attn).astype(jnp.bfloat16)
    base_shift = -(base_share * inner)
    base_grad, base_soft = score_grads(q_own, k_own, v_own, base_total, base_low, base_shift)
    base_dq = query_part(base_grad, k_own)
    base_dk, base_dv = key_parts(base_grad, base_soft, q_own, base_low)

    mid_sel = pick_rows(mid_share[..., None], R1, mid_shift)[..., 0]
    mid_low = (mid_sel[..., None] * pick_rows(grad_attn, R1, mid_shift)).astype(jnp.bfloat16)
    mid_row_shift = -(mid_sel * pick_rows(inner[..., None], R1, mid_shift)[..., 0])
    top_sel = pick_rows(top_share[..., None], ctx_size, top_shift)[..., 0]
    top_low = (top_sel[..., None] * pick_rows(grad_attn, ctx_size, top_shift)).astype(jnp.bfloat16)
    top_row_shift = -(top_sel * pick_rows(inner[..., None], ctx_size, top_shift)[..., 0])

    gain_high, gain_low = split_wide(gain_part)
    shift_high, shift_low = split_wide(top_row_shift.reshape(-1))
    top_flat = jnp.concatenate(
        [top_low.reshape(-1), gain_high, gain_low, shift_high, shift_low]
    )
    top_flat = jnp.pad(top_flat, (0, -top_flat.shape[0] % HEAD_DIM))
    mid_gathered, gathered = ctx_gather(
        pack_grads(mid_low, mid_row_shift, flat_width + HEAD_DIM),
        lane_dense(top_flat),
        SPAN,
        1,
    )
    mid_low_all, mid_shift_all = unpack_grads(
        mid_gathered.reshape(-1, mid_gathered.shape[-1]), head_count
    )
    gathered = gathered.reshape(ctx_size, -1)
    grad_width = top_rows * flat_width
    top_low_all = gathered[:, :grad_width].reshape(-1, head_count, HEAD_DIM)
    gain_cols = gathered[:, grad_width : grad_width + 2 * flat_width]
    gain_grad = lax.psum(
        jnp.sum(join_wide(gain_cols[:, :flat_width], gain_cols[:, flat_width:]), axis=0), "dp"
    )
    shift_start = grad_width + 2 * flat_width
    shift_count = top_rows * head_count
    top_shift_all = join_wide(
        gathered[:, shift_start : shift_start + shift_count],
        gathered[:, shift_start + shift_count : shift_start + 2 * shift_count],
    ).reshape(-1, head_count)

    mid_grad, mid_soft = score_grads(
        mid_q, mid_k, mid_v, mid_total_all, mid_low_all, mid_shift_all
    )
    mid_dq = query_part(mid_grad[:, :mid_rows], mid_k)
    mid_dk, mid_dv = key_parts(
        mid_grad[:, :, :mid_rows], mid_soft[:, :, :mid_rows], mid_q, mid_low_all
    )
    top_grad, top_soft = score_grads(
        top_q, top_k, top_v, top_total_all, top_low_all, top_shift_all
    )
    top_dq = query_part(top_grad[:, :top_rows], top_k)
    top_dk, top_dv = key_parts(
        top_grad[:, :, :top_rows], top_soft[:, :, :top_rows], top_q, top_low_all
    )
    query_grad = (
        base_dq + place_rows(mid_dq, R1, mid_shift) + place_rows(top_dq, ctx_size, top_shift)
    )
    key_grad = base_dk + place_rows(mid_dk, R1, mid_shift) + place_rows(top_dk, ctx_size, top_shift)
    value_grad = (
        base_dv + place_rows(mid_dv, R1, mid_shift) + place_rows(top_dv, ctx_size, top_shift)
    )
    out_shape = (1, tokens, flat_width)
    return (
        attended,
        query_grad.astype(jnp.bfloat16).reshape(out_shape),
        key_grad.astype(jnp.bfloat16).reshape(out_shape),
        value_grad.astype(jnp.bfloat16).reshape(out_shape),
        gain_grad,
    )


def solution(mesh):
    in_specs = (
        P("dp", "ctx", "head"),
        P("dp", "ctx", "head"),
        P("dp", "ctx", "head"),
        P("dp", "ctx", "head"),
        P("head"),
        P(None, "head"),
    )
    out_specs = (
        P("dp", "ctx", "head"),
        P("dp", "ctx", "head"),
        P("dp", "ctx", "head"),
        P("dp", "ctx", "head"),
        P("head"),
    )
    return jax.shard_map(shards, mesh=mesh, in_specs=in_specs, out_specs=out_specs, check_vma=False)
```

```python
import functools
import math

import jax
import jax.numpy as jnp
from jax import lax
from jax.experimental import pallas as pl
from jax.experimental.pallas import tpu as pltpu
from jax.sharding import PartitionSpec as P

HEAD_DIM = 128
SPAN = 4
R1 = 8
RING = 8


EPS = 1e-06


def gather_kernel(group, inner, has_sum, *refs):
    if has_sum:
        (mid_x, top_x, sum_x, mid_out, top_out, sum_out, stage, sum_stage, row_sum,
         send_mid, recv_mid, send_a, recv_a, send_b, recv_b, local_sem,
         send_sa, recv_sa, send_sb, recv_sb) = refs
    else:
        (mid_x, top_x, mid_out, top_out, stage,
         send_mid, recv_mid, send_a, recv_a, send_b, recv_b, local_sem) = refs
    count = lax.axis_size("ctx")
    outer = count // inner
    me = lax.axis_index("ctx")
    row = lax.axis_index("dp")
    col = lax.axis_index("head")
    lo = me % inner
    hi = me // inner
    base = me - me % group
    mesh_ids = pl.DeviceIdType.MESH

    def inner_peer(j):
        return hi * inner + lax.rem(lo + j, inner)

    def outer_peer(j):
        return lax.rem(hi + j, outer) * inner + lo

    barrier = pltpu.get_barrier_semaphore()
    for j in range(1, inner):
        pl.semaphore_signal(barrier, 1, device_id=(row, inner_peer(j), col), device_id_type=mesh_ids)
    for j in range(1, outer):
        pl.semaphore_signal(barrier, 1, device_id=(row, outer_peer(j), col), device_id_type=mesh_ids)
    pl.semaphore_wait(barrier, inner + outer - 2)

    def remote(src, dst, send, recv, peer):
        return pltpu.make_async_remote_copy(
            src, dst, send, recv, device_id=(row, peer, col), device_id_type=mesh_ids
        )

    def mid_copy(j):
        peer = base + lax.rem(me % group + j, group)
        return remote(mid_x, mid_out.at[j], send_mid.at[j], recv_mid.at[j], peer)

    def copy_a(j):
        return remote(top_x, stage.at[j], send_a.at[j], recv_a.at[j], inner_peer(j))

    def copy_b(j):
        return remote(stage, top_out.at[j], send_b.at[j], recv_b.at[j], outer_peer(j))

    def sum_a(j):
        return remote(sum_x, sum_stage.at[j], send_sa.at[j], recv_sa.at[j], inner_peer(j))

    def sum_b(j):
        return remote(row_sum, sum_out.at[j], send_sb.at[j], recv_sb.at[j], outer_peer(j))

    for j in range(1, inner):
        copy_a(j).start()
        if has_sum:
            sum_a(j).start()
    for j in range(1, group):
        mid_copy(j).start()
    own = pltpu.make_async_copy(top_x, stage.at[0], local_sem)
    own.start()
    mid_out[0] = mid_x[...]
    own.wait()
    for j in range(1, inner):
        copy_a(j).wait()
    for j in range(1, outer):
        copy_b(j).start()
    if has_sum:
        total = sum_x[...]
        for j in range(1, inner):
            sum_a(j).wait()
            total = total + sum_stage[j]
        row_sum[...] = total
        for j in range(1, outer):
            sum_b(j).start()
        sum_out[0] = total
    top_out[0] = stage[...]
    for j in range(1, group):
        mid_copy(j).wait()
    for j in range(1, outer):
        copy_b(j).wait()
        if has_sum:
            sum_b(j).wait()


def ctx_gather(mid_x, top_x, group, tag, sum_x=None):
    count = lax.axis_size("ctx")
    inner = RING
    outer = count // inner
    has_sum = sum_x is not None
    operands = (mid_x, top_x) + ((sum_x,) if has_sum else ())
    out_shape = (
        jax.ShapeDtypeStruct((group,) + mid_x.shape, mid_x.dtype),
        jax.ShapeDtypeStruct((outer, inner) + top_x.shape, top_x.dtype),
    )
    scratch = [pltpu.VMEM((inner,) + top_x.shape, top_x.dtype)]
    if has_sum:
        out_shape += (jax.ShapeDtypeStruct((outer,) + sum_x.shape, sum_x.dtype),)
        scratch += [
            pltpu.VMEM((inner,) + sum_x.shape, sum_x.dtype),
            pltpu.VMEM(sum_x.shape, sum_x.dtype),
        ]
    scratch += [
        pltpu.SemaphoreType.DMA((group,)),
        pltpu.SemaphoreType.DMA((group,)),
        pltpu.SemaphoreType.DMA((inner,)),
        pltpu.SemaphoreType.DMA((inner,)),
        pltpu.SemaphoreType.DMA((outer,)),
        pltpu.SemaphoreType.DMA((outer,)),
        pltpu.SemaphoreType.DMA,
    ]
    if has_sum:
        scratch += [
            pltpu.SemaphoreType.DMA((inner,)),
            pltpu.SemaphoreType.DMA((inner,)),
            pltpu.SemaphoreType.DMA((outer,)),
            pltpu.SemaphoreType.DMA((outer,)),
        ]
    return pl.pallas_call(
        functools.partial(gather_kernel, group, inner, has_sum),
        out_shape=out_shape,
        in_specs=[pl.BlockSpec(memory_space=pltpu.VMEM)] * len(operands),
        out_specs=(pl.BlockSpec(memory_space=pltpu.VMEM),) * len(out_shape),
        scratch_shapes=scratch,
        compiler_params=pltpu.CompilerParams(collective_id=tag, has_side_effects=True),
    )(*operands)


def lane_dense(block):
    return block.reshape(-1, HEAD_DIM)


def pick_rows(source_rows, dilation, shifts):
    row_count, head_count, head_width = source_rows.shape
    grouped = source_rows.reshape(row_count // dilation, dilation, head_count, head_width)
    hit_mask = jnp.arange(dilation, dtype=jnp.int32).reshape(1, dilation, 1, 1) == shifts.reshape(
        1, 1, head_count, 1
    )
    chosen = jnp.where(hit_mask, grouped, jnp.zeros((), source_rows.dtype))
    return jnp.sum(chosen, axis=1, dtype=source_rows.dtype)


def place_rows(row_values, dilation, shifts):
    row_count, head_count, head_width = row_values.shape
    hit_mask = jnp.arange(dilation, dtype=jnp.int32).reshape(1, dilation, 1, 1) == shifts.reshape(
        1, 1, head_count, 1
    )
    spread = jnp.where(hit_mask, row_values[:, None], jnp.zeros((), row_values.dtype))
    return spread.reshape(row_count * dilation, head_count, head_width)


def level_scores(q_rows, k_rows):
    score_scale = 1.0 / math.sqrt(q_rows.shape[-1])
    return (
        jnp.einsum("qhe,khe->hqk", q_rows, k_rows, preferred_element_type=jnp.float32) * score_scale
    )


def attend(q_rows, k_rows, v_rows):
    scores = level_scores(q_rows, k_rows)
    row_max = jnp.max(scores, axis=-1, keepdims=True)
    log_total = row_max[..., 0] + jnp.log(jnp.sum(jnp.exp(scores - row_max), axis=-1))
    soft_rows = jnp.exp(scores - log_total[..., None]).astype(jnp.bfloat16)
    level_out = jnp.einsum("hqk,khe->qhe", soft_rows, v_rows, preferred_element_type=jnp.float32)
    return (level_out, log_total.T)


def score_grads(q_rows, k_rows, v_rows, log_total, grad_low, row_shift):
    score_scale = 1.0 / math.sqrt(q_rows.shape[-1])
    scores = level_scores(q_rows, k_rows)
    exact_soft = jnp.exp(scores - log_total.T[..., None])
    prob_grad = jnp.einsum("qhe,khe->hqk", grad_low, v_rows, preferred_element_type=jnp.float32)
    score_grad = (exact_soft * (prob_grad + row_shift.T[..., None]) * score_scale).astype(
        jnp.bfloat16
    )
    return (score_grad, exact_soft.astype(jnp.bfloat16))


def key_parts(score_grad, soft_low, q_rows, grad_low):
    k_part = jnp.einsum("hqk,qhe->khe", score_grad, q_rows, preferred_element_type=jnp.float32)
    v_part = jnp.einsum("hqk,qhe->khe", soft_low, grad_low, preferred_element_type=jnp.float32)
    return (k_part, v_part)


def query_part(score_grad, k_rows):
    return jnp.einsum("hqk,khe->qhe", score_grad, k_rows, preferred_element_type=jnp.float32)


def split_qkv(packed, head_count):
    width = head_count * HEAD_DIM
    shape = (packed.shape[0], head_count, HEAD_DIM)
    return tuple(packed[:, i * width : (i + 1) * width].reshape(shape) for i in range(3))


def split_wide(values):
    high = values.astype(jnp.bfloat16)
    low = (values - high.astype(jnp.float32)).astype(jnp.bfloat16)
    return high, low


def join_wide(high, low):
    return high.astype(jnp.float32) + low.astype(jnp.float32)


def pack_grads(grad_low, row_shift, width):
    rows = grad_low.shape[0]
    high, low = split_wide(row_shift)
    used = grad_low.shape[1] * grad_low.shape[2] + 2 * row_shift.shape[1]
    return jnp.concatenate(
        [grad_low.reshape(rows, -1), high, low, jnp.zeros((rows, width - used), jnp.bfloat16)], 1
    )


def unpack_grads(packed, head_count):
    width = head_count * HEAD_DIM
    grad_low = packed[:, :width].reshape(-1, head_count, HEAD_DIM)
    return grad_low, join_wide(
        packed[:, width : width + head_count], packed[:, width + head_count : width + 2 * head_count]
    )


def shards(queries, keys, values, grad_y, out_gain, offsets):
    tokens = queries.shape[1]
    flat_width = queries.shape[2]
    head_count = flat_width // HEAD_DIM
    row_shape = (tokens, head_count, HEAD_DIM)
    q_own = queries[0].reshape(row_shape)
    k_own = keys[0].reshape(row_shape)
    v_own = values[0].reshape(row_shape)
    ctx_size = lax.axis_size("ctx")
    mid_shift = offsets[0]
    top_shift = offsets[1]
    positions = jnp.arange(tokens, dtype=jnp.int32)
    mid_hit = (positions % R1)[:, None] == mid_shift[None, :]
    top_hit = (positions % ctx_size)[:, None] == top_shift[None, :]
    mid_pack = jnp.concatenate(
        [pick_rows(x, R1, mid_shift).reshape(-1, flat_width) for x in (q_own, k_own, v_own)], 1
    )
    top_pack = jnp.concatenate(
        [pick_rows(x, ctx_size, top_shift).reshape(-1, flat_width) for x in (q_own, k_own, v_own)],
        1,
    )
    mid_rows = mid_pack.shape[0]
    top_rows = top_pack.shape[0]
    mid_all, top_all = ctx_gather(mid_pack, lane_dense(top_pack), SPAN, 0)
    mid_all = mid_all.reshape(-1, mid_pack.shape[1])
    top_all = top_all.reshape(-1, top_pack.shape[1])
    mid_q, mid_k, mid_v = split_qkv(mid_all, head_count)
    top_q, top_k, top_v = split_qkv(top_all, head_count)
    base_out, base_total = attend(q_own, k_own, v_own)
    mid_out_all, mid_total_all = attend(mid_q, mid_k, mid_v)
    top_out_all, top_total_all = attend(top_q, top_k, top_v)
    mid_out = mid_out_all[:mid_rows]
    mid_total = mid_total_all[:mid_rows]
    top_out = top_out_all[:top_rows]
    top_total = top_total_all[:top_rows]
    mid_full = place_rows(mid_total[..., None], R1, mid_shift)[..., 0]
    top_full = place_rows(top_total[..., None], ctx_size, top_shift)[..., 0]
    row_max = jnp.maximum(base_total, jnp.where(mid_hit, mid_full, base_total))
    row_max = jnp.maximum(row_max, jnp.where(top_hit, top_full, base_total))
    base_expo = jnp.exp(base_total - row_max)
    mid_expo = jnp.where(mid_hit, jnp.exp(mid_full - row_max), 0.0)
    top_expo = jnp.where(top_hit, jnp.exp(top_full - row_max), 0.0)
    denom = base_expo + mid_expo + top_expo
    base_share = base_expo / denom
    mid_share = mid_expo / denom
    top_share = top_expo / denom
    attn = (
        base_share[..., None] * base_out
        + mid_share[..., None] * place_rows(mid_out, R1, mid_shift)
        + top_share[..., None] * place_rows(top_out, ctx_size, top_shift)
    )
    inv_rms = lax.rsqrt(jnp.mean(attn * attn, axis=-1, keepdims=True) + EPS)
    normed = attn * inv_rms
    gain_rows = out_gain.reshape(head_count, HEAD_DIM)
    attended = (normed * gain_rows).astype(jnp.bfloat16).reshape(1, tokens, flat_width)
    grad_full = grad_y[0].reshape(row_shape).astype(jnp.float32)
    gain_part = jnp.sum(grad_full * normed, axis=0).reshape(flat_width)
    grad_norm = grad_full * gain_rows
    grad_attn = inv_rms * (
        grad_norm - normed * jnp.mean(grad_norm * normed, axis=-1, keepdims=True)
    )
    inner = jnp.sum(grad_attn * attn, axis=-1)
    base_low = (base_share[..., None] * grad_attn).astype(jnp.bfloat16)
    base_shift = -(base_share * inner)
    base_grad, base_soft = score_grads(q_own, k_own, v_own, base_total, base_low, base_shift)
    base_dq = query_part(base_grad, k_own)
    base_dk, base_dv = key_parts(base_grad, base_soft, q_own, base_low)

    mid_sel = pick_rows(mid_share[..., None], R1, mid_shift)[..., 0]
    mid_low = (mid_sel[..., None] * pick_rows(grad_attn, R1, mid_shift)).astype(jnp.bfloat16)
    mid_row_shift = -(mid_sel * pick_rows(inner[..., None], R1, mid_shift)[..., 0])
    top_sel = pick_rows(top_share[..., None], ctx_size, top_shift)[..., 0]
    top_low = (top_sel[..., None] * pick_rows(grad_attn, ctx_size, top_shift)).astype(jnp.bfloat16)
    top_row_shift = -(top_sel * pick_rows(inner[..., None], ctx_size, top_shift)[..., 0])

    shift_high, shift_low = split_wide(top_row_shift.reshape(-1))
    top_flat = jnp.concatenate([top_low.reshape(-1), shift_high, shift_low])
    top_flat = jnp.pad(top_flat, (0, -top_flat.shape[0] % HEAD_DIM))
    mid_gathered, gathered, gain_rows_sum = ctx_gather(
        pack_grads(mid_low, mid_row_shift, flat_width + HEAD_DIM),
        lane_dense(top_flat),
        SPAN,
        1,
        sum_x=lane_dense(gain_part),
    )
    mid_low_all, mid_shift_all = unpack_grads(
        mid_gathered.reshape(-1, mid_gathered.shape[-1]), head_count
    )
    gathered = gathered.reshape(ctx_size, -1)
    grad_width = top_rows * flat_width
    top_low_all = gathered[:, :grad_width].reshape(-1, head_count, HEAD_DIM)
    gain_grad = lax.psum(jnp.sum(gain_rows_sum, axis=0).reshape(flat_width), "dp")
    shift_count = top_rows * head_count
    top_shift_all = join_wide(
        gathered[:, grad_width : grad_width + shift_count],
        gathered[:, grad_width + shift_count : grad_width + 2 * shift_count],
    ).reshape(-1, head_count)

    mid_grad, mid_soft = score_grads(
        mid_q, mid_k, mid_v, mid_total_all, mid_low_all, mid_shift_all
    )
    mid_dq = query_part(mid_grad[:, :mid_rows], mid_k)
    mid_dk, mid_dv = key_parts(
        mid_grad[:, :, :mid_rows], mid_soft[:, :, :mid_rows], mid_q, mid_low_all
    )
    top_grad, top_soft = score_grads(
        top_q, top_k, top_v, top_total_all, top_low_all, top_shift_all
    )
    top_dq = query_part(top_grad[:, :top_rows], top_k)
    top_dk, top_dv = key_parts(
        top_grad[:, :, :top_rows], top_soft[:, :, :top_rows], top_q, top_low_all
    )
    query_grad = (
        base_dq + place_rows(mid_dq, R1, mid_shift) + place_rows(top_dq, ctx_size, top_shift)
    )
    key_grad = base_dk + place_rows(mid_dk, R1, mid_shift) + place_rows(top_dk, ctx_size, top_shift)
    value_grad = (
        base_dv + place_rows(mid_dv, R1, mid_shift) + place_rows(top_dv, ctx_size, top_shift)
    )
    out_shape = (1, tokens, flat_width)
    return (
        attended,
        query_grad.astype(jnp.bfloat16).reshape(out_shape),
        key_grad.astype(jnp.bfloat16).reshape(out_shape),
        value_grad.astype(jnp.bfloat16).reshape(out_shape),
        gain_grad,
    )


def solution(mesh):
    in_specs = (
        P("dp", "ctx", "head"),
        P("dp", "ctx", "head"),
        P("dp", "ctx", "head"),
        P("dp", "ctx", "head"),
        P("head"),
        P(None, "head"),
    )
    out_specs = (
        P("dp", "ctx", "head"),
        P("dp", "ctx", "head"),
        P("dp", "ctx", "head"),
        P("dp", "ctx", "head"),
        P("head"),
    )
    return jax.shard_map(shards, mesh=mesh, in_specs=in_specs, out_specs=out_specs, check_vma=False)
```

```python
import functools
import math

import jax
import jax.numpy as jnp
from jax import lax
from jax.experimental import pallas as pl
from jax.experimental.pallas import tpu as pltpu
from jax.sharding import PartitionSpec as P

HEAD_DIM = 128
SPAN = 4
R1 = 8
RING = 8


EPS = 1e-06


def gather_kernel(group, inner, has_sum, *refs):
    if has_sum:
        (mid_x, top_y, top_z, sum_x, mid_out, out_y, out_z, sum_out,
         stage_y, stage_z, sum_stage, row_sum, *sems) = refs
    else:
        (mid_x, top_y, top_z, mid_out, out_y, out_z, stage_y, stage_z, *sems) = refs
    (send_mid, recv_mid, send_ay, recv_ay, send_by, recv_by,
     send_az, recv_az, send_bz, recv_bz, local_sem) = sems[:11]
    if has_sum:
        send_sa, recv_sa, send_sb, recv_sb = sems[11:]
    count = lax.axis_size("ctx")
    outer = count // inner
    me = lax.axis_index("ctx")
    row = lax.axis_index("dp")
    col = lax.axis_index("head")
    lo = me % inner
    hi = me // inner
    base = me - me % group
    mesh_ids = pl.DeviceIdType.MESH

    def inner_peer(j):
        return hi * inner + lax.rem(lo + j, inner)

    def outer_peer(j):
        return lax.rem(hi + j, outer) * inner + lo

    barrier = pltpu.get_barrier_semaphore()
    for j in range(1, inner):
        pl.semaphore_signal(barrier, 1, device_id=(row, inner_peer(j), col), device_id_type=mesh_ids)
    for j in range(1, outer):
        pl.semaphore_signal(barrier, 1, device_id=(row, outer_peer(j), col), device_id_type=mesh_ids)
    pl.semaphore_wait(barrier, inner + outer - 2)

    def remote(src, dst, send, recv, peer):
        return pltpu.make_async_remote_copy(
            src, dst, send, recv, device_id=(row, peer, col), device_id_type=mesh_ids
        )

    def mid_copy(j):
        peer = base + lax.rem(me % group + j, group)
        return remote(mid_x, mid_out.at[j], send_mid.at[j], recv_mid.at[j], peer)

    def copy_ay(j):
        return remote(top_y, stage_y.at[j], send_ay.at[j], recv_ay.at[j], inner_peer(j))

    def copy_by(j):
        return remote(stage_y, out_y.at[j], send_by.at[j], recv_by.at[j], outer_peer(j))

    def copy_az(j):
        return remote(top_z, stage_z.at[j], send_az.at[j], recv_az.at[j], outer_peer(j))

    def copy_bz(j):
        return remote(stage_z, out_z.at[j], send_bz.at[j], recv_bz.at[j], inner_peer(j))

    def sum_a(j):
        return remote(sum_x, sum_stage.at[j], send_sa.at[j], recv_sa.at[j], inner_peer(j))

    def sum_b(j):
        return remote(row_sum, sum_out.at[j], send_sb.at[j], recv_sb.at[j], outer_peer(j))

    for j in range(1, inner):
        copy_ay(j).start()
    for j in range(1, outer):
        copy_az(j).start()
    if has_sum:
        for j in range(1, inner):
            sum_a(j).start()
    for j in range(1, group):
        mid_copy(j).start()
    own_y = pltpu.make_async_copy(top_y, stage_y.at[0], local_sem.at[0])
    own_z = pltpu.make_async_copy(top_z, stage_z.at[0], local_sem.at[1])
    own_y.start()
    own_z.start()
    mid_out[0] = mid_x[...]
    own_y.wait()
    own_z.wait()
    for j in range(1, inner):
        copy_ay(j).wait()
    for j in range(1, outer):
        copy_by(j).start()
    for j in range(1, outer):
        copy_az(j).wait()
    for j in range(1, inner):
        copy_bz(j).start()
    if has_sum:
        total = sum_x[...]
        for j in range(1, inner):
            sum_a(j).wait()
            total = total + sum_stage[j]
        row_sum[...] = total
        for j in range(1, outer):
            sum_b(j).start()
        sum_out[0] = total
    out_y[0] = stage_y[...]
    out_z[0] = stage_z[...]
    for j in range(1, group):
        mid_copy(j).wait()
    for j in range(1, outer):
        copy_by(j).wait()
        if has_sum:
            sum_b(j).wait()
    for j in range(1, inner):
        copy_bz(j).wait()


def ctx_gather(mid_x, top_x, group, tag, sum_x=None):
    count = lax.axis_size("ctx")
    inner = RING
    outer = count // inner
    half = (top_x.shape[0] + 1) // 2
    top_y = top_x[:half]
    top_z = top_x[half:]
    has_sum = sum_x is not None
    operands = (mid_x, top_y, top_z) + ((sum_x,) if has_sum else ())
    out_shape = (
        jax.ShapeDtypeStruct((group,) + mid_x.shape, mid_x.dtype),
        jax.ShapeDtypeStruct((outer, inner) + top_y.shape, top_x.dtype),
        jax.ShapeDtypeStruct((inner, outer) + top_z.shape, top_x.dtype),
    )
    scratch = [
        pltpu.VMEM((inner,) + top_y.shape, top_x.dtype),
        pltpu.VMEM((outer,) + top_z.shape, top_x.dtype),
    ]
    if has_sum:
        out_shape += (jax.ShapeDtypeStruct((outer,) + sum_x.shape, sum_x.dtype),)
        scratch += [
            pltpu.VMEM((inner,) + sum_x.shape, sum_x.dtype),
            pltpu.VMEM(sum_x.shape, sum_x.dtype),
        ]
    for size in (group, inner, outer, outer, inner):
        scratch += [pltpu.SemaphoreType.DMA((size,)), pltpu.SemaphoreType.DMA((size,))]
    scratch.append(pltpu.SemaphoreType.DMA((2,)))
    if has_sum:
        for size in (inner, outer):
            scratch += [pltpu.SemaphoreType.DMA((size,)), pltpu.SemaphoreType.DMA((size,))]
    outs = pl.pallas_call(
        functools.partial(gather_kernel, group, inner, has_sum),
        out_shape=out_shape,
        in_specs=[pl.BlockSpec(memory_space=pltpu.VMEM)] * len(operands),
        out_specs=(pl.BlockSpec(memory_space=pltpu.VMEM),) * len(out_shape),
        scratch_shapes=scratch,
        compiler_params=pltpu.CompilerParams(collective_id=tag, has_side_effects=True),
    )(*operands)
    top_all = jnp.concatenate([outs[1], jnp.transpose(outs[2], (1, 0, 2, 3))], 2)
    return (outs[0], top_all) + tuple(outs[3:])


def lane_dense(block):
    return block.reshape(-1, HEAD_DIM)


def pick_rows(source_rows, dilation, shifts):
    row_count, head_count, head_width = source_rows.shape
    grouped = source_rows.reshape(row_count // dilation, dilation, head_count, head_width)
    hit_mask = jnp.arange(dilation, dtype=jnp.int32).reshape(1, dilation, 1, 1) == shifts.reshape(
        1, 1, head_count, 1
    )
    chosen = jnp.where(hit_mask, grouped, jnp.zeros((), source_rows.dtype))
    return jnp.sum(chosen, axis=1, dtype=source_rows.dtype)


def place_rows(row_values, dilation, shifts):
    row_count, head_count, head_width = row_values.shape
    hit_mask = jnp.arange(dilation, dtype=jnp.int32).reshape(1, dilation, 1, 1) == shifts.reshape(
        1, 1, head_count, 1
    )
    spread = jnp.where(hit_mask, row_values[:, None], jnp.zeros((), row_values.dtype))
    return spread.reshape(row_count * dilation, head_count, head_width)


def level_scores(q_rows, k_rows):
    score_scale = 1.0 / math.sqrt(q_rows.shape[-1])
    return (
        jnp.einsum("qhe,khe->hqk", q_rows, k_rows, preferred_element_type=jnp.float32) * score_scale
    )


def attend(q_rows, k_rows, v_rows):
    scores = level_scores(q_rows, k_rows)
    row_max = jnp.max(scores, axis=-1, keepdims=True)
    log_total = row_max[..., 0] + jnp.log(jnp.sum(jnp.exp(scores - row_max), axis=-1))
    soft_rows = jnp.exp(scores - log_total[..., None]).astype(jnp.bfloat16)
    level_out = jnp.einsum("hqk,khe->qhe", soft_rows, v_rows, preferred_element_type=jnp.float32)
    return (level_out, log_total.T)


def score_grads(q_rows, k_rows, v_rows, log_total, grad_low, row_shift):
    score_scale = 1.0 / math.sqrt(q_rows.shape[-1])
    scores = level_scores(q_rows, k_rows)
    exact_soft = jnp.exp(scores - log_total.T[..., None])
    prob_grad = jnp.einsum("qhe,khe->hqk", grad_low, v_rows, preferred_element_type=jnp.float32)
    score_grad = (exact_soft * (prob_grad + row_shift.T[..., None]) * score_scale).astype(
        jnp.bfloat16
    )
    return (score_grad, exact_soft.astype(jnp.bfloat16))


def key_parts(score_grad, soft_low, q_rows, grad_low):
    k_part = jnp.einsum("hqk,qhe->khe", score_grad, q_rows, preferred_element_type=jnp.float32)
    v_part = jnp.einsum("hqk,qhe->khe", soft_low, grad_low, preferred_element_type=jnp.float32)
    return (k_part, v_part)


def query_part(score_grad, k_rows):
    return jnp.einsum("hqk,khe->qhe", score_grad, k_rows, preferred_element_type=jnp.float32)


def split_qkv(packed, head_count):
    width = head_count * HEAD_DIM
    shape = (packed.shape[0], head_count, HEAD_DIM)
    return tuple(packed[:, i * width : (i + 1) * width].reshape(shape) for i in range(3))


def split_wide(values):
    high = values.astype(jnp.bfloat16)
    low = (values - high.astype(jnp.float32)).astype(jnp.bfloat16)
    return high, low


def join_wide(high, low):
    return high.astype(jnp.float32) + low.astype(jnp.float32)


def pack_grads(grad_low, row_shift, width):
    rows = grad_low.shape[0]
    high, low = split_wide(row_shift)
    used = grad_low.shape[1] * grad_low.shape[2] + 2 * row_shift.shape[1]
    return jnp.concatenate(
        [grad_low.reshape(rows, -1), high, low, jnp.zeros((rows, width - used), jnp.bfloat16)], 1
    )


def unpack_grads(packed, head_count):
    width = head_count * HEAD_DIM
    grad_low = packed[:, :width].reshape(-1, head_count, HEAD_DIM)
    return grad_low, join_wide(
        packed[:, width : width + head_count], packed[:, width + head_count : width + 2 * head_count]
    )


def shards(queries, keys, values, grad_y, out_gain, offsets):
    tokens = queries.shape[1]
    flat_width = queries.shape[2]
    head_count = flat_width // HEAD_DIM
    row_shape = (tokens, head_count, HEAD_DIM)
    q_own = queries[0].reshape(row_shape)
    k_own = keys[0].reshape(row_shape)
    v_own = values[0].reshape(row_shape)
    ctx_size = lax.axis_size("ctx")
    mid_shift = offsets[0]
    top_shift = offsets[1]
    positions = jnp.arange(tokens, dtype=jnp.int32)
    mid_hit = (positions % R1)[:, None] == mid_shift[None, :]
    top_hit = (positions % ctx_size)[:, None] == top_shift[None, :]
    mid_pack = jnp.concatenate(
        [pick_rows(x, R1, mid_shift).reshape(-1, flat_width) for x in (q_own, k_own, v_own)], 1
    )
    top_pack = jnp.concatenate(
        [pick_rows(x, ctx_size, top_shift).reshape(-1, flat_width) for x in (q_own, k_own, v_own)],
        1,
    )
    mid_rows = mid_pack.shape[0]
    top_rows = top_pack.shape[0]
    mid_all, top_all = ctx_gather(mid_pack, lane_dense(top_pack), SPAN, 0)
    mid_all = mid_all.reshape(-1, mid_pack.shape[1])
    top_all = top_all.reshape(-1, top_pack.shape[1])
    mid_q, mid_k, mid_v = split_qkv(mid_all, head_count)
    top_q, top_k, top_v = split_qkv(top_all, head_count)
    base_out, base_total = attend(q_own, k_own, v_own)
    mid_out_all, mid_total_all = attend(mid_q, mid_k, mid_v)
    top_out_all, top_total_all = attend(top_q, top_k, top_v)
    mid_out = mid_out_all[:mid_rows]
    mid_total = mid_total_all[:mid_rows]
    top_out = top_out_all[:top_rows]
    top_total = top_total_all[:top_rows]
    mid_full = place_rows(mid_total[..., None], R1, mid_shift)[..., 0]
    top_full = place_rows(top_total[..., None], ctx_size, top_shift)[..., 0]
    row_max = jnp.maximum(base_total, jnp.where(mid_hit, mid_full, base_total))
    row_max = jnp.maximum(row_max, jnp.where(top_hit, top_full, base_total))
    base_expo = jnp.exp(base_total - row_max)
    mid_expo = jnp.where(mid_hit, jnp.exp(mid_full - row_max), 0.0)
    top_expo = jnp.where(top_hit, jnp.exp(top_full - row_max), 0.0)
    denom = base_expo + mid_expo + top_expo
    base_share = base_expo / denom
    mid_share = mid_expo / denom
    top_share = top_expo / denom
    attn = (
        base_share[..., None] * base_out
        + mid_share[..., None] * place_rows(mid_out, R1, mid_shift)
        + top_share[..., None] * place_rows(top_out, ctx_size, top_shift)
    )
    inv_rms = lax.rsqrt(jnp.mean(attn * attn, axis=-1, keepdims=True) + EPS)
    normed = attn * inv_rms
    gain_rows = out_gain.reshape(head_count, HEAD_DIM)
    attended = (normed * gain_rows).astype(jnp.bfloat16).reshape(1, tokens, flat_width)
    grad_full = grad_y[0].reshape(row_shape).astype(jnp.float32)
    gain_part = jnp.sum(grad_full * normed, axis=0).reshape(flat_width)
    grad_norm = grad_full * gain_rows
    grad_attn = inv_rms * (
        grad_norm - normed * jnp.mean(grad_norm * normed, axis=-1, keepdims=True)
    )
    inner = jnp.sum(grad_attn * attn, axis=-1)
    base_low = (base_share[..., None] * grad_attn).astype(jnp.bfloat16)
    base_shift = -(base_share * inner)
    base_grad, base_soft = score_grads(q_own, k_own, v_own, base_total, base_low, base_shift)
    base_dq = query_part(base_grad, k_own)
    base_dk, base_dv = key_parts(base_grad, base_soft, q_own, base_low)

    mid_sel = pick_rows(mid_share[..., None], R1, mid_shift)[..., 0]
    mid_low = (mid_sel[..., None] * pick_rows(grad_attn, R1, mid_shift)).astype(jnp.bfloat16)
    mid_row_shift = -(mid_sel * pick_rows(inner[..., None], R1, mid_shift)[..., 0])
    top_sel = pick_rows(top_share[..., None], ctx_size, top_shift)[..., 0]
    top_low = (top_sel[..., None] * pick_rows(grad_attn, ctx_size, top_shift)).astype(jnp.bfloat16)
    top_row_shift = -(top_sel * pick_rows(inner[..., None], ctx_size, top_shift)[..., 0])

    shift_high, shift_low = split_wide(top_row_shift.reshape(-1))
    top_flat = jnp.concatenate([top_low.reshape(-1), shift_high, shift_low])
    top_flat = jnp.pad(top_flat, (0, -top_flat.shape[0] % HEAD_DIM))
    mid_gathered, gathered, gain_rows_sum = ctx_gather(
        pack_grads(mid_low, mid_row_shift, flat_width + HEAD_DIM),
        lane_dense(top_flat),
        SPAN,
        1,
        sum_x=lane_dense(gain_part),
    )
    mid_low_all, mid_shift_all = unpack_grads(
        mid_gathered.reshape(-1, mid_gathered.shape[-1]), head_count
    )
    gathered = gathered.reshape(ctx_size, -1)
    grad_width = top_rows * flat_width
    top_low_all = gathered[:, :grad_width].reshape(-1, head_count, HEAD_DIM)
    gain_grad = lax.psum(jnp.sum(gain_rows_sum, axis=0).reshape(flat_width), "dp")
    shift_count = top_rows * head_count
    top_shift_all = join_wide(
        gathered[:, grad_width : grad_width + shift_count],
        gathered[:, grad_width + shift_count : grad_width + 2 * shift_count],
    ).reshape(-1, head_count)

    mid_grad, mid_soft = score_grads(
        mid_q, mid_k, mid_v, mid_total_all, mid_low_all, mid_shift_all
    )
    mid_dq = query_part(mid_grad[:, :mid_rows], mid_k)
    mid_dk, mid_dv = key_parts(
        mid_grad[:, :, :mid_rows], mid_soft[:, :, :mid_rows], mid_q, mid_low_all
    )
    top_grad, top_soft = score_grads(
        top_q, top_k, top_v, top_total_all, top_low_all, top_shift_all
    )
    top_dq = query_part(top_grad[:, :top_rows], top_k)
    top_dk, top_dv = key_parts(
        top_grad[:, :, :top_rows], top_soft[:, :, :top_rows], top_q, top_low_all
    )
    query_grad = (
        base_dq + place_rows(mid_dq, R1, mid_shift) + place_rows(top_dq, ctx_size, top_shift)
    )
    key_grad = base_dk + place_rows(mid_dk, R1, mid_shift) + place_rows(top_dk, ctx_size, top_shift)
    value_grad = (
        base_dv + place_rows(mid_dv, R1, mid_shift) + place_rows(top_dv, ctx_size, top_shift)
    )
    out_shape = (1, tokens, flat_width)
    return (
        attended,
        query_grad.astype(jnp.bfloat16).reshape(out_shape),
        key_grad.astype(jnp.bfloat16).reshape(out_shape),
        value_grad.astype(jnp.bfloat16).reshape(out_shape),
        gain_grad,
    )


def solution(mesh):
    in_specs = (
        P("dp", "ctx", "head"),
        P("dp", "ctx", "head"),
        P("dp", "ctx", "head"),
        P("dp", "ctx", "head"),
        P("head"),
        P(None, "head"),
    )
    out_specs = (
        P("dp", "ctx", "head"),
        P("dp", "ctx", "head"),
        P("dp", "ctx", "head"),
        P("dp", "ctx", "head"),
        P("head"),
    )
    return jax.shard_map(shards, mesh=mesh, in_specs=in_specs, out_specs=out_specs, check_vma=False)
```

```python
import functools
import math

import jax
import jax.numpy as jnp
from jax import lax
from jax.experimental import pallas as pl
from jax.experimental.pallas import tpu as pltpu
from jax.sharding import PartitionSpec as P

HEAD_DIM = 128
SPAN = 4
R1 = 8
RING = 8


EPS = 1e-06


def gather_kernel(group, inner, has_sum, *refs):
    if has_sum:
        (mid_x, top_y, top_z, sum_x, mid_out, out_y, out_z, sum_out,
         stage_y, stage_z, sum_stage, row_sum, *sems) = refs
    else:
        (mid_x, top_y, top_z, mid_out, out_y, out_z, stage_y, stage_z, *sems) = refs
    (send_mid, recv_mid, send_ay, recv_ay, send_by, recv_by,
     send_az, recv_az, send_bz, recv_bz, local_sem) = sems[:11]
    if has_sum:
        send_sa, recv_sa, send_sb, recv_sb = sems[11:]
    count = lax.axis_size("ctx")
    outer = count // inner
    me = lax.axis_index("ctx")
    row = lax.axis_index("dp")
    col = lax.axis_index("head")
    lo = me % inner
    hi = me // inner
    base = me - me % group
    mesh_ids = pl.DeviceIdType.MESH

    def inner_peer(j):
        return hi * inner + lax.rem(lo + j, inner)

    def outer_peer(j):
        return lax.rem(hi + j, outer) * inner + lo

    barrier = pltpu.get_barrier_semaphore()
    for j in range(1, inner):
        pl.semaphore_signal(barrier, 1, device_id=(row, inner_peer(j), col), device_id_type=mesh_ids)
    for j in range(1, outer):
        pl.semaphore_signal(barrier, 1, device_id=(row, outer_peer(j), col), device_id_type=mesh_ids)
    pl.semaphore_wait(barrier, inner + outer - 2)

    def remote(src, dst, send, recv, peer):
        return pltpu.make_async_remote_copy(
            src, dst, send, recv, device_id=(row, peer, col), device_id_type=mesh_ids
        )

    def mid_copy(j):
        peer = base + lax.rem(me % group + j, group)
        return remote(mid_x, mid_out.at[j], send_mid.at[j], recv_mid.at[j], peer)

    def copy_ay(j):
        return remote(top_y, stage_y.at[j], send_ay.at[j], recv_ay.at[j], inner_peer(j))

    def copy_by(j):
        return remote(stage_y, out_y.at[j], send_by.at[j], recv_by.at[j], outer_peer(j))

    def copy_az(j):
        return remote(top_z, stage_z.at[j], send_az.at[j], recv_az.at[j], outer_peer(j))

    def copy_bz(j):
        return remote(stage_z, out_z.at[j], send_bz.at[j], recv_bz.at[j], inner_peer(j))

    def sum_a(j):
        return remote(sum_x, sum_stage.at[j], send_sa.at[j], recv_sa.at[j], inner_peer(j))

    def sum_b(j):
        return remote(row_sum, sum_out.at[j], send_sb.at[j], recv_sb.at[j], outer_peer(j))

    for j in range(1, inner):
        copy_ay(j).start()
    for j in range(1, outer):
        copy_az(j).start()
    if has_sum:
        for j in range(1, inner):
            sum_a(j).start()
    for j in range(1, group):
        mid_copy(j).start()
    own_y = pltpu.make_async_copy(top_y, stage_y.at[0], local_sem.at[0])
    own_z = pltpu.make_async_copy(top_z, stage_z.at[0], local_sem.at[1])
    own_y.start()
    own_z.start()
    mid_out[0] = mid_x[...]
    own_y.wait()
    own_z.wait()
    for j in range(1, inner):
        copy_ay(j).wait()
    for j in range(1, outer):
        copy_by(j).start()
    for j in range(1, outer):
        copy_az(j).wait()
    for j in range(1, inner):
        copy_bz(j).start()
    if has_sum:
        total = sum_x[...]
        for j in range(1, inner):
            sum_a(j).wait()
            total = total + sum_stage[j]
        row_sum[...] = total
        for j in range(1, outer):
            sum_b(j).start()
        sum_out[0] = total
    out_y[0] = stage_y[...]
    out_z[0] = stage_z[...]
    for j in range(1, group):
        mid_copy(j).wait()
    for j in range(1, outer):
        copy_by(j).wait()
        if has_sum:
            sum_b(j).wait()
    for j in range(1, inner):
        copy_bz(j).wait()


def ctx_gather(mid_x, top_x, group, tag, sum_x=None):
    count = lax.axis_size("ctx")
    inner = RING
    outer = count // inner
    rows = top_x.shape[0]
    half = max(1, min(rows - 1, 8 * round(0.75 * rows / 8)))
    top_y = top_x[:half]
    top_z = top_x[half:]
    has_sum = sum_x is not None
    operands = (mid_x, top_y, top_z) + ((sum_x,) if has_sum else ())
    out_shape = (
        jax.ShapeDtypeStruct((group,) + mid_x.shape, mid_x.dtype),
        jax.ShapeDtypeStruct((outer, inner) + top_y.shape, top_x.dtype),
        jax.ShapeDtypeStruct((inner, outer) + top_z.shape, top_x.dtype),
    )
    scratch = [
        pltpu.VMEM((inner,) + top_y.shape, top_x.dtype),
        pltpu.VMEM((outer,) + top_z.shape, top_x.dtype),
    ]
    if has_sum:
        out_shape += (jax.ShapeDtypeStruct((outer,) + sum_x.shape, sum_x.dtype),)
        scratch += [
            pltpu.VMEM((inner,) + sum_x.shape, sum_x.dtype),
            pltpu.VMEM(sum_x.shape, sum_x.dtype),
        ]
    for size in (group, inner, outer, outer, inner):
        scratch += [pltpu.SemaphoreType.DMA((size,)), pltpu.SemaphoreType.DMA((size,))]
    scratch.append(pltpu.SemaphoreType.DMA((2,)))
    if has_sum:
        for size in (inner, outer):
            scratch += [pltpu.SemaphoreType.DMA((size,)), pltpu.SemaphoreType.DMA((size,))]
    outs = pl.pallas_call(
        functools.partial(gather_kernel, group, inner, has_sum),
        out_shape=out_shape,
        in_specs=[pl.BlockSpec(memory_space=pltpu.VMEM)] * len(operands),
        out_specs=(pl.BlockSpec(memory_space=pltpu.VMEM),) * len(out_shape),
        scratch_shapes=scratch,
        compiler_params=pltpu.CompilerParams(collective_id=tag, has_side_effects=True),
    )(*operands)
    top_all = jnp.concatenate([outs[1], jnp.transpose(outs[2], (1, 0, 2, 3))], 2)
    return (outs[0], top_all) + tuple(outs[3:])


def lane_dense(block):
    return block.reshape(-1, HEAD_DIM)


def pick_rows(source_rows, dilation, shifts):
    row_count, head_count, head_width = source_rows.shape
    grouped = source_rows.reshape(row_count // dilation, dilation, head_count, head_width)
    hit_mask = jnp.arange(dilation, dtype=jnp.int32).reshape(1, dilation, 1, 1) == shifts.reshape(
        1, 1, head_count, 1
    )
    chosen = jnp.where(hit_mask, grouped, jnp.zeros((), source_rows.dtype))
    return jnp.sum(chosen, axis=1, dtype=source_rows.dtype)


def place_rows(row_values, dilation, shifts):
    row_count, head_count, head_width = row_values.shape
    hit_mask = jnp.arange(dilation, dtype=jnp.int32).reshape(1, dilation, 1, 1) == shifts.reshape(
        1, 1, head_count, 1
    )
    spread = jnp.where(hit_mask, row_values[:, None], jnp.zeros((), row_values.dtype))
    return spread.reshape(row_count * dilation, head_count, head_width)


def level_scores(q_rows, k_rows):
    score_scale = 1.0 / math.sqrt(q_rows.shape[-1])
    return (
        jnp.einsum("qhe,khe->hqk", q_rows, k_rows, preferred_element_type=jnp.float32) * score_scale
    )


def attend(q_rows, k_rows, v_rows):
    scores = level_scores(q_rows, k_rows)
    row_max = jnp.max(scores, axis=-1, keepdims=True)
    log_total = row_max[..., 0] + jnp.log(jnp.sum(jnp.exp(scores - row_max), axis=-1))
    soft_rows = jnp.exp(scores - log_total[..., None]).astype(jnp.bfloat16)
    level_out = jnp.einsum("hqk,khe->qhe", soft_rows, v_rows, preferred_element_type=jnp.float32)
    return (level_out, log_total.T)


def score_grads(q_rows, k_rows, v_rows, log_total, grad_low, row_shift):
    score_scale = 1.0 / math.sqrt(q_rows.shape[-1])
    scores = level_scores(q_rows, k_rows)
    exact_soft = jnp.exp(scores - log_total.T[..., None])
    prob_grad = jnp.einsum("qhe,khe->hqk", grad_low, v_rows, preferred_element_type=jnp.float32)
    score_grad = (exact_soft * (prob_grad + row_shift.T[..., None]) * score_scale).astype(
        jnp.bfloat16
    )
    return (score_grad, exact_soft.astype(jnp.bfloat16))


def key_parts(score_grad, soft_low, q_rows, grad_low):
    k_part = jnp.einsum("hqk,qhe->khe", score_grad, q_rows, preferred_element_type=jnp.float32)
    v_part = jnp.einsum("hqk,qhe->khe", soft_low, grad_low, preferred_element_type=jnp.float32)
    return (k_part, v_part)


def query_part(score_grad, k_rows):
    return jnp.einsum("hqk,khe->qhe", score_grad, k_rows, preferred_element_type=jnp.float32)


def split_qkv(packed, head_count):
    width = head_count * HEAD_DIM
    shape = (packed.shape[0], head_count, HEAD_DIM)
    return tuple(packed[:, i * width : (i + 1) * width].reshape(shape) for i in range(3))


def split_wide(values):
    high = values.astype(jnp.bfloat16)
    low = (values - high.astype(jnp.float32)).astype(jnp.bfloat16)
    return high, low


def join_wide(high, low):
    return high.astype(jnp.float32) + low.astype(jnp.float32)


def pack_grads(grad_low, row_shift, width):
    rows = grad_low.shape[0]
    high, low = split_wide(row_shift)
    used = grad_low.shape[1] * grad_low.shape[2] + 2 * row_shift.shape[1]
    return jnp.concatenate(
        [grad_low.reshape(rows, -1), high, low, jnp.zeros((rows, width - used), jnp.bfloat16)], 1
    )


def unpack_grads(packed, head_count):
    width = head_count * HEAD_DIM
    grad_low = packed[:, :width].reshape(-1, head_count, HEAD_DIM)
    return grad_low, join_wide(
        packed[:, width : width + head_count], packed[:, width + head_count : width + 2 * head_count]
    )


def shards(queries, keys, values, grad_y, out_gain, offsets):
    tokens = queries.shape[1]
    flat_width = queries.shape[2]
    head_count = flat_width // HEAD_DIM
    row_shape = (tokens, head_count, HEAD_DIM)
    q_own = queries[0].reshape(row_shape)
    k_own = keys[0].reshape(row_shape)
    v_own = values[0].reshape(row_shape)
    ctx_size = lax.axis_size("ctx")
    mid_shift = offsets[0]
    top_shift = offsets[1]
    positions = jnp.arange(tokens, dtype=jnp.int32)
    mid_hit = (positions % R1)[:, None] == mid_shift[None, :]
    top_hit = (positions % ctx_size)[:, None] == top_shift[None, :]
    mid_pack = jnp.concatenate(
        [pick_rows(x, R1, mid_shift).reshape(-1, flat_width) for x in (q_own, k_own, v_own)], 1
    )
    top_pack = jnp.concatenate(
        [pick_rows(x, ctx_size, top_shift).reshape(-1, flat_width) for x in (q_own, k_own, v_own)],
        1,
    )
    mid_rows = mid_pack.shape[0]
    top_rows = top_pack.shape[0]
    mid_all, top_all = ctx_gather(mid_pack, lane_dense(top_pack), SPAN, 0)
    mid_all = mid_all.reshape(-1, mid_pack.shape[1])
    top_all = top_all.reshape(-1, top_pack.shape[1])
    mid_q, mid_k, mid_v = split_qkv(mid_all, head_count)
    top_q, top_k, top_v = split_qkv(top_all, head_count)
    base_out, base_total = attend(q_own, k_own, v_own)
    mid_out_all, mid_total_all = attend(mid_q, mid_k, mid_v)
    top_out_all, top_total_all = attend(top_q, top_k, top_v)
    mid_out = mid_out_all[:mid_rows]
    mid_total = mid_total_all[:mid_rows]
    top_out = top_out_all[:top_rows]
    top_total = top_total_all[:top_rows]
    mid_full = place_rows(mid_total[..., None], R1, mid_shift)[..., 0]
    top_full = place_rows(top_total[..., None], ctx_size, top_shift)[..., 0]
    row_max = jnp.maximum(base_total, jnp.where(mid_hit, mid_full, base_total))
    row_max = jnp.maximum(row_max, jnp.where(top_hit, top_full, base_total))
    base_expo = jnp.exp(base_total - row_max)
    mid_expo = jnp.where(mid_hit, jnp.exp(mid_full - row_max), 0.0)
    top_expo = jnp.where(top_hit, jnp.exp(top_full - row_max), 0.0)
    denom = base_expo + mid_expo + top_expo
    base_share = base_expo / denom
    mid_share = mid_expo / denom
    top_share = top_expo / denom
    attn = (
        base_share[..., None] * base_out
        + mid_share[..., None] * place_rows(mid_out, R1, mid_shift)
        + top_share[..., None] * place_rows(top_out, ctx_size, top_shift)
    )
    inv_rms = lax.rsqrt(jnp.mean(attn * attn, axis=-1, keepdims=True) + EPS)
    normed = attn * inv_rms
    gain_rows = out_gain.reshape(head_count, HEAD_DIM)
    attended = (normed * gain_rows).astype(jnp.bfloat16).reshape(1, tokens, flat_width)
    grad_full = grad_y[0].reshape(row_shape).astype(jnp.float32)
    gain_part = jnp.sum(grad_full * normed, axis=0).reshape(flat_width)
    grad_norm = grad_full * gain_rows
    grad_attn = inv_rms * (
        grad_norm - normed * jnp.mean(grad_norm * normed, axis=-1, keepdims=True)
    )
    inner = jnp.sum(grad_attn * attn, axis=-1)
    base_low = (base_share[..., None] * grad_attn).astype(jnp.bfloat16)
    base_shift = -(base_share * inner)
    base_grad, base_soft = score_grads(q_own, k_own, v_own, base_total, base_low, base_shift)
    base_dq = query_part(base_grad, k_own)
    base_dk, base_dv = key_parts(base_grad, base_soft, q_own, base_low)

    mid_sel = pick_rows(mid_share[..., None], R1, mid_shift)[..., 0]
    mid_low = (mid_sel[..., None] * pick_rows(grad_attn, R1, mid_shift)).astype(jnp.bfloat16)
    mid_row_shift = -(mid_sel * pick_rows(inner[..., None], R1, mid_shift)[..., 0])
    top_sel = pick_rows(top_share[..., None], ctx_size, top_shift)[..., 0]
    top_low = (top_sel[..., None] * pick_rows(grad_attn, ctx_size, top_shift)).astype(jnp.bfloat16)
    top_row_shift = -(top_sel * pick_rows(inner[..., None], ctx_size, top_shift)[..., 0])

    shift_high, shift_low = split_wide(top_row_shift.reshape(-1))
    top_flat = jnp.concatenate([top_low.reshape(-1), shift_high, shift_low])
    top_flat = jnp.pad(top_flat, (0, -top_flat.shape[0] % HEAD_DIM))
    mid_gathered, gathered, gain_rows_sum = ctx_gather(
        pack_grads(mid_low, mid_row_shift, flat_width + HEAD_DIM),
        lane_dense(top_flat),
        SPAN,
        1,
        sum_x=lane_dense(gain_part),
    )
    mid_low_all, mid_shift_all = unpack_grads(
        mid_gathered.reshape(-1, mid_gathered.shape[-1]), head_count
    )
    gathered = gathered.reshape(ctx_size, -1)
    grad_width = top_rows * flat_width
    top_low_all = gathered[:, :grad_width].reshape(-1, head_count, HEAD_DIM)
    gain_grad = lax.psum(jnp.sum(gain_rows_sum, axis=0).reshape(flat_width), "dp")
    shift_count = top_rows * head_count
    top_shift_all = join_wide(
        gathered[:, grad_width : grad_width + shift_count],
        gathered[:, grad_width + shift_count : grad_width + 2 * shift_count],
    ).reshape(-1, head_count)

    mid_grad, mid_soft = score_grads(
        mid_q, mid_k, mid_v, mid_total_all, mid_low_all, mid_shift_all
    )
    mid_dq = query_part(mid_grad[:, :mid_rows], mid_k)
    mid_dk, mid_dv = key_parts(
        mid_grad[:, :, :mid_rows], mid_soft[:, :, :mid_rows], mid_q, mid_low_all
    )
    top_grad, top_soft = score_grads(
        top_q, top_k, top_v, top_total_all, top_low_all, top_shift_all
    )
    top_dq = query_part(top_grad[:, :top_rows], top_k)
    top_dk, top_dv = key_parts(
        top_grad[:, :, :top_rows], top_soft[:, :, :top_rows], top_q, top_low_all
    )
    query_grad = (
        base_dq + place_rows(mid_dq, R1, mid_shift) + place_rows(top_dq, ctx_size, top_shift)
    )
    key_grad = base_dk + place_rows(mid_dk, R1, mid_shift) + place_rows(top_dk, ctx_size, top_shift)
    value_grad = (
        base_dv + place_rows(mid_dv, R1, mid_shift) + place_rows(top_dv, ctx_size, top_shift)
    )
    out_shape = (1, tokens, flat_width)
    return (
        attended,
        query_grad.astype(jnp.bfloat16).reshape(out_shape),
        key_grad.astype(jnp.bfloat16).reshape(out_shape),
        value_grad.astype(jnp.bfloat16).reshape(out_shape),
        gain_grad,
    )


def solution(mesh):
    in_specs = (
        P("dp", "ctx", "head"),
        P("dp", "ctx", "head"),
        P("dp", "ctx", "head"),
        P("dp", "ctx", "head"),
        P("head"),
        P(None, "head"),
    )
    out_specs = (
        P("dp", "ctx", "head"),
        P("dp", "ctx", "head"),
        P("dp", "ctx", "head"),
        P("dp", "ctx", "head"),
        P("head"),
    )
    return jax.shard_map(shards, mesh=mesh, in_specs=in_specs, out_specs=out_specs, check_vma=False)
```

```python
import functools
import math

import jax
import jax.numpy as jnp
from jax import lax
from jax.experimental import pallas as pl
from jax.experimental.pallas import tpu as pltpu
from jax.sharding import PartitionSpec as P

HEAD_DIM = 128
SPAN = 4
R1 = 8
RING = 8


EPS = 1e-06


def gather_kernel(group, inner, has_sum, *refs):
    if has_sum:
        (mid_x, top_y, top_z, sum_x, mid_out, out_y, out_z, sum_out,
         stage_y, stage_z, sum_stage, row_sum, *sems) = refs
    else:
        (mid_x, top_y, top_z, mid_out, out_y, out_z, stage_y, stage_z, *sems) = refs
    (send_mid, recv_mid, send_ay, recv_ay, send_by, recv_by,
     send_az, recv_az, send_bz, recv_bz, local_sem) = sems[:11]
    if has_sum:
        send_sa, recv_sa, send_sb, recv_sb = sems[11:]
    count = lax.axis_size("ctx")
    outer = count // inner
    me = lax.axis_index("ctx")
    row = lax.axis_index("dp")
    col = lax.axis_index("head")
    lo = me % inner
    hi = me // inner
    base = me - me % group
    mesh_ids = pl.DeviceIdType.MESH

    def inner_peer(j):
        return hi * inner + lax.rem(lo + j, inner)

    def outer_peer(j):
        return lax.rem(hi + j, outer) * inner + lo

    barrier = pltpu.get_barrier_semaphore()
    for j in range(1, inner):
        pl.semaphore_signal(barrier, 1, device_id=(row, inner_peer(j), col), device_id_type=mesh_ids)
    for j in range(1, outer):
        pl.semaphore_signal(barrier, 1, device_id=(row, outer_peer(j), col), device_id_type=mesh_ids)
    pl.semaphore_wait(barrier, inner + outer - 2)

    def remote(src, dst, send, recv, peer):
        return pltpu.make_async_remote_copy(
            src, dst, send, recv, device_id=(row, peer, col), device_id_type=mesh_ids
        )

    def mid_copy(j):
        peer = base + lax.rem(me % group + j, group)
        return remote(mid_x, mid_out.at[j], send_mid.at[j], recv_mid.at[j], peer)

    def copy_ay(j):
        return remote(top_y, stage_y.at[j], send_ay.at[j], recv_ay.at[j], inner_peer(j))

    def copy_by(j):
        return remote(stage_y, out_y.at[j], send_by.at[j], recv_by.at[j], outer_peer(j))

    def copy_az(j):
        return remote(top_z, stage_z.at[j], send_az.at[j], recv_az.at[j], outer_peer(j))

    def copy_bz(j):
        return remote(stage_z, out_z.at[j], send_bz.at[j], recv_bz.at[j], inner_peer(j))

    def sum_a(j):
        return remote(sum_x, sum_stage.at[j], send_sa.at[j], recv_sa.at[j], inner_peer(j))

    def sum_b(j):
        return remote(row_sum, sum_out.at[j], send_sb.at[j], recv_sb.at[j], outer_peer(j))

    for j in range(1, inner):
        copy_ay(j).start()
    for j in range(1, outer):
        copy_az(j).start()
    if has_sum:
        for j in range(1, inner):
            sum_a(j).start()
    for j in range(1, group):
        mid_copy(j).start()
    own_y = pltpu.make_async_copy(top_y, stage_y.at[0], local_sem.at[0])
    own_z = pltpu.make_async_copy(top_z, stage_z.at[0], local_sem.at[1])
    own_y.start()
    own_z.start()
    mid_out[0] = mid_x[...]
    own_y.wait()
    own_z.wait()
    for j in range(1, inner):
        copy_ay(j).wait()
    for j in range(1, outer):
        copy_by(j).start()
    for j in range(1, outer):
        copy_az(j).wait()
    for j in range(1, inner):
        copy_bz(j).start()
    if has_sum:
        total = sum_x[...]
        for j in range(1, inner):
            sum_a(j).wait()
            total = total + sum_stage[j]
        row_sum[...] = total
        for j in range(1, outer):
            sum_b(j).start()
        sum_out[0] = total
    out_y[0] = stage_y[...]
    out_z[0] = stage_z[...]
    for j in range(1, group):
        mid_copy(j).wait()
    for j in range(1, outer):
        copy_by(j).wait()
        if has_sum:
            sum_b(j).wait()
    for j in range(1, inner):
        copy_bz(j).wait()


def ctx_gather(mid_x, top_x, group, tag, sum_x=None):
    count = lax.axis_size("ctx")
    inner = RING
    outer = count // inner
    rows = top_x.shape[0]
    half = max(1, min(rows - 1, 8 * round(0.25 * rows / 8)))
    top_y = top_x[:half]
    top_z = top_x[half:]
    has_sum = sum_x is not None
    operands = (mid_x, top_y, top_z) + ((sum_x,) if has_sum else ())
    out_shape = (
        jax.ShapeDtypeStruct((group,) + mid_x.shape, mid_x.dtype),
        jax.ShapeDtypeStruct((outer, inner) + top_y.shape, top_x.dtype),
        jax.ShapeDtypeStruct((inner, outer) + top_z.shape, top_x.dtype),
    )
    scratch = [
        pltpu.VMEM((inner,) + top_y.shape, top_x.dtype),
        pltpu.VMEM((outer,) + top_z.shape, top_x.dtype),
    ]
    if has_sum:
        out_shape += (jax.ShapeDtypeStruct((outer,) + sum_x.shape, sum_x.dtype),)
        scratch += [
            pltpu.VMEM((inner,) + sum_x.shape, sum_x.dtype),
            pltpu.VMEM(sum_x.shape, sum_x.dtype),
        ]
    for size in (group, inner, outer, outer, inner):
        scratch += [pltpu.SemaphoreType.DMA((size,)), pltpu.SemaphoreType.DMA((size,))]
    scratch.append(pltpu.SemaphoreType.DMA((2,)))
    if has_sum:
        for size in (inner, outer):
            scratch += [pltpu.SemaphoreType.DMA((size,)), pltpu.SemaphoreType.DMA((size,))]
    outs = pl.pallas_call(
        functools.partial(gather_kernel, group, inner, has_sum),
        out_shape=out_shape,
        in_specs=[pl.BlockSpec(memory_space=pltpu.VMEM)] * len(operands),
        out_specs=(pl.BlockSpec(memory_space=pltpu.VMEM),) * len(out_shape),
        scratch_shapes=scratch,
        compiler_params=pltpu.CompilerParams(collective_id=tag, has_side_effects=True),
    )(*operands)
    top_all = jnp.concatenate([outs[1], jnp.transpose(outs[2], (1, 0, 2, 3))], 2)
    return (outs[0], top_all) + tuple(outs[3:])


def lane_dense(block):
    return block.reshape(-1, HEAD_DIM)


def pick_rows(source_rows, dilation, shifts):
    row_count, head_count, head_width = source_rows.shape
    grouped = source_rows.reshape(row_count // dilation, dilation, head_count, head_width)
    hit_mask = jnp.arange(dilation, dtype=jnp.int32).reshape(1, dilation, 1, 1) == shifts.reshape(
        1, 1, head_count, 1
    )
    chosen = jnp.where(hit_mask, grouped, jnp.zeros((), source_rows.dtype))
    return jnp.sum(chosen, axis=1, dtype=source_rows.dtype)


def place_rows(row_values, dilation, shifts):
    row_count, head_count, head_width = row_values.shape
    hit_mask = jnp.arange(dilation, dtype=jnp.int32).reshape(1, dilation, 1, 1) == shifts.reshape(
        1, 1, head_count, 1
    )
    spread = jnp.where(hit_mask, row_values[:, None], jnp.zeros((), row_values.dtype))
    return spread.reshape(row_count * dilation, head_count, head_width)


def level_scores(q_rows, k_rows):
    score_scale = 1.0 / math.sqrt(q_rows.shape[-1])
    return (
        jnp.einsum("qhe,khe->hqk", q_rows, k_rows, preferred_element_type=jnp.float32) * score_scale
    )


def attend(q_rows, k_rows, v_rows):
    scores = level_scores(q_rows, k_rows)
    row_max = jnp.max(scores, axis=-1, keepdims=True)
    log_total = row_max[..., 0] + jnp.log(jnp.sum(jnp.exp(scores - row_max), axis=-1))
    soft_rows = jnp.exp(scores - log_total[..., None]).astype(jnp.bfloat16)
    level_out = jnp.einsum("hqk,khe->qhe", soft_rows, v_rows, preferred_element_type=jnp.float32)
    return (level_out, log_total.T)


def score_grads(q_rows, k_rows, v_rows, log_total, grad_low, row_shift):
    score_scale = 1.0 / math.sqrt(q_rows.shape[-1])
    scores = level_scores(q_rows, k_rows)
    exact_soft = jnp.exp(scores - log_total.T[..., None])
    prob_grad = jnp.einsum("qhe,khe->hqk", grad_low, v_rows, preferred_element_type=jnp.float32)
    score_grad = (exact_soft * (prob_grad + row_shift.T[..., None]) * score_scale).astype(
        jnp.bfloat16
    )
    return (score_grad, exact_soft.astype(jnp.bfloat16))


def key_parts(score_grad, soft_low, q_rows, grad_low):
    k_part = jnp.einsum("hqk,qhe->khe", score_grad, q_rows, preferred_element_type=jnp.float32)
    v_part = jnp.einsum("hqk,qhe->khe", soft_low, grad_low, preferred_element_type=jnp.float32)
    return (k_part, v_part)


def query_part(score_grad, k_rows):
    return jnp.einsum("hqk,khe->qhe", score_grad, k_rows, preferred_element_type=jnp.float32)


def split_qkv(packed, head_count):
    width = head_count * HEAD_DIM
    shape = (packed.shape[0], head_count, HEAD_DIM)
    return tuple(packed[:, i * width : (i + 1) * width].reshape(shape) for i in range(3))


def split_wide(values):
    high = values.astype(jnp.bfloat16)
    low = (values - high.astype(jnp.float32)).astype(jnp.bfloat16)
    return high, low


def join_wide(high, low):
    return high.astype(jnp.float32) + low.astype(jnp.float32)


def pack_grads(grad_low, row_shift, width):
    rows = grad_low.shape[0]
    high, low = split_wide(row_shift)
    used = grad_low.shape[1] * grad_low.shape[2] + 2 * row_shift.shape[1]
    return jnp.concatenate(
        [grad_low.reshape(rows, -1), high, low, jnp.zeros((rows, width - used), jnp.bfloat16)], 1
    )


def unpack_grads(packed, head_count):
    width = head_count * HEAD_DIM
    grad_low = packed[:, :width].reshape(-1, head_count, HEAD_DIM)
    return grad_low, join_wide(
        packed[:, width : width + head_count], packed[:, width + head_count : width + 2 * head_count]
    )


def shards(queries, keys, values, grad_y, out_gain, offsets):
    tokens = queries.shape[1]
    flat_width = queries.shape[2]
    head_count = flat_width // HEAD_DIM
    row_shape = (tokens, head_count, HEAD_DIM)
    q_own = queries[0].reshape(row_shape)
    k_own = keys[0].reshape(row_shape)
    v_own = values[0].reshape(row_shape)
    ctx_size = lax.axis_size("ctx")
    mid_shift = offsets[0]
    top_shift = offsets[1]
    positions = jnp.arange(tokens, dtype=jnp.int32)
    mid_hit = (positions % R1)[:, None] == mid_shift[None, :]
    top_hit = (positions % ctx_size)[:, None] == top_shift[None, :]
    mid_pack = jnp.concatenate(
        [pick_rows(x, R1, mid_shift).reshape(-1, flat_width) for x in (q_own, k_own, v_own)], 1
    )
    top_pack = jnp.concatenate(
        [pick_rows(x, ctx_size, top_shift).reshape(-1, flat_width) for x in (q_own, k_own, v_own)],
        1,
    )
    mid_rows = mid_pack.shape[0]
    top_rows = top_pack.shape[0]
    mid_all, top_all = ctx_gather(mid_pack, lane_dense(top_pack), SPAN, 0)
    mid_all = mid_all.reshape(-1, mid_pack.shape[1])
    top_all = top_all.reshape(-1, top_pack.shape[1])
    mid_q, mid_k, mid_v = split_qkv(mid_all, head_count)
    top_q, top_k, top_v = split_qkv(top_all, head_count)
    base_out, base_total = attend(q_own, k_own, v_own)
    mid_out_all, mid_total_all = attend(mid_q, mid_k, mid_v)
    top_out_all, top_total_all = attend(top_q, top_k, top_v)
    mid_out = mid_out_all[:mid_rows]
    mid_total = mid_total_all[:mid_rows]
    top_out = top_out_all[:top_rows]
    top_total = top_total_all[:top_rows]
    mid_full = place_rows(mid_total[..., None], R1, mid_shift)[..., 0]
    top_full = place_rows(top_total[..., None], ctx_size, top_shift)[..., 0]
    row_max = jnp.maximum(base_total, jnp.where(mid_hit, mid_full, base_total))
    row_max = jnp.maximum(row_max, jnp.where(top_hit, top_full, base_total))
    base_expo = jnp.exp(base_total - row_max)
    mid_expo = jnp.where(mid_hit, jnp.exp(mid_full - row_max), 0.0)
    top_expo = jnp.where(top_hit, jnp.exp(top_full - row_max), 0.0)
    denom = base_expo + mid_expo + top_expo
    base_share = base_expo / denom
    mid_share = mid_expo / denom
    top_share = top_expo / denom
    attn = (
        base_share[..., None] * base_out
        + mid_share[..., None] * place_rows(mid_out, R1, mid_shift)
        + top_share[..., None] * place_rows(top_out, ctx_size, top_shift)
    )
    inv_rms = lax.rsqrt(jnp.mean(attn * attn, axis=-1, keepdims=True) + EPS)
    normed = attn * inv_rms
    gain_rows = out_gain.reshape(head_count, HEAD_DIM)
    attended = (normed * gain_rows).astype(jnp.bfloat16).reshape(1, tokens, flat_width)
    grad_full = grad_y[0].reshape(row_shape).astype(jnp.float32)
    gain_part = jnp.sum(grad_full * normed, axis=0).reshape(flat_width)
    grad_norm = grad_full * gain_rows
    grad_attn = inv_rms * (
        grad_norm - normed * jnp.mean(grad_norm * normed, axis=-1, keepdims=True)
    )
    inner = jnp.sum(grad_attn * attn, axis=-1)
    base_low = (base_share[..., None] * grad_attn).astype(jnp.bfloat16)
    base_shift = -(base_share * inner)
    base_grad, base_soft = score_grads(q_own, k_own, v_own, base_total, base_low, base_shift)
    base_dq = query_part(base_grad, k_own)
    base_dk, base_dv = key_parts(base_grad, base_soft, q_own, base_low)

    mid_sel = pick_rows(mid_share[..., None], R1, mid_shift)[..., 0]
    mid_low = (mid_sel[..., None] * pick_rows(grad_attn, R1, mid_shift)).astype(jnp.bfloat16)
    mid_row_shift = -(mid_sel * pick_rows(inner[..., None], R1, mid_shift)[..., 0])
    top_sel = pick_rows(top_share[..., None], ctx_size, top_shift)[..., 0]
    top_low = (top_sel[..., None] * pick_rows(grad_attn, ctx_size, top_shift)).astype(jnp.bfloat16)
    top_row_shift = -(top_sel * pick_rows(inner[..., None], ctx_size, top_shift)[..., 0])

    shift_high, shift_low = split_wide(top_row_shift.reshape(-1))
    top_flat = jnp.concatenate([top_low.reshape(-1), shift_high, shift_low])
    top_flat = jnp.pad(top_flat, (0, -top_flat.shape[0] % HEAD_DIM))
    mid_gathered, gathered, gain_rows_sum = ctx_gather(
        pack_grads(mid_low, mid_row_shift, flat_width + HEAD_DIM),
        lane_dense(top_flat),
        SPAN,
        1,
        sum_x=lane_dense(gain_part),
    )
    mid_low_all, mid_shift_all = unpack_grads(
        mid_gathered.reshape(-1, mid_gathered.shape[-1]), head_count
    )
    gathered = gathered.reshape(ctx_size, -1)
    grad_width = top_rows * flat_width
    top_low_all = gathered[:, :grad_width].reshape(-1, head_count, HEAD_DIM)
    gain_grad = lax.psum(jnp.sum(gain_rows_sum, axis=0).reshape(flat_width), "dp")
    shift_count = top_rows * head_count
    top_shift_all = join_wide(
        gathered[:, grad_width : grad_width + shift_count],
        gathered[:, grad_width + shift_count : grad_width + 2 * shift_count],
    ).reshape(-1, head_count)

    mid_grad, mid_soft = score_grads(
        mid_q, mid_k, mid_v, mid_total_all, mid_low_all, mid_shift_all
    )
    mid_dq = query_part(mid_grad[:, :mid_rows], mid_k)
    mid_dk, mid_dv = key_parts(
        mid_grad[:, :, :mid_rows], mid_soft[:, :, :mid_rows], mid_q, mid_low_all
    )
    top_grad, top_soft = score_grads(
        top_q, top_k, top_v, top_total_all, top_low_all, top_shift_all
    )
    top_dq = query_part(top_grad[:, :top_rows], top_k)
    top_dk, top_dv = key_parts(
        top_grad[:, :, :top_rows], top_soft[:, :, :top_rows], top_q, top_low_all
    )
    query_grad = (
        base_dq + place_rows(mid_dq, R1, mid_shift) + place_rows(top_dq, ctx_size, top_shift)
    )
    key_grad = base_dk + place_rows(mid_dk, R1, mid_shift) + place_rows(top_dk, ctx_size, top_shift)
    value_grad = (
        base_dv + place_rows(mid_dv, R1, mid_shift) + place_rows(top_dv, ctx_size, top_shift)
    )
    out_shape = (1, tokens, flat_width)
    return (
        attended,
        query_grad.astype(jnp.bfloat16).reshape(out_shape),
        key_grad.astype(jnp.bfloat16).reshape(out_shape),
        value_grad.astype(jnp.bfloat16).reshape(out_shape),
        gain_grad,
    )


def solution(mesh):
    in_specs = (
        P("dp", "ctx", "head"),
        P("dp", "ctx", "head"),
        P("dp", "ctx", "head"),
        P("dp", "ctx", "head"),
        P("head"),
        P(None, "head"),
    )
    out_specs = (
        P("dp", "ctx", "head"),
        P("dp", "ctx", "head"),
        P("dp", "ctx", "head"),
        P("dp", "ctx", "head"),
        P("head"),
    )
    return jax.shard_map(shards, mesh=mesh, in_specs=in_specs, out_specs=out_specs, check_vma=False)
```

```python
import functools
import math

import jax
import jax.numpy as jnp
from jax import lax
from jax.experimental import pallas as pl
from jax.experimental.pallas import tpu as pltpu
from jax.sharding import PartitionSpec as P

HEAD_DIM = 128
SPAN = 4
R1 = 8
RING = 8


EPS = 1e-06


def gather_kernel(group, inner, has_sum, *refs):
    if has_sum:
        (mid_x, top_y, top_z, sum_x, mid_out, out_y, out_z, sum_out,
         stage_y, stage_z, sum_stage, row_sum, *sems) = refs
    else:
        (mid_x, top_y, top_z, mid_out, out_y, out_z, stage_y, stage_z, *sems) = refs
    (send_mid, recv_mid, send_ay, recv_ay, send_by, recv_by,
     send_az, recv_az, send_bz, recv_bz, local_sem) = sems[:11]
    if has_sum:
        send_sa, recv_sa, send_sb, recv_sb = sems[11:]
    count = lax.axis_size("ctx")
    outer = count // inner
    me = lax.axis_index("ctx")
    row = lax.axis_index("dp")
    col = lax.axis_index("head")
    lo = me % inner
    hi = me // inner
    base = me - me % group
    mesh_ids = pl.DeviceIdType.MESH

    def inner_peer(j):
        return hi * inner + lax.rem(lo + j, inner)

    def outer_peer(j):
        return lax.rem(hi + j, outer) * inner + lo

    barrier = pltpu.get_barrier_semaphore()
    for j in range(1, inner):
        pl.semaphore_signal(barrier, 1, device_id=(row, inner_peer(j), col), device_id_type=mesh_ids)
    for j in range(1, outer):
        pl.semaphore_signal(barrier, 1, device_id=(row, outer_peer(j), col), device_id_type=mesh_ids)
    if has_sum:
        for j in range(outer):
            pl.semaphore_signal(
                barrier, 1, device_id=(1 - row, outer_peer(j), col), device_id_type=mesh_ids
            )
    pl.semaphore_wait(barrier, inner + outer - 2 + (outer if has_sum else 0))

    def remote(src, dst, send, recv, peer, core=None):
        return pltpu.make_async_remote_copy(
            src, dst, send, recv, device_id=(row if core is None else core, peer, col),
            device_id_type=mesh_ids,
        )

    def mid_copy(j):
        peer = base + lax.rem(me % group + j, group)
        return remote(mid_x, mid_out.at[j], send_mid.at[j], recv_mid.at[j], peer)

    def copy_ay(j):
        return remote(top_y, stage_y.at[j], send_ay.at[j], recv_ay.at[j], inner_peer(j))

    def copy_by(j):
        return remote(stage_y, out_y.at[j], send_by.at[j], recv_by.at[j], outer_peer(j))

    def copy_az(j):
        return remote(top_z, stage_z.at[j], send_az.at[j], recv_az.at[j], outer_peer(j))

    def copy_bz(j):
        return remote(stage_z, out_z.at[j], send_bz.at[j], recv_bz.at[j], inner_peer(j))

    def sum_a(j):
        return remote(sum_x, sum_stage.at[j], send_sa.at[j], recv_sa.at[j], inner_peer(j))

    def sum_b(c, j):
        slot = c * outer + j
        return remote(
            row_sum, sum_out.at[c, j], send_sb.at[slot], recv_sb.at[slot], outer_peer(j),
            core=(1 - row) if c else row,
        )

    sum_peers = [(0, j) for j in range(1, outer)] + [(1, j) for j in range(outer)]

    for j in range(1, inner):
        copy_ay(j).start()
    for j in range(1, outer):
        copy_az(j).start()
    if has_sum:
        for j in range(1, inner):
            sum_a(j).start()
    for j in range(1, group):
        mid_copy(j).start()
    own_y = pltpu.make_async_copy(top_y, stage_y.at[0], local_sem.at[0])
    own_z = pltpu.make_async_copy(top_z, stage_z.at[0], local_sem.at[1])
    own_y.start()
    own_z.start()
    mid_out[0] = mid_x[...]
    own_y.wait()
    own_z.wait()
    for j in range(1, inner):
        copy_ay(j).wait()
    for j in range(1, outer):
        copy_by(j).start()
    for j in range(1, outer):
        copy_az(j).wait()
    for j in range(1, inner):
        copy_bz(j).start()
    if has_sum:
        total = sum_x[...]
        for j in range(1, inner):
            sum_a(j).wait()
            total = total + sum_stage[j]
        row_sum[...] = total
        for c, j in sum_peers:
            sum_b(c, j).start()
        sum_out[0, 0] = total
    out_y[0] = stage_y[...]
    out_z[0] = stage_z[...]
    for j in range(1, group):
        mid_copy(j).wait()
    for j in range(1, outer):
        copy_by(j).wait()
    if has_sum:
        for c, j in sum_peers:
            sum_b(c, j).wait()
    for j in range(1, inner):
        copy_bz(j).wait()


def ctx_gather(mid_x, top_x, group, tag, sum_x=None):
    count = lax.axis_size("ctx")
    inner = RING
    outer = count // inner
    half = (top_x.shape[0] + 1) // 2
    top_y = top_x[:half]
    top_z = top_x[half:]
    has_sum = sum_x is not None
    operands = (mid_x, top_y, top_z) + ((sum_x,) if has_sum else ())
    out_shape = (
        jax.ShapeDtypeStruct((group,) + mid_x.shape, mid_x.dtype),
        jax.ShapeDtypeStruct((outer, inner) + top_y.shape, top_x.dtype),
        jax.ShapeDtypeStruct((inner, outer) + top_z.shape, top_x.dtype),
    )
    scratch = [
        pltpu.VMEM((inner,) + top_y.shape, top_x.dtype),
        pltpu.VMEM((outer,) + top_z.shape, top_x.dtype),
    ]
    if has_sum:
        out_shape += (jax.ShapeDtypeStruct((2, outer) + sum_x.shape, sum_x.dtype),)
        scratch += [
            pltpu.VMEM((inner,) + sum_x.shape, sum_x.dtype),
            pltpu.VMEM(sum_x.shape, sum_x.dtype),
        ]
    for size in (group, inner, outer, outer, inner):
        scratch += [pltpu.SemaphoreType.DMA((size,)), pltpu.SemaphoreType.DMA((size,))]
    scratch.append(pltpu.SemaphoreType.DMA((2,)))
    if has_sum:
        for size in (inner, 2 * outer):
            scratch += [pltpu.SemaphoreType.DMA((size,)), pltpu.SemaphoreType.DMA((size,))]
    outs = pl.pallas_call(
        functools.partial(gather_kernel, group, inner, has_sum),
        out_shape=out_shape,
        in_specs=[pl.BlockSpec(memory_space=pltpu.VMEM)] * len(operands),
        out_specs=(pl.BlockSpec(memory_space=pltpu.VMEM),) * len(out_shape),
        scratch_shapes=scratch,
        compiler_params=pltpu.CompilerParams(collective_id=tag, has_side_effects=True),
    )(*operands)
    top_all = jnp.concatenate([outs[1], jnp.transpose(outs[2], (1, 0, 2, 3))], 2)
    return (outs[0], top_all) + tuple(outs[3:])


def lane_dense(block):
    return block.reshape(-1, HEAD_DIM)


def pick_rows(source_rows, dilation, shifts):
    row_count, head_count, head_width = source_rows.shape
    grouped = source_rows.reshape(row_count // dilation, dilation, head_count, head_width)
    hit_mask = jnp.arange(dilation, dtype=jnp.int32).reshape(1, dilation, 1, 1) == shifts.reshape(
        1, 1, head_count, 1
    )
    chosen = jnp.where(hit_mask, grouped, jnp.zeros((), source_rows.dtype))
    return jnp.sum(chosen, axis=1, dtype=source_rows.dtype)


def place_rows(row_values, dilation, shifts):
    row_count, head_count, head_width = row_values.shape
    hit_mask = jnp.arange(dilation, dtype=jnp.int32).reshape(1, dilation, 1, 1) == shifts.reshape(
        1, 1, head_count, 1
    )
    spread = jnp.where(hit_mask, row_values[:, None], jnp.zeros((), row_values.dtype))
    return spread.reshape(row_count * dilation, head_count, head_width)


def level_scores(q_rows, k_rows):
    score_scale = 1.0 / math.sqrt(q_rows.shape[-1])
    return (
        jnp.einsum("qhe,khe->hqk", q_rows, k_rows, preferred_element_type=jnp.float32) * score_scale
    )


def attend(q_rows, k_rows, v_rows):
    scores = level_scores(q_rows, k_rows)
    row_max = jnp.max(scores, axis=-1, keepdims=True)
    log_total = row_max[..., 0] + jnp.log(jnp.sum(jnp.exp(scores - row_max), axis=-1))
    soft_rows = jnp.exp(scores - log_total[..., None]).astype(jnp.bfloat16)
    level_out = jnp.einsum("hqk,khe->qhe", soft_rows, v_rows, preferred_element_type=jnp.float32)
    return (level_out, log_total.T)


def score_grads(q_rows, k_rows, v_rows, log_total, grad_low, row_shift):
    score_scale = 1.0 / math.sqrt(q_rows.shape[-1])
    scores = level_scores(q_rows, k_rows)
    exact_soft = jnp.exp(scores - log_total.T[..., None])
    prob_grad = jnp.einsum("qhe,khe->hqk", grad_low, v_rows, preferred_element_type=jnp.float32)
    score_grad = (exact_soft * (prob_grad + row_shift.T[..., None]) * score_scale).astype(
        jnp.bfloat16
    )
    return (score_grad, exact_soft.astype(jnp.bfloat16))


def key_parts(score_grad, soft_low, q_rows, grad_low):
    k_part = jnp.einsum("hqk,qhe->khe", score_grad, q_rows, preferred_element_type=jnp.float32)
    v_part = jnp.einsum("hqk,qhe->khe", soft_low, grad_low, preferred_element_type=jnp.float32)
    return (k_part, v_part)


def query_part(score_grad, k_rows):
    return jnp.einsum("hqk,khe->qhe", score_grad, k_rows, preferred_element_type=jnp.float32)


def split_qkv(packed, head_count):
    width = head_count * HEAD_DIM
    shape = (packed.shape[0], head_count, HEAD_DIM)
    return tuple(packed[:, i * width : (i + 1) * width].reshape(shape) for i in range(3))


def split_wide(values):
    high = values.astype(jnp.bfloat16)
    low = (values - high.astype(jnp.float32)).astype(jnp.bfloat16)
    return high, low


def join_wide(high, low):
    return high.astype(jnp.float32) + low.astype(jnp.float32)


def pack_grads(grad_low, row_shift, width):
    rows = grad_low.shape[0]
    high, low = split_wide(row_shift)
    used = grad_low.shape[1] * grad_low.shape[2] + 2 * row_shift.shape[1]
    return jnp.concatenate(
        [grad_low.reshape(rows, -1), high, low, jnp.zeros((rows, width - used), jnp.bfloat16)], 1
    )


def unpack_grads(packed, head_count):
    width = head_count * HEAD_DIM
    grad_low = packed[:, :width].reshape(-1, head_count, HEAD_DIM)
    return grad_low, join_wide(
        packed[:, width : width + head_count], packed[:, width + head_count : width + 2 * head_count]
    )


def shards(queries, keys, values, grad_y, out_gain, offsets):
    tokens = queries.shape[1]
    flat_width = queries.shape[2]
    head_count = flat_width // HEAD_DIM
    row_shape = (tokens, head_count, HEAD_DIM)
    q_own = queries[0].reshape(row_shape)
    k_own = keys[0].reshape(row_shape)
    v_own = values[0].reshape(row_shape)
    ctx_size = lax.axis_size("ctx")
    mid_shift = offsets[0]
    top_shift = offsets[1]
    positions = jnp.arange(tokens, dtype=jnp.int32)
    mid_hit = (positions % R1)[:, None] == mid_shift[None, :]
    top_hit = (positions % ctx_size)[:, None] == top_shift[None, :]
    mid_pack = jnp.concatenate(
        [pick_rows(x, R1, mid_shift).reshape(-1, flat_width) for x in (q_own, k_own, v_own)], 1
    )
    top_pack = jnp.concatenate(
        [pick_rows(x, ctx_size, top_shift).reshape(-1, flat_width) for x in (q_own, k_own, v_own)],
        1,
    )
    mid_rows = mid_pack.shape[0]
    top_rows = top_pack.shape[0]
    mid_all, top_all = ctx_gather(mid_pack, lane_dense(top_pack), SPAN, 0)
    mid_all = mid_all.reshape(-1, mid_pack.shape[1])
    top_all = top_all.reshape(-1, top_pack.shape[1])
    mid_q, mid_k, mid_v = split_qkv(mid_all, head_count)
    top_q, top_k, top_v = split_qkv(top_all, head_count)
    base_out, base_total = attend(q_own, k_own, v_own)
    mid_out_all, mid_total_all = attend(mid_q, mid_k, mid_v)
    top_out_all, top_total_all = attend(top_q, top_k, top_v)
    mid_out = mid_out_all[:mid_rows]
    mid_total = mid_total_all[:mid_rows]
    top_out = top_out_all[:top_rows]
    top_total = top_total_all[:top_rows]
    mid_full = place_rows(mid_total[..., None], R1, mid_shift)[..., 0]
    top_full = place_rows(top_total[..., None], ctx_size, top_shift)[..., 0]
    row_max = jnp.maximum(base_total, jnp.where(mid_hit, mid_full, base_total))
    row_max = jnp.maximum(row_max, jnp.where(top_hit, top_full, base_total))
    base_expo = jnp.exp(base_total - row_max)
    mid_expo = jnp.where(mid_hit, jnp.exp(mid_full - row_max), 0.0)
    top_expo = jnp.where(top_hit, jnp.exp(top_full - row_max), 0.0)
    denom = base_expo + mid_expo + top_expo
    base_share = base_expo / denom
    mid_share = mid_expo / denom
    top_share = top_expo / denom
    attn = (
        base_share[..., None] * base_out
        + mid_share[..., None] * place_rows(mid_out, R1, mid_shift)
        + top_share[..., None] * place_rows(top_out, ctx_size, top_shift)
    )
    inv_rms = lax.rsqrt(jnp.mean(attn * attn, axis=-1, keepdims=True) + EPS)
    normed = attn * inv_rms
    gain_rows = out_gain.reshape(head_count, HEAD_DIM)
    attended = (normed * gain_rows).astype(jnp.bfloat16).reshape(1, tokens, flat_width)
    grad_full = grad_y[0].reshape(row_shape).astype(jnp.float32)
    gain_part = jnp.sum(grad_full * normed, axis=0).reshape(flat_width)
    grad_norm = grad_full * gain_rows
    grad_attn = inv_rms * (
        grad_norm - normed * jnp.mean(grad_norm * normed, axis=-1, keepdims=True)
    )
    inner = jnp.sum(grad_attn * attn, axis=-1)
    base_low = (base_share[..., None] * grad_attn).astype(jnp.bfloat16)
    base_shift = -(base_share * inner)
    base_grad, base_soft = score_grads(q_own, k_own, v_own, base_total, base_low, base_shift)
    base_dq = query_part(base_grad, k_own)
    base_dk, base_dv = key_parts(base_grad, base_soft, q_own, base_low)

    mid_sel = pick_rows(mid_share[..., None], R1, mid_shift)[..., 0]
    mid_low = (mid_sel[..., None] * pick_rows(grad_attn, R1, mid_shift)).astype(jnp.bfloat16)
    mid_row_shift = -(mid_sel * pick_rows(inner[..., None], R1, mid_shift)[..., 0])
    top_sel = pick_rows(top_share[..., None], ctx_size, top_shift)[..., 0]
    top_low = (top_sel[..., None] * pick_rows(grad_attn, ctx_size, top_shift)).astype(jnp.bfloat16)
    top_row_shift = -(top_sel * pick_rows(inner[..., None], ctx_size, top_shift)[..., 0])

    shift_high, shift_low = split_wide(top_row_shift.reshape(-1))
    top_flat = jnp.concatenate([top_low.reshape(-1), shift_high, shift_low])
    top_flat = jnp.pad(top_flat, (0, -top_flat.shape[0] % HEAD_DIM))
    mid_gathered, gathered, gain_rows_sum = ctx_gather(
        pack_grads(mid_low, mid_row_shift, flat_width + HEAD_DIM),
        lane_dense(top_flat),
        SPAN,
        1,
        sum_x=lane_dense(gain_part),
    )
    mid_low_all, mid_shift_all = unpack_grads(
        mid_gathered.reshape(-1, mid_gathered.shape[-1]), head_count
    )
    gathered = gathered.reshape(ctx_size, -1)
    grad_width = top_rows * flat_width
    top_low_all = gathered[:, :grad_width].reshape(-1, head_count, HEAD_DIM)
    gain_grad = jnp.sum(gain_rows_sum, axis=(0, 1)).reshape(flat_width)
    shift_count = top_rows * head_count
    top_shift_all = join_wide(
        gathered[:, grad_width : grad_width + shift_count],
        gathered[:, grad_width + shift_count : grad_width + 2 * shift_count],
    ).reshape(-1, head_count)

    mid_grad, mid_soft = score_grads(
        mid_q, mid_k, mid_v, mid_total_all, mid_low_all, mid_shift_all
    )
    mid_dq = query_part(mid_grad[:, :mid_rows], mid_k)
    mid_dk, mid_dv = key_parts(
        mid_grad[:, :, :mid_rows], mid_soft[:, :, :mid_rows], mid_q, mid_low_all
    )
    top_grad, top_soft = score_grads(
        top_q, top_k, top_v, top_total_all, top_low_all, top_shift_all
    )
    top_dq = query_part(top_grad[:, :top_rows], top_k)
    top_dk, top_dv = key_parts(
        top_grad[:, :, :top_rows], top_soft[:, :, :top_rows], top_q, top_low_all
    )
    query_grad = (
        base_dq + place_rows(mid_dq, R1, mid_shift) + place_rows(top_dq, ctx_size, top_shift)
    )
    key_grad = base_dk + place_rows(mid_dk, R1, mid_shift) + place_rows(top_dk, ctx_size, top_shift)
    value_grad = (
        base_dv + place_rows(mid_dv, R1, mid_shift) + place_rows(top_dv, ctx_size, top_shift)
    )
    out_shape = (1, tokens, flat_width)
    return (
        attended,
        query_grad.astype(jnp.bfloat16).reshape(out_shape),
        key_grad.astype(jnp.bfloat16).reshape(out_shape),
        value_grad.astype(jnp.bfloat16).reshape(out_shape),
        gain_grad,
    )


def solution(mesh):
    in_specs = (
        P("dp", "ctx", "head"),
        P("dp", "ctx", "head"),
        P("dp", "ctx", "head"),
        P("dp", "ctx", "head"),
        P("head"),
        P(None, "head"),
    )
    out_specs = (
        P("dp", "ctx", "head"),
        P("dp", "ctx", "head"),
        P("dp", "ctx", "head"),
        P("dp", "ctx", "head"),
        P("head"),
    )
    return jax.shard_map(shards, mesh=mesh, in_specs=in_specs, out_specs=out_specs, check_vma=False)
```

```python
import functools
import math

import jax
import jax.numpy as jnp
from jax import lax
from jax.experimental import pallas as pl
from jax.experimental.pallas import tpu as pltpu
from jax.sharding import PartitionSpec as P

HEAD_DIM = 128
SPAN = 4
R1 = 8
RING = 8


EPS = 1e-06


def gather_kernel(group, inner, has_sum, *refs):
    if has_sum:
        (mid_x, top_y, top_z, sum_x, mid_out, out_y, out_z, sum_out,
         stage_y, stage_z, sum_stage, row_sum, *sems) = refs
    else:
        (mid_x, top_y, top_z, mid_out, out_y, out_z, stage_y, stage_z, *sems) = refs
    (send_mid, recv_mid, send_ay, recv_ay, send_by, recv_by,
     send_az, recv_az, send_bz, recv_bz, local_sem) = sems[:11]
    if has_sum:
        send_sa, recv_sa, send_sb, recv_sb = sems[11:]
    count = lax.axis_size("ctx")
    outer = count // inner
    me = lax.axis_index("ctx")
    row = lax.axis_index("dp")
    col = lax.axis_index("head")
    lo = me % inner
    hi = me // inner
    base = me - me % group
    mesh_ids = pl.DeviceIdType.MESH

    def inner_peer(j):
        return hi * inner + lax.rem(lo + j, inner)

    def outer_peer(j):
        return lax.rem(hi + j, outer) * inner + lo

    barrier = pltpu.get_barrier_semaphore()
    for j in range(1, inner):
        pl.semaphore_signal(barrier, 1, device_id=(row, inner_peer(j), col), device_id_type=mesh_ids)
    for j in range(1, outer):
        pl.semaphore_signal(barrier, 1, device_id=(row, outer_peer(j), col), device_id_type=mesh_ids)
    if has_sum:
        for j in range(outer):
            pl.semaphore_signal(
                barrier, 1, device_id=(1 - row, outer_peer(j), col), device_id_type=mesh_ids
            )
    pl.semaphore_wait(barrier, inner + outer - 2 + (outer if has_sum else 0))

    def remote(src, dst, send, recv, peer, core=None):
        return pltpu.make_async_remote_copy(
            src, dst, send, recv, device_id=(row if core is None else core, peer, col),
            device_id_type=mesh_ids,
        )

    def mid_copy(j):
        peer = base + lax.rem(me % group + j, group)
        return remote(mid_x, mid_out.at[j], send_mid.at[j], recv_mid.at[j], peer)

    def copy_ay(j):
        return remote(top_y, stage_y.at[j], send_ay.at[j], recv_ay.at[j], inner_peer(j))

    def copy_by(j):
        return remote(stage_y, out_y.at[j], send_by.at[j], recv_by.at[j], outer_peer(j))

    def copy_az(j):
        return remote(top_z, stage_z.at[j], send_az.at[j], recv_az.at[j], outer_peer(j))

    def copy_bz(j):
        return remote(stage_z, out_z.at[j], send_bz.at[j], recv_bz.at[j], inner_peer(j))

    def sum_a(j):
        return remote(sum_x, sum_stage.at[j], send_sa.at[j], recv_sa.at[j], inner_peer(j))

    def sum_b(c, j):
        slot = c * outer + j
        return remote(
            row_sum, sum_out.at[c, j], send_sb.at[slot], recv_sb.at[slot], outer_peer(j),
            core=(1 - row) if c else row,
        )

    sum_peers = [(0, j) for j in range(1, outer)] + [(1, j) for j in range(outer)]

    for j in range(1, inner):
        copy_ay(j).start()
    for j in range(1, outer):
        copy_az(j).start()
    if has_sum:
        for j in range(1, inner):
            sum_a(j).start()
    for j in range(1, group):
        mid_copy(j).start()
    own_y = pltpu.make_async_copy(top_y, stage_y.at[0], local_sem.at[0])
    own_z = pltpu.make_async_copy(top_z, stage_z.at[0], local_sem.at[1])
    own_y.start()
    own_z.start()
    mid_out[0] = mid_x[...]
    own_y.wait()
    own_z.wait()
    for j in range(1, inner):
        copy_ay(j).wait()
    if has_sum:
        total = sum_x[...]
        for j in range(1, inner):
            sum_a(j).wait()
            total = total + sum_stage[j]
        row_sum[...] = total
    for j in range(1, outer):
        copy_by(j).start()
    for j in range(1, outer):
        copy_az(j).wait()
    for j in range(1, inner):
        copy_bz(j).start()
    out_y[0] = stage_y[...]
    out_z[0] = stage_z[...]
    if has_sum:
        sum_out[0, 0] = total
        for c, j in sum_peers:
            sum_b(c, j).start()
    for j in range(1, group):
        mid_copy(j).wait()
    for j in range(1, outer):
        copy_by(j).wait()
    if has_sum:
        for c, j in sum_peers:
            sum_b(c, j).wait()
    for j in range(1, inner):
        copy_bz(j).wait()


def ctx_gather(mid_x, top_x, group, tag, sum_x=None):
    count = lax.axis_size("ctx")
    inner = RING
    outer = count // inner
    half = (top_x.shape[0] + 1) // 2
    top_y = top_x[:half]
    top_z = top_x[half:]
    has_sum = sum_x is not None
    operands = (mid_x, top_y, top_z) + ((sum_x,) if has_sum else ())
    out_shape = (
        jax.ShapeDtypeStruct((group,) + mid_x.shape, mid_x.dtype),
        jax.ShapeDtypeStruct((outer, inner) + top_y.shape, top_x.dtype),
        jax.ShapeDtypeStruct((inner, outer) + top_z.shape, top_x.dtype),
    )
    scratch = [
        pltpu.VMEM((inner,) + top_y.shape, top_x.dtype),
        pltpu.VMEM((outer,) + top_z.shape, top_x.dtype),
    ]
    if has_sum:
        out_shape += (jax.ShapeDtypeStruct((2, outer) + sum_x.shape, sum_x.dtype),)
        scratch += [
            pltpu.VMEM((inner,) + sum_x.shape, sum_x.dtype),
            pltpu.VMEM(sum_x.shape, sum_x.dtype),
        ]
    for size in (group, inner, outer, outer, inner):
        scratch += [pltpu.SemaphoreType.DMA((size,)), pltpu.SemaphoreType.DMA((size,))]
    scratch.append(pltpu.SemaphoreType.DMA((2,)))
    if has_sum:
        for size in (inner, 2 * outer):
            scratch += [pltpu.SemaphoreType.DMA((size,)), pltpu.SemaphoreType.DMA((size,))]
    outs = pl.pallas_call(
        functools.partial(gather_kernel, group, inner, has_sum),
        out_shape=out_shape,
        in_specs=[pl.BlockSpec(memory_space=pltpu.VMEM)] * len(operands),
        out_specs=(pl.BlockSpec(memory_space=pltpu.VMEM),) * len(out_shape),
        scratch_shapes=scratch,
        compiler_params=pltpu.CompilerParams(collective_id=tag, has_side_effects=True),
    )(*operands)
    top_all = jnp.concatenate([outs[1], jnp.transpose(outs[2], (1, 0, 2, 3))], 2)
    return (outs[0], top_all) + tuple(outs[3:])


def lane_dense(block):
    return block.reshape(-1, HEAD_DIM)


def pick_rows(source_rows, dilation, shifts):
    row_count, head_count, head_width = source_rows.shape
    grouped = source_rows.reshape(row_count // dilation, dilation, head_count, head_width)
    hit_mask = jnp.arange(dilation, dtype=jnp.int32).reshape(1, dilation, 1, 1) == shifts.reshape(
        1, 1, head_count, 1
    )
    chosen = jnp.where(hit_mask, grouped, jnp.zeros((), source_rows.dtype))
    return jnp.sum(chosen, axis=1, dtype=source_rows.dtype)


def place_rows(row_values, dilation, shifts):
    row_count, head_count, head_width = row_values.shape
    hit_mask = jnp.arange(dilation, dtype=jnp.int32).reshape(1, dilation, 1, 1) == shifts.reshape(
        1, 1, head_count, 1
    )
    spread = jnp.where(hit_mask, row_values[:, None], jnp.zeros((), row_values.dtype))
    return spread.reshape(row_count * dilation, head_count, head_width)


def level_scores(q_rows, k_rows):
    score_scale = 1.0 / math.sqrt(q_rows.shape[-1])
    return (
        jnp.einsum("qhe,khe->hqk", q_rows, k_rows, preferred_element_type=jnp.float32) * score_scale
    )


def attend(q_rows, k_rows, v_rows):
    scores = level_scores(q_rows, k_rows)
    row_max = jnp.max(scores, axis=-1, keepdims=True)
    log_total = row_max[..., 0] + jnp.log(jnp.sum(jnp.exp(scores - row_max), axis=-1))
    soft_rows = jnp.exp(scores - log_total[..., None]).astype(jnp.bfloat16)
    level_out = jnp.einsum("hqk,khe->qhe", soft_rows, v_rows, preferred_element_type=jnp.float32)
    return (level_out, log_total.T)


def score_grads(q_rows, k_rows, v_rows, log_total, grad_low, row_shift):
    score_scale = 1.0 / math.sqrt(q_rows.shape[-1])
    scores = level_scores(q_rows, k_rows)
    exact_soft = jnp.exp(scores - log_total.T[..., None])
    prob_grad = jnp.einsum("qhe,khe->hqk", grad_low, v_rows, preferred_element_type=jnp.float32)
    score_grad = (exact_soft * (prob_grad + row_shift.T[..., None]) * score_scale).astype(
        jnp.bfloat16
    )
    return (score_grad, exact_soft.astype(jnp.bfloat16))


def key_parts(score_grad, soft_low, q_rows, grad_low):
    k_part = jnp.einsum("hqk,qhe->khe", score_grad, q_rows, preferred_element_type=jnp.float32)
    v_part = jnp.einsum("hqk,qhe->khe", soft_low, grad_low, preferred_element_type=jnp.float32)
    return (k_part, v_part)


def query_part(score_grad, k_rows):
    return jnp.einsum("hqk,khe->qhe", score_grad, k_rows, preferred_element_type=jnp.float32)


def split_qkv(packed, head_count):
    width = head_count * HEAD_DIM
    shape = (packed.shape[0], head_count, HEAD_DIM)
    return tuple(packed[:, i * width : (i + 1) * width].reshape(shape) for i in range(3))


def split_wide(values):
    high = values.astype(jnp.bfloat16)
    low = (values - high.astype(jnp.float32)).astype(jnp.bfloat16)
    return high, low


def join_wide(high, low):
    return high.astype(jnp.float32) + low.astype(jnp.float32)


def pack_grads(grad_low, row_shift, width):
    rows = grad_low.shape[0]
    high, low = split_wide(row_shift)
    used = grad_low.shape[1] * grad_low.shape[2] + 2 * row_shift.shape[1]
    return jnp.concatenate(
        [grad_low.reshape(rows, -1), high, low, jnp.zeros((rows, width - used), jnp.bfloat16)], 1
    )


def unpack_grads(packed, head_count):
    width = head_count * HEAD_DIM
    grad_low = packed[:, :width].reshape(-1, head_count, HEAD_DIM)
    return grad_low, join_wide(
        packed[:, width : width + head_count], packed[:, width + head_count : width + 2 * head_count]
    )


def shards(queries, keys, values, grad_y, out_gain, offsets):
    tokens = queries.shape[1]
    flat_width = queries.shape[2]
    head_count = flat_width // HEAD_DIM
    row_shape = (tokens, head_count, HEAD_DIM)
    q_own = queries[0].reshape(row_shape)
    k_own = keys[0].reshape(row_shape)
    v_own = values[0].reshape(row_shape)
    ctx_size = lax.axis_size("ctx")
    mid_shift = offsets[0]
    top_shift = offsets[1]
    positions = jnp.arange(tokens, dtype=jnp.int32)
    mid_hit = (positions % R1)[:, None] == mid_shift[None, :]
    top_hit = (positions % ctx_size)[:, None] == top_shift[None, :]
    mid_pack = jnp.concatenate(
        [pick_rows(x, R1, mid_shift).reshape(-1, flat_width) for x in (q_own, k_own, v_own)], 1
    )
    top_pack = jnp.concatenate(
        [pick_rows(x, ctx_size, top_shift).reshape(-1, flat_width) for x in (q_own, k_own, v_own)],
        1,
    )
    mid_rows = mid_pack.shape[0]
    top_rows = top_pack.shape[0]
    mid_all, top_all = ctx_gather(mid_pack, lane_dense(top_pack), SPAN, 0)
    mid_all = mid_all.reshape(-1, mid_pack.shape[1])
    top_all = top_all.reshape(-1, top_pack.shape[1])
    mid_q, mid_k, mid_v = split_qkv(mid_all, head_count)
    top_q, top_k, top_v = split_qkv(top_all, head_count)
    base_out, base_total = attend(q_own, k_own, v_own)
    mid_out_all, mid_total_all = attend(mid_q, mid_k, mid_v)
    top_out_all, top_total_all = attend(top_q, top_k, top_v)
    mid_out = mid_out_all[:mid_rows]
    mid_total = mid_total_all[:mid_rows]
    top_out = top_out_all[:top_rows]
    top_total = top_total_all[:top_rows]
    mid_full = place_rows(mid_total[..., None], R1, mid_shift)[..., 0]
    top_full = place_rows(top_total[..., None], ctx_size, top_shift)[..., 0]
    row_max = jnp.maximum(base_total, jnp.where(mid_hit, mid_full, base_total))
    row_max = jnp.maximum(row_max, jnp.where(top_hit, top_full, base_total))
    base_expo = jnp.exp(base_total - row_max)
    mid_expo = jnp.where(mid_hit, jnp.exp(mid_full - row_max), 0.0)
    top_expo = jnp.where(top_hit, jnp.exp(top_full - row_max), 0.0)
    denom = base_expo + mid_expo + top_expo
    base_share = base_expo / denom
    mid_share = mid_expo / denom
    top_share = top_expo / denom
    attn = (
        base_share[..., None] * base_out
        + mid_share[..., None] * place_rows(mid_out, R1, mid_shift)
        + top_share[..., None] * place_rows(top_out, ctx_size, top_shift)
    )
    inv_rms = lax.rsqrt(jnp.mean(attn * attn, axis=-1, keepdims=True) + EPS)
    normed = attn * inv_rms
    gain_rows = out_gain.reshape(head_count, HEAD_DIM)
    attended = (normed * gain_rows).astype(jnp.bfloat16).reshape(1, tokens, flat_width)
    grad_full = grad_y[0].reshape(row_shape).astype(jnp.float32)
    gain_part = jnp.sum(grad_full * normed, axis=0).reshape(flat_width)
    grad_norm = grad_full * gain_rows
    grad_attn = inv_rms * (
        grad_norm - normed * jnp.mean(grad_norm * normed, axis=-1, keepdims=True)
    )
    inner = jnp.sum(grad_attn * attn, axis=-1)
    base_low = (base_share[..., None] * grad_attn).astype(jnp.bfloat16)
    base_shift = -(base_share * inner)
    base_grad, base_soft = score_grads(q_own, k_own, v_own, base_total, base_low, base_shift)
    base_dq = query_part(base_grad, k_own)
    base_dk, base_dv = key_parts(base_grad, base_soft, q_own, base_low)

    mid_sel = pick_rows(mid_share[..., None], R1, mid_shift)[..., 0]
    mid_low = (mid_sel[..., None] * pick_rows(grad_attn, R1, mid_shift)).astype(jnp.bfloat16)
    mid_row_shift = -(mid_sel * pick_rows(inner[..., None], R1, mid_shift)[..., 0])
    top_sel = pick_rows(top_share[..., None], ctx_size, top_shift)[..., 0]
    top_low = (top_sel[..., None] * pick_rows(grad_attn, ctx_size, top_shift)).astype(jnp.bfloat16)
    top_row_shift = -(top_sel * pick_rows(inner[..., None], ctx_size, top_shift)[..., 0])

    shift_high, shift_low = split_wide(top_row_shift.reshape(-1))
    top_flat = jnp.concatenate([top_low.reshape(-1), shift_high, shift_low])
    top_flat = jnp.pad(top_flat, (0, -top_flat.shape[0] % HEAD_DIM))
    mid_gathered, gathered, gain_rows_sum = ctx_gather(
        pack_grads(mid_low, mid_row_shift, flat_width + HEAD_DIM),
        lane_dense(top_flat),
        SPAN,
        1,
        sum_x=lane_dense(gain_part),
    )
    mid_low_all, mid_shift_all = unpack_grads(
        mid_gathered.reshape(-1, mid_gathered.shape[-1]), head_count
    )
    gathered = gathered.reshape(ctx_size, -1)
    grad_width = top_rows * flat_width
    top_low_all = gathered[:, :grad_width].reshape(-1, head_count, HEAD_DIM)
    gain_grad = jnp.sum(gain_rows_sum, axis=(0, 1)).reshape(flat_width)
    shift_count = top_rows * head_count
    top_shift_all = join_wide(
        gathered[:, grad_width : grad_width + shift_count],
        gathered[:, grad_width + shift_count : grad_width + 2 * shift_count],
    ).reshape(-1, head_count)

    mid_grad, mid_soft = score_grads(
        mid_q, mid_k, mid_v, mid_total_all, mid_low_all, mid_shift_all
    )
    mid_dq = query_part(mid_grad[:, :mid_rows], mid_k)
    mid_dk, mid_dv = key_parts(
        mid_grad[:, :, :mid_rows], mid_soft[:, :, :mid_rows], mid_q, mid_low_all
    )
    top_grad, top_soft = score_grads(
        top_q, top_k, top_v, top_total_all, top_low_all, top_shift_all
    )
    top_dq = query_part(top_grad[:, :top_rows], top_k)
    top_dk, top_dv = key_parts(
        top_grad[:, :, :top_rows], top_soft[:, :, :top_rows], top_q, top_low_all
    )
    query_grad = (
        base_dq + place_rows(mid_dq, R1, mid_shift) + place_rows(top_dq, ctx_size, top_shift)
    )
    key_grad = base_dk + place_rows(mid_dk, R1, mid_shift) + place_rows(top_dk, ctx_size, top_shift)
    value_grad = (
        base_dv + place_rows(mid_dv, R1, mid_shift) + place_rows(top_dv, ctx_size, top_shift)
    )
    out_shape = (1, tokens, flat_width)
    return (
        attended,
        query_grad.astype(jnp.bfloat16).reshape(out_shape),
        key_grad.astype(jnp.bfloat16).reshape(out_shape),
        value_grad.astype(jnp.bfloat16).reshape(out_shape),
        gain_grad,
    )


def solution(mesh):
    in_specs = (
        P("dp", "ctx", "head"),
        P("dp", "ctx", "head"),
        P("dp", "ctx", "head"),
        P("dp", "ctx", "head"),
        P("head"),
        P(None, "head"),
    )
    out_specs = (
        P("dp", "ctx", "head"),
        P("dp", "ctx", "head"),
        P("dp", "ctx", "head"),
        P("dp", "ctx", "head"),
        P("head"),
    )
    return jax.shard_map(shards, mesh=mesh, in_specs=in_specs, out_specs=out_specs, check_vma=False)
```

```python
import functools
import math

import jax
import jax.numpy as jnp
from jax import lax
from jax.experimental import pallas as pl
from jax.experimental.pallas import tpu as pltpu
from jax.sharding import PartitionSpec as P

HEAD_DIM = 128
SPAN = 4
R1 = 8
RING = 8


EPS = 1e-06


def gather_kernel(group, inner, has_sum, *refs):
    if has_sum:
        (mid_x, top_y, top_z, sum_x, mid_out, out_y, out_z, sum_out,
         stage_y, stage_z, sum_stage, row_sum, *sems) = refs
    else:
        (mid_x, top_y, top_z, mid_out, out_y, out_z, stage_y, stage_z, *sems) = refs
    (send_mid, recv_mid, send_ay, recv_ay, send_by, recv_by,
     send_az, recv_az, send_bz, recv_bz, local_sem) = sems[:11]
    if has_sum:
        send_sa, recv_sa, send_sb, recv_sb = sems[11:]
    count = lax.axis_size("ctx")
    outer = count // inner
    me = lax.axis_index("ctx")
    row = lax.axis_index("dp")
    col = lax.axis_index("head")
    lo = me % inner
    hi = me // inner
    base = me - me % group
    mesh_ids = pl.DeviceIdType.MESH

    def inner_peer(j):
        return hi * inner + lax.rem(lo + j, inner)

    def outer_peer(j):
        return lax.rem(hi + j, outer) * inner + lo

    barrier = pltpu.get_barrier_semaphore()
    for j in range(1, inner):
        pl.semaphore_signal(barrier, 1, device_id=(row, inner_peer(j), col), device_id_type=mesh_ids)
    for j in range(1, outer):
        pl.semaphore_signal(barrier, 1, device_id=(row, outer_peer(j), col), device_id_type=mesh_ids)
    if has_sum:
        for j in range(outer):
            pl.semaphore_signal(
                barrier, 1, device_id=(1 - row, outer_peer(j), col), device_id_type=mesh_ids
            )
    pl.semaphore_wait(barrier, inner + outer - 2 + (outer if has_sum else 0))

    def remote(src, dst, send, recv, peer, core=None):
        return pltpu.make_async_remote_copy(
            src, dst, send, recv, device_id=(row if core is None else core, peer, col),
            device_id_type=mesh_ids,
        )

    def mid_copy(j):
        peer = base + lax.rem(me % group + j, group)
        return remote(mid_x, mid_out.at[j], send_mid.at[j], recv_mid.at[j], peer)

    def copy_ay(j):
        return remote(top_y, stage_y.at[j], send_ay.at[j], recv_ay.at[j], inner_peer(j))

    def copy_by(j):
        return remote(stage_y, out_y.at[j], send_by.at[j], recv_by.at[j], outer_peer(j))

    def copy_az(j):
        return remote(top_z, stage_z.at[j], send_az.at[j], recv_az.at[j], outer_peer(j))

    def copy_bz(j):
        return remote(stage_z, out_z.at[j], send_bz.at[j], recv_bz.at[j], inner_peer(j))

    def sum_a(j):
        return remote(sum_x, sum_stage.at[j], send_sa.at[j], recv_sa.at[j], inner_peer(j))

    def sum_b(c, j):
        slot = c * outer + j
        return remote(
            row_sum, sum_out.at[c, j], send_sb.at[slot], recv_sb.at[slot], outer_peer(j),
            core=(1 - row) if c else row,
        )

    sum_peers = [(0, j) for j in range(1, outer)] + [(1, j) for j in range(outer)]

    for j in range(1, inner):
        copy_ay(j).start()
    for j in range(1, outer):
        copy_az(j).start()
    if has_sum:
        for j in range(1, inner):
            sum_a(j).start()
    for j in range(1, group):
        mid_copy(j).start()
    own_y = pltpu.make_async_copy(top_y, stage_y.at[0], local_sem.at[0])
    own_z = pltpu.make_async_copy(top_z, stage_z.at[0], local_sem.at[1])
    own_y.start()
    own_z.start()
    mid_out[0] = mid_x[...]
    own_y.wait()
    own_z.wait()
    for j in range(1, inner):
        copy_ay(j).wait()
    if has_sum:
        total = sum_x[...]
        for j in range(1, inner):
            sum_a(j).wait()
            total = total + sum_stage[j]
        row_sum[...] = total
    for j in range(1, outer):
        copy_by(j).start()
    for j in range(1, outer):
        copy_az(j).wait()
    for j in range(1, inner):
        copy_bz(j).start()
    out_y[0] = stage_y[...]
    out_z[0] = stage_z[...]
    if has_sum:
        sum_out[0, 0] = total
        for c, j in sum_peers:
            sum_b(c, j).start()
    for j in range(1, group):
        mid_copy(j).wait()
    for j in range(1, outer):
        copy_by(j).wait()
    if has_sum:
        for c, j in sum_peers:
            sum_b(c, j).wait()
    for j in range(1, inner):
        copy_bz(j).wait()


def ctx_gather(mid_x, top_x, group, tag, sum_x=None):
    count = lax.axis_size("ctx")
    inner = RING
    outer = count // inner
    half = (top_x.shape[0] + 1) // 2
    top_y = top_x[:half]
    top_z = top_x[half:]
    has_sum = sum_x is not None
    operands = (mid_x, top_y, top_z) + ((sum_x,) if has_sum else ())
    out_shape = (
        jax.ShapeDtypeStruct((group,) + mid_x.shape, mid_x.dtype),
        jax.ShapeDtypeStruct((outer, inner) + top_y.shape, top_x.dtype),
        jax.ShapeDtypeStruct((inner, outer) + top_z.shape, top_x.dtype),
    )
    scratch = [
        pltpu.VMEM((inner,) + top_y.shape, top_x.dtype),
        pltpu.VMEM((outer,) + top_z.shape, top_x.dtype),
    ]
    if has_sum:
        out_shape += (jax.ShapeDtypeStruct((2, outer) + sum_x.shape, sum_x.dtype),)
        scratch += [
            pltpu.VMEM((inner,) + sum_x.shape, sum_x.dtype),
            pltpu.VMEM(sum_x.shape, sum_x.dtype),
        ]
    for size in (group, inner, outer, outer, inner):
        scratch += [pltpu.SemaphoreType.DMA((size,)), pltpu.SemaphoreType.DMA((size,))]
    scratch.append(pltpu.SemaphoreType.DMA((2,)))
    if has_sum:
        for size in (inner, 2 * outer):
            scratch += [pltpu.SemaphoreType.DMA((size,)), pltpu.SemaphoreType.DMA((size,))]
    outs = pl.pallas_call(
        functools.partial(gather_kernel, group, inner, has_sum),
        out_shape=out_shape,
        in_specs=[pl.BlockSpec(memory_space=pltpu.VMEM)] * len(operands),
        out_specs=(pl.BlockSpec(memory_space=pltpu.VMEM),) * len(out_shape),
        scratch_shapes=scratch,
        compiler_params=pltpu.CompilerParams(collective_id=tag, has_side_effects=True),
    )(*operands)
    top_all = jnp.concatenate([outs[1], jnp.transpose(outs[2], (1, 0, 2, 3))], 2)
    return (outs[0], top_all) + tuple(outs[3:])


def token_major(rows):
    parts = [rows[:, h, :] for h in range(rows.shape[1])]
    return jnp.concatenate(parts, axis=1).astype(jnp.bfloat16)[None]


def lane_dense(block):
    return block.reshape(-1, HEAD_DIM)


def pick_rows(source_rows, dilation, shifts):
    row_count, head_count, head_width = source_rows.shape
    grouped = source_rows.reshape(row_count // dilation, dilation, head_count, head_width)
    hit_mask = jnp.arange(dilation, dtype=jnp.int32).reshape(1, dilation, 1, 1) == shifts.reshape(
        1, 1, head_count, 1
    )
    chosen = jnp.where(hit_mask, grouped, jnp.zeros((), source_rows.dtype))
    return jnp.sum(chosen, axis=1, dtype=source_rows.dtype)


def place_rows(row_values, dilation, shifts):
    row_count, head_count, head_width = row_values.shape
    hit_mask = jnp.arange(dilation, dtype=jnp.int32).reshape(1, dilation, 1, 1) == shifts.reshape(
        1, 1, head_count, 1
    )
    spread = jnp.where(hit_mask, row_values[:, None], jnp.zeros((), row_values.dtype))
    return spread.reshape(row_count * dilation, head_count, head_width)


def level_scores(q_rows, k_rows):
    score_scale = 1.0 / math.sqrt(q_rows.shape[-1])
    return (
        jnp.einsum("qhe,khe->hqk", q_rows, k_rows, preferred_element_type=jnp.float32) * score_scale
    )


def attend(q_rows, k_rows, v_rows):
    scores = level_scores(q_rows, k_rows)
    row_max = jnp.max(scores, axis=-1, keepdims=True)
    log_total = row_max[..., 0] + jnp.log(jnp.sum(jnp.exp(scores - row_max), axis=-1))
    soft_rows = jnp.exp(scores - log_total[..., None]).astype(jnp.bfloat16)
    level_out = jnp.einsum("hqk,khe->qhe", soft_rows, v_rows, preferred_element_type=jnp.float32)
    return (level_out, log_total.T)


def score_grads(q_rows, k_rows, v_rows, log_total, grad_low, row_shift):
    score_scale = 1.0 / math.sqrt(q_rows.shape[-1])
    scores = level_scores(q_rows, k_rows)
    exact_soft = jnp.exp(scores - log_total.T[..., None])
    prob_grad = jnp.einsum("qhe,khe->hqk", grad_low, v_rows, preferred_element_type=jnp.float32)
    score_grad = (exact_soft * (prob_grad + row_shift.T[..., None]) * score_scale).astype(
        jnp.bfloat16
    )
    return (score_grad, exact_soft.astype(jnp.bfloat16))


def key_parts(score_grad, soft_low, q_rows, grad_low):
    k_part = jnp.einsum("hqk,qhe->khe", score_grad, q_rows, preferred_element_type=jnp.float32)
    v_part = jnp.einsum("hqk,qhe->khe", soft_low, grad_low, preferred_element_type=jnp.float32)
    return (k_part, v_part)


def query_part(score_grad, k_rows):
    return jnp.einsum("hqk,khe->qhe", score_grad, k_rows, preferred_element_type=jnp.float32)


def split_qkv(packed, head_count):
    width = head_count * HEAD_DIM
    shape = (packed.shape[0], head_count, HEAD_DIM)
    return tuple(packed[:, i * width : (i + 1) * width].reshape(shape) for i in range(3))


def split_wide(values):
    high = values.astype(jnp.bfloat16)
    low = (values - high.astype(jnp.float32)).astype(jnp.bfloat16)
    return high, low


def join_wide(high, low):
    return high.astype(jnp.float32) + low.astype(jnp.float32)


def pack_grads(grad_low, row_shift, width):
    rows = grad_low.shape[0]
    high, low = split_wide(row_shift)
    used = grad_low.shape[1] * grad_low.shape[2] + 2 * row_shift.shape[1]
    return jnp.concatenate(
        [grad_low.reshape(rows, -1), high, low, jnp.zeros((rows, width - used), jnp.bfloat16)], 1
    )


def unpack_grads(packed, head_count):
    width = head_count * HEAD_DIM
    grad_low = packed[:, :width].reshape(-1, head_count, HEAD_DIM)
    return grad_low, join_wide(
        packed[:, width : width + head_count], packed[:, width + head_count : width + 2 * head_count]
    )


def shards(queries, keys, values, grad_y, out_gain, offsets):
    tokens = queries.shape[1]
    flat_width = queries.shape[2]
    head_count = flat_width // HEAD_DIM
    row_shape = (tokens, head_count, HEAD_DIM)
    q_own = queries[0].reshape(row_shape)
    k_own = keys[0].reshape(row_shape)
    v_own = values[0].reshape(row_shape)
    ctx_size = lax.axis_size("ctx")
    mid_shift = offsets[0]
    top_shift = offsets[1]
    positions = jnp.arange(tokens, dtype=jnp.int32)
    mid_hit = (positions % R1)[:, None] == mid_shift[None, :]
    top_hit = (positions % ctx_size)[:, None] == top_shift[None, :]
    mid_pack = jnp.concatenate(
        [pick_rows(x, R1, mid_shift).reshape(-1, flat_width) for x in (q_own, k_own, v_own)], 1
    )
    top_pack = jnp.concatenate(
        [pick_rows(x, ctx_size, top_shift).reshape(-1, flat_width) for x in (q_own, k_own, v_own)],
        1,
    )
    mid_rows = mid_pack.shape[0]
    top_rows = top_pack.shape[0]
    mid_all, top_all = ctx_gather(mid_pack, lane_dense(top_pack), SPAN, 0)
    mid_all = mid_all.reshape(-1, mid_pack.shape[1])
    top_all = top_all.reshape(-1, top_pack.shape[1])
    mid_q, mid_k, mid_v = split_qkv(mid_all, head_count)
    top_q, top_k, top_v = split_qkv(top_all, head_count)
    base_out, base_total = attend(q_own, k_own, v_own)
    mid_out_all, mid_total_all = attend(mid_q, mid_k, mid_v)
    top_out_all, top_total_all = attend(top_q, top_k, top_v)
    mid_out = mid_out_all[:mid_rows]
    mid_total = mid_total_all[:mid_rows]
    top_out = top_out_all[:top_rows]
    top_total = top_total_all[:top_rows]
    mid_full = place_rows(mid_total[..., None], R1, mid_shift)[..., 0]
    top_full = place_rows(top_total[..., None], ctx_size, top_shift)[..., 0]
    row_max = jnp.maximum(base_total, jnp.where(mid_hit, mid_full, base_total))
    row_max = jnp.maximum(row_max, jnp.where(top_hit, top_full, base_total))
    base_expo = jnp.exp(base_total - row_max)
    mid_expo = jnp.where(mid_hit, jnp.exp(mid_full - row_max), 0.0)
    top_expo = jnp.where(top_hit, jnp.exp(top_full - row_max), 0.0)
    denom = base_expo + mid_expo + top_expo
    base_share = base_expo / denom
    mid_share = mid_expo / denom
    top_share = top_expo / denom
    attn = (
        base_share[..., None] * base_out
        + mid_share[..., None] * place_rows(mid_out, R1, mid_shift)
        + top_share[..., None] * place_rows(top_out, ctx_size, top_shift)
    )
    inv_rms = lax.rsqrt(jnp.mean(attn * attn, axis=-1, keepdims=True) + EPS)
    normed = attn * inv_rms
    gain_rows = out_gain.reshape(head_count, HEAD_DIM)
    attended = token_major(normed * gain_rows)
    grad_full = grad_y[0].reshape(row_shape).astype(jnp.float32)
    gain_part = jnp.sum(grad_full * normed, axis=0).reshape(flat_width)
    grad_norm = grad_full * gain_rows
    grad_attn = inv_rms * (
        grad_norm - normed * jnp.mean(grad_norm * normed, axis=-1, keepdims=True)
    )
    inner = jnp.sum(grad_attn * attn, axis=-1)
    base_low = (base_share[..., None] * grad_attn).astype(jnp.bfloat16)
    base_shift = -(base_share * inner)
    base_grad, base_soft = score_grads(q_own, k_own, v_own, base_total, base_low, base_shift)
    base_dq = query_part(base_grad, k_own)
    base_dk, base_dv = key_parts(base_grad, base_soft, q_own, base_low)

    mid_sel = pick_rows(mid_share[..., None], R1, mid_shift)[..., 0]
    mid_low = (mid_sel[..., None] * pick_rows(grad_attn, R1, mid_shift)).astype(jnp.bfloat16)
    mid_row_shift = -(mid_sel * pick_rows(inner[..., None], R1, mid_shift)[..., 0])
    top_sel = pick_rows(top_share[..., None], ctx_size, top_shift)[..., 0]
    top_low = (top_sel[..., None] * pick_rows(grad_attn, ctx_size, top_shift)).astype(jnp.bfloat16)
    top_row_shift = -(top_sel * pick_rows(inner[..., None], ctx_size, top_shift)[..., 0])

    shift_high, shift_low = split_wide(top_row_shift.reshape(-1))
    top_flat = jnp.concatenate([top_low.reshape(-1), shift_high, shift_low])
    top_flat = jnp.pad(top_flat, (0, -top_flat.shape[0] % HEAD_DIM))
    mid_gathered, gathered, gain_rows_sum = ctx_gather(
        pack_grads(mid_low, mid_row_shift, flat_width + HEAD_DIM),
        lane_dense(top_flat),
        SPAN,
        1,
        sum_x=lane_dense(gain_part),
    )
    mid_low_all, mid_shift_all = unpack_grads(
        mid_gathered.reshape(-1, mid_gathered.shape[-1]), head_count
    )
    gathered = gathered.reshape(ctx_size, -1)
    grad_width = top_rows * flat_width
    top_low_all = gathered[:, :grad_width].reshape(-1, head_count, HEAD_DIM)
    gain_grad = jnp.sum(gain_rows_sum, axis=(0, 1)).reshape(flat_width)
    shift_count = top_rows * head_count
    top_shift_all = join_wide(
        gathered[:, grad_width : grad_width + shift_count],
        gathered[:, grad_width + shift_count : grad_width + 2 * shift_count],
    ).reshape(-1, head_count)

    mid_grad, mid_soft = score_grads(
        mid_q, mid_k, mid_v, mid_total_all, mid_low_all, mid_shift_all
    )
    mid_dq = query_part(mid_grad[:, :mid_rows], mid_k)
    mid_dk, mid_dv = key_parts(
        mid_grad[:, :, :mid_rows], mid_soft[:, :, :mid_rows], mid_q, mid_low_all
    )
    top_grad, top_soft = score_grads(
        top_q, top_k, top_v, top_total_all, top_low_all, top_shift_all
    )
    top_dq = query_part(top_grad[:, :top_rows], top_k)
    top_dk, top_dv = key_parts(
        top_grad[:, :, :top_rows], top_soft[:, :, :top_rows], top_q, top_low_all
    )
    query_grad = (
        base_dq + place_rows(mid_dq, R1, mid_shift) + place_rows(top_dq, ctx_size, top_shift)
    )
    key_grad = base_dk + place_rows(mid_dk, R1, mid_shift) + place_rows(top_dk, ctx_size, top_shift)
    value_grad = (
        base_dv + place_rows(mid_dv, R1, mid_shift) + place_rows(top_dv, ctx_size, top_shift)
    )
    return (
        attended,
        token_major(query_grad),
        token_major(key_grad),
        token_major(value_grad),
        gain_grad,
    )


def solution(mesh):
    in_specs = (
        P("dp", "ctx", "head"),
        P("dp", "ctx", "head"),
        P("dp", "ctx", "head"),
        P("dp", "ctx", "head"),
        P("head"),
        P(None, "head"),
    )
    out_specs = (
        P("dp", "ctx", "head"),
        P("dp", "ctx", "head"),
        P("dp", "ctx", "head"),
        P("dp", "ctx", "head"),
        P("head"),
    )
    return jax.shard_map(shards, mesh=mesh, in_specs=in_specs, out_specs=out_specs, check_vma=False)
```

```python
import functools
import math

import jax
import jax.numpy as jnp
from jax import lax
from jax.experimental import pallas as pl
from jax.experimental.pallas import tpu as pltpu
from jax.sharding import PartitionSpec as P

HEAD_DIM = 128
SPAN = 4
R1 = 8
RING = 8


EPS = 1e-06


def gather_kernel(group, inner, has_sum, *refs):
    if has_sum:
        (mid_x, top_y, top_z, sum_x, mid_out, out_y, out_z, sum_out,
         stage_y, stage_z, sum_stage, row_sum, *sems) = refs
    else:
        (mid_x, top_y, top_z, mid_out, out_y, out_z, stage_y, stage_z, *sems) = refs
    (send_mid, recv_mid, send_ay, recv_ay, send_by, recv_by,
     send_az, recv_az, send_bz, recv_bz, local_sem) = sems[:11]
    if has_sum:
        send_sa, recv_sa, send_sb, recv_sb = sems[11:]
    count = lax.axis_size("ctx")
    outer = count // inner
    me = lax.axis_index("ctx")
    row = lax.axis_index("dp")
    col = lax.axis_index("head")
    lo = me % inner
    hi = me // inner
    base = me - me % group
    mesh_ids = pl.DeviceIdType.MESH

    def inner_peer(j):
        return hi * inner + lax.rem(lo + j, inner)

    def outer_peer(j):
        return lax.rem(hi + j, outer) * inner + lo

    barrier = pltpu.get_barrier_semaphore()
    for j in range(1, inner):
        pl.semaphore_signal(barrier, 1, device_id=(row, inner_peer(j), col), device_id_type=mesh_ids)
    for j in range(1, outer):
        pl.semaphore_signal(barrier, 1, device_id=(row, outer_peer(j), col), device_id_type=mesh_ids)
    if has_sum:
        for j in range(outer):
            pl.semaphore_signal(
                barrier, 1, device_id=(1 - row, outer_peer(j), col), device_id_type=mesh_ids
            )
    pl.semaphore_wait(barrier, inner + outer - 2 + (outer if has_sum else 0))

    def remote(src, dst, send, recv, peer, core=None):
        return pltpu.make_async_remote_copy(
            src, dst, send, recv, device_id=(row if core is None else core, peer, col),
            device_id_type=mesh_ids,
        )

    def mid_copy(j):
        peer = base + lax.rem(me % group + j, group)
        return remote(mid_x, mid_out.at[j], send_mid.at[j], recv_mid.at[j], peer)

    def copy_ay(j):
        return remote(top_y, stage_y.at[j], send_ay.at[j], recv_ay.at[j], inner_peer(j))

    def copy_by(j):
        return remote(stage_y, out_y.at[j], send_by.at[j], recv_by.at[j], outer_peer(j))

    def copy_az(j):
        return remote(top_z, stage_z.at[j], send_az.at[j], recv_az.at[j], outer_peer(j))

    def copy_bz(j):
        return remote(stage_z, out_z.at[j], send_bz.at[j], recv_bz.at[j], inner_peer(j))

    def sum_a(j):
        return remote(sum_x, sum_stage.at[j], send_sa.at[j], recv_sa.at[j], inner_peer(j))

    def sum_b(c, j):
        slot = c * outer + j
        return remote(
            row_sum, sum_out.at[c, j], send_sb.at[slot], recv_sb.at[slot], outer_peer(j),
            core=(1 - row) if c else row,
        )

    sum_peers = [(0, j) for j in range(1, outer)] + [(1, j) for j in range(outer)]

    for j in range(1, inner):
        copy_ay(j).start()
    for j in range(1, outer):
        copy_az(j).start()
    if has_sum:
        for j in range(1, inner):
            sum_a(j).start()
    for j in range(1, group):
        mid_copy(j).start()
    own_y = pltpu.make_async_copy(top_y, stage_y.at[0], local_sem.at[0])
    own_z = pltpu.make_async_copy(top_z, stage_z.at[0], local_sem.at[1])
    own_y.start()
    own_z.start()
    mid_out[0] = mid_x[...]
    own_y.wait()
    own_z.wait()
    for j in range(1, inner):
        copy_ay(j).wait()
    if has_sum:
        total = sum_x[...]
        for j in range(1, inner):
            sum_a(j).wait()
            total = total + sum_stage[j]
        row_sum[...] = total
    for j in range(1, outer):
        copy_by(j).start()
    for j in range(1, outer):
        copy_az(j).wait()
    for j in range(1, inner):
        copy_bz(j).start()
    out_y[0] = stage_y[...]
    out_z[0] = stage_z[...]
    if has_sum:
        sum_out[0, 0] = total
        for c, j in sum_peers:
            sum_b(c, j).start()
    for j in range(1, group):
        mid_copy(j).wait()
    for j in range(1, outer):
        copy_by(j).wait()
    if has_sum:
        for c, j in sum_peers:
            sum_b(c, j).wait()
    for j in range(1, inner):
        copy_bz(j).wait()


def ctx_gather(mid_x, top_x, group, tag, sum_x=None):
    count = lax.axis_size("ctx")
    inner = RING
    outer = count // inner
    half = (top_x.shape[0] + 1) // 2
    top_y = top_x[:half]
    top_z = top_x[half:]
    has_sum = sum_x is not None
    operands = (mid_x, top_y, top_z) + ((sum_x,) if has_sum else ())
    out_shape = (
        jax.ShapeDtypeStruct((group,) + mid_x.shape, mid_x.dtype),
        jax.ShapeDtypeStruct((outer, inner) + top_y.shape, top_x.dtype),
        jax.ShapeDtypeStruct((inner, outer) + top_z.shape, top_x.dtype),
    )
    scratch = [
        pltpu.VMEM((inner,) + top_y.shape, top_x.dtype),
        pltpu.VMEM((outer,) + top_z.shape, top_x.dtype),
    ]
    if has_sum:
        out_shape += (jax.ShapeDtypeStruct((2, outer) + sum_x.shape, sum_x.dtype),)
        scratch += [
            pltpu.VMEM((inner,) + sum_x.shape, sum_x.dtype),
            pltpu.VMEM(sum_x.shape, sum_x.dtype),
        ]
    for size in (group, inner, outer, outer, inner):
        scratch += [pltpu.SemaphoreType.DMA((size,)), pltpu.SemaphoreType.DMA((size,))]
    scratch.append(pltpu.SemaphoreType.DMA((2,)))
    if has_sum:
        for size in (inner, 2 * outer):
            scratch += [pltpu.SemaphoreType.DMA((size,)), pltpu.SemaphoreType.DMA((size,))]
    outs = pl.pallas_call(
        functools.partial(gather_kernel, group, inner, has_sum),
        out_shape=out_shape,
        in_specs=[pl.BlockSpec(memory_space=pltpu.VMEM)] * len(operands),
        out_specs=(pl.BlockSpec(memory_space=pltpu.VMEM),) * len(out_shape),
        scratch_shapes=scratch,
        compiler_params=pltpu.CompilerParams(collective_id=tag, has_side_effects=True),
    )(*operands)
    top_all = jnp.concatenate([outs[1], jnp.transpose(outs[2], (1, 0, 2, 3))], 2)
    return (outs[0], top_all) + tuple(outs[3:])


def token_major(rows):
    parts = [rows[:, h, :] for h in range(rows.shape[1])]
    return jnp.concatenate(parts, axis=1).astype(jnp.bfloat16)[None]


def lane_dense(block):
    return block.reshape(-1, HEAD_DIM)


def pick_rows(source_rows, dilation, shifts):
    row_count, head_count, head_width = source_rows.shape
    grouped = source_rows.reshape(row_count // dilation, dilation, head_count, head_width)
    hit_mask = jnp.arange(dilation, dtype=jnp.int32).reshape(1, dilation, 1, 1) == shifts.reshape(
        1, 1, head_count, 1
    )
    chosen = jnp.where(hit_mask, grouped, jnp.zeros((), source_rows.dtype))
    return jnp.sum(chosen, axis=1, dtype=source_rows.dtype)


def place_rows(row_values, dilation, shifts):
    row_count, head_count, head_width = row_values.shape
    hit_mask = jnp.arange(dilation, dtype=jnp.int32).reshape(1, dilation, 1, 1) == shifts.reshape(
        1, 1, head_count, 1
    )
    spread = jnp.where(hit_mask, row_values[:, None], jnp.zeros((), row_values.dtype))
    return spread.reshape(row_count * dilation, head_count, head_width)


def level_scores(q_rows, k_rows):
    score_scale = 1.0 / math.sqrt(q_rows.shape[-1])
    return (
        jnp.einsum("qhe,khe->hqk", q_rows, k_rows, preferred_element_type=jnp.float32) * score_scale
    )


def attend(q_rows, k_rows, v_rows, own_rows=None):
    scores = level_scores(q_rows, k_rows)
    row_max = jnp.max(scores, axis=-1, keepdims=True)
    log_total = row_max[..., 0] + jnp.log(jnp.sum(jnp.exp(scores - row_max), axis=-1))
    if own_rows is not None:
        scores = scores[:, :own_rows]
    soft_rows = jnp.exp(scores - log_total[:, : scores.shape[1], None]).astype(jnp.bfloat16)
    level_out = jnp.einsum("hqk,khe->qhe", soft_rows, v_rows, preferred_element_type=jnp.float32)
    return (level_out, log_total.T)


def score_grads(q_rows, k_rows, v_rows, log_total, grad_low, row_shift):
    score_scale = 1.0 / math.sqrt(q_rows.shape[-1])
    scores = level_scores(q_rows, k_rows)
    exact_soft = jnp.exp(scores - log_total.T[..., None])
    prob_grad = jnp.einsum("qhe,khe->hqk", grad_low, v_rows, preferred_element_type=jnp.float32)
    score_grad = (exact_soft * (prob_grad + row_shift.T[..., None]) * score_scale).astype(
        jnp.bfloat16
    )
    return (score_grad, exact_soft.astype(jnp.bfloat16))


def key_parts(score_grad, soft_low, q_rows, grad_low):
    k_part = jnp.einsum("hqk,qhe->khe", score_grad, q_rows, preferred_element_type=jnp.float32)
    v_part = jnp.einsum("hqk,qhe->khe", soft_low, grad_low, preferred_element_type=jnp.float32)
    return (k_part, v_part)


def query_part(score_grad, k_rows):
    return jnp.einsum("hqk,khe->qhe", score_grad, k_rows, preferred_element_type=jnp.float32)


def split_qkv(packed, head_count):
    width = head_count * HEAD_DIM
    shape = (packed.shape[0], head_count, HEAD_DIM)
    return tuple(packed[:, i * width : (i + 1) * width].reshape(shape) for i in range(3))


def split_wide(values):
    high = values.astype(jnp.bfloat16)
    low = (values - high.astype(jnp.float32)).astype(jnp.bfloat16)
    return high, low


def join_wide(high, low):
    return high.astype(jnp.float32) + low.astype(jnp.float32)


def pack_grads(grad_low, row_shift, width):
    rows = grad_low.shape[0]
    high, low = split_wide(row_shift)
    used = grad_low.shape[1] * grad_low.shape[2] + 2 * row_shift.shape[1]
    return jnp.concatenate(
        [grad_low.reshape(rows, -1), high, low, jnp.zeros((rows, width - used), jnp.bfloat16)], 1
    )


def unpack_grads(packed, head_count):
    width = head_count * HEAD_DIM
    grad_low = packed[:, :width].reshape(-1, head_count, HEAD_DIM)
    return grad_low, join_wide(
        packed[:, width : width + head_count], packed[:, width + head_count : width + 2 * head_count]
    )


def shards(queries, keys, values, grad_y, out_gain, offsets):
    tokens = queries.shape[1]
    flat_width = queries.shape[2]
    head_count = flat_width // HEAD_DIM
    row_shape = (tokens, head_count, HEAD_DIM)
    q_own = queries[0].reshape(row_shape)
    k_own = keys[0].reshape(row_shape)
    v_own = values[0].reshape(row_shape)
    ctx_size = lax.axis_size("ctx")
    mid_shift = offsets[0]
    top_shift = offsets[1]
    positions = jnp.arange(tokens, dtype=jnp.int32)
    mid_hit = (positions % R1)[:, None] == mid_shift[None, :]
    top_hit = (positions % ctx_size)[:, None] == top_shift[None, :]
    mid_pack = jnp.concatenate(
        [pick_rows(x, R1, mid_shift).reshape(-1, flat_width) for x in (q_own, k_own, v_own)], 1
    )
    top_pack = jnp.concatenate(
        [pick_rows(x, ctx_size, top_shift).reshape(-1, flat_width) for x in (q_own, k_own, v_own)],
        1,
    )
    mid_rows = mid_pack.shape[0]
    top_rows = top_pack.shape[0]
    mid_all, top_all = ctx_gather(mid_pack, lane_dense(top_pack), SPAN, 0)
    mid_all = mid_all.reshape(-1, mid_pack.shape[1])
    top_all = top_all.reshape(-1, top_pack.shape[1])
    mid_q, mid_k, mid_v = split_qkv(mid_all, head_count)
    top_q, top_k, top_v = split_qkv(top_all, head_count)
    base_out, base_total = attend(q_own, k_own, v_own)
    mid_out_all, mid_total_all = attend(mid_q, mid_k, mid_v, mid_rows)
    top_out_all, top_total_all = attend(top_q, top_k, top_v, top_rows)
    mid_out = mid_out_all[:mid_rows]
    mid_total = mid_total_all[:mid_rows]
    top_out = top_out_all[:top_rows]
    top_total = top_total_all[:top_rows]
    mid_full = place_rows(mid_total[..., None], R1, mid_shift)[..., 0]
    top_full = place_rows(top_total[..., None], ctx_size, top_shift)[..., 0]
    row_max = jnp.maximum(base_total, jnp.where(mid_hit, mid_full, base_total))
    row_max = jnp.maximum(row_max, jnp.where(top_hit, top_full, base_total))
    base_expo = jnp.exp(base_total - row_max)
    mid_expo = jnp.where(mid_hit, jnp.exp(mid_full - row_max), 0.0)
    top_expo = jnp.where(top_hit, jnp.exp(top_full - row_max), 0.0)
    denom = base_expo + mid_expo + top_expo
    base_share = base_expo / denom
    mid_share = mid_expo / denom
    top_share = top_expo / denom
    attn = (
        base_share[..., None] * base_out
        + mid_share[..., None] * place_rows(mid_out, R1, mid_shift)
        + top_share[..., None] * place_rows(top_out, ctx_size, top_shift)
    )
    inv_rms = lax.rsqrt(jnp.mean(attn * attn, axis=-1, keepdims=True) + EPS)
    normed = attn * inv_rms
    gain_rows = out_gain.reshape(head_count, HEAD_DIM)
    attended = token_major(normed * gain_rows)
    grad_full = grad_y[0].reshape(row_shape).astype(jnp.float32)
    gain_part = jnp.sum(grad_full * normed, axis=0).reshape(flat_width)
    grad_norm = grad_full * gain_rows
    grad_attn = inv_rms * (
        grad_norm - normed * jnp.mean(grad_norm * normed, axis=-1, keepdims=True)
    )
    inner = jnp.sum(grad_attn * attn, axis=-1)
    base_low = (base_share[..., None] * grad_attn).astype(jnp.bfloat16)
    base_shift = -(base_share * inner)
    base_grad, base_soft = score_grads(q_own, k_own, v_own, base_total, base_low, base_shift)
    base_dq = query_part(base_grad, k_own)
    base_dk, base_dv = key_parts(base_grad, base_soft, q_own, base_low)

    mid_sel = pick_rows(mid_share[..., None], R1, mid_shift)[..., 0]
    mid_low = (mid_sel[..., None] * pick_rows(grad_attn, R1, mid_shift)).astype(jnp.bfloat16)
    mid_row_shift = -(mid_sel * pick_rows(inner[..., None], R1, mid_shift)[..., 0])
    top_sel = pick_rows(top_share[..., None], ctx_size, top_shift)[..., 0]
    top_low = (top_sel[..., None] * pick_rows(grad_attn, ctx_size, top_shift)).astype(jnp.bfloat16)
    top_row_shift = -(top_sel * pick_rows(inner[..., None], ctx_size, top_shift)[..., 0])

    shift_high, shift_low = split_wide(top_row_shift.reshape(-1))
    top_flat = jnp.concatenate([top_low.reshape(-1), shift_high, shift_low])
    top_flat = jnp.pad(top_flat, (0, -top_flat.shape[0] % HEAD_DIM))
    mid_gathered, gathered, gain_rows_sum = ctx_gather(
        pack_grads(mid_low, mid_row_shift, flat_width + HEAD_DIM),
        lane_dense(top_flat),
        SPAN,
        1,
        sum_x=lane_dense(gain_part),
    )
    mid_low_all, mid_shift_all = unpack_grads(
        mid_gathered.reshape(-1, mid_gathered.shape[-1]), head_count
    )
    gathered = gathered.reshape(ctx_size, -1)
    grad_width = top_rows * flat_width
    top_low_all = gathered[:, :grad_width].reshape(-1, head_count, HEAD_DIM)
    gain_grad = jnp.sum(gain_rows_sum, axis=(0, 1)).reshape(flat_width)
    shift_count = top_rows * head_count
    top_shift_all = join_wide(
        gathered[:, grad_width : grad_width + shift_count],
        gathered[:, grad_width + shift_count : grad_width + 2 * shift_count],
    ).reshape(-1, head_count)

    mid_grad, mid_soft = score_grads(
        mid_q, mid_k, mid_v, mid_total_all, mid_low_all, mid_shift_all
    )
    mid_dq = query_part(mid_grad[:, :mid_rows], mid_k)
    mid_dk, mid_dv = key_parts(
        mid_grad[:, :, :mid_rows], mid_soft[:, :, :mid_rows], mid_q, mid_low_all
    )
    top_grad, top_soft = score_grads(
        top_q, top_k, top_v, top_total_all, top_low_all, top_shift_all
    )
    top_dq = query_part(top_grad[:, :top_rows], top_k)
    top_dk, top_dv = key_parts(
        top_grad[:, :, :top_rows], top_soft[:, :, :top_rows], top_q, top_low_all
    )
    query_grad = (
        base_dq + place_rows(mid_dq, R1, mid_shift) + place_rows(top_dq, ctx_size, top_shift)
    )
    key_grad = base_dk + place_rows(mid_dk, R1, mid_shift) + place_rows(top_dk, ctx_size, top_shift)
    value_grad = (
        base_dv + place_rows(mid_dv, R1, mid_shift) + place_rows(top_dv, ctx_size, top_shift)
    )
    return (
        attended,
        token_major(query_grad),
        token_major(key_grad),
        token_major(value_grad),
        gain_grad,
    )


def solution(mesh):
    in_specs = (
        P("dp", "ctx", "head"),
        P("dp", "ctx", "head"),
        P("dp", "ctx", "head"),
        P("dp", "ctx", "head"),
        P("head"),
        P(None, "head"),
    )
    out_specs = (
        P("dp", "ctx", "head"),
        P("dp", "ctx", "head"),
        P("dp", "ctx", "head"),
        P("dp", "ctx", "head"),
        P("head"),
    )
    return jax.shard_map(shards, mesh=mesh, in_specs=in_specs, out_specs=out_specs, check_vma=False)
```

```python
import functools
import math

import jax
import jax.numpy as jnp
from jax import lax
from jax.experimental import pallas as pl
from jax.experimental.pallas import tpu as pltpu
from jax.sharding import PartitionSpec as P

HEAD_DIM = 128
SPAN = 4
R1 = 8
RING = 8


EPS = 1e-06


def gather_kernel(group, inner, has_sum, *refs):
    if has_sum:
        (mid_x, top_y, top_z, sum_x, mid_out, out_y, out_z, sum_out,
         stage_y, stage_z, sum_stage, row_sum, *sems) = refs
    else:
        (mid_x, top_y, top_z, mid_out, out_y, out_z, stage_y, stage_z, *sems) = refs
    (send_mid, recv_mid, send_ay, recv_ay, send_by, recv_by,
     send_az, recv_az, send_bz, recv_bz, local_sem) = sems[:11]
    if has_sum:
        send_sa, recv_sa, send_sb, recv_sb = sems[11:]
    count = lax.axis_size("ctx")
    outer = count // inner
    me = lax.axis_index("ctx")
    row = lax.axis_index("dp")
    col = lax.axis_index("head")
    lo = me % inner
    hi = me // inner
    base = me - me % group
    mesh_ids = pl.DeviceIdType.MESH

    def inner_peer(j):
        return hi * inner + lax.rem(lo + j, inner)

    def outer_peer(j):
        return lax.rem(hi + j, outer) * inner + lo

    barrier = pltpu.get_barrier_semaphore()
    for j in range(1, inner):
        pl.semaphore_signal(barrier, 1, device_id=(row, inner_peer(j), col), device_id_type=mesh_ids)
    for j in range(1, outer):
        pl.semaphore_signal(barrier, 1, device_id=(row, outer_peer(j), col), device_id_type=mesh_ids)
    if has_sum:
        for j in range(outer):
            pl.semaphore_signal(
                barrier, 1, device_id=(1 - row, outer_peer(j), col), device_id_type=mesh_ids
            )
    pl.semaphore_wait(barrier, inner + outer - 2 + (outer if has_sum else 0))

    def remote(src, dst, send, recv, peer, core=None):
        return pltpu.make_async_remote_copy(
            src, dst, send, recv, device_id=(row if core is None else core, peer, col),
            device_id_type=mesh_ids,
        )

    def mid_copy(j):
        peer = base + lax.rem(me % group + j, group)
        return remote(mid_x, mid_out.at[j], send_mid.at[j], recv_mid.at[j], peer)

    def copy_ay(j):
        return remote(top_y, stage_y.at[j], send_ay.at[j], recv_ay.at[j], inner_peer(j))

    def copy_by(j):
        return remote(stage_y, out_y.at[j], send_by.at[j], recv_by.at[j], outer_peer(j))

    def copy_az(j):
        return remote(top_z, stage_z.at[j], send_az.at[j], recv_az.at[j], outer_peer(j))

    def copy_bz(j):
        return remote(stage_z, out_z.at[j], send_bz.at[j], recv_bz.at[j], inner_peer(j))

    def sum_a(j):
        return remote(sum_x, sum_stage.at[j], send_sa.at[j], recv_sa.at[j], inner_peer(j))

    def sum_b(c, j):
        slot = c * outer + j
        return remote(
            row_sum, sum_out.at[c, j], send_sb.at[slot], recv_sb.at[slot], outer_peer(j),
            core=(1 - row) if c else row,
        )

    sum_peers = [(0, j) for j in range(1, outer)] + [(1, j) for j in range(outer)]

    for j in range(1, inner):
        copy_ay(j).start()
    for j in range(1, outer):
        copy_az(j).start()
    if has_sum:
        for j in range(1, inner):
            sum_a(j).start()
    for j in range(1, group):
        mid_copy(j).start()
    own_y = pltpu.make_async_copy(top_y, stage_y.at[0], local_sem.at[0])
    own_z = pltpu.make_async_copy(top_z, stage_z.at[0], local_sem.at[1])
    own_y.start()
    own_z.start()
    mid_out[0] = mid_x[...]
    own_y.wait()
    own_z.wait()
    for j in range(1, inner):
        copy_ay(j).wait()
    if has_sum:
        total = sum_x[...]
        for j in range(1, inner):
            sum_a(j).wait()
            total = total + sum_stage[j]
        row_sum[...] = total
    for j in range(1, outer):
        copy_by(j).start()
    for j in range(1, outer):
        copy_az(j).wait()
    for j in range(1, inner):
        copy_bz(j).start()
    out_y[0] = stage_y[...]
    out_z[0] = stage_z[...]
    if has_sum:
        sum_out[0, 0] = total
        for c, j in sum_peers:
            sum_b(c, j).start()
    for j in range(1, group):
        mid_copy(j).wait()
    for j in range(1, outer):
        copy_by(j).wait()
    if has_sum:
        for c, j in sum_peers:
            sum_b(c, j).wait()
    for j in range(1, inner):
        copy_bz(j).wait()


def ctx_gather(mid_x, top_x, group, tag, sum_x=None):
    count = lax.axis_size("ctx")
    inner = RING
    outer = count // inner
    half = (top_x.shape[0] + 1) // 2
    top_y = top_x[:half]
    top_z = top_x[half:]
    has_sum = sum_x is not None
    operands = (mid_x, top_y, top_z) + ((sum_x,) if has_sum else ())
    out_shape = (
        jax.ShapeDtypeStruct((group,) + mid_x.shape, mid_x.dtype),
        jax.ShapeDtypeStruct((outer, inner) + top_y.shape, top_x.dtype),
        jax.ShapeDtypeStruct((inner, outer) + top_z.shape, top_x.dtype),
    )
    scratch = [
        pltpu.VMEM((inner,) + top_y.shape, top_x.dtype),
        pltpu.VMEM((outer,) + top_z.shape, top_x.dtype),
    ]
    if has_sum:
        out_shape += (jax.ShapeDtypeStruct((2, outer) + sum_x.shape, sum_x.dtype),)
        scratch += [
            pltpu.VMEM((inner,) + sum_x.shape, sum_x.dtype),
            pltpu.VMEM(sum_x.shape, sum_x.dtype),
        ]
    for size in (group, inner, outer, outer, inner):
        scratch += [pltpu.SemaphoreType.DMA((size,)), pltpu.SemaphoreType.DMA((size,))]
    scratch.append(pltpu.SemaphoreType.DMA((2,)))
    if has_sum:
        for size in (inner, 2 * outer):
            scratch += [pltpu.SemaphoreType.DMA((size,)), pltpu.SemaphoreType.DMA((size,))]
    outs = pl.pallas_call(
        functools.partial(gather_kernel, group, inner, has_sum),
        out_shape=out_shape,
        in_specs=[pl.BlockSpec(memory_space=pltpu.VMEM)] * len(operands),
        out_specs=(pl.BlockSpec(memory_space=pltpu.VMEM),) * len(out_shape),
        scratch_shapes=scratch,
        compiler_params=pltpu.CompilerParams(collective_id=tag, has_side_effects=True),
    )(*operands)
    top_all = jnp.concatenate([outs[1], jnp.transpose(outs[2], (1, 0, 2, 3))], 2)
    return (outs[0], top_all) + tuple(outs[3:])


def token_major(rows):
    parts = [rows[:, h, :] for h in range(rows.shape[1])]
    return jnp.concatenate(parts, axis=1).astype(jnp.bfloat16)[None]


def lane_dense(block):
    return block.reshape(-1, HEAD_DIM)


def pick_rows(source_rows, dilation, shifts):
    row_count, head_count, head_width = source_rows.shape
    grouped = source_rows.reshape(row_count // dilation, dilation, head_count, head_width)
    index = jnp.broadcast_to(
        shifts.astype(jnp.int32).reshape(1, 1, head_count, 1),
        (row_count // dilation, 1, head_count, head_width),
    )
    return jnp.take_along_axis(grouped, index, axis=1)[:, 0]


def place_rows(row_values, dilation, shifts):
    row_count, head_count, head_width = row_values.shape
    hit_mask = jnp.arange(dilation, dtype=jnp.int32).reshape(1, dilation, 1, 1) == shifts.reshape(
        1, 1, head_count, 1
    )
    spread = jnp.where(hit_mask, row_values[:, None], jnp.zeros((), row_values.dtype))
    return spread.reshape(row_count * dilation, head_count, head_width)


def level_scores(q_rows, k_rows):
    score_scale = 1.0 / math.sqrt(q_rows.shape[-1])
    return (
        jnp.einsum("qhe,khe->hqk", q_rows, k_rows, preferred_element_type=jnp.float32) * score_scale
    )


def attend(q_rows, k_rows, v_rows):
    scores = level_scores(q_rows, k_rows)
    row_max = jnp.max(scores, axis=-1, keepdims=True)
    log_total = row_max[..., 0] + jnp.log(jnp.sum(jnp.exp(scores - row_max), axis=-1))
    soft_rows = jnp.exp(scores - log_total[..., None]).astype(jnp.bfloat16)
    level_out = jnp.einsum("hqk,khe->qhe", soft_rows, v_rows, preferred_element_type=jnp.float32)
    return (level_out, log_total.T)


def score_grads(q_rows, k_rows, v_rows, log_total, grad_low, row_shift):
    score_scale = 1.0 / math.sqrt(q_rows.shape[-1])
    scores = level_scores(q_rows, k_rows)
    exact_soft = jnp.exp(scores - log_total.T[..., None])
    prob_grad = jnp.einsum("qhe,khe->hqk", grad_low, v_rows, preferred_element_type=jnp.float32)
    score_grad = (exact_soft * (prob_grad + row_shift.T[..., None]) * score_scale).astype(
        jnp.bfloat16
    )
    return (score_grad, exact_soft.astype(jnp.bfloat16))


def key_parts(score_grad, soft_low, q_rows, grad_low):
    k_part = jnp.einsum("hqk,qhe->khe", score_grad, q_rows, preferred_element_type=jnp.float32)
    v_part = jnp.einsum("hqk,qhe->khe", soft_low, grad_low, preferred_element_type=jnp.float32)
    return (k_part, v_part)


def query_part(score_grad, k_rows):
    return jnp.einsum("hqk,khe->qhe", score_grad, k_rows, preferred_element_type=jnp.float32)


def split_qkv(packed, head_count):
    width = head_count * HEAD_DIM
    shape = (packed.shape[0], head_count, HEAD_DIM)
    return tuple(packed[:, i * width : (i + 1) * width].reshape(shape) for i in range(3))


def split_wide(values):
    high = values.astype(jnp.bfloat16)
    low = (values - high.astype(jnp.float32)).astype(jnp.bfloat16)
    return high, low


def join_wide(high, low):
    return high.astype(jnp.float32) + low.astype(jnp.float32)


def pack_grads(grad_low, row_shift, width):
    rows = grad_low.shape[0]
    high, low = split_wide(row_shift)
    used = grad_low.shape[1] * grad_low.shape[2] + 2 * row_shift.shape[1]
    return jnp.concatenate(
        [grad_low.reshape(rows, -1), high, low, jnp.zeros((rows, width - used), jnp.bfloat16)], 1
    )


def unpack_grads(packed, head_count):
    width = head_count * HEAD_DIM
    grad_low = packed[:, :width].reshape(-1, head_count, HEAD_DIM)
    return grad_low, join_wide(
        packed[:, width : width + head_count], packed[:, width + head_count : width + 2 * head_count]
    )


def shards(queries, keys, values, grad_y, out_gain, offsets):
    tokens = queries.shape[1]
    flat_width = queries.shape[2]
    head_count = flat_width // HEAD_DIM
    row_shape = (tokens, head_count, HEAD_DIM)
    q_own = queries[0].reshape(row_shape)
    k_own = keys[0].reshape(row_shape)
    v_own = values[0].reshape(row_shape)
    ctx_size = lax.axis_size("ctx")
    mid_shift = offsets[0]
    top_shift = offsets[1]
    positions = jnp.arange(tokens, dtype=jnp.int32)
    mid_hit = (positions % R1)[:, None] == mid_shift[None, :]
    top_hit = (positions % ctx_size)[:, None] == top_shift[None, :]
    mid_pack = jnp.concatenate(
        [pick_rows(x, R1, mid_shift).reshape(-1, flat_width) for x in (q_own, k_own, v_own)], 1
    )
    top_pack = jnp.concatenate(
        [pick_rows(x, ctx_size, top_shift).reshape(-1, flat_width) for x in (q_own, k_own, v_own)],
        1,
    )
    mid_rows = mid_pack.shape[0]
    top_rows = top_pack.shape[0]
    mid_all, top_all = ctx_gather(mid_pack, lane_dense(top_pack), SPAN, 0)
    mid_all = mid_all.reshape(-1, mid_pack.shape[1])
    top_all = top_all.reshape(-1, top_pack.shape[1])
    mid_q, mid_k, mid_v = split_qkv(mid_all, head_count)
    top_q, top_k, top_v = split_qkv(top_all, head_count)
    base_out, base_total = attend(q_own, k_own, v_own)
    mid_out_all, mid_total_all = attend(mid_q, mid_k, mid_v)
    top_out_all, top_total_all = attend(top_q, top_k, top_v)
    mid_out = mid_out_all[:mid_rows]
    mid_total = mid_total_all[:mid_rows]
    top_out = top_out_all[:top_rows]
    top_total = top_total_all[:top_rows]
    mid_full = place_rows(mid_total[..., None], R1, mid_shift)[..., 0]
    top_full = place_rows(top_total[..., None], ctx_size, top_shift)[..., 0]
    row_max = jnp.maximum(base_total, jnp.where(mid_hit, mid_full, base_total))
    row_max = jnp.maximum(row_max, jnp.where(top_hit, top_full, base_total))
    base_expo = jnp.exp(base_total - row_max)
    mid_expo = jnp.where(mid_hit, jnp.exp(mid_full - row_max), 0.0)
    top_expo = jnp.where(top_hit, jnp.exp(top_full - row_max), 0.0)
    denom = base_expo + mid_expo + top_expo
    base_share = base_expo / denom
    mid_share = mid_expo / denom
    top_share = top_expo / denom
    attn = (
        base_share[..., None] * base_out
        + mid_share[..., None] * place_rows(mid_out, R1, mid_shift)
        + top_share[..., None] * place_rows(top_out, ctx_size, top_shift)
    )
    inv_rms = lax.rsqrt(jnp.mean(attn * attn, axis=-1, keepdims=True) + EPS)
    normed = attn * inv_rms
    gain_rows = out_gain.reshape(head_count, HEAD_DIM)
    attended = token_major(normed * gain_rows)
    grad_full = grad_y[0].reshape(row_shape).astype(jnp.float32)
    gain_part = jnp.sum(grad_full * normed, axis=0).reshape(flat_width)
    grad_norm = grad_full * gain_rows
    grad_attn = inv_rms * (
        grad_norm - normed * jnp.mean(grad_norm * normed, axis=-1, keepdims=True)
    )
    inner = jnp.sum(grad_attn * attn, axis=-1)
    base_low = (base_share[..., None] * grad_attn).astype(jnp.bfloat16)
    base_shift = -(base_share * inner)
    base_grad, base_soft = score_grads(q_own, k_own, v_own, base_total, base_low, base_shift)
    base_dq = query_part(base_grad, k_own)
    base_dk, base_dv = key_parts(base_grad, base_soft, q_own, base_low)

    mid_sel = pick_rows(mid_share[..., None], R1, mid_shift)[..., 0]
    mid_low = (mid_sel[..., None] * pick_rows(grad_attn, R1, mid_shift)).astype(jnp.bfloat16)
    mid_row_shift = -(mid_sel * pick_rows(inner[..., None], R1, mid_shift)[..., 0])
    top_sel = pick_rows(top_share[..., None], ctx_size, top_shift)[..., 0]
    top_low = (top_sel[..., None] * pick_rows(grad_attn, ctx_size, top_shift)).astype(jnp.bfloat16)
    top_row_shift = -(top_sel * pick_rows(inner[..., None], ctx_size, top_shift)[..., 0])

    shift_high, shift_low = split_wide(top_row_shift.reshape(-1))
    top_flat = jnp.concatenate([top_low.reshape(-1), shift_high, shift_low])
    top_flat = jnp.pad(top_flat, (0, -top_flat.shape[0] % HEAD_DIM))
    mid_gathered, gathered, gain_rows_sum = ctx_gather(
        pack_grads(mid_low, mid_row_shift, flat_width + HEAD_DIM),
        lane_dense(top_flat),
        SPAN,
        1,
        sum_x=lane_dense(gain_part),
    )
    mid_low_all, mid_shift_all = unpack_grads(
        mid_gathered.reshape(-1, mid_gathered.shape[-1]), head_count
    )
    gathered = gathered.reshape(ctx_size, -1)
    grad_width = top_rows * flat_width
    top_low_all = gathered[:, :grad_width].reshape(-1, head_count, HEAD_DIM)
    gain_grad = jnp.sum(gain_rows_sum, axis=(0, 1)).reshape(flat_width)
    shift_count = top_rows * head_count
    top_shift_all = join_wide(
        gathered[:, grad_width : grad_width + shift_count],
        gathered[:, grad_width + shift_count : grad_width + 2 * shift_count],
    ).reshape(-1, head_count)

    mid_grad, mid_soft = score_grads(
        mid_q, mid_k, mid_v, mid_total_all, mid_low_all, mid_shift_all
    )
    mid_dq = query_part(mid_grad[:, :mid_rows], mid_k)
    mid_dk, mid_dv = key_parts(
        mid_grad[:, :, :mid_rows], mid_soft[:, :, :mid_rows], mid_q, mid_low_all
    )
    top_grad, top_soft = score_grads(
        top_q, top_k, top_v, top_total_all, top_low_all, top_shift_all
    )
    top_dq = query_part(top_grad[:, :top_rows], top_k)
    top_dk, top_dv = key_parts(
        top_grad[:, :, :top_rows], top_soft[:, :, :top_rows], top_q, top_low_all
    )
    query_grad = (
        base_dq + place_rows(mid_dq, R1, mid_shift) + place_rows(top_dq, ctx_size, top_shift)
    )
    key_grad = base_dk + place_rows(mid_dk, R1, mid_shift) + place_rows(top_dk, ctx_size, top_shift)
    value_grad = (
        base_dv + place_rows(mid_dv, R1, mid_shift) + place_rows(top_dv, ctx_size, top_shift)
    )
    return (
        attended,
        token_major(query_grad),
        token_major(key_grad),
        token_major(value_grad),
        gain_grad,
    )


def solution(mesh):
    in_specs = (
        P("dp", "ctx", "head"),
        P("dp", "ctx", "head"),
        P("dp", "ctx", "head"),
        P("dp", "ctx", "head"),
        P("head"),
        P(None, "head"),
    )
    out_specs = (
        P("dp", "ctx", "head"),
        P("dp", "ctx", "head"),
        P("dp", "ctx", "head"),
        P("dp", "ctx", "head"),
        P("head"),
    )
    return jax.shard_map(shards, mesh=mesh, in_specs=in_specs, out_specs=out_specs, check_vma=False)
```

```python
import functools
import math

import jax
import jax.numpy as jnp
from jax import lax
from jax.experimental import pallas as pl
from jax.experimental.pallas import tpu as pltpu
from jax.sharding import PartitionSpec as P

HEAD_DIM = 128
SPAN = 4
R1 = 8
RING = 8


EPS = 1e-06


def gather_kernel(group, inner, has_sum, *refs):
    if has_sum:
        (mid_x, top_y, top_z, sum_x, q_ref, k_ref, v_ref, lse_ref, grad_ref, shift_ref,
         mid_out, out_y, out_z, sum_out, dq_ref, dk_ref, dv_ref,
         stage_y, stage_z, sum_stage, row_sum, *sems) = refs
    else:
        (mid_x, top_y, top_z, mid_out, out_y, out_z, stage_y, stage_z, *sems) = refs
    (send_mid, recv_mid, send_ay, recv_ay, send_by, recv_by,
     send_az, recv_az, send_bz, recv_bz, local_sem) = sems[:11]
    if has_sum:
        send_sa, recv_sa, send_sb, recv_sb = sems[11:]
    count = lax.axis_size("ctx")
    outer = count // inner
    me = lax.axis_index("ctx")
    row = lax.axis_index("dp")
    col = lax.axis_index("head")
    lo = me % inner
    hi = me // inner
    base = me - me % group
    mesh_ids = pl.DeviceIdType.MESH

    def inner_peer(j):
        return hi * inner + lax.rem(lo + j, inner)

    def outer_peer(j):
        return lax.rem(hi + j, outer) * inner + lo

    barrier = pltpu.get_barrier_semaphore()
    for j in range(1, inner):
        pl.semaphore_signal(barrier, 1, device_id=(row, inner_peer(j), col), device_id_type=mesh_ids)
    for j in range(1, outer):
        pl.semaphore_signal(barrier, 1, device_id=(row, outer_peer(j), col), device_id_type=mesh_ids)
    if has_sum:
        for j in range(outer):
            pl.semaphore_signal(
                barrier, 1, device_id=(1 - row, outer_peer(j), col), device_id_type=mesh_ids
            )
    pl.semaphore_wait(barrier, inner + outer - 2 + (outer if has_sum else 0))

    def remote(src, dst, send, recv, peer, core=None):
        return pltpu.make_async_remote_copy(
            src, dst, send, recv, device_id=(row if core is None else core, peer, col),
            device_id_type=mesh_ids,
        )

    def mid_copy(j):
        peer = base + lax.rem(me % group + j, group)
        return remote(mid_x, mid_out.at[j], send_mid.at[j], recv_mid.at[j], peer)

    def copy_ay(j):
        return remote(top_y, stage_y.at[j], send_ay.at[j], recv_ay.at[j], inner_peer(j))

    def copy_by(j):
        return remote(stage_y, out_y.at[j], send_by.at[j], recv_by.at[j], outer_peer(j))

    def copy_az(j):
        return remote(top_z, stage_z.at[j], send_az.at[j], recv_az.at[j], outer_peer(j))

    def copy_bz(j):
        return remote(stage_z, out_z.at[j], send_bz.at[j], recv_bz.at[j], inner_peer(j))

    def sum_a(j):
        return remote(sum_x, sum_stage.at[j], send_sa.at[j], recv_sa.at[j], inner_peer(j))

    def sum_b(c, j):
        slot = c * outer + j
        return remote(
            row_sum, sum_out.at[c, j], send_sb.at[slot], recv_sb.at[slot], outer_peer(j),
            core=(1 - row) if c else row,
        )

    sum_peers = [(0, j) for j in range(1, outer)] + [(1, j) for j in range(outer)]

    for j in range(1, inner):
        copy_ay(j).start()
    for j in range(1, outer):
        copy_az(j).start()
    if has_sum:
        for j in range(1, inner):
            sum_a(j).start()
    for j in range(1, group):
        mid_copy(j).start()
    own_y = pltpu.make_async_copy(top_y, stage_y.at[0], local_sem.at[0])
    own_z = pltpu.make_async_copy(top_z, stage_z.at[0], local_sem.at[1])
    own_y.start()
    own_z.start()
    mid_out[0] = mid_x[...]
    own_y.wait()
    own_z.wait()
    for j in range(1, inner):
        copy_ay(j).wait()
    if has_sum:
        total = sum_x[...]
        for j in range(1, inner):
            sum_a(j).wait()
            total = total + sum_stage[j]
        row_sum[...] = total
    for j in range(1, outer):
        copy_by(j).start()
    for j in range(1, outer):
        copy_az(j).wait()
    for j in range(1, inner):
        copy_bz(j).start()
    out_y[0] = stage_y[...]
    out_z[0] = stage_z[...]
    if has_sum:
        sum_out[0, 0] = total
        for c, j in sum_peers:
            sum_b(c, j).start()
    if has_sum:
        base_backward(q_ref, k_ref, v_ref, lse_ref, grad_ref, shift_ref, dq_ref, dk_ref, dv_ref)
    for j in range(1, group):
        mid_copy(j).wait()
    for j in range(1, outer):
        copy_by(j).wait()
    if has_sum:
        for c, j in sum_peers:
            sum_b(c, j).wait()
    for j in range(1, inner):
        copy_bz(j).wait()


def base_backward(q_ref, k_ref, v_ref, lse_ref, grad_ref, shift_ref, dq_ref, dk_ref, dv_ref):
    score_scale = 1.0 / math.sqrt(HEAD_DIM)
    lse = lse_ref[...]
    shift = shift_ref[...]
    rows_by_rows = (((1,), (1,)), ((), ()))
    cols_by_cols = (((0,), (0,)), ((), ()))
    for h in range(lse.shape[1]):
        cols = pl.ds(h * HEAD_DIM, HEAD_DIM)
        q_h = q_ref[:, cols]
        k_h = k_ref[:, cols]
        v_h = v_ref[:, cols]
        g_h = grad_ref[:, cols]
        scores = lax.dot_general(q_h, k_h, rows_by_rows, preferred_element_type=jnp.float32)
        exact_soft = jnp.exp(scores * score_scale - lse[:, h : h + 1])
        prob_grad = lax.dot_general(g_h, v_h, rows_by_rows, preferred_element_type=jnp.float32)
        score_grad = (exact_soft * (prob_grad + shift[:, h : h + 1]) * score_scale).astype(
            jnp.bfloat16
        )
        dq_ref[:, cols] = jnp.dot(score_grad, k_h, preferred_element_type=jnp.float32)
        dk_ref[:, cols] = lax.dot_general(
            score_grad, q_h, cols_by_cols, preferred_element_type=jnp.float32
        )
        dv_ref[:, cols] = lax.dot_general(
            exact_soft.astype(jnp.bfloat16), g_h, cols_by_cols, preferred_element_type=jnp.float32
        )


def ctx_gather(mid_x, top_x, group, tag, sum_x=None, base=None):
    count = lax.axis_size("ctx")
    inner = RING
    outer = count // inner
    half = (top_x.shape[0] + 1) // 2
    top_y = top_x[:half]
    top_z = top_x[half:]
    has_sum = sum_x is not None
    operands = (mid_x, top_y, top_z) + ((sum_x,) + tuple(base) if has_sum else ())
    out_shape = (
        jax.ShapeDtypeStruct((group,) + mid_x.shape, mid_x.dtype),
        jax.ShapeDtypeStruct((outer, inner) + top_y.shape, top_x.dtype),
        jax.ShapeDtypeStruct((inner, outer) + top_z.shape, top_x.dtype),
    )
    scratch = [
        pltpu.VMEM((inner,) + top_y.shape, top_x.dtype),
        pltpu.VMEM((outer,) + top_z.shape, top_x.dtype),
    ]
    if has_sum:
        out_shape += (jax.ShapeDtypeStruct((2, outer) + sum_x.shape, sum_x.dtype),)
        out_shape += (jax.ShapeDtypeStruct(base[0].shape, jnp.float32),) * 3
        scratch += [
            pltpu.VMEM((inner,) + sum_x.shape, sum_x.dtype),
            pltpu.VMEM(sum_x.shape, sum_x.dtype),
        ]
    for size in (group, inner, outer, outer, inner):
        scratch += [pltpu.SemaphoreType.DMA((size,)), pltpu.SemaphoreType.DMA((size,))]
    scratch.append(pltpu.SemaphoreType.DMA((2,)))
    if has_sum:
        for size in (inner, 2 * outer):
            scratch += [pltpu.SemaphoreType.DMA((size,)), pltpu.SemaphoreType.DMA((size,))]
    outs = pl.pallas_call(
        functools.partial(gather_kernel, group, inner, has_sum),
        out_shape=out_shape,
        in_specs=[pl.BlockSpec(memory_space=pltpu.VMEM)] * len(operands),
        out_specs=(pl.BlockSpec(memory_space=pltpu.VMEM),) * len(out_shape),
        scratch_shapes=scratch,
        compiler_params=pltpu.CompilerParams(collective_id=tag, has_side_effects=True),
    )(*operands)
    top_all = jnp.concatenate([outs[1], jnp.transpose(outs[2], (1, 0, 2, 3))], 2)
    return (outs[0], top_all) + tuple(outs[3:])


def token_major(rows):
    parts = [rows[:, h, :] for h in range(rows.shape[1])]
    return jnp.concatenate(parts, axis=1).astype(jnp.bfloat16)[None]


def lane_dense(block):
    return block.reshape(-1, HEAD_DIM)


def pick_rows(source_rows, dilation, shifts):
    row_count, head_count, head_width = source_rows.shape
    grouped = source_rows.reshape(row_count // dilation, dilation, head_count, head_width)
    hit_mask = jnp.arange(dilation, dtype=jnp.int32).reshape(1, dilation, 1, 1) == shifts.reshape(
        1, 1, head_count, 1
    )
    chosen = jnp.where(hit_mask, grouped, jnp.zeros((), source_rows.dtype))
    return jnp.sum(chosen, axis=1, dtype=source_rows.dtype)


def place_rows(row_values, dilation, shifts):
    row_count, head_count, head_width = row_values.shape
    hit_mask = jnp.arange(dilation, dtype=jnp.int32).reshape(1, dilation, 1, 1) == shifts.reshape(
        1, 1, head_count, 1
    )
    spread = jnp.where(hit_mask, row_values[:, None], jnp.zeros((), row_values.dtype))
    return spread.reshape(row_count * dilation, head_count, head_width)


def level_scores(q_rows, k_rows):
    score_scale = 1.0 / math.sqrt(q_rows.shape[-1])
    return (
        jnp.einsum("qhe,khe->hqk", q_rows, k_rows, preferred_element_type=jnp.float32) * score_scale
    )


def attend(q_rows, k_rows, v_rows):
    scores = level_scores(q_rows, k_rows)
    row_max = jnp.max(scores, axis=-1, keepdims=True)
    log_total = row_max[..., 0] + jnp.log(jnp.sum(jnp.exp(scores - row_max), axis=-1))
    soft_rows = jnp.exp(scores - log_total[..., None]).astype(jnp.bfloat16)
    level_out = jnp.einsum("hqk,khe->qhe", soft_rows, v_rows, preferred_element_type=jnp.float32)
    return (level_out, log_total.T)


def score_grads(q_rows, k_rows, v_rows, log_total, grad_low, row_shift):
    score_scale = 1.0 / math.sqrt(q_rows.shape[-1])
    scores = level_scores(q_rows, k_rows)
    exact_soft = jnp.exp(scores - log_total.T[..., None])
    prob_grad = jnp.einsum("qhe,khe->hqk", grad_low, v_rows, preferred_element_type=jnp.float32)
    score_grad = (exact_soft * (prob_grad + row_shift.T[..., None]) * score_scale).astype(
        jnp.bfloat16
    )
    return (score_grad, exact_soft.astype(jnp.bfloat16))


def key_parts(score_grad, soft_low, q_rows, grad_low):
    k_part = jnp.einsum("hqk,qhe->khe", score_grad, q_rows, preferred_element_type=jnp.float32)
    v_part = jnp.einsum("hqk,qhe->khe", soft_low, grad_low, preferred_element_type=jnp.float32)
    return (k_part, v_part)


def query_part(score_grad, k_rows):
    return jnp.einsum("hqk,khe->qhe", score_grad, k_rows, preferred_element_type=jnp.float32)


def split_qkv(packed, head_count):
    width = head_count * HEAD_DIM
    shape = (packed.shape[0], head_count, HEAD_DIM)
    return tuple(packed[:, i * width : (i + 1) * width].reshape(shape) for i in range(3))


def split_wide(values):
    high = values.astype(jnp.bfloat16)
    low = (values - high.astype(jnp.float32)).astype(jnp.bfloat16)
    return high, low


def join_wide(high, low):
    return high.astype(jnp.float32) + low.astype(jnp.float32)


def pack_grads(grad_low, row_shift, width):
    rows = grad_low.shape[0]
    high, low = split_wide(row_shift)
    used = grad_low.shape[1] * grad_low.shape[2] + 2 * row_shift.shape[1]
    return jnp.concatenate(
        [grad_low.reshape(rows, -1), high, low, jnp.zeros((rows, width - used), jnp.bfloat16)], 1
    )


def unpack_grads(packed, head_count):
    width = head_count * HEAD_DIM
    grad_low = packed[:, :width].reshape(-1, head_count, HEAD_DIM)
    return grad_low, join_wide(
        packed[:, width : width + head_count], packed[:, width + head_count : width + 2 * head_count]
    )


def shards(queries, keys, values, grad_y, out_gain, offsets):
    tokens = queries.shape[1]
    flat_width = queries.shape[2]
    head_count = flat_width // HEAD_DIM
    row_shape = (tokens, head_count, HEAD_DIM)
    q_own = queries[0].reshape(row_shape)
    k_own = keys[0].reshape(row_shape)
    v_own = values[0].reshape(row_shape)
    ctx_size = lax.axis_size("ctx")
    mid_shift = offsets[0]
    top_shift = offsets[1]
    positions = jnp.arange(tokens, dtype=jnp.int32)
    mid_hit = (positions % R1)[:, None] == mid_shift[None, :]
    top_hit = (positions % ctx_size)[:, None] == top_shift[None, :]
    mid_pack = jnp.concatenate(
        [pick_rows(x, R1, mid_shift).reshape(-1, flat_width) for x in (q_own, k_own, v_own)], 1
    )
    top_pack = jnp.concatenate(
        [pick_rows(x, ctx_size, top_shift).reshape(-1, flat_width) for x in (q_own, k_own, v_own)],
        1,
    )
    mid_rows = mid_pack.shape[0]
    top_rows = top_pack.shape[0]
    mid_all, top_all = ctx_gather(mid_pack, lane_dense(top_pack), SPAN, 0)
    mid_all = mid_all.reshape(-1, mid_pack.shape[1])
    top_all = top_all.reshape(-1, top_pack.shape[1])
    mid_q, mid_k, mid_v = split_qkv(mid_all, head_count)
    top_q, top_k, top_v = split_qkv(top_all, head_count)
    base_out, base_total = attend(q_own, k_own, v_own)
    mid_out_all, mid_total_all = attend(mid_q, mid_k, mid_v)
    top_out_all, top_total_all = attend(top_q, top_k, top_v)
    mid_out = mid_out_all[:mid_rows]
    mid_total = mid_total_all[:mid_rows]
    top_out = top_out_all[:top_rows]
    top_total = top_total_all[:top_rows]
    mid_full = place_rows(mid_total[..., None], R1, mid_shift)[..., 0]
    top_full = place_rows(top_total[..., None], ctx_size, top_shift)[..., 0]
    row_max = jnp.maximum(base_total, jnp.where(mid_hit, mid_full, base_total))
    row_max = jnp.maximum(row_max, jnp.where(top_hit, top_full, base_total))
    base_expo = jnp.exp(base_total - row_max)
    mid_expo = jnp.where(mid_hit, jnp.exp(mid_full - row_max), 0.0)
    top_expo = jnp.where(top_hit, jnp.exp(top_full - row_max), 0.0)
    denom = base_expo + mid_expo + top_expo
    base_share = base_expo / denom
    mid_share = mid_expo / denom
    top_share = top_expo / denom
    attn = (
        base_share[..., None] * base_out
        + mid_share[..., None] * place_rows(mid_out, R1, mid_shift)
        + top_share[..., None] * place_rows(top_out, ctx_size, top_shift)
    )
    inv_rms = lax.rsqrt(jnp.mean(attn * attn, axis=-1, keepdims=True) + EPS)
    normed = attn * inv_rms
    gain_rows = out_gain.reshape(head_count, HEAD_DIM)
    attended = token_major(normed * gain_rows)
    grad_full = grad_y[0].reshape(row_shape).astype(jnp.float32)
    gain_part = jnp.sum(grad_full * normed, axis=0).reshape(flat_width)
    grad_norm = grad_full * gain_rows
    grad_attn = inv_rms * (
        grad_norm - normed * jnp.mean(grad_norm * normed, axis=-1, keepdims=True)
    )
    inner = jnp.sum(grad_attn * attn, axis=-1)
    base_low = (base_share[..., None] * grad_attn).astype(jnp.bfloat16)
    base_shift = -(base_share * inner)

    mid_sel = pick_rows(mid_share[..., None], R1, mid_shift)[..., 0]
    mid_low = (mid_sel[..., None] * pick_rows(grad_attn, R1, mid_shift)).astype(jnp.bfloat16)
    mid_row_shift = -(mid_sel * pick_rows(inner[..., None], R1, mid_shift)[..., 0])
    top_sel = pick_rows(top_share[..., None], ctx_size, top_shift)[..., 0]
    top_low = (top_sel[..., None] * pick_rows(grad_attn, ctx_size, top_shift)).astype(jnp.bfloat16)
    top_row_shift = -(top_sel * pick_rows(inner[..., None], ctx_size, top_shift)[..., 0])

    shift_high, shift_low = split_wide(top_row_shift.reshape(-1))
    top_flat = jnp.concatenate([top_low.reshape(-1), shift_high, shift_low])
    top_flat = jnp.pad(top_flat, (0, -top_flat.shape[0] % HEAD_DIM))
    base_inputs = (
        queries[0], keys[0], values[0], base_total, base_low.reshape(tokens, flat_width), base_shift
    )
    mid_gathered, gathered, gain_rows_sum, base_dq, base_dk, base_dv = ctx_gather(
        pack_grads(mid_low, mid_row_shift, flat_width + HEAD_DIM),
        lane_dense(top_flat),
        SPAN,
        1,
        sum_x=lane_dense(gain_part),
        base=base_inputs,
    )
    base_dq, base_dk, base_dv = (x.reshape(row_shape) for x in (base_dq, base_dk, base_dv))
    mid_low_all, mid_shift_all = unpack_grads(
        mid_gathered.reshape(-1, mid_gathered.shape[-1]), head_count
    )
    gathered = gathered.reshape(ctx_size, -1)
    grad_width = top_rows * flat_width
    top_low_all = gathered[:, :grad_width].reshape(-1, head_count, HEAD_DIM)
    gain_grad = jnp.sum(gain_rows_sum, axis=(0, 1)).reshape(flat_width)
    shift_count = top_rows * head_count
    top_shift_all = join_wide(
        gathered[:, grad_width : grad_width + shift_count],
        gathered[:, grad_width + shift_count : grad_width + 2 * shift_count],
    ).reshape(-1, head_count)

    mid_grad, mid_soft = score_grads(
        mid_q, mid_k, mid_v, mid_total_all, mid_low_all, mid_shift_all
    )
    mid_dq = query_part(mid_grad[:, :mid_rows], mid_k)
    mid_dk, mid_dv = key_parts(
        mid_grad[:, :, :mid_rows], mid_soft[:, :, :mid_rows], mid_q, mid_low_all
    )
    top_grad, top_soft = score_grads(
        top_q, top_k, top_v, top_total_all, top_low_all, top_shift_all
    )
    top_dq = query_part(top_grad[:, :top_rows], top_k)
    top_dk, top_dv = key_parts(
        top_grad[:, :, :top_rows], top_soft[:, :, :top_rows], top_q, top_low_all
    )
    query_grad = (
        base_dq + place_rows(mid_dq, R1, mid_shift) + place_rows(top_dq, ctx_size, top_shift)
    )
    key_grad = base_dk + place_rows(mid_dk, R1, mid_shift) + place_rows(top_dk, ctx_size, top_shift)
    value_grad = (
        base_dv + place_rows(mid_dv, R1, mid_shift) + place_rows(top_dv, ctx_size, top_shift)
    )
    return (
        attended,
        token_major(query_grad),
        token_major(key_grad),
        token_major(value_grad),
        gain_grad,
    )


def solution(mesh):
    in_specs = (
        P("dp", "ctx", "head"),
        P("dp", "ctx", "head"),
        P("dp", "ctx", "head"),
        P("dp", "ctx", "head"),
        P("head"),
        P(None, "head"),
    )
    out_specs = (
        P("dp", "ctx", "head"),
        P("dp", "ctx", "head"),
        P("dp", "ctx", "head"),
        P("dp", "ctx", "head"),
        P("head"),
    )
    return jax.shard_map(shards, mesh=mesh, in_specs=in_specs, out_specs=out_specs, check_vma=False)
```

```python
import functools
import math

import jax
import jax.numpy as jnp
from jax import lax
from jax.experimental import pallas as pl
from jax.experimental.pallas import tpu as pltpu
from jax.sharding import PartitionSpec as P

HEAD_DIM = 128
SPAN = 4
R1 = 8
RING = 8


EPS = 1e-06


def gather_kernel(group, inner, has_sum, *refs):
    if has_sum:
        (mid_x, top_y, top_z, sum_x, mid_out, out_y, out_z, sum_out,
         stage_y, stage_z, sum_stage, row_sum, *sems) = refs
    else:
        (mid_x, top_y, top_z, mid_out, out_y, out_z, stage_y, stage_z, *sems) = refs
    (send_mid, recv_mid, send_ay, recv_ay, send_by, recv_by,
     send_az, recv_az, send_bz, recv_bz, local_sem) = sems[:11]
    if has_sum:
        send_sa, recv_sa, send_sb, recv_sb = sems[11:]
    count = lax.axis_size("ctx")
    outer = count // inner
    me = lax.axis_index("ctx")
    row = lax.axis_index("dp")
    col = lax.axis_index("head")
    lo = me % inner
    hi = me // inner
    base = me - me % group
    mesh_ids = pl.DeviceIdType.MESH

    def inner_peer(j):
        return hi * inner + lax.rem(lo + j, inner)

    def outer_peer(j):
        return lax.rem(hi + j, outer) * inner + lo

    barrier = pltpu.get_barrier_semaphore()
    for j in range(1, inner):
        pl.semaphore_signal(barrier, 1, device_id=(row, inner_peer(j), col), device_id_type=mesh_ids)
    for j in range(1, outer):
        pl.semaphore_signal(barrier, 1, device_id=(row, outer_peer(j), col), device_id_type=mesh_ids)
    if has_sum:
        for j in range(outer):
            pl.semaphore_signal(
                barrier, 1, device_id=(1 - row, outer_peer(j), col), device_id_type=mesh_ids
            )
    pl.semaphore_wait(barrier, inner + outer - 2 + (outer if has_sum else 0))

    def remote(src, dst, send, recv, peer, core=None):
        return pltpu.make_async_remote_copy(
            src, dst, send, recv, device_id=(row if core is None else core, peer, col),
            device_id_type=mesh_ids,
        )

    def mid_copy(j):
        peer = base + lax.rem(me % group + j, group)
        return remote(mid_x, mid_out.at[j], send_mid.at[j], recv_mid.at[j], peer)

    def copy_ay(j):
        return remote(top_y, stage_y.at[j], send_ay.at[j], recv_ay.at[j], inner_peer(j))

    def copy_by(j):
        return remote(stage_y, out_y.at[j], send_by.at[j], recv_by.at[j], outer_peer(j))

    def copy_az(j):
        return remote(top_z, stage_z.at[j], send_az.at[j], recv_az.at[j], outer_peer(j))

    def copy_bz(j):
        return remote(stage_z, out_z.at[j], send_bz.at[j], recv_bz.at[j], inner_peer(j))

    def sum_a(j):
        return remote(sum_x, sum_stage.at[j], send_sa.at[j], recv_sa.at[j], inner_peer(j))

    def sum_b(c, j):
        slot = c * outer + j
        return remote(
            row_sum, sum_out.at[c, j], send_sb.at[slot], recv_sb.at[slot], outer_peer(j),
            core=(1 - row) if c else row,
        )

    sum_peers = [(0, j) for j in range(1, outer)] + [(1, j) for j in range(outer)]

    for j in range(1, inner):
        copy_ay(j).start()
    for j in range(1, outer):
        copy_az(j).start()
    if has_sum:
        for j in range(1, inner):
            sum_a(j).start()
    for j in range(1, group):
        mid_copy(j).start()
    own_y = pltpu.make_async_copy(top_y, stage_y.at[0], local_sem.at[0])
    own_z = pltpu.make_async_copy(top_z, stage_z.at[0], local_sem.at[1])
    own_y.start()
    own_z.start()
    mid_out[0] = mid_x[...]
    own_y.wait()
    own_z.wait()
    for j in range(1, inner):
        copy_ay(j).wait()
    if has_sum:
        total = sum_x[...]
        for j in range(1, inner):
            sum_a(j).wait()
            total = total + sum_stage[j]
        row_sum[...] = total
    for j in range(1, outer):
        copy_by(j).start()
    for j in range(1, outer):
        copy_az(j).wait()
    for j in range(1, inner):
        copy_bz(j).start()
    out_y[0] = stage_y[...]
    out_z[0] = stage_z[...]
    if has_sum:
        sum_out[0, 0] = total
        for c, j in sum_peers:
            sum_b(c, j).start()
    for j in range(1, group):
        mid_copy(j).wait()
    for j in range(1, outer):
        copy_by(j).wait()
    if has_sum:
        for c, j in sum_peers:
            sum_b(c, j).wait()
    for j in range(1, inner):
        copy_bz(j).wait()


def ctx_gather(mid_x, top_x, group, tag, sum_x=None):
    count = lax.axis_size("ctx")
    inner = RING
    outer = count // inner
    half = (top_x.shape[0] + 1) // 2
    top_y = top_x[:half]
    top_z = top_x[half:]
    has_sum = sum_x is not None
    operands = (mid_x, top_y, top_z) + ((sum_x,) if has_sum else ())
    out_shape = (
        jax.ShapeDtypeStruct((group,) + mid_x.shape, mid_x.dtype),
        jax.ShapeDtypeStruct((outer, inner) + top_y.shape, top_x.dtype),
        jax.ShapeDtypeStruct((inner, outer) + top_z.shape, top_x.dtype),
    )
    scratch = [
        pltpu.VMEM((inner,) + top_y.shape, top_x.dtype),
        pltpu.VMEM((outer,) + top_z.shape, top_x.dtype),
    ]
    if has_sum:
        out_shape += (jax.ShapeDtypeStruct((2, outer) + sum_x.shape, sum_x.dtype),)
        scratch += [
            pltpu.VMEM((inner,) + sum_x.shape, sum_x.dtype),
            pltpu.VMEM(sum_x.shape, sum_x.dtype),
        ]
    for size in (group, inner, outer, outer, inner):
        scratch += [pltpu.SemaphoreType.DMA((size,)), pltpu.SemaphoreType.DMA((size,))]
    scratch.append(pltpu.SemaphoreType.DMA((2,)))
    if has_sum:
        for size in (inner, 2 * outer):
            scratch += [pltpu.SemaphoreType.DMA((size,)), pltpu.SemaphoreType.DMA((size,))]
    outs = pl.pallas_call(
        functools.partial(gather_kernel, group, inner, has_sum),
        out_shape=out_shape,
        in_specs=[pl.BlockSpec(memory_space=pltpu.VMEM)] * len(operands),
        out_specs=(pl.BlockSpec(memory_space=pltpu.VMEM),) * len(out_shape),
        scratch_shapes=scratch,
        compiler_params=pltpu.CompilerParams(collective_id=tag, has_side_effects=True),
    )(*operands)
    top_all = jnp.concatenate([outs[1], jnp.transpose(outs[2], (1, 0, 2, 3))], 2)
    return (outs[0], top_all) + tuple(outs[3:])


def token_major(rows):
    parts = [rows[:, h, :] for h in range(rows.shape[1])]
    return jnp.concatenate(parts, axis=1).astype(jnp.bfloat16)[None]


def lane_dense(block):
    return block.reshape(-1, HEAD_DIM)


def pick_rows(source_rows, dilation, shifts):
    row_count, head_count, head_width = source_rows.shape
    grouped = source_rows.reshape(row_count // dilation, dilation, head_count, head_width)
    hit_mask = jnp.arange(dilation, dtype=jnp.int32).reshape(1, dilation, 1, 1) == shifts.reshape(
        1, 1, head_count, 1
    )
    chosen = jnp.where(hit_mask, grouped, jnp.zeros((), source_rows.dtype))
    return jnp.sum(chosen, axis=1, dtype=source_rows.dtype)


def place_rows(row_values, dilation, shifts):
    row_count, head_count, head_width = row_values.shape
    hit_mask = jnp.arange(dilation, dtype=jnp.int32).reshape(1, dilation, 1, 1) == shifts.reshape(
        1, 1, head_count, 1
    )
    spread = jnp.where(hit_mask, row_values[:, None], jnp.zeros((), row_values.dtype))
    return spread.reshape(row_count * dilation, head_count, head_width)


def level_scores(q_rows, k_rows):
    score_scale = 1.0 / math.sqrt(q_rows.shape[-1])
    return (
        jnp.einsum("qhe,khe->hqk", q_rows, k_rows, preferred_element_type=jnp.float32) * score_scale
    )


def attend(q_rows, k_rows, v_rows):
    scores = level_scores(q_rows, k_rows)
    row_max = jnp.max(scores, axis=-1, keepdims=True)
    log_total = row_max[..., 0] + jnp.log(jnp.sum(jnp.exp(scores - row_max), axis=-1))
    soft_rows = jnp.exp(scores - log_total[..., None]).astype(jnp.bfloat16)
    level_out = jnp.einsum("hqk,khe->qhe", soft_rows, v_rows, preferred_element_type=jnp.float32)
    return (level_out, log_total.T)


def score_grads(q_rows, k_rows, v_rows, log_total, grad_low, row_shift):
    score_scale = 1.0 / math.sqrt(q_rows.shape[-1])
    scores = level_scores(q_rows, k_rows)
    exact_soft = jnp.exp(scores - log_total.T[..., None])
    prob_grad = jnp.einsum("qhe,khe->hqk", grad_low, v_rows, preferred_element_type=jnp.float32)
    score_grad = (exact_soft * (prob_grad + row_shift.T[..., None]) * score_scale).astype(
        jnp.bfloat16
    )
    return (score_grad, exact_soft.astype(jnp.bfloat16))


def key_parts(score_grad, soft_low, q_rows, grad_low):
    k_part = jnp.einsum("hqk,qhe->khe", score_grad, q_rows, preferred_element_type=jnp.float32)
    v_part = jnp.einsum("hqk,qhe->khe", soft_low, grad_low, preferred_element_type=jnp.float32)
    return (k_part, v_part)


def query_part(score_grad, k_rows):
    return jnp.einsum("hqk,khe->qhe", score_grad, k_rows, preferred_element_type=jnp.float32)


def split_qkv(packed, head_count, parts=3):
    width = head_count * HEAD_DIM
    shape = (packed.shape[0], head_count, HEAD_DIM)
    return tuple(packed[:, i * width : (i + 1) * width].reshape(shape) for i in range(parts))


def log_totals(q_rows, k_rows):
    scores = level_scores(q_rows, k_rows)
    row_max = jnp.max(scores, axis=-1, keepdims=True)
    log_total = row_max[..., 0] + jnp.log(jnp.sum(jnp.exp(scores - row_max), axis=-1))
    return log_total.T


def split_wide(values):
    high = values.astype(jnp.bfloat16)
    low = (values - high.astype(jnp.float32)).astype(jnp.bfloat16)
    return high, low


def join_wide(high, low):
    return high.astype(jnp.float32) + low.astype(jnp.float32)


def pack_grads(grad_low, row_shift, width):
    rows = grad_low.shape[0]
    high, low = split_wide(row_shift)
    used = grad_low.shape[1] * grad_low.shape[2] + 2 * row_shift.shape[1]
    return jnp.concatenate(
        [grad_low.reshape(rows, -1), high, low, jnp.zeros((rows, width - used), jnp.bfloat16)], 1
    )


def unpack_grads(packed, head_count):
    width = head_count * HEAD_DIM
    grad_low = packed[:, :width].reshape(-1, head_count, HEAD_DIM)
    return grad_low, join_wide(
        packed[:, width : width + head_count], packed[:, width + head_count : width + 2 * head_count]
    )


def shards(queries, keys, values, grad_y, out_gain, offsets):
    tokens = queries.shape[1]
    flat_width = queries.shape[2]
    head_count = flat_width // HEAD_DIM
    row_shape = (tokens, head_count, HEAD_DIM)
    q_own = queries[0].reshape(row_shape)
    k_own = keys[0].reshape(row_shape)
    v_own = values[0].reshape(row_shape)
    ctx_size = lax.axis_size("ctx")
    mid_shift = offsets[0]
    top_shift = offsets[1]
    positions = jnp.arange(tokens, dtype=jnp.int32)
    mid_hit = (positions % R1)[:, None] == mid_shift[None, :]
    top_hit = (positions % ctx_size)[:, None] == top_shift[None, :]
    mid_pack = jnp.concatenate(
        [pick_rows(x, R1, mid_shift).reshape(-1, flat_width) for x in (q_own, k_own, v_own)], 1
    )
    top_q_own = pick_rows(q_own, ctx_size, top_shift)
    top_pack = jnp.concatenate(
        [pick_rows(x, ctx_size, top_shift).reshape(-1, flat_width) for x in (k_own, v_own)], 1
    )
    mid_rows = mid_pack.shape[0]
    top_rows = top_pack.shape[0]
    mid_all, top_all = ctx_gather(mid_pack, lane_dense(top_pack), SPAN, 0)
    mid_all = mid_all.reshape(-1, mid_pack.shape[1])
    top_all = top_all.reshape(-1, top_pack.shape[1])
    mid_q, mid_k, mid_v = split_qkv(mid_all, head_count)
    top_k, top_v = split_qkv(top_all, head_count, 2)
    base_out, base_total = attend(q_own, k_own, v_own)
    mid_out_all, mid_total_all = attend(mid_q, mid_k, mid_v)
    top_out, top_total = attend(top_q_own, top_k, top_v)
    mid_out = mid_out_all[:mid_rows]
    mid_total = mid_total_all[:mid_rows]
    mid_full = place_rows(mid_total[..., None], R1, mid_shift)[..., 0]
    top_full = place_rows(top_total[..., None], ctx_size, top_shift)[..., 0]
    row_max = jnp.maximum(base_total, jnp.where(mid_hit, mid_full, base_total))
    row_max = jnp.maximum(row_max, jnp.where(top_hit, top_full, base_total))
    base_expo = jnp.exp(base_total - row_max)
    mid_expo = jnp.where(mid_hit, jnp.exp(mid_full - row_max), 0.0)
    top_expo = jnp.where(top_hit, jnp.exp(top_full - row_max), 0.0)
    denom = base_expo + mid_expo + top_expo
    base_share = base_expo / denom
    mid_share = mid_expo / denom
    top_share = top_expo / denom
    attn = (
        base_share[..., None] * base_out
        + mid_share[..., None] * place_rows(mid_out, R1, mid_shift)
        + top_share[..., None] * place_rows(top_out, ctx_size, top_shift)
    )
    inv_rms = lax.rsqrt(jnp.mean(attn * attn, axis=-1, keepdims=True) + EPS)
    normed = attn * inv_rms
    gain_rows = out_gain.reshape(head_count, HEAD_DIM)
    attended = token_major(normed * gain_rows)
    grad_full = grad_y[0].reshape(row_shape).astype(jnp.float32)
    gain_part = jnp.sum(grad_full * normed, axis=0).reshape(flat_width)
    grad_norm = grad_full * gain_rows
    grad_attn = inv_rms * (
        grad_norm - normed * jnp.mean(grad_norm * normed, axis=-1, keepdims=True)
    )
    inner = jnp.sum(grad_attn * attn, axis=-1)
    base_low = (base_share[..., None] * grad_attn).astype(jnp.bfloat16)
    base_shift = -(base_share * inner)
    base_grad, base_soft = score_grads(q_own, k_own, v_own, base_total, base_low, base_shift)
    base_dq = query_part(base_grad, k_own)
    base_dk, base_dv = key_parts(base_grad, base_soft, q_own, base_low)

    mid_sel = pick_rows(mid_share[..., None], R1, mid_shift)[..., 0]
    mid_low = (mid_sel[..., None] * pick_rows(grad_attn, R1, mid_shift)).astype(jnp.bfloat16)
    mid_row_shift = -(mid_sel * pick_rows(inner[..., None], R1, mid_shift)[..., 0])
    top_sel = pick_rows(top_share[..., None], ctx_size, top_shift)[..., 0]
    top_low = (top_sel[..., None] * pick_rows(grad_attn, ctx_size, top_shift)).astype(jnp.bfloat16)
    top_row_shift = -(top_sel * pick_rows(inner[..., None], ctx_size, top_shift)[..., 0])

    shift_high, shift_low = split_wide(top_row_shift.reshape(-1))
    top_flat = jnp.concatenate(
        [top_q_own.reshape(-1), top_low.reshape(-1), shift_high, shift_low]
    )
    top_flat = jnp.pad(top_flat, (0, -top_flat.shape[0] % HEAD_DIM))
    mid_gathered, gathered, gain_rows_sum = ctx_gather(
        pack_grads(mid_low, mid_row_shift, flat_width + HEAD_DIM),
        lane_dense(top_flat),
        SPAN,
        1,
        sum_x=lane_dense(gain_part),
    )
    mid_low_all, mid_shift_all = unpack_grads(
        mid_gathered.reshape(-1, mid_gathered.shape[-1]), head_count
    )
    gathered = gathered.reshape(ctx_size, -1)
    q_width = top_rows * flat_width
    top_q = gathered[:, :q_width].reshape(-1, head_count, HEAD_DIM)
    grad_width = 2 * q_width
    top_low_all = gathered[:, q_width:grad_width].reshape(-1, head_count, HEAD_DIM)
    top_total_all = log_totals(top_q, top_k)
    gain_grad = jnp.sum(gain_rows_sum, axis=(0, 1)).reshape(flat_width)
    shift_count = top_rows * head_count
    top_shift_all = join_wide(
        gathered[:, grad_width : grad_width + shift_count],
        gathered[:, grad_width + shift_count : grad_width + 2 * shift_count],
    ).reshape(-1, head_count)

    mid_grad, mid_soft = score_grads(
        mid_q, mid_k, mid_v, mid_total_all, mid_low_all, mid_shift_all
    )
    mid_dq = query_part(mid_grad[:, :mid_rows], mid_k)
    mid_dk, mid_dv = key_parts(
        mid_grad[:, :, :mid_rows], mid_soft[:, :, :mid_rows], mid_q, mid_low_all
    )
    top_grad, top_soft = score_grads(
        top_q, top_k, top_v, top_total_all, top_low_all, top_shift_all
    )
    top_dq = query_part(top_grad[:, :top_rows], top_k)
    top_dk, top_dv = key_parts(
        top_grad[:, :, :top_rows], top_soft[:, :, :top_rows], top_q, top_low_all
    )
    query_grad = (
        base_dq + place_rows(mid_dq, R1, mid_shift) + place_rows(top_dq, ctx_size, top_shift)
    )
    key_grad = base_dk + place_rows(mid_dk, R1, mid_shift) + place_rows(top_dk, ctx_size, top_shift)
    value_grad = (
        base_dv + place_rows(mid_dv, R1, mid_shift) + place_rows(top_dv, ctx_size, top_shift)
    )
    return (
        attended,
        token_major(query_grad),
        token_major(key_grad),
        token_major(value_grad),
        gain_grad,
    )


def solution(mesh):
    in_specs = (
        P("dp", "ctx", "head"),
        P("dp", "ctx", "head"),
        P("dp", "ctx", "head"),
        P("dp", "ctx", "head"),
        P("head"),
        P(None, "head"),
    )
    out_specs = (
        P("dp", "ctx", "head"),
        P("dp", "ctx", "head"),
        P("dp", "ctx", "head"),
        P("dp", "ctx", "head"),
        P("head"),
    )
    return jax.shard_map(shards, mesh=mesh, in_specs=in_specs, out_specs=out_specs, check_vma=False)
```

```python
import functools
import math

import jax
import jax.numpy as jnp
from jax import lax
from jax.experimental import pallas as pl
from jax.experimental.pallas import tpu as pltpu
from jax.sharding import PartitionSpec as P

HEAD_DIM = 128
SPAN = 4
R1 = 8
RING = 8


EPS = 1e-06


def gather_kernel(group, inner, has_sum, *refs):
    if has_sum:
        (mid_x, top_y, top_z, sum_x, mid_out, out_y, out_z, sum_total,
         stage_y, stage_z, sum_stage, row_sum, sum_out, *sems) = refs
    else:
        (mid_x, top_y, top_z, mid_out, out_y, out_z, stage_y, stage_z, *sems) = refs
    (send_mid, recv_mid, send_ay, recv_ay, send_by, recv_by,
     send_az, recv_az, send_bz, recv_bz, local_sem) = sems[:11]
    if has_sum:
        send_sa, recv_sa, send_sb, recv_sb = sems[11:]
    count = lax.axis_size("ctx")
    outer = count // inner
    me = lax.axis_index("ctx")
    row = lax.axis_index("dp")
    col = lax.axis_index("head")
    lo = me % inner
    hi = me // inner
    base = me - me % group
    mesh_ids = pl.DeviceIdType.MESH

    def inner_peer(j):
        return hi * inner + lax.rem(lo + j, inner)

    def outer_peer(j):
        return lax.rem(hi + j, outer) * inner + lo

    barrier = pltpu.get_barrier_semaphore()
    for j in range(1, inner):
        pl.semaphore_signal(barrier, 1, device_id=(row, inner_peer(j), col), device_id_type=mesh_ids)
    for j in range(1, outer):
        pl.semaphore_signal(barrier, 1, device_id=(row, outer_peer(j), col), device_id_type=mesh_ids)
    if has_sum:
        for j in range(outer):
            pl.semaphore_signal(
                barrier, 1, device_id=(1 - row, outer_peer(j), col), device_id_type=mesh_ids
            )
    pl.semaphore_wait(barrier, inner + outer - 2 + (outer if has_sum else 0))

    def remote(src, dst, send, recv, peer, core=None):
        return pltpu.make_async_remote_copy(
            src, dst, send, recv, device_id=(row if core is None else core, peer, col),
            device_id_type=mesh_ids,
        )

    def mid_copy(j):
        peer = base + lax.rem(me % group + j, group)
        return remote(mid_x, mid_out.at[j], send_mid.at[j], recv_mid.at[j], peer)

    def copy_ay(j):
        return remote(top_y, stage_y.at[j], send_ay.at[j], recv_ay.at[j], inner_peer(j))

    def copy_by(j):
        return remote(stage_y, out_y.at[j], send_by.at[j], recv_by.at[j], outer_peer(j))

    def copy_az(j):
        return remote(top_z, stage_z.at[j], send_az.at[j], recv_az.at[j], outer_peer(j))

    def copy_bz(j):
        return remote(stage_z, out_z.at[j], send_bz.at[j], recv_bz.at[j], inner_peer(j))

    def sum_a(j):
        return remote(sum_x, sum_stage.at[j], send_sa.at[j], recv_sa.at[j], inner_peer(j))

    def sum_b(c, j):
        slot = c * outer + j
        return remote(
            row_sum, sum_out.at[c, j], send_sb.at[slot], recv_sb.at[slot], outer_peer(j),
            core=(1 - row) if c else row,
        )

    sum_peers = [(0, j) for j in range(1, outer)] + [(1, j) for j in range(outer)]

    for j in range(1, inner):
        copy_ay(j).start()
    for j in range(1, outer):
        copy_az(j).start()
    if has_sum:
        for j in range(1, inner):
            sum_a(j).start()
    for j in range(1, group):
        mid_copy(j).start()
    own_y = pltpu.make_async_copy(top_y, stage_y.at[0], local_sem.at[0])
    own_z = pltpu.make_async_copy(top_z, stage_z.at[0], local_sem.at[1])
    own_y.start()
    own_z.start()
    mid_out[0] = mid_x[...]
    own_y.wait()
    own_z.wait()
    for j in range(1, inner):
        copy_ay(j).wait()
    if has_sum:
        total = sum_x[...]
        for j in range(1, inner):
            sum_a(j).wait()
            total = total + sum_stage[j]
        row_sum[...] = total
    for j in range(1, outer):
        copy_by(j).start()
    for j in range(1, outer):
        copy_az(j).wait()
    for j in range(1, inner):
        copy_bz(j).start()
    out_y[0] = stage_y[...]
    out_z[0] = stage_z[...]
    if has_sum:
        sum_out[0, 0] = total
        for c, j in sum_peers:
            sum_b(c, j).start()
    for j in range(1, group):
        mid_copy(j).wait()
    for j in range(1, outer):
        copy_by(j).wait()
    if has_sum:
        for c, j in sum_peers:
            sum_b(c, j).wait()
    for j in range(1, inner):
        copy_bz(j).wait()
    if has_sum:
        total = sum_out[0, 0]
        for c, j in sum_peers:
            total = total + sum_out[c, j]
        sum_total[...] = total


def ctx_gather(mid_x, top_x, group, tag, sum_x=None):
    count = lax.axis_size("ctx")
    inner = RING
    outer = count // inner
    half = (top_x.shape[0] + 1) // 2
    top_y = top_x[:half]
    top_z = top_x[half:]
    has_sum = sum_x is not None
    operands = (mid_x, top_y, top_z) + ((sum_x,) if has_sum else ())
    out_shape = (
        jax.ShapeDtypeStruct((group,) + mid_x.shape, mid_x.dtype),
        jax.ShapeDtypeStruct((outer, inner) + top_y.shape, top_x.dtype),
        jax.ShapeDtypeStruct((inner, outer) + top_z.shape, top_x.dtype),
    )
    scratch = [
        pltpu.VMEM((inner,) + top_y.shape, top_x.dtype),
        pltpu.VMEM((outer,) + top_z.shape, top_x.dtype),
    ]
    if has_sum:
        out_shape += (jax.ShapeDtypeStruct(sum_x.shape, sum_x.dtype),)
        scratch += [
            pltpu.VMEM((inner,) + sum_x.shape, sum_x.dtype),
            pltpu.VMEM(sum_x.shape, sum_x.dtype),
            pltpu.VMEM((2, outer) + sum_x.shape, sum_x.dtype),
        ]
    for size in (group, inner, outer, outer, inner):
        scratch += [pltpu.SemaphoreType.DMA((size,)), pltpu.SemaphoreType.DMA((size,))]
    scratch.append(pltpu.SemaphoreType.DMA((2,)))
    if has_sum:
        for size in (inner, 2 * outer):
            scratch += [pltpu.SemaphoreType.DMA((size,)), pltpu.SemaphoreType.DMA((size,))]
    outs = pl.pallas_call(
        functools.partial(gather_kernel, group, inner, has_sum),
        out_shape=out_shape,
        in_specs=[pl.BlockSpec(memory_space=pltpu.VMEM)] * len(operands),
        out_specs=(pl.BlockSpec(memory_space=pltpu.VMEM),) * len(out_shape),
        scratch_shapes=scratch,
        compiler_params=pltpu.CompilerParams(collective_id=tag, has_side_effects=True),
    )(*operands)
    top_all = jnp.concatenate([outs[1], jnp.transpose(outs[2], (1, 0, 2, 3))], 2)
    return (outs[0], top_all) + tuple(outs[3:])


def token_major(rows):
    parts = [rows[:, h, :] for h in range(rows.shape[1])]
    return jnp.concatenate(parts, axis=1).astype(jnp.bfloat16)[None]


def lane_dense(block):
    return block.reshape(-1, HEAD_DIM)


def pick_rows(source_rows, dilation, shifts):
    row_count, head_count, head_width = source_rows.shape
    grouped = source_rows.reshape(row_count // dilation, dilation, head_count, head_width)
    hit_mask = jnp.arange(dilation, dtype=jnp.int32).reshape(1, dilation, 1, 1) == shifts.reshape(
        1, 1, head_count, 1
    )
    chosen = jnp.where(hit_mask, grouped, jnp.zeros((), source_rows.dtype))
    return jnp.sum(chosen, axis=1, dtype=source_rows.dtype)


def place_rows(row_values, dilation, shifts):
    row_count, head_count, head_width = row_values.shape
    hit_mask = jnp.arange(dilation, dtype=jnp.int32).reshape(1, dilation, 1, 1) == shifts.reshape(
        1, 1, head_count, 1
    )
    spread = jnp.where(hit_mask, row_values[:, None], jnp.zeros((), row_values.dtype))
    return spread.reshape(row_count * dilation, head_count, head_width)


def level_scores(q_rows, k_rows):
    score_scale = 1.0 / math.sqrt(q_rows.shape[-1])
    return (
        jnp.einsum("qhe,khe->hqk", q_rows, k_rows, preferred_element_type=jnp.float32) * score_scale
    )


def attend(q_rows, k_rows, v_rows):
    scores = level_scores(q_rows, k_rows)
    row_max = jnp.max(scores, axis=-1, keepdims=True)
    log_total = row_max[..., 0] + jnp.log(jnp.sum(jnp.exp(scores - row_max), axis=-1))
    soft_rows = jnp.exp(scores - log_total[..., None]).astype(jnp.bfloat16)
    level_out = jnp.einsum("hqk,khe->qhe", soft_rows, v_rows, preferred_element_type=jnp.float32)
    return (level_out, log_total.T)


def score_grads(q_rows, k_rows, v_rows, log_total, grad_low, row_shift):
    score_scale = 1.0 / math.sqrt(q_rows.shape[-1])
    scores = level_scores(q_rows, k_rows)
    exact_soft = jnp.exp(scores - log_total.T[..., None])
    prob_grad = jnp.einsum("qhe,khe->hqk", grad_low, v_rows, preferred_element_type=jnp.float32)
    score_grad = (exact_soft * (prob_grad + row_shift.T[..., None]) * score_scale).astype(
        jnp.bfloat16
    )
    return (score_grad, exact_soft.astype(jnp.bfloat16))


def key_parts(score_grad, soft_low, q_rows, grad_low):
    k_part = jnp.einsum("hqk,qhe->khe", score_grad, q_rows, preferred_element_type=jnp.float32)
    v_part = jnp.einsum("hqk,qhe->khe", soft_low, grad_low, preferred_element_type=jnp.float32)
    return (k_part, v_part)


def query_part(score_grad, k_rows):
    return jnp.einsum("hqk,khe->qhe", score_grad, k_rows, preferred_element_type=jnp.float32)


def split_qkv(packed, head_count):
    width = head_count * HEAD_DIM
    shape = (packed.shape[0], head_count, HEAD_DIM)
    return tuple(packed[:, i * width : (i + 1) * width].reshape(shape) for i in range(3))


def split_wide(values):
    high = values.astype(jnp.bfloat16)
    low = (values - high.astype(jnp.float32)).astype(jnp.bfloat16)
    return high, low


def join_wide(high, low):
    return high.astype(jnp.float32) + low.astype(jnp.float32)


def pack_grads(grad_low, row_shift, width):
    rows = grad_low.shape[0]
    high, low = split_wide(row_shift)
    used = grad_low.shape[1] * grad_low.shape[2] + 2 * row_shift.shape[1]
    return jnp.concatenate(
        [grad_low.reshape(rows, -1), high, low, jnp.zeros((rows, width - used), jnp.bfloat16)], 1
    )


def unpack_grads(packed, head_count):
    width = head_count * HEAD_DIM
    grad_low = packed[:, :width].reshape(-1, head_count, HEAD_DIM)
    return grad_low, join_wide(
        packed[:, width : width + head_count], packed[:, width + head_count : width + 2 * head_count]
    )


def shards(queries, keys, values, grad_y, out_gain, offsets):
    tokens = queries.shape[1]
    flat_width = queries.shape[2]
    head_count = flat_width // HEAD_DIM
    row_shape = (tokens, head_count, HEAD_DIM)
    q_own = queries[0].reshape(row_shape)
    k_own = keys[0].reshape(row_shape)
    v_own = values[0].reshape(row_shape)
    ctx_size = lax.axis_size("ctx")
    mid_shift = offsets[0]
    top_shift = offsets[1]
    positions = jnp.arange(tokens, dtype=jnp.int32)
    mid_hit = (positions % R1)[:, None] == mid_shift[None, :]
    top_hit = (positions % ctx_size)[:, None] == top_shift[None, :]
    mid_pack = jnp.concatenate(
        [pick_rows(x, R1, mid_shift).reshape(-1, flat_width) for x in (q_own, k_own, v_own)], 1
    )
    top_pack = jnp.concatenate(
        [pick_rows(x, ctx_size, top_shift).reshape(-1, flat_width) for x in (q_own, k_own, v_own)],
        1,
    )
    mid_rows = mid_pack.shape[0]
    top_rows = top_pack.shape[0]
    mid_all, top_all = ctx_gather(mid_pack, lane_dense(top_pack), SPAN, 0)
    mid_all = mid_all.reshape(-1, mid_pack.shape[1])
    top_all = top_all.reshape(-1, top_pack.shape[1])
    mid_q, mid_k, mid_v = split_qkv(mid_all, head_count)
    top_q, top_k, top_v = split_qkv(top_all, head_count)
    base_out, base_total = attend(q_own, k_own, v_own)
    mid_out_all, mid_total_all = attend(mid_q, mid_k, mid_v)
    top_out_all, top_total_all = attend(top_q, top_k, top_v)
    mid_out = mid_out_all[:mid_rows]
    mid_total = mid_total_all[:mid_rows]
    top_out = top_out_all[:top_rows]
    top_total = top_total_all[:top_rows]
    mid_full = place_rows(mid_total[..., None], R1, mid_shift)[..., 0]
    top_full = place_rows(top_total[..., None], ctx_size, top_shift)[..., 0]
    row_max = jnp.maximum(base_total, jnp.where(mid_hit, mid_full, base_total))
    row_max = jnp.maximum(row_max, jnp.where(top_hit, top_full, base_total))
    base_expo = jnp.exp(base_total - row_max)
    mid_expo = jnp.where(mid_hit, jnp.exp(mid_full - row_max), 0.0)
    top_expo = jnp.where(top_hit, jnp.exp(top_full - row_max), 0.0)
    denom = base_expo + mid_expo + top_expo
    base_share = base_expo / denom
    mid_share = mid_expo / denom
    top_share = top_expo / denom
    attn = (
        base_share[..., None] * base_out
        + mid_share[..., None] * place_rows(mid_out, R1, mid_shift)
        + top_share[..., None] * place_rows(top_out, ctx_size, top_shift)
    )
    inv_rms = lax.rsqrt(jnp.mean(attn * attn, axis=-1, keepdims=True) + EPS)
    normed = attn * inv_rms
    gain_rows = out_gain.reshape(head_count, HEAD_DIM)
    attended = token_major(normed * gain_rows)
    grad_full = grad_y[0].reshape(row_shape).astype(jnp.float32)
    gain_part = jnp.sum(grad_full * normed, axis=0).reshape(flat_width)
    grad_norm = grad_full * gain_rows
    grad_attn = inv_rms * (
        grad_norm - normed * jnp.mean(grad_norm * normed, axis=-1, keepdims=True)
    )
    inner = jnp.sum(grad_attn * attn, axis=-1)
    base_low = (base_share[..., None] * grad_attn).astype(jnp.bfloat16)
    base_shift = -(base_share * inner)
    base_grad, base_soft = score_grads(q_own, k_own, v_own, base_total, base_low, base_shift)
    base_dq = query_part(base_grad, k_own)
    base_dk, base_dv = key_parts(base_grad, base_soft, q_own, base_low)

    mid_sel = pick_rows(mid_share[..., None], R1, mid_shift)[..., 0]
    mid_low = (mid_sel[..., None] * pick_rows(grad_attn, R1, mid_shift)).astype(jnp.bfloat16)
    mid_row_shift = -(mid_sel * pick_rows(inner[..., None], R1, mid_shift)[..., 0])
    top_sel = pick_rows(top_share[..., None], ctx_size, top_shift)[..., 0]
    top_low = (top_sel[..., None] * pick_rows(grad_attn, ctx_size, top_shift)).astype(jnp.bfloat16)
    top_row_shift = -(top_sel * pick_rows(inner[..., None], ctx_size, top_shift)[..., 0])

    shift_high, shift_low = split_wide(top_row_shift.reshape(-1))
    top_flat = jnp.concatenate([top_low.reshape(-1), shift_high, shift_low])
    top_flat = jnp.pad(top_flat, (0, -top_flat.shape[0] % HEAD_DIM))
    mid_gathered, gathered, gain_rows_sum = ctx_gather(
        pack_grads(mid_low, mid_row_shift, flat_width + HEAD_DIM),
        lane_dense(top_flat),
        SPAN,
        1,
        sum_x=lane_dense(gain_part),
    )
    mid_low_all, mid_shift_all = unpack_grads(
        mid_gathered.reshape(-1, mid_gathered.shape[-1]), head_count
    )
    gathered = gathered.reshape(ctx_size, -1)
    grad_width = top_rows * flat_width
    top_low_all = gathered[:, :grad_width].reshape(-1, head_count, HEAD_DIM)
    gain_grad = gain_rows_sum.reshape(flat_width)
    shift_count = top_rows * head_count
    top_shift_all = join_wide(
        gathered[:, grad_width : grad_width + shift_count],
        gathered[:, grad_width + shift_count : grad_width + 2 * shift_count],
    ).reshape(-1, head_count)

    mid_grad, mid_soft = score_grads(
        mid_q, mid_k, mid_v, mid_total_all, mid_low_all, mid_shift_all
    )
    mid_dq = query_part(mid_grad[:, :mid_rows], mid_k)
    mid_dk, mid_dv = key_parts(
        mid_grad[:, :, :mid_rows], mid_soft[:, :, :mid_rows], mid_q, mid_low_all
    )
    top_grad, top_soft = score_grads(
        top_q, top_k, top_v, top_total_all, top_low_all, top_shift_all
    )
    top_dq = query_part(top_grad[:, :top_rows], top_k)
    top_dk, top_dv = key_parts(
        top_grad[:, :, :top_rows], top_soft[:, :, :top_rows], top_q, top_low_all
    )
    query_grad = (
        base_dq + place_rows(mid_dq, R1, mid_shift) + place_rows(top_dq, ctx_size, top_shift)
    )
    key_grad = base_dk + place_rows(mid_dk, R1, mid_shift) + place_rows(top_dk, ctx_size, top_shift)
    value_grad = (
        base_dv + place_rows(mid_dv, R1, mid_shift) + place_rows(top_dv, ctx_size, top_shift)
    )
    return (
        attended,
        token_major(query_grad),
        token_major(key_grad),
        token_major(value_grad),
        gain_grad,
    )


def solution(mesh):
    in_specs = (
        P("dp", "ctx", "head"),
        P("dp", "ctx", "head"),
        P("dp", "ctx", "head"),
        P("dp", "ctx", "head"),
        P("head"),
        P(None, "head"),
    )
    out_specs = (
        P("dp", "ctx", "head"),
        P("dp", "ctx", "head"),
        P("dp", "ctx", "head"),
        P("dp", "ctx", "head"),
        P("head"),
    )
    return jax.shard_map(shards, mesh=mesh, in_specs=in_specs, out_specs=out_specs, check_vma=False)
```

```python
import functools
import math

import jax
import jax.numpy as jnp
from jax import lax
from jax.experimental import pallas as pl
from jax.experimental.pallas import tpu as pltpu
from jax.sharding import PartitionSpec as P

HEAD_DIM = 128
SPAN = 4
R1 = 8
RING = 8


EPS = 1e-06


def gather_kernel(group, inner, has_sum, *refs):
    if has_sum:
        (mid_x, top_y, top_z, sum_x, mid_out, out_y, out_z, sum_total,
         stage_y, stage_z, sum_stage, row_sum, sum_out, *sems) = refs
    else:
        (mid_x, top_y, top_z, mid_out, out_y, out_z, stage_y, stage_z, *sems) = refs
    (send_mid, recv_mid, send_ay, recv_ay, send_by, recv_by,
     send_az, recv_az, send_bz, recv_bz, local_sem) = sems[:11]
    if has_sum:
        send_sa, recv_sa, send_sb, recv_sb = sems[11:]
    count = lax.axis_size("ctx")
    outer = count // inner
    me = lax.axis_index("ctx")
    row = lax.axis_index("dp")
    col = lax.axis_index("head")
    lo = me % inner
    hi = me // inner
    base = me - me % group
    mesh_ids = pl.DeviceIdType.MESH

    def inner_peer(j):
        return hi * inner + lax.rem(lo + j, inner)

    def outer_peer(j):
        return lax.rem(hi + j, outer) * inner + lo

    barrier = pltpu.get_barrier_semaphore()
    for j in range(1, inner):
        pl.semaphore_signal(barrier, 1, device_id=(row, inner_peer(j), col), device_id_type=mesh_ids)
    for j in range(1, outer):
        pl.semaphore_signal(barrier, 1, device_id=(row, outer_peer(j), col), device_id_type=mesh_ids)
    if has_sum:
        for j in range(outer):
            pl.semaphore_signal(
                barrier, 1, device_id=(1 - row, outer_peer(j), col), device_id_type=mesh_ids
            )
    pl.semaphore_wait(barrier, inner + outer - 2 + (outer if has_sum else 0))

    def remote(src, dst, send, recv, peer, core=None):
        return pltpu.make_async_remote_copy(
            src, dst, send, recv, device_id=(row if core is None else core, peer, col),
            device_id_type=mesh_ids,
        )

    def mid_copy(j):
        peer = base + lax.rem(me % group + j, group)
        return remote(mid_x, mid_out.at[j], send_mid.at[j], recv_mid.at[j], peer)

    def copy_ay(j):
        return remote(top_y, stage_y.at[j], send_ay.at[j], recv_ay.at[j], inner_peer(j))

    def copy_by(j):
        return remote(stage_y, out_y.at[j], send_by.at[j], recv_by.at[j], outer_peer(j))

    def copy_az(j):
        return remote(top_z, stage_z.at[j], send_az.at[j], recv_az.at[j], outer_peer(j))

    def copy_bz(j):
        return remote(stage_z, out_z.at[j], send_bz.at[j], recv_bz.at[j], inner_peer(j))

    def sum_a(j):
        return remote(sum_x, sum_stage.at[j], send_sa.at[j], recv_sa.at[j], inner_peer(j))

    def sum_b(c, j):
        slot = c * outer + j
        return remote(
            row_sum, sum_out.at[c, j], send_sb.at[slot], recv_sb.at[slot], outer_peer(j),
            core=(1 - row) if c else row,
        )

    sum_peers = [(0, j) for j in range(1, outer)] + [(1, j) for j in range(outer)]

    for j in range(1, inner):
        copy_ay(j).start()
    for j in range(1, outer):
        copy_az(j).start()
    if has_sum:
        for j in range(1, inner):
            sum_a(j).start()
    for j in range(1, group):
        mid_copy(j).start()
    own_y = pltpu.make_async_copy(top_y, stage_y.at[0], local_sem.at[0])
    own_z = pltpu.make_async_copy(top_z, stage_z.at[0], local_sem.at[1])
    own_y.start()
    own_z.start()
    mid_out[0] = mid_x[...]
    own_y.wait()
    own_z.wait()
    for j in range(1, inner):
        copy_ay(j).wait()
    if has_sum:
        total = sum_x[...]
        for j in range(1, inner):
            sum_a(j).wait()
            total = total + sum_stage[j]
        row_sum[...] = total
    for j in range(1, outer):
        copy_by(j).start()
    for j in range(1, outer):
        copy_az(j).wait()
    for j in range(1, inner):
        copy_bz(j).start()
    out_y[0] = stage_y[...]
    out_z[0] = stage_z[...]
    if has_sum:
        sum_out[0, 0] = total
        for c, j in sum_peers:
            sum_b(c, j).start()
    for j in range(1, group):
        mid_copy(j).wait()
    for j in range(1, outer):
        copy_by(j).wait()
    if has_sum:
        for c, j in sum_peers:
            sum_b(c, j).wait()
    for j in range(1, inner):
        copy_bz(j).wait()
    if has_sum:
        total = sum_out[0, 0]
        for c, j in sum_peers:
            total = total + sum_out[c, j]
        sum_total[...] = total


def ctx_gather(mid_x, top_x, group, tag, sum_x=None, raw=False):
    count = lax.axis_size("ctx")
    inner = RING
    outer = count // inner
    half = (top_x.shape[0] + 1) // 2
    top_y = top_x[:half]
    top_z = top_x[half:]
    has_sum = sum_x is not None
    operands = (mid_x, top_y, top_z) + ((sum_x,) if has_sum else ())
    out_shape = (
        jax.ShapeDtypeStruct((group,) + mid_x.shape, mid_x.dtype),
        jax.ShapeDtypeStruct((outer, inner) + top_y.shape, top_x.dtype),
        jax.ShapeDtypeStruct((inner, outer) + top_z.shape, top_x.dtype),
    )
    scratch = [
        pltpu.VMEM((inner,) + top_y.shape, top_x.dtype),
        pltpu.VMEM((outer,) + top_z.shape, top_x.dtype),
    ]
    if has_sum:
        out_shape += (jax.ShapeDtypeStruct(sum_x.shape, sum_x.dtype),)
        scratch += [
            pltpu.VMEM((inner,) + sum_x.shape, sum_x.dtype),
            pltpu.VMEM(sum_x.shape, sum_x.dtype),
            pltpu.VMEM((2, outer) + sum_x.shape, sum_x.dtype),
        ]
    for size in (group, inner, outer, outer, inner):
        scratch += [pltpu.SemaphoreType.DMA((size,)), pltpu.SemaphoreType.DMA((size,))]
    scratch.append(pltpu.SemaphoreType.DMA((2,)))
    if has_sum:
        for size in (inner, 2 * outer):
            scratch += [pltpu.SemaphoreType.DMA((size,)), pltpu.SemaphoreType.DMA((size,))]
    outs = pl.pallas_call(
        functools.partial(gather_kernel, group, inner, has_sum),
        out_shape=out_shape,
        in_specs=[pl.BlockSpec(memory_space=pltpu.VMEM)] * len(operands),
        out_specs=(pl.BlockSpec(memory_space=pltpu.VMEM),) * len(out_shape),
        scratch_shapes=scratch,
        compiler_params=pltpu.CompilerParams(collective_id=tag, has_side_effects=True),
    )(*operands)
    if raw:
        return outs
    top_all = jnp.concatenate([outs[1], jnp.transpose(outs[2], (1, 0, 2, 3))], 2)
    return (outs[0], top_all) + tuple(outs[3:])


def token_major(rows):
    parts = [rows[:, h, :] for h in range(rows.shape[1])]
    return jnp.concatenate(parts, axis=1).astype(jnp.bfloat16)[None]


def lane_dense(block):
    return block.reshape(-1, HEAD_DIM)


def pick_rows(source_rows, dilation, shifts):
    row_count, head_count, head_width = source_rows.shape
    grouped = source_rows.reshape(row_count // dilation, dilation, head_count, head_width)
    hit_mask = jnp.arange(dilation, dtype=jnp.int32).reshape(1, dilation, 1, 1) == shifts.reshape(
        1, 1, head_count, 1
    )
    chosen = jnp.where(hit_mask, grouped, jnp.zeros((), source_rows.dtype))
    return jnp.sum(chosen, axis=1, dtype=source_rows.dtype)


def place_rows(row_values, dilation, shifts):
    row_count, head_count, head_width = row_values.shape
    hit_mask = jnp.arange(dilation, dtype=jnp.int32).reshape(1, dilation, 1, 1) == shifts.reshape(
        1, 1, head_count, 1
    )
    spread = jnp.where(hit_mask, row_values[:, None], jnp.zeros((), row_values.dtype))
    return spread.reshape(row_count * dilation, head_count, head_width)


def level_scores(q_rows, k_rows):
    score_scale = 1.0 / math.sqrt(q_rows.shape[-1])
    return (
        jnp.einsum("qhe,khe->hqk", q_rows, k_rows, preferred_element_type=jnp.float32) * score_scale
    )


def attend(q_rows, k_rows, v_rows):
    scores = level_scores(q_rows, k_rows)
    row_max = jnp.max(scores, axis=-1, keepdims=True)
    log_total = row_max[..., 0] + jnp.log(jnp.sum(jnp.exp(scores - row_max), axis=-1))
    soft_rows = jnp.exp(scores - log_total[..., None]).astype(jnp.bfloat16)
    level_out = jnp.einsum("hqk,khe->qhe", soft_rows, v_rows, preferred_element_type=jnp.float32)
    return (level_out, log_total.T)


def score_grads(q_rows, k_rows, v_rows, log_total, grad_low, row_shift):
    score_scale = 1.0 / math.sqrt(q_rows.shape[-1])
    scores = level_scores(q_rows, k_rows)
    exact_soft = jnp.exp(scores - log_total.T[..., None])
    prob_grad = jnp.einsum("qhe,khe->hqk", grad_low, v_rows, preferred_element_type=jnp.float32)
    score_grad = (exact_soft * (prob_grad + row_shift.T[..., None]) * score_scale).astype(
        jnp.bfloat16
    )
    return (score_grad, exact_soft.astype(jnp.bfloat16))


def key_parts(score_grad, soft_low, q_rows, grad_low):
    k_part = jnp.einsum("hqk,qhe->khe", score_grad, q_rows, preferred_element_type=jnp.float32)
    v_part = jnp.einsum("hqk,qhe->khe", soft_low, grad_low, preferred_element_type=jnp.float32)
    return (k_part, v_part)


def query_part(score_grad, k_rows):
    return jnp.einsum("hqk,khe->qhe", score_grad, k_rows, preferred_element_type=jnp.float32)


def split_qkv(packed, head_count):
    width = head_count * HEAD_DIM
    shape = (packed.shape[0], head_count, HEAD_DIM)
    return tuple(packed[:, i * width : (i + 1) * width].reshape(shape) for i in range(3))


def split_wide(values):
    high = values.astype(jnp.bfloat16)
    low = (values - high.astype(jnp.float32)).astype(jnp.bfloat16)
    return high, low


def join_wide(high, low):
    return high.astype(jnp.float32) + low.astype(jnp.float32)


def pack_grads(grad_low, row_shift, width):
    rows = grad_low.shape[0]
    high, low = split_wide(row_shift)
    used = grad_low.shape[1] * grad_low.shape[2] + 2 * row_shift.shape[1]
    return jnp.concatenate(
        [grad_low.reshape(rows, -1), high, low, jnp.zeros((rows, width - used), jnp.bfloat16)], 1
    )


def unpack_grads(packed, head_count):
    width = head_count * HEAD_DIM
    grad_low = packed[:, :width].reshape(-1, head_count, HEAD_DIM)
    return grad_low, join_wide(
        packed[:, width : width + head_count], packed[:, width + head_count : width + 2 * head_count]
    )


def shards(queries, keys, values, grad_y, out_gain, offsets):
    tokens = queries.shape[1]
    flat_width = queries.shape[2]
    head_count = flat_width // HEAD_DIM
    row_shape = (tokens, head_count, HEAD_DIM)
    q_own = queries[0].reshape(row_shape)
    k_own = keys[0].reshape(row_shape)
    v_own = values[0].reshape(row_shape)
    ctx_size = lax.axis_size("ctx")
    mid_shift = offsets[0]
    top_shift = offsets[1]
    positions = jnp.arange(tokens, dtype=jnp.int32)
    mid_hit = (positions % R1)[:, None] == mid_shift[None, :]
    top_hit = (positions % ctx_size)[:, None] == top_shift[None, :]
    mid_pack = jnp.concatenate(
        [pick_rows(x, R1, mid_shift).reshape(-1, flat_width) for x in (q_own, k_own, v_own)], 1
    )
    top_blocks = jnp.concatenate(
        [pick_rows(x, ctx_size, top_shift) for x in (q_own, k_own, v_own)], 1
    )
    top_pack = jnp.pad(top_blocks, ((0, 0), (0, 16 - top_blocks.shape[1]), (0, 0)))
    mid_rows = mid_pack.shape[0]
    top_rows = top_pack.shape[0]
    mid_all, rows_y, rows_z = ctx_gather(mid_pack, lane_dense(top_pack), SPAN, 0, raw=True)
    mid_all = mid_all.reshape(-1, mid_pack.shape[1])
    mid_q, mid_k, mid_v = split_qkv(mid_all, head_count)
    rows_y = rows_y.reshape((ctx_size,) + rows_y.shape[2:])
    rows_z = jnp.transpose(rows_z, (1, 0, 2, 3)).reshape((ctx_size,) + rows_z.shape[2:])
    top_q, top_k, top_v = (
        jnp.stack(
            [rows_y[:, p * head_count : (p + 1) * head_count],
             rows_z[:, p * head_count : (p + 1) * head_count]], 1
        ).reshape(-1, head_count, HEAD_DIM)
        for p in range(3)
    )
    base_out, base_total = attend(q_own, k_own, v_own)
    mid_out_all, mid_total_all = attend(mid_q, mid_k, mid_v)
    top_out_all, top_total_all = attend(top_q, top_k, top_v)
    mid_out = mid_out_all[:mid_rows]
    mid_total = mid_total_all[:mid_rows]
    top_out = top_out_all[:top_rows]
    top_total = top_total_all[:top_rows]
    mid_full = place_rows(mid_total[..., None], R1, mid_shift)[..., 0]
    top_full = place_rows(top_total[..., None], ctx_size, top_shift)[..., 0]
    row_max = jnp.maximum(base_total, jnp.where(mid_hit, mid_full, base_total))
    row_max = jnp.maximum(row_max, jnp.where(top_hit, top_full, base_total))
    base_expo = jnp.exp(base_total - row_max)
    mid_expo = jnp.where(mid_hit, jnp.exp(mid_full - row_max), 0.0)
    top_expo = jnp.where(top_hit, jnp.exp(top_full - row_max), 0.0)
    denom = base_expo + mid_expo + top_expo
    base_share = base_expo / denom
    mid_share = mid_expo / denom
    top_share = top_expo / denom
    attn = (
        base_share[..., None] * base_out
        + mid_share[..., None] * place_rows(mid_out, R1, mid_shift)
        + top_share[..., None] * place_rows(top_out, ctx_size, top_shift)
    )
    inv_rms = lax.rsqrt(jnp.mean(attn * attn, axis=-1, keepdims=True) + EPS)
    normed = attn * inv_rms
    gain_rows = out_gain.reshape(head_count, HEAD_DIM)
    attended = token_major(normed * gain_rows)
    grad_full = grad_y[0].reshape(row_shape).astype(jnp.float32)
    gain_part = jnp.sum(grad_full * normed, axis=0).reshape(flat_width)
    grad_norm = grad_full * gain_rows
    grad_attn = inv_rms * (
        grad_norm - normed * jnp.mean(grad_norm * normed, axis=-1, keepdims=True)
    )
    inner = jnp.sum(grad_attn * attn, axis=-1)
    base_low = (base_share[..., None] * grad_attn).astype(jnp.bfloat16)
    base_shift = -(base_share * inner)
    base_grad, base_soft = score_grads(q_own, k_own, v_own, base_total, base_low, base_shift)
    base_dq = query_part(base_grad, k_own)
    base_dk, base_dv = key_parts(base_grad, base_soft, q_own, base_low)

    mid_sel = pick_rows(mid_share[..., None], R1, mid_shift)[..., 0]
    mid_low = (mid_sel[..., None] * pick_rows(grad_attn, R1, mid_shift)).astype(jnp.bfloat16)
    mid_row_shift = -(mid_sel * pick_rows(inner[..., None], R1, mid_shift)[..., 0])
    top_sel = pick_rows(top_share[..., None], ctx_size, top_shift)[..., 0]
    top_low = (top_sel[..., None] * pick_rows(grad_attn, ctx_size, top_shift)).astype(jnp.bfloat16)
    top_row_shift = -(top_sel * pick_rows(inner[..., None], ctx_size, top_shift)[..., 0])

    shift_high, shift_low = split_wide(top_row_shift.reshape(-1))
    top_flat = jnp.concatenate([top_low.reshape(-1), shift_high, shift_low])
    top_flat = jnp.pad(top_flat, (0, -top_flat.shape[0] % HEAD_DIM))
    mid_gathered, gathered, gain_rows_sum = ctx_gather(
        pack_grads(mid_low, mid_row_shift, flat_width + HEAD_DIM),
        lane_dense(top_flat),
        SPAN,
        1,
        sum_x=lane_dense(gain_part),
    )
    mid_low_all, mid_shift_all = unpack_grads(
        mid_gathered.reshape(-1, mid_gathered.shape[-1]), head_count
    )
    gathered = gathered.reshape(ctx_size, -1)
    grad_width = top_rows * flat_width
    top_low_all = gathered[:, :grad_width].reshape(-1, head_count, HEAD_DIM)
    gain_grad = gain_rows_sum.reshape(flat_width)
    shift_count = top_rows * head_count
    top_shift_all = join_wide(
        gathered[:, grad_width : grad_width + shift_count],
        gathered[:, grad_width + shift_count : grad_width + 2 * shift_count],
    ).reshape(-1, head_count)

    mid_grad, mid_soft = score_grads(
        mid_q, mid_k, mid_v, mid_total_all, mid_low_all, mid_shift_all
    )
    mid_dq = query_part(mid_grad[:, :mid_rows], mid_k)
    mid_dk, mid_dv = key_parts(
        mid_grad[:, :, :mid_rows], mid_soft[:, :, :mid_rows], mid_q, mid_low_all
    )
    top_grad, top_soft = score_grads(
        top_q, top_k, top_v, top_total_all, top_low_all, top_shift_all
    )
    top_dq = query_part(top_grad[:, :top_rows], top_k)
    top_dk, top_dv = key_parts(
        top_grad[:, :, :top_rows], top_soft[:, :, :top_rows], top_q, top_low_all
    )
    query_grad = (
        base_dq + place_rows(mid_dq, R1, mid_shift) + place_rows(top_dq, ctx_size, top_shift)
    )
    key_grad = base_dk + place_rows(mid_dk, R1, mid_shift) + place_rows(top_dk, ctx_size, top_shift)
    value_grad = (
        base_dv + place_rows(mid_dv, R1, mid_shift) + place_rows(top_dv, ctx_size, top_shift)
    )
    return (
        attended,
        token_major(query_grad),
        token_major(key_grad),
        token_major(value_grad),
        gain_grad,
    )


def solution(mesh):
    in_specs = (
        P("dp", "ctx", "head"),
        P("dp", "ctx", "head"),
        P("dp", "ctx", "head"),
        P("dp", "ctx", "head"),
        P("head"),
        P(None, "head"),
    )
    out_specs = (
        P("dp", "ctx", "head"),
        P("dp", "ctx", "head"),
        P("dp", "ctx", "head"),
        P("dp", "ctx", "head"),
        P("head"),
    )
    return jax.shard_map(shards, mesh=mesh, in_specs=in_specs, out_specs=out_specs, check_vma=False)
```

```python
import functools
import math

import jax
import jax.numpy as jnp
from jax import lax
from jax.experimental import pallas as pl
from jax.experimental.pallas import tpu as pltpu
from jax.sharding import PartitionSpec as P

HEAD_DIM = 128
SPAN = 4
R1 = 8
RING = 8


EPS = 1e-06


def gather_kernel(group, inner, has_sum, *refs):
    if has_sum:
        (mid_x, top_y, top_z, sum_x, mid_out, out_y, out_z, sum_total,
         stage_y, stage_z, sum_stage, row_sum, sum_out, *sems) = refs
    else:
        (mid_x, top_y, top_z, mid_out, out_y, out_z, stage_y, stage_z, *sems) = refs
    (send_mid, recv_mid, send_ay, recv_ay, send_by, recv_by,
     send_az, recv_az, send_bz, recv_bz, local_sem) = sems[:11]
    if has_sum:
        send_sa, recv_sa, send_sb, recv_sb = sems[11:]
    count = lax.axis_size("ctx")
    outer = count // inner
    me = lax.axis_index("ctx")
    row = lax.axis_index("dp")
    col = lax.axis_index("head")
    lo = me % inner
    hi = me // inner
    base = me - me % group
    mesh_ids = pl.DeviceIdType.MESH

    def inner_peer(j):
        return hi * inner + lax.rem(lo + j, inner)

    def outer_peer(j):
        return lax.rem(hi + j, outer) * inner + lo

    barrier = pltpu.get_barrier_semaphore()
    for j in range(1, inner):
        pl.semaphore_signal(barrier, 1, device_id=(row, inner_peer(j), col), device_id_type=mesh_ids)
    for j in range(1, outer):
        pl.semaphore_signal(barrier, 1, device_id=(row, outer_peer(j), col), device_id_type=mesh_ids)
    if has_sum:
        for j in range(outer):
            pl.semaphore_signal(
                barrier, 1, device_id=(1 - row, outer_peer(j), col), device_id_type=mesh_ids
            )
    pl.semaphore_wait(barrier, inner + outer - 2 + (outer if has_sum else 0))

    def remote(src, dst, send, recv, peer, core=None):
        return pltpu.make_async_remote_copy(
            src, dst, send, recv, device_id=(row if core is None else core, peer, col),
            device_id_type=mesh_ids,
        )

    def mid_copy(j):
        peer = base + lax.rem(me % group + j, group)
        return remote(mid_x, mid_out.at[j], send_mid.at[j], recv_mid.at[j], peer)

    def copy_ay(j):
        return remote(top_y, stage_y.at[j], send_ay.at[j], recv_ay.at[j], inner_peer(j))

    def copy_by(j):
        return remote(stage_y, out_y.at[j], send_by.at[j], recv_by.at[j], outer_peer(j))

    def copy_az(j):
        return remote(top_z, stage_z.at[j], send_az.at[j], recv_az.at[j], outer_peer(j))

    def copy_bz(j):
        return remote(stage_z, out_z.at[j], send_bz.at[j], recv_bz.at[j], inner_peer(j))

    def sum_a(j):
        return remote(sum_x, sum_stage.at[j], send_sa.at[j], recv_sa.at[j], inner_peer(j))

    def sum_b(c, j):
        slot = c * outer + j
        return remote(
            row_sum, sum_out.at[c, j], send_sb.at[slot], recv_sb.at[slot], outer_peer(j),
            core=(1 - row) if c else row,
        )

    sum_peers = [(0, j) for j in range(1, outer)] + [(1, j) for j in range(outer)]

    for j in range(1, inner):
        copy_ay(j).start()
    for j in range(1, outer):
        copy_az(j).start()
    if has_sum:
        for j in range(1, inner):
            sum_a(j).start()
    for j in range(1, group):
        mid_copy(j).start()
    own_y = pltpu.make_async_copy(top_y, stage_y.at[0], local_sem.at[0])
    own_z = pltpu.make_async_copy(top_z, stage_z.at[0], local_sem.at[1])
    own_y.start()
    own_z.start()
    mid_out[0] = mid_x[...]
    own_y.wait()
    own_z.wait()
    for j in range(1, inner):
        copy_ay(j).wait()
    if has_sum:
        total = sum_x[...]
        for j in range(1, inner):
            sum_a(j).wait()
            total = total + sum_stage[j]
        row_sum[...] = total
    for j in range(1, outer):
        copy_by(j).start()
    for j in range(1, outer):
        copy_az(j).wait()
    for j in range(1, inner):
        copy_bz(j).start()
    out_y[0] = stage_y[...]
    out_z[0] = stage_z[...]
    if has_sum:
        sum_out[0, 0] = total
        for c, j in sum_peers:
            sum_b(c, j).start()
    for j in range(1, group):
        mid_copy(j).wait()
    for j in range(1, outer):
        copy_by(j).wait()
    if has_sum:
        for c, j in sum_peers:
            sum_b(c, j).wait()
    for j in range(1, inner):
        copy_bz(j).wait()
    if has_sum:
        total = sum_out[0, 0]
        for c, j in sum_peers:
            total = total + sum_out[c, j]
        sum_total[...] = total


def ctx_gather(mid_x, top_x, group, tag, sum_x=None, raw=False):
    count = lax.axis_size("ctx")
    inner = RING
    outer = count // inner
    half = (top_x.shape[0] + 1) // 2
    top_y = top_x[:half]
    top_z = top_x[half:]
    has_sum = sum_x is not None
    operands = (mid_x, top_y, top_z) + ((sum_x,) if has_sum else ())
    out_shape = (
        jax.ShapeDtypeStruct((group,) + mid_x.shape, mid_x.dtype),
        jax.ShapeDtypeStruct((outer, inner) + top_y.shape, top_x.dtype),
        jax.ShapeDtypeStruct((inner, outer) + top_z.shape, top_x.dtype),
    )
    scratch = [
        pltpu.VMEM((inner,) + top_y.shape, top_x.dtype),
        pltpu.VMEM((outer,) + top_z.shape, top_x.dtype),
    ]
    if has_sum:
        out_shape += (jax.ShapeDtypeStruct(sum_x.shape, sum_x.dtype),)
        scratch += [
            pltpu.VMEM((inner,) + sum_x.shape, sum_x.dtype),
            pltpu.VMEM(sum_x.shape, sum_x.dtype),
            pltpu.VMEM((2, outer) + sum_x.shape, sum_x.dtype),
        ]
    for size in (group, inner, outer, outer, inner):
        scratch += [pltpu.SemaphoreType.DMA((size,)), pltpu.SemaphoreType.DMA((size,))]
    scratch.append(pltpu.SemaphoreType.DMA((2,)))
    if has_sum:
        for size in (inner, 2 * outer):
            scratch += [pltpu.SemaphoreType.DMA((size,)), pltpu.SemaphoreType.DMA((size,))]
    outs = pl.pallas_call(
        functools.partial(gather_kernel, group, inner, has_sum),
        out_shape=out_shape,
        in_specs=[pl.BlockSpec(memory_space=pltpu.VMEM)] * len(operands),
        out_specs=(pl.BlockSpec(memory_space=pltpu.VMEM),) * len(out_shape),
        scratch_shapes=scratch,
        compiler_params=pltpu.CompilerParams(collective_id=tag, has_side_effects=True),
    )(*operands)
    if raw:
        return outs
    top_all = jnp.concatenate([outs[1], jnp.transpose(outs[2], (1, 0, 2, 3))], 2)
    return (outs[0], top_all) + tuple(outs[3:])


def token_major(rows):
    parts = [rows[:, h, :] for h in range(rows.shape[1])]
    return jnp.concatenate(parts, axis=1).astype(jnp.bfloat16)[None]


def lane_dense(block):
    return block.reshape(-1, HEAD_DIM)


def pick_rows(source_rows, dilation, shifts):
    row_count, head_count, head_width = source_rows.shape
    grouped = source_rows.reshape(row_count // dilation, dilation, head_count, head_width)
    hit_mask = jnp.arange(dilation, dtype=jnp.int32).reshape(1, dilation, 1, 1) == shifts.reshape(
        1, 1, head_count, 1
    )
    chosen = jnp.where(hit_mask, grouped, jnp.zeros((), source_rows.dtype))
    return jnp.sum(chosen, axis=1, dtype=source_rows.dtype)


def place_rows(row_values, dilation, shifts):
    row_count, head_count, head_width = row_values.shape
    hit_mask = jnp.arange(dilation, dtype=jnp.int32).reshape(1, dilation, 1, 1) == shifts.reshape(
        1, 1, head_count, 1
    )
    spread = jnp.where(hit_mask, row_values[:, None], jnp.zeros((), row_values.dtype))
    return spread.reshape(row_count * dilation, head_count, head_width)


def level_scores(q_rows, k_rows):
    score_scale = 1.0 / math.sqrt(q_rows.shape[-1])
    return (
        jnp.einsum("qhe,khe->hqk", q_rows, k_rows, preferred_element_type=jnp.float32) * score_scale
    )


def attend(q_rows, k_rows, v_rows):
    scores = level_scores(q_rows, k_rows)
    row_max = jnp.max(scores, axis=-1, keepdims=True)
    log_total = row_max[..., 0] + jnp.log(jnp.sum(jnp.exp(scores - row_max), axis=-1))
    soft_rows = jnp.exp(scores - log_total[..., None]).astype(jnp.bfloat16)
    level_out = jnp.einsum("hqk,khe->qhe", soft_rows, v_rows, preferred_element_type=jnp.float32)
    return (level_out, log_total.T)


def score_grads(q_rows, k_rows, v_rows, log_total, grad_low, row_shift):
    score_scale = 1.0 / math.sqrt(q_rows.shape[-1])
    scores = level_scores(q_rows, k_rows)
    exact_soft = jnp.exp(scores - log_total.T[..., None])
    prob_grad = jnp.einsum("qhe,khe->hqk", grad_low, v_rows, preferred_element_type=jnp.float32)
    score_grad = (exact_soft * (prob_grad + row_shift.T[..., None]) * score_scale).astype(
        jnp.bfloat16
    )
    return (score_grad, exact_soft.astype(jnp.bfloat16))


def key_parts(score_grad, soft_low, q_rows, grad_low):
    k_part = jnp.einsum("hqk,qhe->khe", score_grad, q_rows, preferred_element_type=jnp.float32)
    v_part = jnp.einsum("hqk,qhe->khe", soft_low, grad_low, preferred_element_type=jnp.float32)
    return (k_part, v_part)


def query_part(score_grad, k_rows):
    return jnp.einsum("hqk,khe->qhe", score_grad, k_rows, preferred_element_type=jnp.float32)


def split_qkv(packed, head_count):
    width = head_count * HEAD_DIM
    shape = (packed.shape[0], head_count, HEAD_DIM)
    return tuple(packed[:, i * width : (i + 1) * width].reshape(shape) for i in range(3))


def split_wide(values):
    high = values.astype(jnp.bfloat16)
    low = (values - high.astype(jnp.float32)).astype(jnp.bfloat16)
    return high, low


def join_wide(high, low):
    return high.astype(jnp.float32) + low.astype(jnp.float32)


def pack_grads(grad_low, row_shift, width):
    rows = grad_low.shape[0]
    high, low = split_wide(row_shift)
    used = grad_low.shape[1] * grad_low.shape[2] + 2 * row_shift.shape[1]
    return jnp.concatenate(
        [grad_low.reshape(rows, -1), high, low, jnp.zeros((rows, width - used), jnp.bfloat16)], 1
    )


def unpack_grads(packed, head_count):
    width = head_count * HEAD_DIM
    grad_low = packed[:, :width].reshape(-1, head_count, HEAD_DIM)
    return grad_low, join_wide(
        packed[:, width : width + head_count], packed[:, width + head_count : width + 2 * head_count]
    )


def shards(queries, keys, values, grad_y, out_gain, offsets):
    tokens = queries.shape[1]
    flat_width = queries.shape[2]
    head_count = flat_width // HEAD_DIM
    row_shape = (tokens, head_count, HEAD_DIM)
    q_own = queries[0].reshape(row_shape)
    k_own = keys[0].reshape(row_shape)
    v_own = values[0].reshape(row_shape)
    ctx_size = lax.axis_size("ctx")
    mid_shift = offsets[0]
    top_shift = offsets[1]
    positions = jnp.arange(tokens, dtype=jnp.int32)
    mid_hit = (positions % R1)[:, None] == mid_shift[None, :]
    top_hit = (positions % ctx_size)[:, None] == top_shift[None, :]
    mid_pack = jnp.concatenate(
        [pick_rows(x, R1, mid_shift).reshape(-1, flat_width) for x in (q_own, k_own, v_own)], 1
    )
    top_blocks = jnp.concatenate(
        [pick_rows(x, ctx_size, top_shift) for x in (q_own, k_own, v_own)], 1
    )
    top_pack = jnp.pad(top_blocks, ((0, 0), (0, 16 - top_blocks.shape[1]), (0, 0)))
    mid_rows = mid_pack.shape[0]
    top_rows = top_pack.shape[0]
    mid_all, rows_y, rows_z = ctx_gather(mid_pack, lane_dense(top_pack), SPAN, 0, raw=True)
    mid_all = mid_all.reshape(-1, mid_pack.shape[1])
    mid_q, mid_k, mid_v = split_qkv(mid_all, head_count)
    rows_y = rows_y.reshape((ctx_size,) + rows_y.shape[2:])
    rows_z = jnp.transpose(rows_z, (1, 0, 2, 3)).reshape((ctx_size,) + rows_z.shape[2:])
    top_q, top_k, top_v = (
        jnp.stack(
            [rows_y[:, p * head_count : (p + 1) * head_count],
             rows_z[:, p * head_count : (p + 1) * head_count]], 1
        ).reshape(-1, head_count, HEAD_DIM)
        for p in range(3)
    )
    base_out, base_total = attend(q_own, k_own, v_own)
    mid_out_all, mid_total_all = attend(mid_q, mid_k, mid_v)
    top_out_all, top_total_all = attend(top_q, top_k, top_v)
    mid_out = mid_out_all[:mid_rows]
    mid_total = mid_total_all[:mid_rows]
    top_out = top_out_all[:top_rows]
    top_total = top_total_all[:top_rows]
    mid_full = place_rows(mid_total[..., None], R1, mid_shift)[..., 0]
    top_full = place_rows(top_total[..., None], ctx_size, top_shift)[..., 0]
    row_max = jnp.maximum(base_total, jnp.where(mid_hit, mid_full, base_total))
    row_max = jnp.maximum(row_max, jnp.where(top_hit, top_full, base_total))
    base_expo = jnp.exp(base_total - row_max)
    mid_expo = jnp.where(mid_hit, jnp.exp(mid_full - row_max), 0.0)
    top_expo = jnp.where(top_hit, jnp.exp(top_full - row_max), 0.0)
    denom = base_expo + mid_expo + top_expo
    base_share = base_expo / denom
    mid_share = mid_expo / denom
    top_share = top_expo / denom
    attn = (
        base_share[..., None] * base_out
        + mid_share[..., None] * place_rows(mid_out, R1, mid_shift)
        + top_share[..., None] * place_rows(top_out, ctx_size, top_shift)
    )
    inv_rms = lax.rsqrt(jnp.mean(attn * attn, axis=-1, keepdims=True) + EPS)
    normed = attn * inv_rms
    gain_rows = out_gain.reshape(head_count, HEAD_DIM)
    attended = token_major(normed * gain_rows)
    grad_full = grad_y[0].reshape(row_shape).astype(jnp.float32)
    gain_part = jnp.sum(grad_full * normed, axis=0).reshape(flat_width)
    grad_norm = grad_full * gain_rows
    grad_attn = inv_rms * (
        grad_norm - normed * jnp.mean(grad_norm * normed, axis=-1, keepdims=True)
    )
    inner = jnp.sum(grad_attn * attn, axis=-1)
    base_low = (base_share[..., None] * grad_attn).astype(jnp.bfloat16)
    base_shift = -(base_share * inner)
    base_grad, base_soft = score_grads(q_own, k_own, v_own, base_total, base_low, base_shift)
    base_dq = query_part(base_grad, k_own)
    base_dk, base_dv = key_parts(base_grad, base_soft, q_own, base_low)

    mid_sel = pick_rows(mid_share[..., None], R1, mid_shift)[..., 0]
    mid_low = (mid_sel[..., None] * pick_rows(grad_attn, R1, mid_shift)).astype(jnp.bfloat16)
    mid_row_shift = -(mid_sel * pick_rows(inner[..., None], R1, mid_shift)[..., 0])
    top_sel = pick_rows(top_share[..., None], ctx_size, top_shift)[..., 0]
    top_low = (top_sel[..., None] * pick_rows(grad_attn, ctx_size, top_shift)).astype(jnp.bfloat16)
    top_row_shift = -(top_sel * pick_rows(inner[..., None], ctx_size, top_shift)[..., 0])

    shift_high, shift_low = split_wide(top_row_shift)
    shift_block = jnp.concatenate([shift_high, shift_low], 1)
    shift_block = jnp.pad(shift_block, ((0, 0), (0, HEAD_DIM - shift_block.shape[1])))[:, None]
    top_block = jnp.concatenate([top_low, shift_block], 1)
    mid_gathered, grads_y, grads_z, gain_rows_sum = ctx_gather(
        pack_grads(mid_low, mid_row_shift, flat_width + HEAD_DIM),
        lane_dense(top_block),
        SPAN,
        1,
        sum_x=lane_dense(gain_part),
        raw=True,
    )
    mid_low_all, mid_shift_all = unpack_grads(
        mid_gathered.reshape(-1, mid_gathered.shape[-1]), head_count
    )
    grads_y = grads_y.reshape((ctx_size,) + grads_y.shape[2:])
    grads_z = jnp.transpose(grads_z, (1, 0, 2, 3)).reshape((ctx_size,) + grads_z.shape[2:])
    both = jnp.stack([grads_y, grads_z], 1).reshape((-1,) + grads_y.shape[1:])
    top_low_all = both[:, :head_count]
    top_shift_all = join_wide(
        both[:, head_count, :head_count], both[:, head_count, head_count : 2 * head_count]
    )
    gain_grad = gain_rows_sum.reshape(flat_width)

    mid_grad, mid_soft = score_grads(
        mid_q, mid_k, mid_v, mid_total_all, mid_low_all, mid_shift_all
    )
    mid_dq = query_part(mid_grad[:, :mid_rows], mid_k)
    mid_dk, mid_dv = key_parts(
        mid_grad[:, :, :mid_rows], mid_soft[:, :, :mid_rows], mid_q, mid_low_all
    )
    top_grad, top_soft = score_grads(
        top_q, top_k, top_v, top_total_all, top_low_all, top_shift_all
    )
    top_dq = query_part(top_grad[:, :top_rows], top_k)
    top_dk, top_dv = key_parts(
        top_grad[:, :, :top_rows], top_soft[:, :, :top_rows], top_q, top_low_all
    )
    query_grad = (
        base_dq + place_rows(mid_dq, R1, mid_shift) + place_rows(top_dq, ctx_size, top_shift)
    )
    key_grad = base_dk + place_rows(mid_dk, R1, mid_shift) + place_rows(top_dk, ctx_size, top_shift)
    value_grad = (
        base_dv + place_rows(mid_dv, R1, mid_shift) + place_rows(top_dv, ctx_size, top_shift)
    )
    return (
        attended,
        token_major(query_grad),
        token_major(key_grad),
        token_major(value_grad),
        gain_grad,
    )


def solution(mesh):
    in_specs = (
        P("dp", "ctx", "head"),
        P("dp", "ctx", "head"),
        P("dp", "ctx", "head"),
        P("dp", "ctx", "head"),
        P("head"),
        P(None, "head"),
    )
    out_specs = (
        P("dp", "ctx", "head"),
        P("dp", "ctx", "head"),
        P("dp", "ctx", "head"),
        P("dp", "ctx", "head"),
        P("head"),
    )
    return jax.shard_map(shards, mesh=mesh, in_specs=in_specs, out_specs=out_specs, check_vma=False)
```

```python
import functools
import math

import jax
import jax.numpy as jnp
from jax import lax
from jax.experimental import pallas as pl
from jax.experimental.pallas import tpu as pltpu
from jax.sharding import PartitionSpec as P

HEAD_DIM = 128
SPAN = 4
R1 = 8
RING = 8


EPS = 1e-06


def gather_kernel(group, inner, has_sum, *refs):
    if has_sum:
        (mid_x, top_y, top_z, sum_x, mid_out, out_y, out_z, sum_total,
         stage_y, stage_z, sum_stage, row_sum, sum_out, *sems) = refs
    else:
        (mid_x, top_y, top_z, mid_out, out_y, out_z, stage_y, stage_z, *sems) = refs
    (send_mid, recv_mid, send_ay, recv_ay, send_by, recv_by,
     send_az, recv_az, send_bz, recv_bz, local_sem) = sems[:11]
    if has_sum:
        send_sa, recv_sa, send_sb, recv_sb = sems[11:]
    count = lax.axis_size("ctx")
    outer = count // inner
    me = lax.axis_index("ctx")
    row = lax.axis_index("dp")
    col = lax.axis_index("head")
    lo = me % inner
    hi = me // inner
    base = me - me % group
    mesh_ids = pl.DeviceIdType.MESH

    def inner_peer(j):
        return hi * inner + lax.rem(lo + j, inner)

    def outer_peer(j):
        return lax.rem(hi + j, outer) * inner + lo

    barrier = pltpu.get_barrier_semaphore()
    for j in range(1, inner):
        pl.semaphore_signal(barrier, 1, device_id=(row, inner_peer(j), col), device_id_type=mesh_ids)
    for j in range(1, outer):
        pl.semaphore_signal(barrier, 1, device_id=(row, outer_peer(j), col), device_id_type=mesh_ids)
    if has_sum:
        for j in range(outer):
            pl.semaphore_signal(
                barrier, 1, device_id=(1 - row, outer_peer(j), col), device_id_type=mesh_ids
            )
    pl.semaphore_wait(barrier, inner + outer - 2 + (outer if has_sum else 0))

    def remote(src, dst, send, recv, peer, core=None):
        return pltpu.make_async_remote_copy(
            src, dst, send, recv, device_id=(row if core is None else core, peer, col),
            device_id_type=mesh_ids,
        )

    def mid_copy(j):
        peer = base + lax.rem(me % group + j, group)
        return remote(mid_x, mid_out.at[j], send_mid.at[j], recv_mid.at[j], peer)

    def copy_ay(j):
        return remote(top_y, stage_y.at[j], send_ay.at[j], recv_ay.at[j], inner_peer(j))

    def copy_by(j):
        return remote(stage_y, out_y.at[j], send_by.at[j], recv_by.at[j], outer_peer(j))

    def copy_az(j):
        return remote(top_z, stage_z.at[j], send_az.at[j], recv_az.at[j], outer_peer(j))

    def copy_bz(j):
        return remote(stage_z, out_z.at[j], send_bz.at[j], recv_bz.at[j], inner_peer(j))

    def sum_a(j):
        return remote(sum_x, sum_stage.at[j], send_sa.at[j], recv_sa.at[j], inner_peer(j))

    def sum_b(c, j):
        slot = c * outer + j
        return remote(
            row_sum, sum_out.at[c, j], send_sb.at[slot], recv_sb.at[slot], outer_peer(j),
            core=(1 - row) if c else row,
        )

    sum_peers = [(0, j) for j in range(1, outer)] + [(1, j) for j in range(outer)]

    for j in range(1, inner):
        copy_ay(j).start()
    for j in range(1, outer):
        copy_az(j).start()
    if has_sum:
        for j in range(1, inner):
            sum_a(j).start()
    for j in range(1, group):
        mid_copy(j).start()
    own_y = pltpu.make_async_copy(top_y, stage_y.at[0], local_sem.at[0])
    own_z = pltpu.make_async_copy(top_z, stage_z.at[0], local_sem.at[1])
    own_y.start()
    own_z.start()
    mid_out[0] = mid_x[...]
    own_y.wait()
    own_z.wait()
    for j in range(1, inner):
        copy_ay(j).wait()
    if has_sum:
        total = sum_x[...]
        for j in range(1, inner):
            sum_a(j).wait()
            total = total + sum_stage[j]
        row_sum[...] = total
    for j in range(1, outer):
        copy_by(j).start()
    for j in range(1, outer):
        copy_az(j).wait()
    for j in range(1, inner):
        copy_bz(j).start()
    out_y[0] = stage_y[...]
    out_z[0] = stage_z[...]
    if has_sum:
        sum_out[0, 0] = total
        for c, j in sum_peers:
            sum_b(c, j).start()
    for j in range(1, group):
        mid_copy(j).wait()
    for j in range(1, outer):
        copy_by(j).wait()
    if has_sum:
        for c, j in sum_peers:
            sum_b(c, j).wait()
    for j in range(1, inner):
        copy_bz(j).wait()
    if has_sum:
        total = sum_out[0, 0]
        for c, j in sum_peers:
            total = total + sum_out[c, j]
        sum_total[...] = total


def ctx_gather(mid_x, top_x, group, tag, sum_x=None, raw=False):
    count = lax.axis_size("ctx")
    inner = RING
    outer = count // inner
    half = (top_x.shape[0] + 1) // 2
    top_y = top_x[:half]
    top_z = top_x[half:]
    has_sum = sum_x is not None
    operands = (mid_x, top_y, top_z) + ((sum_x,) if has_sum else ())
    out_shape = (
        jax.ShapeDtypeStruct((group,) + mid_x.shape, mid_x.dtype),
        jax.ShapeDtypeStruct((outer, inner) + top_y.shape, top_x.dtype),
        jax.ShapeDtypeStruct((inner, outer) + top_z.shape, top_x.dtype),
    )
    scratch = [
        pltpu.VMEM((inner,) + top_y.shape, top_x.dtype),
        pltpu.VMEM((outer,) + top_z.shape, top_x.dtype),
    ]
    if has_sum:
        out_shape += (jax.ShapeDtypeStruct(sum_x.shape, sum_x.dtype),)
        scratch += [
            pltpu.VMEM((inner,) + sum_x.shape, sum_x.dtype),
            pltpu.VMEM(sum_x.shape, sum_x.dtype),
            pltpu.VMEM((2, outer) + sum_x.shape, sum_x.dtype),
        ]
    for size in (group, inner, outer, outer, inner):
        scratch += [pltpu.SemaphoreType.DMA((size,)), pltpu.SemaphoreType.DMA((size,))]
    scratch.append(pltpu.SemaphoreType.DMA((2,)))
    if has_sum:
        for size in (inner, 2 * outer):
            scratch += [pltpu.SemaphoreType.DMA((size,)), pltpu.SemaphoreType.DMA((size,))]
    outs = pl.pallas_call(
        functools.partial(gather_kernel, group, inner, has_sum),
        out_shape=out_shape,
        in_specs=[pl.BlockSpec(memory_space=pltpu.VMEM)] * len(operands),
        out_specs=(pl.BlockSpec(memory_space=pltpu.VMEM),) * len(out_shape),
        scratch_shapes=scratch,
        compiler_params=pltpu.CompilerParams(collective_id=tag, has_side_effects=True),
    )(*operands)
    if raw:
        return outs
    top_all = jnp.concatenate([outs[1], jnp.transpose(outs[2], (1, 0, 2, 3))], 2)
    return (outs[0], top_all) + tuple(outs[3:])


def token_major(rows):
    parts = [rows[:, h, :] for h in range(rows.shape[1])]
    return jnp.concatenate(parts, axis=1).astype(jnp.bfloat16)[None]


def lane_dense(block):
    return block.reshape(-1, HEAD_DIM)


def pick_rows(source_rows, dilation, shifts):
    row_count, head_count, head_width = source_rows.shape
    grouped = source_rows.reshape(row_count // dilation, dilation, head_count, head_width)
    hit_mask = jnp.arange(dilation, dtype=jnp.int32).reshape(1, dilation, 1, 1) == shifts.reshape(
        1, 1, head_count, 1
    )
    chosen = jnp.where(hit_mask, grouped, jnp.zeros((), source_rows.dtype))
    return jnp.sum(chosen, axis=1, dtype=source_rows.dtype)


def place_rows(row_values, dilation, shifts):
    row_count, head_count, head_width = row_values.shape
    hit_mask = jnp.arange(dilation, dtype=jnp.int32).reshape(1, dilation, 1, 1) == shifts.reshape(
        1, 1, head_count, 1
    )
    spread = jnp.where(hit_mask, row_values[:, None], jnp.zeros((), row_values.dtype))
    return spread.reshape(row_count * dilation, head_count, head_width)


def level_scores(q_rows, k_rows):
    score_scale = 1.0 / math.sqrt(q_rows.shape[-1])
    return (
        jnp.einsum("qhe,khe->hqk", q_rows, k_rows, preferred_element_type=jnp.float32) * score_scale
    )


def attend(q_rows, k_rows, v_rows):
    scores = level_scores(q_rows, k_rows)
    row_max = jnp.max(scores, axis=-1, keepdims=True)
    log_total = row_max[..., 0] + jnp.log(jnp.sum(jnp.exp(scores - row_max), axis=-1))
    soft_rows = jnp.exp(scores - log_total[..., None]).astype(jnp.bfloat16)
    level_out = jnp.einsum("hqk,khe->qhe", soft_rows, v_rows, preferred_element_type=jnp.float32)
    return (level_out, log_total.T)


def score_grads(q_rows, k_rows, v_rows, log_total, grad_low, row_shift):
    score_scale = 1.0 / math.sqrt(q_rows.shape[-1])
    scores = level_scores(q_rows, k_rows)
    exact_soft = jnp.exp(scores - log_total.T[..., None])
    prob_grad = jnp.einsum("qhe,khe->hqk", grad_low, v_rows, preferred_element_type=jnp.float32)
    score_grad = (exact_soft * (prob_grad + row_shift.T[..., None]) * score_scale).astype(
        jnp.bfloat16
    )
    return (score_grad, exact_soft.astype(jnp.bfloat16))


def key_parts(score_grad, soft_low, q_rows, grad_low):
    k_part = jnp.einsum("hqk,qhe->khe", score_grad, q_rows, preferred_element_type=jnp.float32)
    v_part = jnp.einsum("hqk,qhe->khe", soft_low, grad_low, preferred_element_type=jnp.float32)
    return (k_part, v_part)


def query_part(score_grad, k_rows):
    return jnp.einsum("hqk,khe->qhe", score_grad, k_rows, preferred_element_type=jnp.float32)


def split_qkv(packed, head_count):
    width = head_count * HEAD_DIM
    shape = (packed.shape[0], head_count, HEAD_DIM)
    return tuple(packed[:, i * width : (i + 1) * width].reshape(shape) for i in range(3))


def split_wide(values):
    high = values.astype(jnp.bfloat16)
    low = (values - high.astype(jnp.float32)).astype(jnp.bfloat16)
    return high, low


def join_wide(high, low):
    return high.astype(jnp.float32) + low.astype(jnp.float32)


def pack_grads(grad_low, row_shift, width):
    rows = grad_low.shape[0]
    high, low = split_wide(row_shift)
    used = grad_low.shape[1] * grad_low.shape[2] + 2 * row_shift.shape[1]
    return jnp.concatenate(
        [grad_low.reshape(rows, -1), high, low, jnp.zeros((rows, width - used), jnp.bfloat16)], 1
    )


def unpack_grads(packed, head_count):
    width = head_count * HEAD_DIM
    grad_low = packed[:, :width].reshape(-1, head_count, HEAD_DIM)
    return grad_low, join_wide(
        packed[:, width : width + head_count], packed[:, width + head_count : width + 2 * head_count]
    )


def shards(queries, keys, values, grad_y, out_gain, offsets):
    tokens = queries.shape[1]
    flat_width = queries.shape[2]
    head_count = flat_width // HEAD_DIM
    row_shape = (tokens, head_count, HEAD_DIM)
    q_own = queries[0].reshape(row_shape)
    k_own = keys[0].reshape(row_shape)
    v_own = values[0].reshape(row_shape)
    ctx_size = lax.axis_size("ctx")
    mid_shift = offsets[0]
    top_shift = offsets[1]
    positions = jnp.arange(tokens, dtype=jnp.int32)
    mid_hit = (positions % R1)[:, None] == mid_shift[None, :]
    top_hit = (positions % ctx_size)[:, None] == top_shift[None, :]
    mid_pack = jnp.concatenate(
        [pick_rows(x, R1, mid_shift).reshape(-1, flat_width) for x in (q_own, k_own, v_own)], 1
    )
    top_pack = jnp.concatenate(
        [pick_rows(x, ctx_size, top_shift) for x in (q_own, k_own, v_own)], 1
    )
    mid_rows = mid_pack.shape[0]
    top_rows = top_pack.shape[0]
    mid_all, rows_y, rows_z = ctx_gather(mid_pack, lane_dense(top_pack), SPAN, 0, raw=True)
    mid_all = mid_all.reshape(-1, mid_pack.shape[1])
    mid_q, mid_k, mid_v = split_qkv(mid_all, head_count)
    rows_y = rows_y.reshape((ctx_size,) + rows_y.shape[2:])
    rows_z = jnp.transpose(rows_z, (1, 0, 2, 3)).reshape((ctx_size,) + rows_z.shape[2:])
    top_q, top_k, top_v = (
        jnp.stack(
            [rows_y[:, p * head_count : (p + 1) * head_count],
             rows_z[:, p * head_count : (p + 1) * head_count]], 1
        ).reshape(-1, head_count, HEAD_DIM)
        for p in range(3)
    )
    base_out, base_total = attend(q_own, k_own, v_own)
    mid_out_all, mid_total_all = attend(mid_q, mid_k, mid_v)
    top_out_all, top_total_all = attend(top_q, top_k, top_v)
    mid_out = mid_out_all[:mid_rows]
    mid_total = mid_total_all[:mid_rows]
    top_out = top_out_all[:top_rows]
    top_total = top_total_all[:top_rows]
    mid_full = place_rows(mid_total[..., None], R1, mid_shift)[..., 0]
    top_full = place_rows(top_total[..., None], ctx_size, top_shift)[..., 0]
    row_max = jnp.maximum(base_total, jnp.where(mid_hit, mid_full, base_total))
    row_max = jnp.maximum(row_max, jnp.where(top_hit, top_full, base_total))
    base_expo = jnp.exp(base_total - row_max)
    mid_expo = jnp.where(mid_hit, jnp.exp(mid_full - row_max), 0.0)
    top_expo = jnp.where(top_hit, jnp.exp(top_full - row_max), 0.0)
    denom = base_expo + mid_expo + top_expo
    base_share = base_expo / denom
    mid_share = mid_expo / denom
    top_share = top_expo / denom
    attn = (
        base_share[..., None] * base_out
        + mid_share[..., None] * place_rows(mid_out, R1, mid_shift)
        + top_share[..., None] * place_rows(top_out, ctx_size, top_shift)
    )
    inv_rms = lax.rsqrt(jnp.mean(attn * attn, axis=-1, keepdims=True) + EPS)
    normed = attn * inv_rms
    gain_rows = out_gain.reshape(head_count, HEAD_DIM)
    attended = token_major(normed * gain_rows)
    grad_full = grad_y[0].reshape(row_shape).astype(jnp.float32)
    gain_part = jnp.sum(grad_full * normed, axis=0).reshape(flat_width)
    grad_norm = grad_full * gain_rows
    grad_attn = inv_rms * (
        grad_norm - normed * jnp.mean(grad_norm * normed, axis=-1, keepdims=True)
    )
    inner = jnp.sum(grad_attn * attn, axis=-1)
    base_low = (base_share[..., None] * grad_attn).astype(jnp.bfloat16)
    base_shift = -(base_share * inner)
    base_grad, base_soft = score_grads(q_own, k_own, v_own, base_total, base_low, base_shift)
    base_dq = query_part(base_grad, k_own)
    base_dk, base_dv = key_parts(base_grad, base_soft, q_own, base_low)

    mid_sel = pick_rows(mid_share[..., None], R1, mid_shift)[..., 0]
    mid_low = (mid_sel[..., None] * pick_rows(grad_attn, R1, mid_shift)).astype(jnp.bfloat16)
    mid_row_shift = -(mid_sel * pick_rows(inner[..., None], R1, mid_shift)[..., 0])
    top_sel = pick_rows(top_share[..., None], ctx_size, top_shift)[..., 0]
    top_low = (top_sel[..., None] * pick_rows(grad_attn, ctx_size, top_shift)).astype(jnp.bfloat16)
    top_row_shift = -(top_sel * pick_rows(inner[..., None], ctx_size, top_shift)[..., 0])

    shift_high, shift_low = split_wide(top_row_shift)
    shift_block = jnp.concatenate([shift_high, shift_low], 1)
    shift_block = jnp.pad(shift_block, ((0, 0), (0, HEAD_DIM - shift_block.shape[1])))[:, None]
    top_block = jnp.concatenate([top_low, shift_block], 1)
    mid_gathered, grads_y, grads_z, gain_rows_sum = ctx_gather(
        pack_grads(mid_low, mid_row_shift, flat_width + HEAD_DIM),
        lane_dense(top_block),
        SPAN,
        1,
        sum_x=lane_dense(gain_part),
        raw=True,
    )
    mid_low_all, mid_shift_all = unpack_grads(
        mid_gathered.reshape(-1, mid_gathered.shape[-1]), head_count
    )
    grads_y = grads_y.reshape((ctx_size,) + grads_y.shape[2:])
    grads_z = jnp.transpose(grads_z, (1, 0, 2, 3)).reshape((ctx_size,) + grads_z.shape[2:])
    both = jnp.stack([grads_y, grads_z], 1).reshape((-1,) + grads_y.shape[1:])
    top_low_all = both[:, :head_count]
    top_shift_all = join_wide(
        both[:, head_count, :head_count], both[:, head_count, head_count : 2 * head_count]
    )
    gain_grad = gain_rows_sum.reshape(flat_width)

    mid_grad, mid_soft = score_grads(
        mid_q, mid_k, mid_v, mid_total_all, mid_low_all, mid_shift_all
    )
    mid_dq = query_part(mid_grad[:, :mid_rows], mid_k)
    mid_dk, mid_dv = key_parts(
        mid_grad[:, :, :mid_rows], mid_soft[:, :, :mid_rows], mid_q, mid_low_all
    )
    top_grad, top_soft = score_grads(
        top_q, top_k, top_v, top_total_all, top_low_all, top_shift_all
    )
    top_dq = query_part(top_grad[:, :top_rows], top_k)
    top_dk, top_dv = key_parts(
        top_grad[:, :, :top_rows], top_soft[:, :, :top_rows], top_q, top_low_all
    )
    query_grad = (
        base_dq + place_rows(mid_dq, R1, mid_shift) + place_rows(top_dq, ctx_size, top_shift)
    )
    key_grad = base_dk + place_rows(mid_dk, R1, mid_shift) + place_rows(top_dk, ctx_size, top_shift)
    value_grad = (
        base_dv + place_rows(mid_dv, R1, mid_shift) + place_rows(top_dv, ctx_size, top_shift)
    )
    return (
        attended,
        token_major(query_grad),
        token_major(key_grad),
        token_major(value_grad),
        gain_grad,
    )


def solution(mesh):
    in_specs = (
        P("dp", "ctx", "head"),
        P("dp", "ctx", "head"),
        P("dp", "ctx", "head"),
        P("dp", "ctx", "head"),
        P("head"),
        P(None, "head"),
    )
    out_specs = (
        P("dp", "ctx", "head"),
        P("dp", "ctx", "head"),
        P("dp", "ctx", "head"),
        P("dp", "ctx", "head"),
        P("head"),
    )
    return jax.shard_map(shards, mesh=mesh, in_specs=in_specs, out_specs=out_specs, check_vma=False)
```

```python
import functools
import math

import jax
import jax.numpy as jnp
from jax import lax
from jax.experimental import pallas as pl
from jax.experimental.pallas import tpu as pltpu
from jax.sharding import PartitionSpec as P

HEAD_DIM = 128
SPAN = 4
R1 = 8
RING = 8


EPS = 1e-06


def gather_kernel(group, inner, has_sum, *refs):
    if has_sum:
        (mid_x, top_y, top_z, sum_x, mid_out, out_y, out_z, sum_total,
         stage_y, stage_z, sum_stage, row_sum, sum_out, *sems) = refs
    else:
        (mid_x, top_y, top_z, mid_out, out_y, out_z, stage_y, stage_z, *sems) = refs
    (send_mid, recv_mid, send_ay, recv_ay, send_by, recv_by,
     send_az, recv_az, send_bz, recv_bz, local_sem) = sems[:11]
    if has_sum:
        send_sa, recv_sa, send_sb, recv_sb = sems[11:]
    count = lax.axis_size("ctx")
    outer = count // inner
    me = lax.axis_index("ctx")
    row = lax.axis_index("dp")
    col = lax.axis_index("head")
    lo = me % inner
    hi = me // inner
    base = me - me % group
    mesh_ids = pl.DeviceIdType.MESH

    def inner_peer(j):
        return hi * inner + lax.rem(lo + j, inner)

    def outer_peer(j):
        return lax.rem(hi + j, outer) * inner + lo

    barrier = pltpu.get_barrier_semaphore()
    for j in range(1, inner):
        pl.semaphore_signal(barrier, 1, device_id=(row, inner_peer(j), col), device_id_type=mesh_ids)
    for j in range(1, outer):
        pl.semaphore_signal(barrier, 1, device_id=(row, outer_peer(j), col), device_id_type=mesh_ids)
    if has_sum:
        for j in range(outer):
            pl.semaphore_signal(
                barrier, 1, device_id=(1 - row, outer_peer(j), col), device_id_type=mesh_ids
            )
    pl.semaphore_wait(barrier, inner + outer - 2 + (outer if has_sum else 0))

    def remote(src, dst, send, recv, peer, core=None):
        return pltpu.make_async_remote_copy(
            src, dst, send, recv, device_id=(row if core is None else core, peer, col),
            device_id_type=mesh_ids,
        )

    def mid_copy(j):
        peer = base + lax.rem(me % group + j, group)
        return remote(mid_x, mid_out.at[j], send_mid.at[j], recv_mid.at[j], peer)

    def copy_ay(j):
        return remote(top_y, stage_y.at[j], send_ay.at[j], recv_ay.at[j], inner_peer(j))

    def copy_by(j):
        return remote(stage_y, out_y.at[j], send_by.at[j], recv_by.at[j], outer_peer(j))

    def copy_az(j):
        return remote(top_z, stage_z.at[j], send_az.at[j], recv_az.at[j], outer_peer(j))

    def copy_bz(j):
        return remote(stage_z, out_z.at[j], send_bz.at[j], recv_bz.at[j], inner_peer(j))

    def sum_a(j):
        return remote(sum_x, sum_stage.at[j], send_sa.at[j], recv_sa.at[j], inner_peer(j))

    def sum_b(c, j):
        slot = c * outer + j
        return remote(
            row_sum, sum_out.at[c, j], send_sb.at[slot], recv_sb.at[slot], outer_peer(j),
            core=(1 - row) if c else row,
        )

    sum_peers = [(0, j) for j in range(1, outer)] + [(1, j) for j in range(outer)]

    for j in range(1, group):
        mid_copy(j).start()
    for j in range(1, inner):
        copy_ay(j).start()
    for j in range(1, outer):
        copy_az(j).start()
    if has_sum:
        for j in range(1, inner):
            sum_a(j).start()
    own_y = pltpu.make_async_copy(top_y, stage_y.at[0], local_sem.at[0])
    own_z = pltpu.make_async_copy(top_z, stage_z.at[0], local_sem.at[1])
    own_y.start()
    own_z.start()
    mid_out[0] = mid_x[...]
    own_y.wait()
    own_z.wait()
    for j in range(1, inner):
        copy_ay(j).wait()
    if has_sum:
        total = sum_x[...]
        for j in range(1, inner):
            sum_a(j).wait()
            total = total + sum_stage[j]
        row_sum[...] = total
    for j in range(1, outer):
        copy_by(j).start()
    for j in range(1, outer):
        copy_az(j).wait()
    for j in range(1, inner):
        copy_bz(j).start()
    out_y[0] = stage_y[...]
    out_z[0] = stage_z[...]
    if has_sum:
        sum_out[0, 0] = total
        for c, j in sum_peers:
            sum_b(c, j).start()
    for j in range(1, group):
        mid_copy(j).wait()
    for j in range(1, outer):
        copy_by(j).wait()
    if has_sum:
        for c, j in sum_peers:
            sum_b(c, j).wait()
    for j in range(1, inner):
        copy_bz(j).wait()
    if has_sum:
        total = sum_out[0, 0]
        for c, j in sum_peers:
            total = total + sum_out[c, j]
        sum_total[...] = total


def ctx_gather(mid_x, top_x, group, tag, sum_x=None, raw=False):
    count = lax.axis_size("ctx")
    inner = RING
    outer = count // inner
    half = (top_x.shape[0] + 1) // 2
    top_y = top_x[:half]
    top_z = top_x[half:]
    has_sum = sum_x is not None
    operands = (mid_x, top_y, top_z) + ((sum_x,) if has_sum else ())
    out_shape = (
        jax.ShapeDtypeStruct((group,) + mid_x.shape, mid_x.dtype),
        jax.ShapeDtypeStruct((outer, inner) + top_y.shape, top_x.dtype),
        jax.ShapeDtypeStruct((inner, outer) + top_z.shape, top_x.dtype),
    )
    scratch = [
        pltpu.VMEM((inner,) + top_y.shape, top_x.dtype),
        pltpu.VMEM((outer,) + top_z.shape, top_x.dtype),
    ]
    if has_sum:
        out_shape += (jax.ShapeDtypeStruct(sum_x.shape, sum_x.dtype),)
        scratch += [
            pltpu.VMEM((inner,) + sum_x.shape, sum_x.dtype),
            pltpu.VMEM(sum_x.shape, sum_x.dtype),
            pltpu.VMEM((2, outer) + sum_x.shape, sum_x.dtype),
        ]
    for size in (group, inner, outer, outer, inner):
        scratch += [pltpu.SemaphoreType.DMA((size,)), pltpu.SemaphoreType.DMA((size,))]
    scratch.append(pltpu.SemaphoreType.DMA((2,)))
    if has_sum:
        for size in (inner, 2 * outer):
            scratch += [pltpu.SemaphoreType.DMA((size,)), pltpu.SemaphoreType.DMA((size,))]
    outs = pl.pallas_call(
        functools.partial(gather_kernel, group, inner, has_sum),
        out_shape=out_shape,
        in_specs=[pl.BlockSpec(memory_space=pltpu.VMEM)] * len(operands),
        out_specs=(pl.BlockSpec(memory_space=pltpu.VMEM),) * len(out_shape),
        scratch_shapes=scratch,
        compiler_params=pltpu.CompilerParams(collective_id=tag, has_side_effects=True),
    )(*operands)
    if raw:
        return outs
    top_all = jnp.concatenate([outs[1], jnp.transpose(outs[2], (1, 0, 2, 3))], 2)
    return (outs[0], top_all) + tuple(outs[3:])


def token_major(rows):
    parts = [rows[:, h, :] for h in range(rows.shape[1])]
    return jnp.concatenate(parts, axis=1).astype(jnp.bfloat16)[None]


def lane_dense(block):
    return block.reshape(-1, HEAD_DIM)


def pick_rows(source_rows, dilation, shifts):
    row_count, head_count, head_width = source_rows.shape
    grouped = source_rows.reshape(row_count // dilation, dilation, head_count, head_width)
    hit_mask = jnp.arange(dilation, dtype=jnp.int32).reshape(1, dilation, 1, 1) == shifts.reshape(
        1, 1, head_count, 1
    )
    chosen = jnp.where(hit_mask, grouped, jnp.zeros((), source_rows.dtype))
    return jnp.sum(chosen, axis=1, dtype=source_rows.dtype)


def place_rows(row_values, dilation, shifts):
    row_count, head_count, head_width = row_values.shape
    hit_mask = jnp.arange(dilation, dtype=jnp.int32).reshape(1, dilation, 1, 1) == shifts.reshape(
        1, 1, head_count, 1
    )
    spread = jnp.where(hit_mask, row_values[:, None], jnp.zeros((), row_values.dtype))
    return spread.reshape(row_count * dilation, head_count, head_width)


def level_scores(q_rows, k_rows):
    score_scale = 1.0 / math.sqrt(q_rows.shape[-1])
    return (
        jnp.einsum("qhe,khe->hqk", q_rows, k_rows, preferred_element_type=jnp.float32) * score_scale
    )


def attend(q_rows, k_rows, v_rows):
    scores = level_scores(q_rows, k_rows)
    row_max = jnp.max(scores, axis=-1, keepdims=True)
    log_total = row_max[..., 0] + jnp.log(jnp.sum(jnp.exp(scores - row_max), axis=-1))
    soft_rows = jnp.exp(scores - log_total[..., None]).astype(jnp.bfloat16)
    level_out = jnp.einsum("hqk,khe->qhe", soft_rows, v_rows, preferred_element_type=jnp.float32)
    return (level_out, log_total.T)


def score_grads(q_rows, k_rows, v_rows, log_total, grad_low, row_shift):
    score_scale = 1.0 / math.sqrt(q_rows.shape[-1])
    scores = level_scores(q_rows, k_rows)
    exact_soft = jnp.exp(scores - log_total.T[..., None])
    prob_grad = jnp.einsum("qhe,khe->hqk", grad_low, v_rows, preferred_element_type=jnp.float32)
    score_grad = (exact_soft * (prob_grad + row_shift.T[..., None]) * score_scale).astype(
        jnp.bfloat16
    )
    return (score_grad, exact_soft.astype(jnp.bfloat16))


def key_parts(score_grad, soft_low, q_rows, grad_low):
    k_part = jnp.einsum("hqk,qhe->khe", score_grad, q_rows, preferred_element_type=jnp.float32)
    v_part = jnp.einsum("hqk,qhe->khe", soft_low, grad_low, preferred_element_type=jnp.float32)
    return (k_part, v_part)


def query_part(score_grad, k_rows):
    return jnp.einsum("hqk,khe->qhe", score_grad, k_rows, preferred_element_type=jnp.float32)


def split_qkv(packed, head_count):
    width = head_count * HEAD_DIM
    shape = (packed.shape[0], head_count, HEAD_DIM)
    return tuple(packed[:, i * width : (i + 1) * width].reshape(shape) for i in range(3))


def split_wide(values):
    high = values.astype(jnp.bfloat16)
    low = (values - high.astype(jnp.float32)).astype(jnp.bfloat16)
    return high, low


def join_wide(high, low):
    return high.astype(jnp.float32) + low.astype(jnp.float32)


def pack_grads(grad_low, row_shift, width):
    rows = grad_low.shape[0]
    high, low = split_wide(row_shift)
    used = grad_low.shape[1] * grad_low.shape[2] + 2 * row_shift.shape[1]
    return jnp.concatenate(
        [grad_low.reshape(rows, -1), high, low, jnp.zeros((rows, width - used), jnp.bfloat16)], 1
    )


def unpack_grads(packed, head_count):
    width = head_count * HEAD_DIM
    grad_low = packed[:, :width].reshape(-1, head_count, HEAD_DIM)
    return grad_low, join_wide(
        packed[:, width : width + head_count], packed[:, width + head_count : width + 2 * head_count]
    )


def shards(queries, keys, values, grad_y, out_gain, offsets):
    tokens = queries.shape[1]
    flat_width = queries.shape[2]
    head_count = flat_width // HEAD_DIM
    row_shape = (tokens, head_count, HEAD_DIM)
    q_own = queries[0].reshape(row_shape)
    k_own = keys[0].reshape(row_shape)
    v_own = values[0].reshape(row_shape)
    ctx_size = lax.axis_size("ctx")
    mid_shift = offsets[0]
    top_shift = offsets[1]
    positions = jnp.arange(tokens, dtype=jnp.int32)
    mid_hit = (positions % R1)[:, None] == mid_shift[None, :]
    top_hit = (positions % ctx_size)[:, None] == top_shift[None, :]
    mid_pack = jnp.concatenate(
        [pick_rows(x, R1, mid_shift).reshape(-1, flat_width) for x in (q_own, k_own, v_own)], 1
    )
    top_blocks = jnp.concatenate(
        [pick_rows(x, ctx_size, top_shift) for x in (q_own, k_own, v_own)], 1
    )
    top_pack = jnp.pad(top_blocks, ((0, 0), (0, 16 - top_blocks.shape[1]), (0, 0)))
    mid_rows = mid_pack.shape[0]
    top_rows = top_pack.shape[0]
    mid_all, rows_y, rows_z = ctx_gather(mid_pack, lane_dense(top_pack), SPAN, 0, raw=True)
    mid_all = mid_all.reshape(-1, mid_pack.shape[1])
    mid_q, mid_k, mid_v = split_qkv(mid_all, head_count)
    rows_y = rows_y.reshape((ctx_size,) + rows_y.shape[2:])
    rows_z = jnp.transpose(rows_z, (1, 0, 2, 3)).reshape((ctx_size,) + rows_z.shape[2:])
    top_q, top_k, top_v = (
        jnp.stack(
            [rows_y[:, p * head_count : (p + 1) * head_count],
             rows_z[:, p * head_count : (p + 1) * head_count]], 1
        ).reshape(-1, head_count, HEAD_DIM)
        for p in range(3)
    )
    base_out, base_total = attend(q_own, k_own, v_own)
    mid_out_all, mid_total_all = attend(mid_q, mid_k, mid_v)
    top_out_all, top_total_all = attend(top_q, top_k, top_v)
    mid_out = mid_out_all[:mid_rows]
    mid_total = mid_total_all[:mid_rows]
    top_out = top_out_all[:top_rows]
    top_total = top_total_all[:top_rows]
    mid_full = place_rows(mid_total[..., None], R1, mid_shift)[..., 0]
    top_full = place_rows(top_total[..., None], ctx_size, top_shift)[..., 0]
    row_max = jnp.maximum(base_total, jnp.where(mid_hit, mid_full, base_total))
    row_max = jnp.maximum(row_max, jnp.where(top_hit, top_full, base_total))
    base_expo = jnp.exp(base_total - row_max)
    mid_expo = jnp.where(mid_hit, jnp.exp(mid_full - row_max), 0.0)
    top_expo = jnp.where(top_hit, jnp.exp(top_full - row_max), 0.0)
    denom = base_expo + mid_expo + top_expo
    base_share = base_expo / denom
    mid_share = mid_expo / denom
    top_share = top_expo / denom
    attn = (
        base_share[..., None] * base_out
        + mid_share[..., None] * place_rows(mid_out, R1, mid_shift)
        + top_share[..., None] * place_rows(top_out, ctx_size, top_shift)
    )
    inv_rms = lax.rsqrt(jnp.mean(attn * attn, axis=-1, keepdims=True) + EPS)
    normed = attn * inv_rms
    gain_rows = out_gain.reshape(head_count, HEAD_DIM)
    attended = token_major(normed * gain_rows)
    grad_full = grad_y[0].reshape(row_shape).astype(jnp.float32)
    gain_part = jnp.sum(grad_full * normed, axis=0).reshape(flat_width)
    grad_norm = grad_full * gain_rows
    grad_attn = inv_rms * (
        grad_norm - normed * jnp.mean(grad_norm * normed, axis=-1, keepdims=True)
    )
    inner = jnp.sum(grad_attn * attn, axis=-1)
    base_low = (base_share[..., None] * grad_attn).astype(jnp.bfloat16)
    base_shift = -(base_share * inner)
    base_grad, base_soft = score_grads(q_own, k_own, v_own, base_total, base_low, base_shift)
    base_dq = query_part(base_grad, k_own)
    base_dk, base_dv = key_parts(base_grad, base_soft, q_own, base_low)

    mid_sel = pick_rows(mid_share[..., None], R1, mid_shift)[..., 0]
    mid_low = (mid_sel[..., None] * pick_rows(grad_attn, R1, mid_shift)).astype(jnp.bfloat16)
    mid_row_shift = -(mid_sel * pick_rows(inner[..., None], R1, mid_shift)[..., 0])
    top_sel = pick_rows(top_share[..., None], ctx_size, top_shift)[..., 0]
    top_low = (top_sel[..., None] * pick_rows(grad_attn, ctx_size, top_shift)).astype(jnp.bfloat16)
    top_row_shift = -(top_sel * pick_rows(inner[..., None], ctx_size, top_shift)[..., 0])

    shift_high, shift_low = split_wide(top_row_shift)
    shift_block = jnp.concatenate([shift_high, shift_low], 1)
    shift_block = jnp.pad(shift_block, ((0, 0), (0, HEAD_DIM - shift_block.shape[1])))[:, None]
    top_block = jnp.concatenate([top_low, shift_block], 1)
    mid_gathered, grads_y, grads_z, gain_rows_sum = ctx_gather(
        pack_grads(mid_low, mid_row_shift, flat_width + HEAD_DIM),
        lane_dense(top_block),
        SPAN,
        1,
        sum_x=lane_dense(gain_part),
        raw=True,
    )
    mid_low_all, mid_shift_all = unpack_grads(
        mid_gathered.reshape(-1, mid_gathered.shape[-1]), head_count
    )
    grads_y = grads_y.reshape((ctx_size,) + grads_y.shape[2:])
    grads_z = jnp.transpose(grads_z, (1, 0, 2, 3)).reshape((ctx_size,) + grads_z.shape[2:])
    both = jnp.stack([grads_y, grads_z], 1).reshape((-1,) + grads_y.shape[1:])
    top_low_all = both[:, :head_count]
    top_shift_all = join_wide(
        both[:, head_count, :head_count], both[:, head_count, head_count : 2 * head_count]
    )
    gain_grad = gain_rows_sum.reshape(flat_width)

    mid_grad, mid_soft = score_grads(
        mid_q, mid_k, mid_v, mid_total_all, mid_low_all, mid_shift_all
    )
    mid_dq = query_part(mid_grad[:, :mid_rows], mid_k)
    mid_dk, mid_dv = key_parts(
        mid_grad[:, :, :mid_rows], mid_soft[:, :, :mid_rows], mid_q, mid_low_all
    )
    top_grad, top_soft = score_grads(
        top_q, top_k, top_v, top_total_all, top_low_all, top_shift_all
    )
    top_dq = query_part(top_grad[:, :top_rows], top_k)
    top_dk, top_dv = key_parts(
        top_grad[:, :, :top_rows], top_soft[:, :, :top_rows], top_q, top_low_all
    )
    query_grad = (
        base_dq + place_rows(mid_dq, R1, mid_shift) + place_rows(top_dq, ctx_size, top_shift)
    )
    key_grad = base_dk + place_rows(mid_dk, R1, mid_shift) + place_rows(top_dk, ctx_size, top_shift)
    value_grad = (
        base_dv + place_rows(mid_dv, R1, mid_shift) + place_rows(top_dv, ctx_size, top_shift)
    )
    return (
        attended,
        token_major(query_grad),
        token_major(key_grad),
        token_major(value_grad),
        gain_grad,
    )


def solution(mesh):
    in_specs = (
        P("dp", "ctx", "head"),
        P("dp", "ctx", "head"),
        P("dp", "ctx", "head"),
        P("dp", "ctx", "head"),
        P("head"),
        P(None, "head"),
    )
    out_specs = (
        P("dp", "ctx", "head"),
        P("dp", "ctx", "head"),
        P("dp", "ctx", "head"),
        P("dp", "ctx", "head"),
        P("head"),
    )
    return jax.shard_map(shards, mesh=mesh, in_specs=in_specs, out_specs=out_specs, check_vma=False)
```
